32 devices in a mesh: batch: 16 (over z, x, core), mlp: 2 (over y).
Axes of the slice: x: 2, y: 2, z: 4, core: 2. Of those that a mesh axis runs over, the one named last changes fastest.
Arguments:
- inputs: bfloat16 [16384, 768], P(('batch', 'mlp')), may hold values from -6 to 6
- doc_lengths: int32 [32, 3], P(('batch', 'mlp')), may hold values from 1 to 256, 512 in all within a row
- ln1_gain: bfloat16 [768], replicated, may hold values from 0.5 to 1.5
- ln1_bias: bfloat16 [768], replicated, may hold values from -1.75 to 1.75
- attn_in: bfloat16 [768, 2304], replicated, may hold values from -0.21875 to 0.21875
- qv_bias: bfloat16 [2, 768], replicated, may hold values from -3 to 3
- attn_out: bfloat16 [768, 768], replicated, may hold values from -0.875 to 0.875
- attn_out_bias: bfloat16 [768], replicated, may hold values from -1.75 to 1.75
- ln2_gain: bfloat16 [768], replicated, may hold values from 0.5 to 1.5
- second_norm_bias: bfloat16 [768], replicated, may hold values from -1.75 to 1.75
- mlp_in: bfloat16 [768, 3072], P(None, 'mlp'), may hold values from -0.21875 to 0.21875
- mlp_in_bias: bfloat16 [3072], P('mlp'), may hold values from -3 to 3
- mlp_out: bfloat16 [3072, 768], P('mlp'), may hold values from -0.109375 to 0.109375
- mlp_out_bias: bfloat16 [768], replicated, may hold values from -1.75 to 1.75
- cotangent: bfloat16 [16384, 768], P(('batch', 'mlp')), may hold values from -6 to 6
Outputs:
- layer_output: bfloat16 [16384, 768], P(('batch', 'mlp'))
- input_grad: bfloat16 [16384, 768], P(('batch', 'mlp'))
- ln1_gain_grad: float32 [768], replicated
- ln1_bias_grad: float32 [768], replicated
- attn_in_grad: float32 [768, 2304], replicated
- qv_bias_grad: float32 [2, 768], replicated
- attn_out_grad: float32 [768, 768], replicated
- attn_out_bias_grad: float32 [768], replicated
- ln2_gain_grad: float32 [768], replicated
- ln2_bias_grad: float32 [768], replicated
- mlp_in_grad: float32 [768, 3072], P(None, 'mlp')
- perceptron_input_bias_gradient: float32 [3072], P('mlp')
- mlp_out_grad: float32 [3072, 768], P('mlp')
- mlp_out_bias_grad: float32 [768], replicated
The draws below stay inside these ranges and needn't reach their ends.
Inputs may be any that keep to these rules, and one draw needn't show every extreme that they name: `doc_lengths`: row s holds the lengths of the 3 documents packed in segment s, in order; they sum to 512. A segment's first document continues the last document of the segment before it in its stream.
All inputs are finite; a program needn't handle non-finite values.
Results may differ from the reference program's by a relative error of at most 0.019.
Values may be sent and summed in bfloat16 or wider, within the bound.
No kernel may reach another device: no remote copies, remote signals or barrier semaphores. Data moves between devices by JAX's collectives and lax.ppermute only.
A program may use at most 192 MiB of HBM per device.

```python
import math
import jax
import jax.numpy as jnp
import numpy as np
from jax import lax

D = 768
H = 12
HD = 64
FF = 3072
NB = 512
L = 512
NDOC = 3
STREAM_SEGMENTS = 2
SEGMENT_TOTAL = 32
TOKENS = 16384
N_MLP = 2


def block_scale(rng, shape, split, least, largest):
    def one(position, parts):
        heights = jax.random.uniform(jax.random.fold_in(jax.random.fold_in(rng, 6), position), (parts,), jnp.float32, least / len(split), largest / len(split))
        return jnp.repeat(jnp.exp(heights), shape[position] // parts).reshape((-1,) + (1,) * (len(shape) - position - 1))

    factor_of = one(*split[0])
    for cut in split[1:]:
        factor_of = factor_of * one(*cut)
    return factor_of


def split_up(count, total, limit, skew):
    portions = [(1 << 20) // math.isqrt(rank ** skew) + 1 for rank in range(2, count + 1)]
    surplus, given = total - limit - (count - 1), [1] * (count - 1)
    while surplus > 0:
        candidates = [i for i in range(count - 1) if given[i] < limit]
        mass, left = sum([portions[i] for i in candidates]), surplus
        for i in candidates:
            extra = min(limit - given[i], max(1, left * portions[i] // mass), surplus)
            given[i] = given[i] + extra
            surplus = surplus - extra
    return np.array([limit] + given)


def uneven_parts(key, count, total, limit, slope):
    if count == 2:
        one = jax.random.randint(key, (), max(1, total - limit), min(limit, total - 1) + 1)
        return jnp.stack([one, total - one])
    lengths = jnp.asarray(split_up(count, total, limit, slope), jnp.int32)
    twos = (count - 1) // 2
    source_of, receiver = lengths[1:1 + 2 * twos:2], lengths[2:2 + 2 * twos:2]
    slack = jnp.minimum(source_of - 1, limit - receiver)
    moved = jax.random.randint(jax.random.fold_in(key, 1), (twos,), 0, 1 << 20) % (slack + 1)
    lengths = lengths.at[1:1 + 2 * twos:2].set(source_of - moved).at[2:2 + 2 * twos:2].set(receiver + moved)
    return lengths[jax.random.permutation(jax.random.fold_in(key, 2), count)]


def gaussian(rng, dims, scale, most, split=(), kind=jnp.bfloat16):
    drawn = jax.random.normal(rng, dims, jnp.float32) * scale
    if len(split) > 0:
        drawn = block_scale(rng, dims, split, -0.22, 0.18) * drawn
    return jnp.clip(drawn, min=-most, max=most).astype(kind)


def setup_inputs(seed: int = 0) -> dict:
    arg_keys = jax.random.split(jax.random.key(seed), 16)
    return {
        "inputs": gaussian(arg_keys[0], (TOKENS, D), 1.0, 6.0, ((0, 32),)),
        "doc_lengths": jax.vmap(lambda own: uneven_parts(own, NDOC, L, L // 2, 1))(jax.random.split(arg_keys[1], SEGMENT_TOTAL)).reshape((SEGMENT_TOTAL, NDOC)).astype(jnp.int32),
        "ln1_gain": jnp.clip(1.0 + 0.1 * jax.random.normal(arg_keys[2], (D,), jnp.float32), 0.5, 1.5).astype(jnp.bfloat16),
        "ln1_bias": gaussian(arg_keys[3], (D,), 0.3, 1.75),
        "attn_in": gaussian(arg_keys[4], (D, 3 * D), D ** -0.5, 0.21875),
        "qv_bias": gaussian(arg_keys[5], (2, D), 0.5, 3.0),
        "attn_out": gaussian(arg_keys[6], (D, D), (D // 16) ** -0.5, 0.875),
        "attn_out_bias": gaussian(arg_keys[7], (D,), 0.3, 1.75),
        "ln2_gain": jnp.clip(1.0 + 0.1 * jax.random.normal(arg_keys[8], (D,), jnp.float32), 0.5, 1.5).astype(jnp.bfloat16),
        "second_norm_bias": gaussian(arg_keys[9], (D,), 0.3, 1.75),
        "mlp_in": gaussian(arg_keys[10], (D, FF), D ** -0.5, 0.21875, ((1, 2),)),
        "mlp_in_bias": gaussian(arg_keys[11], (FF,), 0.5, 3.0, ((0, 2),)),
        "mlp_out": gaussian(arg_keys[12], (FF, D), FF ** -0.5, 0.109375, ((0, 2),)),
        "mlp_out_bias": gaussian(arg_keys[13], (D,), 0.3, 1.75),
        "cotangent": gaussian(arg_keys[14], (TOKENS, D), 1.0, 6.0, ((0, 32),)),
    }


highest = lax.Precision.HIGHEST

@jax.custom_vjp
def low(v):
    return lax.optimization_barrier(v.astype(jnp.bfloat16)).astype(jnp.float32)

@jax.custom_vjp
def low_back(v):
    return v

def low_keep(v):
    return (low(v), None)

def low_pass(kept, grad):
    return (grad,)

def back_keep(v):
    return (v, None)

def back_low(kept, grad):
    return (low(grad),)
low.defvjp(low_keep, low_pass)
low_back.defvjp(back_keep, back_low)

def rounded_length(values):
    return low_back(low(values))

def layer_norm(matrix, gain_row, shift_row):
    center = lax.optimization_barrier(jnp.mean(matrix, axis=-1, keepdims=True))
    centered = matrix - center
    spread = lax.optimization_barrier(jnp.mean(centered * centered, axis=-1, keepdims=True))
    return centered * lax.rsqrt(spread + 1e-05) * gain_row + shift_row

def gelu_tanh(values):
    argument = 0.7978845608028654 * (values + 0.044715 * values * values * values)
    return 0.5 * values * (1.0 + jnp.tanh(argument))

def softmax_rows(scores):
    row_top = lax.optimization_barrier(jnp.max(scores, axis=-1, keepdims=True))
    weights = jnp.exp(scores - row_top)
    return weights / lax.optimization_barrier(jnp.sum(weights, axis=-1, keepdims=True))

def basis_table(doc_lengths):
    last_len = doc_lengths[:, NDOC - 1].astype(jnp.float32)
    places = jnp.arange(L, dtype=jnp.float32)
    centers = (jnp.arange(NB, dtype=jnp.float32) + 0.5) / NB
    offsets = places[None, :] - L + last_len[:, None] + 0.5
    distances = centers[None, :, None] * last_len[:, None, None] - offsets[:, None, :]
    inside = (offsets > 0.0).astype(jnp.float32)
    weights = jnp.exp(-0.5 * distances * distances) * inside[:, None, :]
    return weights / lax.optimization_barrier(jnp.sum(weights, axis=2, keepdims=True))

def doc_tables(doc_lengths):
    places = jnp.arange(L, dtype=jnp.int32)
    segment_bounds = jnp.cumsum(doc_lengths, axis=1)
    documents = lax.optimization_barrier(jnp.sum((places[None, :, None] >= segment_bounds[:, None, :NDOC - 1]).astype(jnp.int32), axis=2))
    tail_mask = places[None, :] >= (L - doc_lengths[:, NDOC - 1])[:, None]
    head_mask = places[None, :] < doc_lengths[:, 0][:, None]
    return (documents, tail_mask, head_mask)

def forward(activations, ln1_gain, ln1_bias, attn_in, qv_bias, attn_out, attn_out_bias, ln2_gain, second_norm_bias, mlp_in, mlp_in_bias, mlp_out, mlp_out_bias, documents, reading, basis):
    blocks = activations.reshape(SEGMENT_TOTAL, L, D)
    normed = low(layer_norm(blocks, ln1_gain, ln1_bias))
    summary = rounded_length(jnp.einsum('sjt,std->sjd', basis, normed, precision=highest))
    later_segment = (jnp.arange(SEGMENT_TOTAL) % STREAM_SEGMENTS != 0).astype(jnp.float32)
    coefficients = jnp.concatenate([jnp.zeros((1, NB, D), jnp.float32), summary[:SEGMENT_TOTAL - 1]], axis=0) * later_segment[:, None, None]
    places = jnp.arange(L, dtype=jnp.int32)
    causal = places[None, :] <= places[:, None]
    score_scale = HD ** (-0.5)

    def segment(pieces_in):
        segment_rows, normed_rows, coeff_rows, doc_ids, reading_rows = pieces_in
        qkv = jnp.dot(normed_rows, attn_in, precision=highest)
        queries = rounded_length(qkv[:, :D] + qv_bias[0]).reshape(L, H, HD)
        key_rows = rounded_length(qkv[:, D:2 * D]).reshape(L, H, HD)
        values = rounded_length(qkv[:, 2 * D:] + qv_bias[1]).reshape(L, H, HD)
        mem_key = rounded_length(jnp.dot(coeff_rows, attn_in[:, D:2 * D], precision=highest)).reshape(NB, H, HD)
        mem_value = rounded_length(jnp.dot(coeff_rows, attn_in[:, 2 * D:], precision=highest) + qv_bias[1]).reshape(NB, H, HD)
        allowed = causal & (doc_ids[:, None] == doc_ids[None, :])
        scores = low_back(jnp.einsum('qhd,khd->hqk', queries, key_rows, precision=highest) * score_scale)
        attention = low(softmax_rows(jnp.where(allowed[None], scores, -1000000000.0)))
        local_out = jnp.einsum('hqk,khd->qhd', attention, values, precision=highest)
        mem_scores = low_back(jnp.einsum('qhd,khd->hqk', queries, mem_key, precision=highest) * score_scale)
        mem_attention = low(softmax_rows(mem_scores))
        remote = jnp.einsum('hqk,khd->qhd', mem_attention, mem_value, precision=highest)
        mixture = rounded_length((local_out + reading_rows[:, None, None] * remote).reshape(L, D))
        branch = low_back(jnp.dot(mixture, attn_out, precision=highest) + attn_out_bias)
        middle = segment_rows + branch
        normed_two = low(layer_norm(middle, ln2_gain, second_norm_bias))
        hidden_pre = low_back(jnp.dot(normed_two, mlp_in, precision=highest) + mlp_in_bias)
        hidden = low(gelu_tanh(hidden_pre))
        partials = jnp.einsum('lkf,kfd->kld', hidden.reshape(L, N_MLP, FF // N_MLP), mlp_out.reshape(N_MLP, FF // N_MLP, D), precision=highest)
        result = low_back(lax.optimization_barrier(jnp.sum(low(partials), axis=0)) + mlp_out_bias)
        return middle + result
    outputs = lax.map(jax.checkpoint(segment), (blocks, normed, coefficients, documents, reading))
    return outputs.reshape(SEGMENT_TOTAL * L, D)

def reference(inputs, doc_lengths, ln1_gain, ln1_bias, attn_in, qv_bias, attn_out, attn_out_bias, ln2_gain, second_norm_bias, mlp_in, mlp_in_bias, mlp_out, mlp_out_bias, cotangent):
    documents, tail_mask, head_mask = doc_tables(doc_lengths)
    later_segment = jnp.arange(SEGMENT_TOTAL) % STREAM_SEGMENTS != 0
    reading = (head_mask & later_segment[:, None]).astype(jnp.float32)
    basis = basis_table(doc_lengths)

    def closed(act_f, gain_one, bias_one, w_in, qv_f, w_out, out_b, gain_two, bias_two, m_in, m_in_b, m_out, m_out_b):
        return forward(act_f, gain_one, bias_one, w_in, qv_f, w_out, out_b, gain_two, bias_two, m_in, m_in_b, m_out, m_out_b, documents, reading, basis)
    output, pullback = jax.vjp(closed, inputs.astype(jnp.float32), ln1_gain.astype(jnp.float32), ln1_bias.astype(jnp.float32), attn_in.astype(jnp.float32), qv_bias.astype(jnp.float32), attn_out.astype(jnp.float32), attn_out_bias.astype(jnp.float32), ln2_gain.astype(jnp.float32), second_norm_bias.astype(jnp.float32), mlp_in.astype(jnp.float32), mlp_in_bias.astype(jnp.float32), mlp_out.astype(jnp.float32), mlp_out_bias.astype(jnp.float32))
    grads = pullback(cotangent.astype(jnp.float32))
    return (output.astype(jnp.bfloat16), grads[0].astype(jnp.bfloat16), grads[1], grads[2], grads[3], grads[4], grads[5], grads[6], grads[7], grads[8], grads[9], grads[10], grads[11], grads[12])
```

```python
import functools

import jax
import jax.numpy as jnp
from jax import lax
from jax.experimental import pallas as pl
from jax.experimental.pallas import tpu as pltpu
from jax.sharding import PartitionSpec as P

D = 768
H = 12
HD = 64
NB = 512
L = 512
NDOC = 3
HALF = L // 2
PAIRS = H // 2
LANES = 2 * HD

LOG2E = 1.4426950408889634
SCORE_LOG2 = LOG2E * HD**-0.5
MASKED = -1e30

bf16 = jnp.bfloat16
f32 = jnp.float32


def dot(a, b):
    return jnp.dot(a, b, preferred_element_type=f32)


def dot_nt(a, b):
    return lax.dot_general(a, b, (((1,), (1,)), ((), ())), preferred_element_type=f32)


def layer_norm(matrix, gain_row, shift_row):
    center = jnp.mean(matrix, axis=-1, keepdims=True)
    centered = matrix - center
    spread = jnp.mean(centered * centered, axis=-1, keepdims=True)
    return centered * lax.rsqrt(spread + 1e-05) * gain_row + shift_row


def norm_backward(matrix, gain_row, shift_row, upstream):
    unused, pullback = jax.vjp(layer_norm, matrix, gain_row, shift_row)
    return pullback(upstream)


def head_lanes(matrix, head):
    lane = lax.broadcasted_iota(jnp.int32, (1, LANES), 1)
    return jnp.where(lane // HD == head, matrix, jnp.zeros_like(matrix))


def fill_mask(lens, mask):
    key = lax.broadcasted_iota(jnp.int32, (L, L), 0)
    query = lax.broadcasted_iota(jnp.int32, (L, L), 1)
    one = lens[0, 0]
    two = one + lens[0, 1]
    start = jnp.where(query >= two, two, jnp.where(query >= one, one, 0))
    mask[...] = jnp.where((key <= query) & (key >= start), 0.0, MASKED)


def local_kernel(lens, q_ref, k_ref, v_ref, out_ref, lse_ref, mask, turned):
    @pl.when(pl.program_id(0) == 0)
    def _():
        fill_mask(lens, mask)

    q, k = q_ref[...], k_ref[...]
    v_t = v_ref[...].T
    for head in range(2):
        q_head = head_lanes(q, head)
        rows = slice(head * HD, (head + 1) * HD)
        for part in range(2):
            keys = HALF * (part + 1)
            cols = slice(part * HALF, (part + 1) * HALF)
            s = dot_nt(k[:keys], q_head[cols]) * SCORE_LOG2 + mask[:keys, cols]
            top = jnp.max(s, axis=0, keepdims=True)
            e = jnp.exp2(s - top)
            total = jnp.sum(e, axis=0, keepdims=True)
            out = dot(v_t[rows, :keys], e.astype(bf16))
            turned[rows, cols] = out / total
            lse_ref[0, head : head + 1, cols] = top + jnp.log2(total)
    out_ref[...] = turned[...].T


def local_attention(lens, qkv):
    column = lambda k: pl.BlockSpec((L, LANES), lambda i: (0, k * PAIRS + i))
    return pl.pallas_call(
        local_kernel,
        grid=(PAIRS,),
        in_specs=[pl.BlockSpec(memory_space=pltpu.SMEM), column(0), column(1), column(2)],
        out_specs=[column(0), pl.BlockSpec((1, 8, L), lambda i: (i, 0, 0))],
        out_shape=[
            jax.ShapeDtypeStruct((L, D), f32),
            jax.ShapeDtypeStruct((PAIRS, 8, L), f32),
        ],
        scratch_shapes=[pltpu.VMEM((L, L), f32), pltpu.VMEM((LANES, L), f32)],
        cost_estimate=pl.CostEstimate(
            flops=H * 12 * HALF * HALF * 256, bytes_accessed=8 * L * D, transcendentals=H * L * L
        ),
        name="local_attention",
    )(lens, qkv, qkv, qkv)


def basis_rows(last_len, transposed):
    shape = (HALF, NB) if transposed else (NB, HALF)
    slot_dim, place_dim = (1, 0) if transposed else (0, 1)
    slot = lax.broadcasted_iota(jnp.int32, shape, slot_dim).astype(f32)
    place = lax.broadcasted_iota(jnp.int32, shape, place_dim).astype(f32)
    offsets = place - HALF + last_len + 0.5
    distances = (slot + 0.5) / NB * last_len - offsets
    weights = jnp.where(offsets > 0.0, jnp.exp(-0.5 * distances * distances), 0.0)
    return weights / jnp.sum(weights, axis=place_dim, keepdims=True)


def memory_kernel(
    reads,
    last_ref,
    q_ref,
    kt_ref,
    vt_ref,
    vb_ref,
    local_ref,
    wo_ref,
    x_ref,
    rows_ref,
    mix_ref,
    mk_ref,
    mv_ref,
    lse_ref,
    middle_ref,
    normed_ref,
    basis_t_ref,
    basis,
    turned,
    acc,
):
    step = pl.program_id(0)

    @pl.when(step == 0)
    def _():
        last_len = last_ref[0:1, 0:1]
        basis[...] = basis_rows(last_len, False).astype(bf16)
        basis_t_ref[...] = basis_rows(last_len, True).astype(bf16)
        acc[...] = jnp.zeros_like(acc)

    mem_k = dot(basis[...], kt_ref[...]).astype(bf16)
    mem_v = (dot(basis[...], vt_ref[...]) + vb_ref[0:1]).astype(bf16)
    mk_ref[...] = mem_k
    mv_ref[...] = mem_v
    v_t = mem_v.T
    query = lax.broadcasted_iota(jnp.int32, (1, HALF), 1)
    reading = query < reads[0, 0]
    q = q_ref[...]
    for head in range(2):
        rows = slice(head * HD, (head + 1) * HD)
        s = dot_nt(mem_k, head_lanes(q, head)) * SCORE_LOG2
        top = jnp.max(s, axis=0, keepdims=True)
        e = jnp.exp2(s - top)
        total = jnp.sum(e, axis=0, keepdims=True)
        out = dot(v_t[rows], e.astype(bf16))
        turned[rows, :] = jnp.where(reading, out / total, 0.0)
        lse_ref[0, head : head + 1, :] = jnp.where(reading, top + jnp.log2(total), -MASKED)
    mixed = jnp.concatenate(
        [local_ref[:HALF] + turned[...].T, local_ref[HALF:]], axis=0
    ).astype(bf16)
    mix_ref[...] = mixed
    acc[...] += dot(mixed, wo_ref[...])

    @pl.when(step == PAIRS - 1)
    def _():
        middle = x_ref[...].astype(f32) + (acc[...] + rows_ref[0:1])
        middle_ref[...] = middle
        normed_ref[...] = layer_norm(middle, rows_ref[1:2], rows_ref[2:3]).astype(bf16)


def memory_attention(reads, last_rows, qkv, tail_kv, value_bias, local, attn_out, inputs, rows):
    whole = lambda shape: pl.BlockSpec(shape, lambda i: (0,) * len(shape))
    return pl.pallas_call(
        memory_kernel,
        grid=(PAIRS,),
        in_specs=[
            pl.BlockSpec(memory_space=pltpu.SMEM),
            whole((16, D)),
            pl.BlockSpec((HALF, LANES), lambda i: (0, i)),
            pl.BlockSpec((HALF, LANES), lambda i: (0, i)),
            pl.BlockSpec((HALF, LANES), lambda i: (0, PAIRS + i)),
            pl.BlockSpec((8, LANES), lambda i: (0, i)),
            pl.BlockSpec((L, LANES), lambda i: (0, i)),
            pl.BlockSpec((LANES, D), lambda i: (i, 0)),
            whole((L, D)),
            whole((8, D)),
        ],
        out_specs=[
            pl.BlockSpec((L, LANES), lambda i: (0, i)),
            pl.BlockSpec((NB, LANES), lambda i: (0, i)),
            pl.BlockSpec((NB, LANES), lambda i: (0, i)),
            pl.BlockSpec((1, 8, HALF), lambda i: (i, 0, 0)),
            whole((L, D)),
            whole((L, D)),
            whole((HALF, NB)),
        ],
        out_shape=[
            jax.ShapeDtypeStruct((L, D), bf16),
            jax.ShapeDtypeStruct((NB, D), bf16),
            jax.ShapeDtypeStruct((NB, D), bf16),
            jax.ShapeDtypeStruct((PAIRS, 8, HALF), f32),
            jax.ShapeDtypeStruct((L, D), f32),
            jax.ShapeDtypeStruct((L, D), bf16),
            jax.ShapeDtypeStruct((HALF, NB), bf16),
        ],
        scratch_shapes=[
            pltpu.VMEM((NB, HALF), bf16),
            pltpu.VMEM((LANES, HALF), f32),
            pltpu.VMEM((L, D), f32),
        ],
        cost_estimate=pl.CostEstimate(
            flops=H * 16 * HALF * HALF * 256, bytes_accessed=16 * L * D, transcendentals=H * L * HALF
        ),
        name="memory_attention",
    )(reads, last_rows, qkv, tail_kv, tail_kv, value_bias, local, attn_out, inputs, rows)


def mlp_kernel(
    x_ref, ct_ref, wi_ref, bi_ref, wo_ref, hid_ref, dpre_ref, bias_ref, y_ref, dx_ref, y_acc, dx_acc
):
    step = pl.program_id(0)
    pre = dot(x_ref[...], wi_ref[...]) + bi_ref[0:1]
    squared = pre * pre
    tanh = jnp.tanh(pre * (0.7978845608028654 + 0.7978845608028654 * 0.044715 * squared))
    half = 0.5 * pre
    hidden = (half + half * tanh).astype(bf16)
    slope = (
        0.5
        + 0.5 * tanh
        + half
        * (1.0 - tanh * tanh)
        * (0.7978845608028654 + 3 * 0.7978845608028654 * 0.044715 * squared)
    )
    d_pre = (slope * dot_nt(ct_ref[...], wo_ref[...])).astype(bf16)
    hid_ref[...] = hidden
    dpre_ref[...] = d_pre
    bias_ref[...] = jnp.broadcast_to(
        jnp.sum(d_pre.astype(f32), axis=0, keepdims=True), bias_ref.shape
    )
    y = dot(hidden, wo_ref[...])
    dx = dot_nt(d_pre, wi_ref[...])

    @pl.when(step == 0)
    def _():
        y_acc[...] = y
        dx_acc[...] = dx

    @pl.when(step > 0)
    def _():
        y_acc[...] += y
        dx_acc[...] += dx

    @pl.when(step == pl.num_programs(0) - 1)
    def _():
        y_ref[...] = y_acc[...].astype(bf16)
        dx_ref[...] = dx_acc[...].astype(bf16)


def mlp_block(rows, cotangent, mlp_in, bias_rows, mlp_out):
    count, hidden = rows.shape[0], mlp_in.shape[1]
    tile = 256 if hidden % 256 == 0 else 128
    fixed = pl.BlockSpec((count, D), lambda i: (0, 0))
    across = pl.BlockSpec((count, tile), lambda i: (0, i))
    return pl.pallas_call(
        mlp_kernel,
        grid=(hidden // tile,),
        in_specs=[
            fixed,
            fixed,
            pl.BlockSpec((D, tile), lambda i: (0, i)),
            pl.BlockSpec((8, tile), lambda i: (0, i)),
            pl.BlockSpec((tile, D), lambda i: (i, 0)),
        ],
        out_specs=[across, across, pl.BlockSpec((8, tile), lambda i: (0, i)), fixed, fixed],
        out_shape=[
            jax.ShapeDtypeStruct((count, hidden), bf16),
            jax.ShapeDtypeStruct((count, hidden), bf16),
            jax.ShapeDtypeStruct((8, hidden), f32),
            jax.ShapeDtypeStruct((count, D), bf16),
            jax.ShapeDtypeStruct((count, D), bf16),
        ],
        scratch_shapes=[pltpu.VMEM((count, D), f32), pltpu.VMEM((count, D), f32)],
        cost_estimate=pl.CostEstimate(
            flops=8 * count * D * hidden,
            bytes_accessed=4 * D * hidden + 4 * count * hidden + 8 * count * D,
            transcendentals=count * hidden,
        ),
        name="mlp_block",
    )(rows, cotangent, mlp_in, bias_rows, mlp_out)


def backward_kernel(
    lens,
    q_ref,
    k_ref,
    v_ref,
    mk_ref,
    mv_ref,
    db_ref,
    wo_ref,
    ll_ref,
    lm_ref,
    bt_ref,
    dqkv_ref,
    dtail_ref,
    sums_ref,
    mask,
    turned,
    dk_acc,
    dv_acc,
):
    @pl.when(pl.program_id(0) == 0)
    def _():
        fill_mask(lens, mask)

    q, k, v = q_ref[...], k_ref[...], v_ref[...]
    mem_k, mem_v = mk_ref[...], mv_ref[...]
    d_mix = dot_nt(db_ref[...], wo_ref[...]).astype(bf16)
    k_t, mk_t = k.T, mem_k.T
    d_mem_k = d_mem_v = None

    def one(keys, values, q_part, d_part, lse, extra):
        s = dot_nt(keys, q_part) * SCORE_LOG2
        if extra is not None:
            s = s + extra
        weights = jnp.exp2(s - lse)
        d_weights = dot_nt(values, d_part)
        inner = jnp.sum(weights * d_weights, axis=0, keepdims=True)
        d_scores = (weights * (d_weights - inner)).astype(bf16)
        return d_scores, dot(d_scores, q_part), dot(weights.astype(bf16), d_part)

    for head in range(2):
        rows = slice(head * HD, (head + 1) * HD)
        q_head, d_head = head_lanes(q, head), head_lanes(d_mix, head)
        for part in range(2):
            keys = HALF * (part + 1)
            cols = slice(part * HALF, (part + 1) * HALF)
            ds, dk, dv = one(
                k[:keys],
                v[:keys],
                q_head[cols],
                d_head[cols],
                ll_ref[0, head : head + 1, cols],
                mask[:keys, cols],
            )
            dq = dot(k_t[rows, :keys], ds)
            if part == 0:
                ds, d_key, d_value = one(
                    mem_k, mem_v, q_head[cols], d_head[cols], lm_ref[0, head : head + 1, :], None
                )
                dq = dq + dot(mk_t[rows], ds)
                d_mem_k = d_key if d_mem_k is None else d_mem_k + d_key
                d_mem_v = d_value if d_mem_v is None else d_mem_v + d_value
            turned[rows, cols] = dq
            if head == 0 and part == 0:
                dk_acc[:HALF] = dk
                dv_acc[:HALF] = dv
            elif head == 0:
                dk_acc[:HALF] += dk[:HALF]
                dv_acc[:HALF] += dv[:HALF]
                dk_acc[HALF:] = dk[HALF:]
                dv_acc[HALF:] = dv[HALF:]
            else:
                dk_acc[:keys] += dk
                dv_acc[:keys] += dv
    scale = HD**-0.5
    d_q = (turned[...].T * scale).astype(bf16)
    d_v = dv_acc[...].astype(bf16)
    dqkv_ref[0] = d_q
    dqkv_ref[1] = (dk_acc[...] * scale).astype(bf16)
    dqkv_ref[2] = d_v
    d_mem_k = (d_mem_k * scale).astype(bf16)
    d_mem_v = d_mem_v.astype(bf16)
    dtail_ref[0] = dot(bt_ref[...], d_mem_k).astype(bf16)
    dtail_ref[1] = dot(bt_ref[...], d_mem_v).astype(bf16)
    sums_ref[0:1] = jnp.sum(d_q.astype(f32), axis=0, keepdims=True)
    sums_ref[1:2] = jnp.sum(d_v.astype(f32), axis=0, keepdims=True) + jnp.sum(
        d_mem_v.astype(f32), axis=0, keepdims=True
    )


def attention_backward(lens, qkv, mem_k, mem_v, d_branch, attn_out, lse_local, lse_mem, basis_t):
    column = lambda k: pl.BlockSpec((L, LANES), lambda i: (0, k * PAIRS + i))
    whole = lambda shape: pl.BlockSpec(shape, lambda i: (0,) * len(shape))
    return pl.pallas_call(
        backward_kernel,
        grid=(PAIRS,),
        in_specs=[
            pl.BlockSpec(memory_space=pltpu.SMEM),
            column(0),
            column(1),
            column(2),
            column(0),
            column(0),
            whole((L, D)),
            pl.BlockSpec((LANES, D), lambda i: (i, 0)),
            pl.BlockSpec((1, 8, L), lambda i: (i, 0, 0)),
            pl.BlockSpec((1, 8, HALF), lambda i: (i, 0, 0)),
            whole((HALF, NB)),
        ],
        out_specs=[
            pl.BlockSpec((3, L, LANES), lambda i: (0, 0, i)),
            pl.BlockSpec((2, HALF, LANES), lambda i: (0, 0, i)),
            pl.BlockSpec((8, LANES), lambda i: (0, i)),
        ],
        out_shape=[
            jax.ShapeDtypeStruct((3, L, D), bf16),
            jax.ShapeDtypeStruct((2, HALF, D), bf16),
            jax.ShapeDtypeStruct((8, D), f32),
        ],
        scratch_shapes=[
            pltpu.VMEM((L, L), f32),
            pltpu.VMEM((LANES, L), f32),
            pltpu.VMEM((L, LANES), f32),
            pltpu.VMEM((L, LANES), f32),
        ],
        cost_estimate=pl.CostEstimate(
            flops=H * 56 * HALF * HALF * 256, bytes_accessed=20 * L * D, transcendentals=H * L * L
        ),
        name="attention_backward",
    )(lens, qkv, qkv, qkv, mem_k, mem_v, d_branch, attn_out, lse_local, lse_mem, basis_t)


def rotated(value, axis, by):
    count = lax.axis_size(axis)
    return lax.ppermute(value, axis, [(i, (i + by) % count) for i in range(count)])


def swapped(value, axis, bit):
    count = lax.axis_size(axis)
    return lax.ppermute(value, axis, [(i, i ^ (1 << bit)) for i in range(count)])


def axis_bits(axis):
    return [(axis, bit) for bit in range(lax.axis_size(axis).bit_length() - 1)]


def side(axis, bit):
    return (lax.axis_index(axis) >> bit) & 1


def halve(value, axis, bit):
    count = value.shape[0] // 2
    mine = side(axis, bit)
    kept = lax.dynamic_slice_in_dim(value, mine * count, count, 0)
    given = lax.dynamic_slice_in_dim(value, (1 - mine) * count, count, 0)
    got = swapped(given, axis, bit)
    return (kept.astype(f32) + got.astype(f32)).astype(value.dtype)


def double(value, axis, bit):
    got = swapped(value, axis, bit)
    first = side(axis, bit) == 0
    return jnp.concatenate([jnp.where(first, value, got), jnp.where(first, got, value)], axis=0)


def sum_rows(value):
    batch, mlp = axis_bits("batch"), axis_bits("mlp")
    core, rest = batch[:1], batch[2:]
    orders = (batch[1:2] + mlp, mlp + batch[1:2])
    for step in core:
        value = halve(value, *step)
    parts = jnp.split(value, 2, axis=0)
    for steps in zip(*orders):
        parts = [halve(part, *step) for part, step in zip(parts, steps)]
    value = jnp.concatenate(parts, axis=0)
    for step in rest:
        value = halve(value, *step)
    for step in rest[::-1]:
        value = double(value, *step)
    parts = jnp.split(value, 2, axis=0)
    for steps in zip(*(order[::-1] for order in orders)):
        parts = [double(part, *step) for part, step in zip(parts, steps)]
    value = jnp.concatenate(parts, axis=0)
    for step in core:
        value = double(value, *step)
    return value


def sum_small(value):
    for step in axis_bits("batch") + axis_bits("mlp"):
        value = value + swapped(value, *step)
    return value


def shards(
    inputs,
    doc_lengths,
    ln1_gain,
    ln1_bias,
    attn_in,
    qv_bias,
    attn_out,
    attn_out_bias,
    ln2_gain,
    second_norm_bias,
    mlp_in,
    mlp_in_bias,
    mlp_out,
    mlp_out_bias,
    cotangent,
):
    n_mlp = lax.axis_size("mlp")
    place = lax.axis_index("mlp")
    gain_one = ln1_gain.astype(f32)
    bias_one = ln1_bias.astype(f32)
    gain_two = ln2_gain.astype(f32)
    bias_two = second_norm_bias.astype(f32)

    own_tail = jnp.concatenate(
        [
            inputs[HALF:],
            jnp.broadcast_to(doc_lengths[:, NDOC - 1 :].astype(bf16), (16, D)),
        ],
        axis=0,
    )
    tail = rotated(own_tail, "mlp", 1)
    cotangents = [cotangent] + [rotated(cotangent, "mlp", by) for by in range(1, n_mlp)]

    activations = inputs.astype(f32)
    normed = layer_norm(activations, gain_one, bias_one).astype(bf16)
    zeros = jnp.zeros((D,), f32)
    qkv_bias = jnp.concatenate([qv_bias[0].astype(f32), zeros, qv_bias[1].astype(f32)])
    qkv = (dot(normed, attn_in) + qkv_bias).astype(bf16)
    local, lse_local = local_attention(doc_lengths, qkv)

    tail_rows = tail[:HALF].astype(f32)
    normed_tail = layer_norm(tail_rows, gain_one, bias_one).astype(bf16)
    tail_kv = dot(normed_tail, attn_in[:, D:]).astype(bf16)
    reads = jnp.where(place == 0, 0, doc_lengths[:, :1])
    value_bias = jnp.broadcast_to(qv_bias[1].astype(f32), (8, D))
    rows = jnp.concatenate(
        [
            jnp.stack([attn_out_bias.astype(f32), gain_two, bias_two]),
            jnp.zeros((5, D), f32),
        ]
    )
    mixture, mem_k, mem_v, lse_mem, middle, normed_two, basis_t = memory_attention(
        reads, tail[HALF:], qkv, tail_kv, value_bias, local, attn_out, inputs, rows
    )

    bias_rows = jnp.broadcast_to(mlp_in_bias.astype(f32), (8, mlp_in.shape[1]))
    result = None
    d_normed_two = None
    d_mlp_in = d_mlp_out = d_mlp_in_bias = None
    arrived = [normed_two] + [rotated(normed_two, "mlp", by) for by in range(1, n_mlp)]
    partial_results = []
    for by in range(n_mlp):
        hidden, d_pre, d_bias, y, dx = mlp_block(
            arrived[by], cotangents[by], mlp_in, bias_rows, mlp_out
        )
        if by:
            dx = rotated(dx, "mlp", -by)
        grad_in = lax.dot_general(
            arrived[by], d_pre, (((0,), (0,)), ((), ())), preferred_element_type=f32
        )
        grad_out = lax.dot_general(
            hidden, cotangents[by], (((0,), (0,)), ((), ())), preferred_element_type=f32
        )
        partial_results.append(y)
        if by:
            d_normed_two = d_normed_two + dx.astype(f32)
            d_mlp_in, d_mlp_out = d_mlp_in + grad_in, d_mlp_out + grad_out
            d_mlp_in_bias = d_mlp_in_bias + d_bias[0]
        else:
            d_normed_two = dx.astype(f32)
            d_mlp_in, d_mlp_out, d_mlp_in_bias = grad_in, grad_out, d_bias[0]
    d_mlp_in, d_mlp_out = lax.psum((d_mlp_in.astype(bf16), d_mlp_out.astype(bf16)), "batch")

    upstream = cotangent.astype(f32)
    d_out_bias = jnp.sum(upstream, axis=0)
    d_middle_norm, d_ln2_gain, d_ln2_bias = norm_backward(middle, gain_two, bias_two, d_normed_two)
    d_middle = upstream + d_middle_norm
    d_branch = d_middle.astype(bf16)
    d_attn_out_bias = jnp.sum(d_branch, axis=0, dtype=f32)
    d_qkv, d_tail, sums = attention_backward(
        doc_lengths, qkv, mem_k, mem_v, d_branch, attn_out, lse_local, lse_mem, basis_t
    )
    over_rows = (((0,), (0,)), ((), ()))
    grads = [
        lax.dot_general(normed, d_qkv[0], over_rows, preferred_element_type=f32),
        lax.dot_general(normed, d_qkv[1], over_rows, preferred_element_type=f32)
        + lax.dot_general(normed_tail, d_tail[0], over_rows, preferred_element_type=f32),
        lax.dot_general(normed, d_qkv[2], over_rows, preferred_element_type=f32)
        + lax.dot_general(normed_tail, d_tail[1], over_rows, preferred_element_type=f32),
        lax.dot_general(mixture, d_branch, over_rows, preferred_element_type=f32),
    ]
    summed = sum_rows(jnp.concatenate([grad.astype(bf16) for grad in grads], axis=0))

    columns = [attn_in[:, i * D : (i + 1) * D] for i in range(3)]
    d_tail_rows = dot_nt(d_tail[0], columns[1]) + dot_nt(d_tail[1], columns[2])
    from_next = rotated(d_tail_rows.astype(bf16), "mlp", -1)
    d_normed = (
        dot_nt(d_qkv[0], columns[0]) + dot_nt(d_qkv[1], columns[1]) + dot_nt(d_qkv[2], columns[2])
    )
    d_normed = jnp.concatenate(
        [d_normed[:HALF], d_normed[HALF:] + from_next.astype(f32)], axis=0
    )
    d_in_norm, d_ln1_gain, d_ln1_bias = norm_backward(activations, gain_one, bias_one, d_normed)
    input_grad = (d_middle + d_in_norm).astype(bf16)

    result = partial_results[0].astype(f32)
    for by in range(1, n_mlp):
        result = result + rotated(partial_results[by], "mlp", -by).astype(f32)
    layer_output = (middle + (result + mlp_out_bias)).astype(bf16)

    hidden_count = mlp_in.shape[1]
    placed_bias = lax.dynamic_update_slice(
        jnp.zeros((n_mlp * hidden_count,), f32), d_mlp_in_bias, (place * hidden_count,)
    )
    vectors = jnp.concatenate(
        [
            jnp.stack(
                [d_ln1_gain, d_ln1_bias, d_attn_out_bias, d_ln2_gain, d_ln2_bias, d_out_bias]
            ),
            sums[:2],
            placed_bias.reshape(-1, D),
        ],
        axis=0,
    )
    vectors = sum_small(vectors)
    d_attn_in = jnp.concatenate([summed[i * D : (i + 1) * D] for i in range(3)], axis=1)
    return (
        layer_output,
        input_grad,
        vectors[0],
        vectors[1],
        d_attn_in.astype(f32),
        vectors[6:8],
        summed[3 * D :].astype(f32),
        vectors[2],
        vectors[3],
        vectors[4],
        d_mlp_in.astype(f32),
        lax.dynamic_slice(vectors[8:].reshape(-1), (place * hidden_count,), (hidden_count,)),
        d_mlp_out.astype(f32),
        vectors[5],
    )


def solution(mesh):
    rows, whole = P(("batch", "mlp"), None), P()
    columns, hidden, depth = P(None, "mlp"), P("mlp"), P("mlp", None)
    return jax.shard_map(
        shards,
        mesh=mesh,
        in_specs=(rows, rows) + (whole,) * 8 + (columns, hidden, depth, whole, rows),
        out_specs=(rows, rows) + (whole,) * 8 + (columns, hidden, depth, whole),
        check_vma=False,
    )
```

```python
import functools

import jax
import jax.numpy as jnp
from jax import lax
from jax.experimental import pallas as pl
from jax.experimental.pallas import tpu as pltpu
from jax.sharding import PartitionSpec as P

D = 768
H = 12
HD = 64
NB = 512
L = 512
NDOC = 3
HALF = L // 2
PAIRS = H // 2
LANES = 2 * HD

LOG2E = 1.4426950408889634
SCORE_LOG2 = LOG2E * HD**-0.5
MASKED = -1e30

bf16 = jnp.bfloat16
f32 = jnp.float32


def dot(a, b):
    return jnp.dot(a, b, preferred_element_type=f32)


def dot_nt(a, b):
    return lax.dot_general(a, b, (((1,), (1,)), ((), ())), preferred_element_type=f32)


def layer_norm(matrix, gain_row, shift_row):
    center = jnp.mean(matrix, axis=-1, keepdims=True)
    centered = matrix - center
    spread = jnp.mean(centered * centered, axis=-1, keepdims=True)
    return centered * lax.rsqrt(spread + 1e-05) * gain_row + shift_row


def norm_backward(matrix, gain_row, shift_row, upstream):
    unused, pullback = jax.vjp(layer_norm, matrix, gain_row, shift_row)
    return pullback(upstream)


def head_lanes(matrix, head):
    lane = lax.broadcasted_iota(jnp.int32, (1, LANES), 1)
    return jnp.where(lane // HD == head, matrix, jnp.zeros_like(matrix))


def fill_mask(lens, mask):
    key = lax.broadcasted_iota(jnp.int32, (L, L), 0)
    query = lax.broadcasted_iota(jnp.int32, (L, L), 1)
    one = lens[0, 0]
    two = one + lens[0, 1]
    start = jnp.where(query >= two, two, jnp.where(query >= one, one, 0))
    mask[...] = jnp.where((key <= query) & (key >= start), 0.0, MASKED)


def local_kernel(
    lens,
    q_ref,
    k_ref,
    v_ref,
    wo_ref,
    x_ref,
    rows_ref,
    out_ref,
    lse_ref,
    mix_ref,
    middle_ref,
    normed_ref,
    mask,
    turned,
    acc,
):
    step = pl.program_id(0)

    @pl.when(step == 0)
    def _():
        fill_mask(lens, mask)
        acc[...] = jnp.zeros_like(acc)

    q, k = q_ref[...], k_ref[...]
    v_t = v_ref[...].T
    for head in range(2):
        q_head = head_lanes(q, head)
        rows = slice(head * HD, (head + 1) * HD)
        for part in range(2):
            keys = HALF * (part + 1)
            cols = slice(part * HALF, (part + 1) * HALF)
            s = dot_nt(k[:keys], q_head[cols]) * SCORE_LOG2 + mask[:keys, cols]
            top = jnp.max(s, axis=0, keepdims=True)
            e = jnp.exp2(s - top)
            total = jnp.sum(e, axis=0, keepdims=True)
            out = dot(v_t[rows, :keys], e.astype(bf16))
            turned[rows, cols] = out / total
            lse_ref[0, head : head + 1, cols] = top + jnp.log2(total)
    out_ref[...] = turned[:, :HALF].T
    mixed = turned[:, HALF:].T.astype(bf16)
    mix_ref[...] = mixed
    acc[...] += dot(mixed, wo_ref[...])

    @pl.when(step == PAIRS - 1)
    def _():
        finish_middle(x_ref, acc, rows_ref, middle_ref, normed_ref)


def finish_middle(x_ref, acc, rows_ref, middle_ref, normed_ref):
    middle = x_ref[...].astype(f32) + (acc[...] + rows_ref[0:1])
    middle_ref[...] = middle
    normed_ref[...] = layer_norm(middle, rows_ref[1:2], rows_ref[2:3]).astype(bf16)


def local_attention(lens, qkv, attn_out, inputs, rows):
    column = lambda k: pl.BlockSpec((L, LANES), lambda i: (0, k * PAIRS + i))
    upper = pl.BlockSpec((HALF, D), lambda i: (1, 0))
    return pl.pallas_call(
        local_kernel,
        grid=(PAIRS,),
        in_specs=[
            pl.BlockSpec(memory_space=pltpu.SMEM),
            column(0),
            column(1),
            column(2),
            pl.BlockSpec((LANES, D), lambda i: (i, 0)),
            upper,
            pl.BlockSpec((8, D), lambda i: (0, 0)),
        ],
        out_specs=[
            pl.BlockSpec((HALF, LANES), lambda i: (0, i)),
            pl.BlockSpec((1, 8, L), lambda i: (i, 0, 0)),
            pl.BlockSpec((HALF, LANES), lambda i: (1, i)),
            upper,
            upper,
        ],
        out_shape=[
            jax.ShapeDtypeStruct((HALF, D), f32),
            jax.ShapeDtypeStruct((PAIRS, 8, L), f32),
            jax.ShapeDtypeStruct((L, D), bf16),
            jax.ShapeDtypeStruct((L, D), f32),
            jax.ShapeDtypeStruct((L, D), bf16),
        ],
        scratch_shapes=[
            pltpu.VMEM((L, L), f32),
            pltpu.VMEM((LANES, L), f32),
            pltpu.VMEM((HALF, D), f32),
        ],
        cost_estimate=pl.CostEstimate(
            flops=H * 12 * HALF * HALF * 256, bytes_accessed=8 * L * D, transcendentals=H * L * L
        ),
        name="local_attention",
    )(lens, qkv, qkv, qkv, attn_out, inputs, rows)


def basis_rows(last_len, transposed):
    shape = (HALF, NB) if transposed else (NB, HALF)
    slot_dim, place_dim = (1, 0) if transposed else (0, 1)
    slot = lax.broadcasted_iota(jnp.int32, shape, slot_dim).astype(f32)
    place = lax.broadcasted_iota(jnp.int32, shape, place_dim).astype(f32)
    offsets = place - HALF + last_len + 0.5
    distances = (slot + 0.5) / NB * last_len - offsets
    weights = jnp.where(offsets > 0.0, jnp.exp(-0.5 * distances * distances), 0.0)
    return weights / jnp.sum(weights, axis=place_dim, keepdims=True)


def memory_kernel(
    reads,
    last_ref,
    q_ref,
    kt_ref,
    vt_ref,
    vb_ref,
    local_ref,
    wo_ref,
    x_ref,
    rows_ref,
    mix_whole,
    middle_whole,
    normed_whole,
    mix_ref,
    mk_ref,
    mv_ref,
    lse_ref,
    middle_ref,
    normed_ref,
    basis_t_ref,
    basis,
    turned,
    acc,
):
    step = pl.program_id(0)

    @pl.when(step == 0)
    def _():
        last_len = last_ref[0:1, 0:1]
        basis[...] = basis_rows(last_len, False).astype(bf16)
        basis_t_ref[...] = basis_rows(last_len, True).astype(bf16)
        acc[...] = jnp.zeros_like(acc)

    mem_k = dot(basis[...], kt_ref[...]).astype(bf16)
    mem_v = (dot(basis[...], vt_ref[...]) + vb_ref[0:1]).astype(bf16)
    mk_ref[...] = mem_k
    mv_ref[...] = mem_v
    v_t = mem_v.T
    query = lax.broadcasted_iota(jnp.int32, (1, HALF), 1)
    reading = query < reads[0, 0]
    q = q_ref[...]
    for head in range(2):
        rows = slice(head * HD, (head + 1) * HD)
        s = dot_nt(mem_k, head_lanes(q, head)) * SCORE_LOG2
        top = jnp.max(s, axis=0, keepdims=True)
        e = jnp.exp2(s - top)
        total = jnp.sum(e, axis=0, keepdims=True)
        out = dot(v_t[rows], e.astype(bf16))
        turned[rows, :] = jnp.where(reading, out / total, 0.0)
        lse_ref[0, head : head + 1, :] = jnp.where(reading, top + jnp.log2(total), -MASKED)
    mixed = (local_ref[...] + turned[...].T).astype(bf16)
    mix_ref[...] = mixed
    acc[...] += dot(mixed, wo_ref[...])

    @pl.when(step == PAIRS - 1)
    def _():
        finish_middle(x_ref, acc, rows_ref, middle_ref, normed_ref)


def memory_attention(
    reads, last_rows, qkv, tail_kv, value_bias, local, attn_out, inputs, rows, mixture, middle, normed
):
    whole = lambda shape: pl.BlockSpec(shape, lambda i: (0,) * len(shape))
    untouched = pl.BlockSpec(memory_space=pl.ANY)
    return pl.pallas_call(
        memory_kernel,
        grid=(PAIRS,),
        in_specs=[
            pl.BlockSpec(memory_space=pltpu.SMEM),
            whole((16, D)),
            pl.BlockSpec((HALF, LANES), lambda i: (0, i)),
            pl.BlockSpec((HALF, LANES), lambda i: (0, i)),
            pl.BlockSpec((HALF, LANES), lambda i: (0, PAIRS + i)),
            pl.BlockSpec((8, LANES), lambda i: (0, i)),
            pl.BlockSpec((HALF, LANES), lambda i: (0, i)),
            pl.BlockSpec((LANES, D), lambda i: (i, 0)),
            whole((HALF, D)),
            whole((8, D)),
            untouched,
            untouched,
            untouched,
        ],
        out_specs=[
            pl.BlockSpec((HALF, LANES), lambda i: (0, i)),
            pl.BlockSpec((NB, LANES), lambda i: (0, i)),
            pl.BlockSpec((NB, LANES), lambda i: (0, i)),
            pl.BlockSpec((1, 8, HALF), lambda i: (i, 0, 0)),
            whole((HALF, D)),
            whole((HALF, D)),
            whole((HALF, NB)),
        ],
        out_shape=[
            jax.ShapeDtypeStruct((L, D), bf16),
            jax.ShapeDtypeStruct((NB, D), bf16),
            jax.ShapeDtypeStruct((NB, D), bf16),
            jax.ShapeDtypeStruct((PAIRS, 8, HALF), f32),
            jax.ShapeDtypeStruct((L, D), f32),
            jax.ShapeDtypeStruct((L, D), bf16),
            jax.ShapeDtypeStruct((HALF, NB), bf16),
        ],
        scratch_shapes=[
            pltpu.VMEM((NB, HALF), bf16),
            pltpu.VMEM((LANES, HALF), f32),
            pltpu.VMEM((HALF, D), f32),
        ],
        input_output_aliases={10: 0, 11: 4, 12: 5},
        cost_estimate=pl.CostEstimate(
            flops=H * 16 * HALF * HALF * 256, bytes_accessed=16 * L * D, transcendentals=H * L * HALF
        ),
        name="memory_attention",
    )(
        reads,
        last_rows,
        qkv,
        tail_kv,
        tail_kv,
        value_bias,
        local,
        attn_out,
        inputs,
        rows,
        mixture,
        middle,
        normed,
    )


def mlp_kernel(x_ref, ct_ref, wi_ref, bi_ref, wo_ref, *refs):
    hid_ref, dpre_ref, bias_ref, y_ref, dx_ref, y_acc, dx_acc = refs[-7:]
    step = pl.program_id(0)
    pre = dot(x_ref[...], wi_ref[...]) + bi_ref[0:1]
    squared = pre * pre
    tanh = jnp.tanh(pre * (0.7978845608028654 + 0.7978845608028654 * 0.044715 * squared))
    half = 0.5 * pre
    hidden = (half + half * tanh).astype(bf16)
    slope = (
        0.5
        + 0.5 * tanh
        + half
        * (1.0 - tanh * tanh)
        * (0.7978845608028654 + 3 * 0.7978845608028654 * 0.044715 * squared)
    )
    d_pre = (slope * dot_nt(ct_ref[...], wo_ref[...])).astype(bf16)
    hid_ref[...] = hidden
    dpre_ref[...] = d_pre
    bias_ref[...] = jnp.broadcast_to(
        jnp.sum(d_pre.astype(f32), axis=0, keepdims=True), bias_ref.shape
    )
    y = dot(hidden, wo_ref[...])
    dx = dot_nt(d_pre, wi_ref[...])

    @pl.when(step == 0)
    def _():
        y_acc[...] = y
        dx_acc[...] = dx

    @pl.when(step > 0)
    def _():
        y_acc[...] += y
        dx_acc[...] += dx

    @pl.when(step == pl.num_programs(0) - 1)
    def _():
        y_ref[...] = y_acc[...].astype(bf16)
        dx_ref[...] = dx_acc[...].astype(bf16)


def mlp_block(rows, cotangent, part, mlp_in, bias_rows, mlp_out, total, place, kept):
    count, hidden = rows.shape[0], mlp_in.shape[1]
    tile = 256 if hidden % 256 == 0 else 128
    fixed = pl.BlockSpec((count, D), lambda i: (0, 0))
    across = pl.BlockSpec((count, tile), lambda i: (place, i))
    return pl.pallas_call(
        mlp_kernel,
        grid=(hidden // tile,),
        in_specs=[
            fixed,
            pl.BlockSpec((count, D), lambda i: (part, 0)),
            pl.BlockSpec((D, tile), lambda i: (0, i)),
            pl.BlockSpec((8, tile), lambda i: (0, i)),
            pl.BlockSpec((tile, D), lambda i: (i, 0)),
        ]
        + [pl.BlockSpec(memory_space=pl.ANY)] * len(kept),
        out_specs=[across, across, pl.BlockSpec((8, tile), lambda i: (0, i)), fixed, fixed],
        out_shape=[
            jax.ShapeDtypeStruct((total, hidden), bf16),
            jax.ShapeDtypeStruct((total, hidden), bf16),
            jax.ShapeDtypeStruct((8, hidden), f32),
            jax.ShapeDtypeStruct((count, D), bf16),
            jax.ShapeDtypeStruct((count, D), bf16),
        ],
        scratch_shapes=[pltpu.VMEM((count, D), f32), pltpu.VMEM((count, D), f32)],
        input_output_aliases={5 + i: i for i in range(len(kept))},
        cost_estimate=pl.CostEstimate(
            flops=8 * count * D * hidden,
            bytes_accessed=4 * D * hidden + 4 * count * hidden + 8 * count * D,
            transcendentals=count * hidden,
        ),
        name="mlp_block",
    )(rows, cotangent, mlp_in, bias_rows, mlp_out, *kept)


def backward_kernel(
    lens,
    q_ref,
    k_ref,
    v_ref,
    mk_ref,
    mv_ref,
    db_ref,
    wo_ref,
    ll_ref,
    lm_ref,
    bt_ref,
    dqkv_ref,
    dtail_ref,
    sums_ref,
    mask,
    turned,
    dk_acc,
    dv_acc,
):
    @pl.when(pl.program_id(0) == 0)
    def _():
        fill_mask(lens, mask)

    q, k, v = q_ref[...], k_ref[...], v_ref[...]
    mem_k, mem_v = mk_ref[...], mv_ref[...]
    d_mix = dot_nt(db_ref[...], wo_ref[...]).astype(bf16)
    k_t, mk_t = k.T, mem_k.T
    d_mem_k = d_mem_v = None

    def one(keys, values, q_part, d_part, lse, extra):
        s = dot_nt(keys, q_part) * SCORE_LOG2
        if extra is not None:
            s = s + extra
        weights = jnp.exp2(s - lse)
        d_weights = dot_nt(values, d_part)
        inner = jnp.sum(weights * d_weights, axis=0, keepdims=True)
        d_scores = (weights * (d_weights - inner)).astype(bf16)
        return d_scores, dot(d_scores, q_part), dot(weights.astype(bf16), d_part)

    for head in range(2):
        rows = slice(head * HD, (head + 1) * HD)
        q_head, d_head = head_lanes(q, head), head_lanes(d_mix, head)
        for part in range(2):
            keys = HALF * (part + 1)
            cols = slice(part * HALF, (part + 1) * HALF)
            ds, dk, dv = one(
                k[:keys],
                v[:keys],
                q_head[cols],
                d_head[cols],
                ll_ref[0, head : head + 1, cols],
                mask[:keys, cols],
            )
            dq = dot(k_t[rows, :keys], ds)
            if part == 0:
                ds, d_key, d_value = one(
                    mem_k, mem_v, q_head[cols], d_head[cols], lm_ref[0, head : head + 1, :], None
                )
                dq = dq + dot(mk_t[rows], ds)
                d_mem_k = d_key if d_mem_k is None else d_mem_k + d_key
                d_mem_v = d_value if d_mem_v is None else d_mem_v + d_value
            turned[rows, cols] = dq
            if head == 0 and part == 0:
                dk_acc[:HALF] = dk
                dv_acc[:HALF] = dv
            elif head == 0:
                dk_acc[:HALF] += dk[:HALF]
                dv_acc[:HALF] += dv[:HALF]
                dk_acc[HALF:] = dk[HALF:]
                dv_acc[HALF:] = dv[HALF:]
            else:
                dk_acc[:keys] += dk
                dv_acc[:keys] += dv
    scale = HD**-0.5
    d_q = (turned[...].T * scale).astype(bf16)
    d_v = dv_acc[...].astype(bf16)
    dqkv_ref[0] = d_q
    dqkv_ref[1] = (dk_acc[...] * scale).astype(bf16)
    dqkv_ref[2] = d_v
    d_mem_k = (d_mem_k * scale).astype(bf16)
    d_mem_v = d_mem_v.astype(bf16)
    dtail_ref[0] = dot(bt_ref[...], d_mem_k).astype(bf16)
    dtail_ref[1] = dot(bt_ref[...], d_mem_v).astype(bf16)
    sums_ref[0:1] = jnp.sum(d_q.astype(f32), axis=0, keepdims=True)
    sums_ref[1:2] = jnp.sum(d_v.astype(f32), axis=0, keepdims=True) + jnp.sum(
        d_mem_v.astype(f32), axis=0, keepdims=True
    )


def attention_backward(
    first, pairs, lens, qkv, mem_k, mem_v, d_branch, attn_out, lse_local, lse_mem, basis_t
):
    column = lambda k: pl.BlockSpec((L, LANES), lambda i: (0, k * PAIRS + first + i))
    whole = lambda shape: pl.BlockSpec(shape, lambda i: (0,) * len(shape))
    width = pairs * LANES
    return pl.pallas_call(
        backward_kernel,
        grid=(pairs,),
        in_specs=[
            pl.BlockSpec(memory_space=pltpu.SMEM),
            column(0),
            column(1),
            column(2),
            column(0),
            column(0),
            whole((L, D)),
            pl.BlockSpec((LANES, D), lambda i: (first + i, 0)),
            pl.BlockSpec((1, 8, L), lambda i: (first + i, 0, 0)),
            pl.BlockSpec((1, 8, HALF), lambda i: (first + i, 0, 0)),
            whole((HALF, NB)),
        ],
        out_specs=[
            pl.BlockSpec((3, L, LANES), lambda i: (0, 0, i)),
            pl.BlockSpec((2, HALF, LANES), lambda i: (0, 0, i)),
            pl.BlockSpec((8, LANES), lambda i: (0, i)),
        ],
        out_shape=[
            jax.ShapeDtypeStruct((3, L, width), bf16),
            jax.ShapeDtypeStruct((2, HALF, width), bf16),
            jax.ShapeDtypeStruct((8, width), f32),
        ],
        scratch_shapes=[
            pltpu.VMEM((L, L), f32),
            pltpu.VMEM((LANES, L), f32),
            pltpu.VMEM((L, LANES), f32),
            pltpu.VMEM((L, LANES), f32),
        ],
        cost_estimate=pl.CostEstimate(
            flops=2 * pairs * 56 * HALF * HALF * 256,
            bytes_accessed=20 * L * width,
            transcendentals=2 * pairs * L * L,
        ),
        name="attention_backward",
    )(lens, qkv, qkv, qkv, mem_k, mem_v, d_branch, attn_out, lse_local, lse_mem, basis_t)


def rotated(value, axis, by):
    count = lax.axis_size(axis)
    return lax.ppermute(value, axis, [(i, (i + by) % count) for i in range(count)])


def swapped(value, axis, bit):
    count = lax.axis_size(axis)
    return lax.ppermute(value, axis, [(i, i ^ (1 << bit)) for i in range(count)])


def axis_bits(axis):
    return [(axis, bit) for bit in range(lax.axis_size(axis).bit_length() - 1)]


def side(axis, bit):
    return (lax.axis_index(axis) >> bit) & 1


def halve(value, axis, bit):
    count = value.shape[0] // 2
    mine = side(axis, bit)
    kept = lax.dynamic_slice_in_dim(value, mine * count, count, 0)
    given = lax.dynamic_slice_in_dim(value, (1 - mine) * count, count, 0)
    got = swapped(given, axis, bit)
    return (kept.astype(f32) + got.astype(f32)).astype(value.dtype)


def double(value, axis, bit):
    got = swapped(value, axis, bit)
    first = side(axis, bit) == 0
    return jnp.concatenate([jnp.where(first, value, got), jnp.where(first, got, value)], axis=0)


def scatter_sum(value, steps):
    for step in steps:
        value = halve(value, *step)
    return value


def gather(value, steps):
    for step in reversed(steps):
        value = double(value, *step)
    return value


def sum_small(value):
    for step in axis_bits("batch") + axis_bits("mlp"):
        value = value + swapped(value, *step)
    return value


def shards(
    inputs,
    doc_lengths,
    ln1_gain,
    ln1_bias,
    attn_in,
    qv_bias,
    attn_out,
    attn_out_bias,
    ln2_gain,
    second_norm_bias,
    mlp_in,
    mlp_in_bias,
    mlp_out,
    mlp_out_bias,
    cotangent,
):
    n_mlp = lax.axis_size("mlp")
    place = lax.axis_index("mlp")
    gain_one = ln1_gain.astype(f32)
    bias_one = ln1_bias.astype(f32)
    gain_two = ln2_gain.astype(f32)
    bias_two = second_norm_bias.astype(f32)

    own_tail = jnp.concatenate(
        [
            inputs[HALF:],
            jnp.broadcast_to(doc_lengths[:, NDOC - 1 :].astype(bf16), (16, D)),
        ],
        axis=0,
    )
    tail = rotated(own_tail, "mlp", 1)
    cotangents = [cotangent] + [rotated(cotangent, "mlp", by) for by in range(1, n_mlp)]

    activations = inputs.astype(f32)
    normed = layer_norm(activations, gain_one, bias_one).astype(bf16)
    zeros = jnp.zeros((D,), f32)
    qkv_bias = jnp.concatenate([qv_bias[0].astype(f32), zeros, qv_bias[1].astype(f32)])
    qkv = (dot(normed, attn_in) + qkv_bias).astype(bf16)
    rows = jnp.concatenate(
        [
            jnp.stack([attn_out_bias.astype(f32), gain_two, bias_two]),
            jnp.zeros((5, D), f32),
        ]
    )
    local, lse_local, mixture, middle, normed_two = local_attention(
        doc_lengths, qkv, attn_out, inputs, rows
    )
    steps = range(1, n_mlp)
    arrived_hi = [rotated(normed_two[HALF:], "mlp", by) for by in steps]

    tail_rows = tail[:HALF].astype(f32)
    normed_tail = layer_norm(tail_rows, gain_one, bias_one).astype(bf16)
    tail_kv = dot(normed_tail, attn_in[:, D:]).astype(bf16)
    reads = jnp.where(place == 0, 0, doc_lengths[:, :1])
    value_bias = jnp.broadcast_to(qv_bias[1].astype(f32), (8, D))
    mixture, mem_k, mem_v, lse_mem, middle, normed_two, basis_t = memory_attention(
        reads,
        tail[HALF:],
        qkv,
        tail_kv,
        value_bias,
        local,
        attn_out,
        inputs,
        rows,
        mixture,
        middle,
        normed_two,
    )
    arrived_lo = [rotated(normed_two[:HALF], "mlp", by) for by in steps]

    bias_rows = jnp.broadcast_to(mlp_in_bias.astype(f32), (8, mlp_in.shape[1]))
    kept = ()
    d_mlp_in_bias = 0.0
    returned_y, returned_dx = [], []
    calls = [(by, part) for by in steps for part in (1, 0)]
    for by, part in calls:
        block = (arrived_lo, arrived_hi)[part][by - 1]
        hidden, d_pre, d_bias, y, dx = mlp_block(
            block, cotangents[by], part, mlp_in, bias_rows, mlp_out, n_mlp * L, 2 * by + part, kept
        )
        kept = (hidden, d_pre)
        d_mlp_in_bias = d_mlp_in_bias + d_bias[0]
        returned_dx.append(rotated(dx, "mlp", -by))
        returned_y.append(y)
    hidden, d_pre, d_bias, y_own, dx_own = mlp_block(
        normed_two, cotangent, 0, mlp_in, bias_rows, mlp_out, n_mlp * L, 0, kept
    )
    d_mlp_in_bias = d_mlp_in_bias + d_bias[0]
    over_rows = lambda a, b: lax.dot_general(
        a, b, (((0,), (0,)), ((), ())), preferred_element_type=f32
    )
    all_rows = jnp.concatenate(
        [normed_two] + [piece for pair in zip(arrived_lo, arrived_hi) for piece in pair], axis=0
    )
    d_mlp_in = over_rows(all_rows, d_pre).astype(bf16)
    d_mlp_out = over_rows(hidden, jnp.concatenate(cotangents, axis=0)).astype(bf16)

    batch_bits, mlp_bits = axis_bits("batch"), axis_bits("mlp")
    core, near, far = batch_bits[:1], batch_bits[1:2], batch_bits[2:]
    d_mlp_in = scatter_sum(d_mlp_in, core)
    d_mlp_out = scatter_sum(d_mlp_out, core)

    returned_dx, returned_y = lax.optimization_barrier((returned_dx, returned_y))
    returned_y = [rotated(y, "mlp", -by) for (by, part), y in zip(calls, returned_y)]
    halves = [dx_own[:HALF].astype(f32), dx_own[HALF:].astype(f32)]
    for (by, part), dx in zip(calls, returned_dx):
        halves[part] = halves[part] + dx.astype(f32)
    d_normed_two = jnp.concatenate(halves, axis=0)
    upstream = cotangent.astype(f32)
    d_out_bias = jnp.sum(upstream, axis=0)
    d_middle_norm, d_ln2_gain, d_ln2_bias = norm_backward(middle, gain_two, bias_two, d_normed_two)
    d_middle = upstream + d_middle_norm
    d_branch = d_middle.astype(bf16)
    d_attn_out_bias = jnp.sum(d_branch, axis=0, dtype=f32)
    d_branch, d_mlp_in, d_mlp_out = lax.optimization_barrier((d_branch, d_mlp_in, d_mlp_out))

    in_steps, out_steps = near + far, far + near
    d_mlp_in = scatter_sum(d_mlp_in, in_steps)
    d_mlp_out = scatter_sum(d_mlp_out, out_steps)

    backward = lambda first, pairs, d: attention_backward(
        first, pairs, doc_lengths, qkv, mem_k, mem_v, d, attn_out, lse_local, lse_mem, basis_t
    )
    early = PAIRS // 3
    d_one, d_tail_one, sums_one = backward(0, early, d_branch)
    d_attn_out = over_rows(mixture, d_branch)

    def weight_grads(d, d_tail):
        return [
            over_rows(normed, d[0]),
            over_rows(normed, d[1]) + over_rows(normed_tail, d_tail[0]),
            over_rows(normed, d[2]) + over_rows(normed_tail, d_tail[1]),
        ]

    join = lambda pieces: jnp.concatenate([piece.astype(bf16) for piece in pieces], axis=1)
    grads_one = scatter_sum(join(weight_grads(d_one, d_tail_one) + [d_attn_out]), core)
    d_branch, grads_one = lax.optimization_barrier((d_branch, grads_one))
    d_two, d_tail_two, sums_two = backward(early, PAIRS - early, d_branch)
    d_two, returned_y = lax.optimization_barrier((d_two, returned_y))
    one_steps, two_steps = mlp_bits + near + far, near + mlp_bits + far
    grads_one = scatter_sum(grads_one, one_steps)
    grads_two = scatter_sum(join(weight_grads(d_two, d_tail_two)), core + two_steps)

    d_qkv = jnp.concatenate([d_one, d_two], axis=2)
    d_tail = jnp.concatenate([d_tail_one, d_tail_two], axis=2)
    sums = jnp.concatenate([sums_one, sums_two], axis=1)
    columns = [attn_in[:, i * D : (i + 1) * D] for i in range(3)]
    d_tail_rows = dot_nt(d_tail[0], columns[1]) + dot_nt(d_tail[1], columns[2])
    from_next = rotated(d_tail_rows.astype(bf16), "mlp", -1)
    d_normed = (
        dot_nt(d_qkv[0], columns[0]) + dot_nt(d_qkv[1], columns[1]) + dot_nt(d_qkv[2], columns[2])
    )
    unused, d_ln1_gain, d_ln1_bias = norm_backward(activations, gain_one, bias_one, d_normed)
    unused, d_tail_gain, d_tail_bias = norm_backward(tail_rows, gain_one, bias_one, d_tail_rows)
    d_ln1_gain, d_ln1_bias = d_ln1_gain + d_tail_gain, d_ln1_bias + d_tail_bias

    hidden_count = mlp_in.shape[1]
    placed_bias = lax.dynamic_update_slice(
        jnp.zeros((n_mlp * hidden_count,), f32), d_mlp_in_bias, (place * hidden_count,)
    )
    vectors = jnp.concatenate(
        [
            jnp.stack(
                [d_ln1_gain, d_ln1_bias, d_attn_out_bias, d_ln2_gain, d_ln2_bias, d_out_bias]
            ),
            sums[:2],
            placed_bias.reshape(-1, D),
        ],
        axis=0,
    )
    vectors = sum_small(vectors)

    d_normed = jnp.concatenate(
        [d_normed[:HALF], d_normed[HALF:] + from_next.astype(f32)], axis=0
    )
    d_in_norm, unused, unused = norm_backward(activations, gain_one, bias_one, d_normed)
    input_grad = (d_middle + d_in_norm).astype(bf16)

    halves = [y_own[:HALF].astype(f32), y_own[HALF:].astype(f32)]
    for (by, part), y in zip(calls, returned_y):
        halves[part] = halves[part] + y.astype(f32)
    result = jnp.concatenate(halves, axis=0)
    layer_output = (middle + (result + mlp_out_bias)).astype(bf16)

    d_mlp_in = gather(d_mlp_in, core + in_steps)
    d_mlp_out = gather(d_mlp_out, core + out_steps)
    grads_one = gather(grads_one, core + one_steps)
    grads_two = gather(grads_two, core + two_steps)
    width = early * LANES
    rest = D - width
    d_attn_in = jnp.concatenate(
        [
            piece
            for i in range(3)
            for piece in (
                grads_one[:, i * width : (i + 1) * width],
                grads_two[:, i * rest : (i + 1) * rest],
            )
        ],
        axis=1,
    )
    return (
        layer_output,
        input_grad,
        vectors[0],
        vectors[1],
        d_attn_in.astype(f32),
        vectors[6:8],
        grads_one[:, 3 * width :].astype(f32),
        vectors[2],
        vectors[3],
        vectors[4],
        d_mlp_in.astype(f32),
        lax.dynamic_slice(vectors[8:].reshape(-1), (place * hidden_count,), (hidden_count,)),
        d_mlp_out.astype(f32),
        vectors[5],
    )


def solution(mesh):
    rows, whole = P(("batch", "mlp"), None), P()
    columns, hidden, depth = P(None, "mlp"), P("mlp"), P("mlp", None)
    return jax.shard_map(
        shards,
        mesh=mesh,
        in_specs=(rows, rows) + (whole,) * 8 + (columns, hidden, depth, whole, rows),
        out_specs=(rows, rows) + (whole,) * 8 + (columns, hidden, depth, whole),
        check_vma=False,
    )
```

```python
import jax
import jax.numpy as jnp
from jax import lax
from jax.experimental import pallas as pl
from jax.experimental.pallas import tpu as pltpu
from jax.sharding import PartitionSpec as P

D = 768
H = 12
HD = 64
NB = 512
L = 512
NDOC = 3
HALF = L // 2
PAIRS = H // 2
LANES = 2 * HD

LOG2E = 1.4426950408889634
SCORE_LOG2 = LOG2E * HD**-0.5
MASKED = -1e30

bf16 = jnp.bfloat16
f32 = jnp.float32


def dot(a, b):
    return jnp.dot(a, b, preferred_element_type=f32)


def dot_nt(a, b):
    return lax.dot_general(a, b, (((1,), (1,)), ((), ())), preferred_element_type=f32)


def layer_norm(matrix, gain_row, shift_row):
    center = jnp.mean(matrix, axis=-1, keepdims=True)
    centered = matrix - center
    spread = jnp.mean(centered * centered, axis=-1, keepdims=True)
    return centered * lax.rsqrt(spread + 1e-05) * gain_row + shift_row


def norm_backward(matrix, gain_row, shift_row, upstream):
    unused, pullback = jax.vjp(layer_norm, matrix, gain_row, shift_row)
    return pullback(upstream)


def head_lanes(matrix, head):
    lane = lax.broadcasted_iota(jnp.int32, (1, LANES), 1)
    return jnp.where(lane // HD == head, matrix, jnp.zeros_like(matrix))


def fill_mask(lens, mask):
    key = lax.broadcasted_iota(jnp.int32, (L, L), 0)
    query = lax.broadcasted_iota(jnp.int32, (L, L), 1)
    one = lens[0, 0]
    two = one + lens[0, 1]
    start = jnp.where(query >= two, two, jnp.where(query >= one, one, 0))
    mask[...] = jnp.where((key <= query) & (key >= start), 0.0, MASKED)


def local_kernel(
    lens,
    q_ref,
    k_ref,
    v_ref,
    wo_ref,
    x_ref,
    rows_ref,
    out_ref,
    lse_ref,
    mix_ref,
    middle_ref,
    normed_ref,
    mask,
    turned,
    acc,
):
    step = pl.program_id(0)

    @pl.when(step == 0)
    def _():
        fill_mask(lens, mask)
        acc[...] = jnp.zeros_like(acc)

    q, k = q_ref[...], k_ref[...]
    v_t = v_ref[...].T
    for head in range(2):
        q_head = head_lanes(q, head)
        rows = slice(head * HD, (head + 1) * HD)
        for part in range(2):
            keys = HALF * (part + 1)
            cols = slice(part * HALF, (part + 1) * HALF)
            s = dot_nt(k[:keys], q_head[cols]) * SCORE_LOG2 + mask[:keys, cols]
            top = jnp.max(s, axis=0, keepdims=True)
            e = jnp.exp2(s - top)
            total = jnp.sum(e, axis=0, keepdims=True)
            out = dot(v_t[rows, :keys], e.astype(bf16))
            turned[rows, cols] = out / total
            lse_ref[0, head : head + 1, cols] = top + jnp.log2(total)
    out_ref[...] = turned[:, :HALF].T
    mixed = turned[:, HALF:].T.astype(bf16)
    mix_ref[...] = mixed
    acc[...] += dot(mixed, wo_ref[...])

    @pl.when(step == PAIRS - 1)
    def _():
        finish_middle(x_ref, acc, rows_ref, middle_ref, normed_ref)


def finish_middle(x_ref, acc, rows_ref, middle_ref, normed_ref):
    middle = x_ref[...].astype(f32) + (acc[...] + rows_ref[0:1])
    middle_ref[...] = middle
    normed_ref[...] = layer_norm(middle, rows_ref[1:2], rows_ref[2:3]).astype(bf16)


def local_attention(lens, qkv, attn_out, inputs, rows):
    column = lambda k: pl.BlockSpec((L, LANES), lambda i: (0, k * PAIRS + i))
    upper = pl.BlockSpec((HALF, D), lambda i: (1, 0))
    return pl.pallas_call(
        local_kernel,
        grid=(PAIRS,),
        in_specs=[
            pl.BlockSpec(memory_space=pltpu.SMEM),
            column(0),
            column(1),
            column(2),
            pl.BlockSpec((LANES, D), lambda i: (i, 0)),
            upper,
            pl.BlockSpec((8, D), lambda i: (0, 0)),
        ],
        out_specs=[
            pl.BlockSpec((HALF, LANES), lambda i: (0, i)),
            pl.BlockSpec((1, 8, L), lambda i: (i, 0, 0)),
            pl.BlockSpec((HALF, LANES), lambda i: (1, i)),
            upper,
            upper,
        ],
        out_shape=[
            jax.ShapeDtypeStruct((HALF, D), f32),
            jax.ShapeDtypeStruct((PAIRS, 8, L), f32),
            jax.ShapeDtypeStruct((L, D), bf16),
            jax.ShapeDtypeStruct((L, D), f32),
            jax.ShapeDtypeStruct((L, D), bf16),
        ],
        scratch_shapes=[
            pltpu.VMEM((L, L), f32),
            pltpu.VMEM((LANES, L), f32),
            pltpu.VMEM((HALF, D), f32),
        ],
        cost_estimate=pl.CostEstimate(
            flops=H * 12 * HALF * HALF * 256, bytes_accessed=8 * L * D, transcendentals=H * L * L
        ),
        name="local_attention",
    )(lens, qkv, qkv, qkv, attn_out, inputs, rows)


def basis_rows(last_len, transposed):
    shape = (HALF, NB) if transposed else (NB, HALF)
    slot_dim, place_dim = (1, 0) if transposed else (0, 1)
    slot = lax.broadcasted_iota(jnp.int32, shape, slot_dim).astype(f32)
    place = lax.broadcasted_iota(jnp.int32, shape, place_dim).astype(f32)
    offsets = place - HALF + last_len + 0.5
    distances = (slot + 0.5) / NB * last_len - offsets
    weights = jnp.where(offsets > 0.0, jnp.exp(-0.5 * distances * distances), 0.0)
    return weights / jnp.sum(weights, axis=place_dim, keepdims=True)


def memory_kernel(
    reads,
    last_ref,
    q_ref,
    kt_ref,
    vt_ref,
    vb_ref,
    local_ref,
    wo_ref,
    x_ref,
    rows_ref,
    mix_whole,
    middle_whole,
    normed_whole,
    mix_ref,
    mk_ref,
    mv_ref,
    lse_ref,
    middle_ref,
    normed_ref,
    basis_t_ref,
    basis,
    turned,
    acc,
):
    step = pl.program_id(0)

    @pl.when(step == 0)
    def _():
        last_len = last_ref[0:1, 0:1]
        basis[...] = basis_rows(last_len, False).astype(bf16)
        basis_t_ref[...] = basis_rows(last_len, True).astype(bf16)
        acc[...] = jnp.zeros_like(acc)

    mem_k = dot(basis[...], kt_ref[...]).astype(bf16)
    mem_v = (dot(basis[...], vt_ref[...]) + vb_ref[0:1]).astype(bf16)
    mk_ref[...] = mem_k
    mv_ref[...] = mem_v
    v_t = mem_v.T
    query = lax.broadcasted_iota(jnp.int32, (1, HALF), 1)
    reading = query < reads[0, 0]
    q = q_ref[...]
    for head in range(2):
        rows = slice(head * HD, (head + 1) * HD)
        s = dot_nt(mem_k, head_lanes(q, head)) * SCORE_LOG2
        top = jnp.max(s, axis=0, keepdims=True)
        e = jnp.exp2(s - top)
        total = jnp.sum(e, axis=0, keepdims=True)
        out = dot(v_t[rows], e.astype(bf16))
        turned[rows, :] = jnp.where(reading, out / total, 0.0)
        lse_ref[0, head : head + 1, :] = jnp.where(reading, top + jnp.log2(total), -MASKED)
    mixed = (local_ref[...] + turned[...].T).astype(bf16)
    mix_ref[...] = mixed
    acc[...] += dot(mixed, wo_ref[...])

    @pl.when(step == PAIRS - 1)
    def _():
        finish_middle(x_ref, acc, rows_ref, middle_ref, normed_ref)


def memory_attention(
    reads, last_rows, qkv, tail_kv, value_bias, local, attn_out, inputs, rows, mixture, middle, normed
):
    whole = lambda shape: pl.BlockSpec(shape, lambda i: (0,) * len(shape))
    untouched = pl.BlockSpec(memory_space=pl.ANY)
    return pl.pallas_call(
        memory_kernel,
        grid=(PAIRS,),
        in_specs=[
            pl.BlockSpec(memory_space=pltpu.SMEM),
            whole((16, D)),
            pl.BlockSpec((HALF, LANES), lambda i: (0, i)),
            pl.BlockSpec((HALF, LANES), lambda i: (0, i)),
            pl.BlockSpec((HALF, LANES), lambda i: (0, PAIRS + i)),
            pl.BlockSpec((8, LANES), lambda i: (0, i)),
            pl.BlockSpec((HALF, LANES), lambda i: (0, i)),
            pl.BlockSpec((LANES, D), lambda i: (i, 0)),
            whole((HALF, D)),
            whole((8, D)),
            untouched,
            untouched,
            untouched,
        ],
        out_specs=[
            pl.BlockSpec((HALF, LANES), lambda i: (0, i)),
            pl.BlockSpec((NB, LANES), lambda i: (0, i)),
            pl.BlockSpec((NB, LANES), lambda i: (0, i)),
            pl.BlockSpec((1, 8, HALF), lambda i: (i, 0, 0)),
            whole((HALF, D)),
            whole((HALF, D)),
            whole((HALF, NB)),
        ],
        out_shape=[
            jax.ShapeDtypeStruct((L, D), bf16),
            jax.ShapeDtypeStruct((NB, D), bf16),
            jax.ShapeDtypeStruct((NB, D), bf16),
            jax.ShapeDtypeStruct((PAIRS, 8, HALF), f32),
            jax.ShapeDtypeStruct((L, D), f32),
            jax.ShapeDtypeStruct((L, D), bf16),
            jax.ShapeDtypeStruct((HALF, NB), bf16),
        ],
        scratch_shapes=[
            pltpu.VMEM((NB, HALF), bf16),
            pltpu.VMEM((LANES, HALF), f32),
            pltpu.VMEM((HALF, D), f32),
        ],
        input_output_aliases={10: 0, 11: 4, 12: 5},
        cost_estimate=pl.CostEstimate(
            flops=H * 16 * HALF * HALF * 256, bytes_accessed=16 * L * D, transcendentals=H * L * HALF
        ),
        name="memory_attention",
    )(
        reads,
        last_rows,
        qkv,
        tail_kv,
        tail_kv,
        value_bias,
        local,
        attn_out,
        inputs,
        rows,
        mixture,
        middle,
        normed,
    )


def mlp_kernel(x_ref, ct_ref, wi_ref, bi_ref, wo_ref, *refs):
    hid_ref, dpre_ref, bias_ref, y_ref, dx_ref, y_acc, dx_acc = refs[-7:]
    step = pl.program_id(0)
    pre = dot(x_ref[...], wi_ref[...]) + bi_ref[0:1]
    squared = pre * pre
    tanh = jnp.tanh(pre * (0.7978845608028654 + 0.7978845608028654 * 0.044715 * squared))
    half = 0.5 * pre
    hidden = (half + half * tanh).astype(bf16)
    slope = (
        0.5
        + 0.5 * tanh
        + half
        * (1.0 - tanh * tanh)
        * (0.7978845608028654 + 3 * 0.7978845608028654 * 0.044715 * squared)
    )
    d_pre = (slope * dot_nt(ct_ref[...], wo_ref[...])).astype(bf16)
    hid_ref[...] = hidden
    dpre_ref[...] = d_pre
    bias_ref[...] = jnp.broadcast_to(
        jnp.sum(d_pre.astype(f32), axis=0, keepdims=True), bias_ref.shape
    )
    y = dot(hidden, wo_ref[...])
    dx = dot_nt(d_pre, wi_ref[...])

    @pl.when(step == 0)
    def _():
        y_acc[...] = y
        dx_acc[...] = dx

    @pl.when(step > 0)
    def _():
        y_acc[...] += y
        dx_acc[...] += dx

    @pl.when(step == pl.num_programs(0) - 1)
    def _():
        y_ref[...] = y_acc[...].astype(bf16)
        dx_ref[...] = dx_acc[...].astype(bf16)


def mlp_block(rows, cotangent, part, mlp_in, bias_rows, mlp_out, total, place, kept):
    count, hidden = rows.shape[0], mlp_in.shape[1]
    tile = 256 if hidden % 256 == 0 else 128
    fixed = pl.BlockSpec((count, D), lambda i: (0, 0))
    across = pl.BlockSpec((count, tile), lambda i: (place, i))
    return pl.pallas_call(
        mlp_kernel,
        grid=(hidden // tile,),
        in_specs=[
            fixed,
            pl.BlockSpec((count, D), lambda i: (part, 0)),
            pl.BlockSpec((D, tile), lambda i: (0, i)),
            pl.BlockSpec((8, tile), lambda i: (0, i)),
            pl.BlockSpec((tile, D), lambda i: (i, 0)),
        ]
        + [pl.BlockSpec(memory_space=pl.ANY)] * len(kept),
        out_specs=[across, across, pl.BlockSpec((8, tile), lambda i: (0, i)), fixed, fixed],
        out_shape=[
            jax.ShapeDtypeStruct((total, hidden), bf16),
            jax.ShapeDtypeStruct((total, hidden), bf16),
            jax.ShapeDtypeStruct((8, hidden), f32),
            jax.ShapeDtypeStruct((count, D), bf16),
            jax.ShapeDtypeStruct((count, D), bf16),
        ],
        scratch_shapes=[pltpu.VMEM((count, D), f32), pltpu.VMEM((count, D), f32)],
        input_output_aliases={5 + i: i for i in range(len(kept))},
        cost_estimate=pl.CostEstimate(
            flops=8 * count * D * hidden,
            bytes_accessed=4 * D * hidden + 4 * count * hidden + 8 * count * D,
            transcendentals=count * hidden,
        ),
        name="mlp_block",
    )(rows, cotangent, mlp_in, bias_rows, mlp_out, *kept)


def backward_kernel(
    lens,
    q_ref,
    k_ref,
    v_ref,
    mk_ref,
    mv_ref,
    db_ref,
    wo_ref,
    ll_ref,
    lm_ref,
    bt_ref,
    dqkv_ref,
    dtail_ref,
    sums_ref,
    mask,
    turned,
    dk_acc,
    dv_acc,
):
    @pl.when(pl.program_id(0) == 0)
    def _():
        fill_mask(lens, mask)

    q, k, v = q_ref[...], k_ref[...], v_ref[...]
    mem_k, mem_v = mk_ref[...], mv_ref[...]
    d_mix = dot_nt(db_ref[...], wo_ref[...]).astype(bf16)
    k_t, mk_t = k.T, mem_k.T
    d_mem_k = d_mem_v = None

    def one(keys, values, q_part, d_part, lse, extra):
        s = dot_nt(keys, q_part) * SCORE_LOG2
        if extra is not None:
            s = s + extra
        weights = jnp.exp2(s - lse)
        d_weights = dot_nt(values, d_part)
        inner = jnp.sum(weights * d_weights, axis=0, keepdims=True)
        d_scores = (weights * (d_weights - inner)).astype(bf16)
        return d_scores, dot(d_scores, q_part), dot(weights.astype(bf16), d_part)

    for head in range(2):
        rows = slice(head * HD, (head + 1) * HD)
        q_head, d_head = head_lanes(q, head), head_lanes(d_mix, head)
        for part in range(2):
            keys = HALF * (part + 1)
            cols = slice(part * HALF, (part + 1) * HALF)
            ds, dk, dv = one(
                k[:keys],
                v[:keys],
                q_head[cols],
                d_head[cols],
                ll_ref[0, head : head + 1, cols],
                mask[:keys, cols],
            )
            dq = dot(k_t[rows, :keys], ds)
            if part == 0:
                ds, d_key, d_value = one(
                    mem_k, mem_v, q_head[cols], d_head[cols], lm_ref[0, head : head + 1, :], None
                )
                dq = dq + dot(mk_t[rows], ds)
                d_mem_k = d_key if d_mem_k is None else d_mem_k + d_key
                d_mem_v = d_value if d_mem_v is None else d_mem_v + d_value
            turned[rows, cols] = dq
            if head == 0 and part == 0:
                dk_acc[:HALF] = dk
                dv_acc[:HALF] = dv
            elif head == 0:
                dk_acc[:HALF] += dk[:HALF]
                dv_acc[:HALF] += dv[:HALF]
                dk_acc[HALF:] = dk[HALF:]
                dv_acc[HALF:] = dv[HALF:]
            else:
                dk_acc[:keys] += dk
                dv_acc[:keys] += dv
    scale = HD**-0.5
    d_q = (turned[...].T * scale).astype(bf16)
    d_v = dv_acc[...].astype(bf16)
    dqkv_ref[0] = d_q
    dqkv_ref[1] = (dk_acc[...] * scale).astype(bf16)
    dqkv_ref[2] = d_v
    d_mem_k = (d_mem_k * scale).astype(bf16)
    d_mem_v = d_mem_v.astype(bf16)
    dtail_ref[0] = dot(bt_ref[...], d_mem_k).astype(bf16)
    dtail_ref[1] = dot(bt_ref[...], d_mem_v).astype(bf16)
    sums_ref[0:1] = jnp.sum(d_q.astype(f32), axis=0, keepdims=True)
    sums_ref[1:2] = jnp.sum(d_v.astype(f32), axis=0, keepdims=True) + jnp.sum(
        d_mem_v.astype(f32), axis=0, keepdims=True
    )


HIDDEN = pl.CostEstimate(flops=1000, bytes_accessed=1000, transcendentals=0)


def attention_backward(
    first, pairs, lens, qkv, mem_k, mem_v, d_branch, attn_out, lse_local, lse_mem, basis_t
):
    column = lambda k: pl.BlockSpec((L, LANES), lambda i: (0, k * PAIRS + first + i))
    whole = lambda shape: pl.BlockSpec(shape, lambda i: (0,) * len(shape))
    width = pairs * LANES
    return pl.pallas_call(
        backward_kernel,
        grid=(pairs,),
        in_specs=[
            pl.BlockSpec(memory_space=pltpu.SMEM),
            column(0),
            column(1),
            column(2),
            column(0),
            column(0),
            whole((L, D)),
            pl.BlockSpec((LANES, D), lambda i: (first + i, 0)),
            pl.BlockSpec((1, 8, L), lambda i: (first + i, 0, 0)),
            pl.BlockSpec((1, 8, HALF), lambda i: (first + i, 0, 0)),
            whole((HALF, NB)),
        ],
        out_specs=[
            pl.BlockSpec((3, L, LANES), lambda i: (0, 0, i)),
            pl.BlockSpec((2, HALF, LANES), lambda i: (0, 0, i)),
            pl.BlockSpec((8, LANES), lambda i: (0, i)),
        ],
        out_shape=[
            jax.ShapeDtypeStruct((3, L, width), bf16),
            jax.ShapeDtypeStruct((2, HALF, width), bf16),
            jax.ShapeDtypeStruct((8, width), f32),
        ],
        scratch_shapes=[
            pltpu.VMEM((L, L), f32),
            pltpu.VMEM((LANES, L), f32),
            pltpu.VMEM((L, LANES), f32),
            pltpu.VMEM((L, LANES), f32),
        ],
        cost_estimate=pl.CostEstimate(
            flops=2 * pairs * 56 * HALF * HALF * 256,
            bytes_accessed=20 * L * width,
            transcendentals=2 * pairs * L * L,
        ),
        name="attention_backward",
    )(lens, qkv, qkv, qkv, mem_k, mem_v, d_branch, attn_out, lse_local, lse_mem, basis_t)


def rotated(value, axis, by):
    count = lax.axis_size(axis)
    return lax.ppermute(value, axis, [(i, (i + by) % count) for i in range(count)])


fence = lax.optimization_barrier
MLP_DUE = 11
GRID = ("batch", "mlp")


def flipped(value, mask):
    count = lax.axis_size("batch") * lax.axis_size("mlp")
    return lax.ppermute(value, GRID, [(i, i ^ mask) for i in range(count)])


def place_in(bits):
    number = lax.axis_index(GRID)
    return sum(((number >> bit) & 1) << i for i, bit in enumerate(bits))


def peers(bits):
    return [sum(((q >> i) & 1) << bit for i, bit in enumerate(bits)) for q in range(1, 1 << len(bits))]


def grouped(bits):
    odd = len(bits) % 2
    return ([bits[:1]] if odd else []) + [bits[i : i + 2] for i in range(odd, len(bits), 2)]


class Chain:
    def __init__(self, kept, given, groups):
        self.stages = [(True, bits) for bits in groups] + [(False, bits) for bits in groups[::-1]]
        self.turn()
        self.kept, self.given = kept, [given]

    def turn(self):
        self.scatters, self.bits = self.stages.pop(0)
        self.place = place_in(self.bits)

    def prepare(self):
        self.turn()
        count = 1 << len(self.bits)
        if self.scatters:
            size = self.value.shape[0] // count
            piece = lambda i: lax.dynamic_slice_in_dim(self.value, i * size, size, 0)
            self.kept = piece(self.place)
            self.given = [piece(self.place ^ q) for q in range(1, count)]
        else:
            self.kept = self.value
            self.given = [self.value]

    def fly(self):
        masks = peers(self.bits)
        given = self.given if self.scatters else self.given * len(masks)
        self.got = [flipped(piece, mask) for piece, mask in zip(given, masks)]

    def land(self):
        if self.scatters:
            total = self.kept.astype(f32)
            for piece in self.got:
                total = total + piece.astype(f32)
            self.value = total.astype(self.kept.dtype)
        else:
            pieces = [self.kept] + self.got
            order = [
                lax.select_n(self.place ^ i, *pieces)
                if len(pieces) > 2
                else jnp.where(self.place == i, *pieces)
                for i in range(len(pieces))
            ]
            self.value = jnp.concatenate(order, axis=0)
        if self.stages:
            self.prepare()
            return True
        return False


def sum_small(value, groups):
    for bits in groups:
        value = value + sum(flipped(value, mask) for mask in peers(bits))
    return value


def weight_grads(normed, normed_tail, d, d_tail, ready, side):
    width = d.shape[2]
    tile = 256
    each = width // tile
    extra = 0 if ready is None else ready.shape[1] // tile
    half = D // 2

    def kernel(side_ref, n_ref, nt_ref, d_ref, dt_ref, *refs):
        kept_ref, given_ref, turned, tail_turned = refs[-4:]
        step = pl.program_id(0)

        @pl.when(step == 0)
        def _():
            turned[...] = n_ref[...].T
            tail_turned[...] = nt_ref[...].T

        def rows(which, ref):
            return ref[pl.ds(pl.multiple_of(which * half, half), half), :]

        for which, out_ref in ((side_ref[0], kept_ref), (1 - side_ref[0], given_ref)):

            @pl.when(step < each)
            def _():
                out_ref[...] = dot(rows(which, turned), d_ref[0]).astype(bf16)

            @pl.when((step >= each) & (step < 3 * each))
            def _():
                out_ref[...] = (
                    dot(rows(which, turned), d_ref[0]) + dot(rows(which, tail_turned), dt_ref[0])
                ).astype(bf16)

            if extra:

                @pl.when(step >= 3 * each)
                def _():
                    out_ref[...] = rows(which, refs[0])

    column = lambda i: jnp.where(i < 3 * each, i % each, each - 1)
    in_specs = [
        pl.BlockSpec(memory_space=pltpu.SMEM),
        pl.BlockSpec((L, D), lambda i: (0, 0)),
        pl.BlockSpec((HALF, D), lambda i: (0, 0)),
        pl.BlockSpec((1, L, tile), lambda i: (jnp.minimum(i // each, 2), 0, column(i))),
        pl.BlockSpec((1, HALF, tile), lambda i: (jnp.clip(i // each - 1, 0, 1), 0, column(i))),
    ]
    operands = [side, normed, normed_tail, d, d_tail]
    if extra:
        in_specs.append(pl.BlockSpec((D, tile), lambda i: (0, jnp.maximum(i - 3 * each, 0))))
        operands.append(ready)
    steps = 3 * each + extra
    return pl.pallas_call(
        kernel,
        grid=(steps,),
        in_specs=in_specs,
        out_specs=[pl.BlockSpec((half, tile), lambda i: (0, i))] * 2,
        out_shape=[jax.ShapeDtypeStruct((half, steps * tile), bf16)] * 2,
        scratch_shapes=[pltpu.VMEM((D, L), bf16), pltpu.VMEM((D, HALF), bf16)],
        cost_estimate=HIDDEN,
        name="weight_grads",
    )(*operands)


def shards(
    inputs,
    doc_lengths,
    ln1_gain,
    ln1_bias,
    attn_in,
    qv_bias,
    attn_out,
    attn_out_bias,
    ln2_gain,
    second_norm_bias,
    mlp_in,
    mlp_in_bias,
    mlp_out,
    mlp_out_bias,
    cotangent,
):
    n_mlp = lax.axis_size("mlp")
    place = lax.axis_index("mlp")
    gain_one = ln1_gain.astype(f32)
    bias_one = ln1_bias.astype(f32)
    gain_two = ln2_gain.astype(f32)
    bias_two = second_norm_bias.astype(f32)

    own_tail = jnp.concatenate(
        [
            inputs[HALF:],
            jnp.broadcast_to(doc_lengths[:, NDOC - 1 :].astype(bf16), (16, D)),
        ],
        axis=0,
    )
    tail = rotated(own_tail, "mlp", 1)
    cotangents = [cotangent] + [rotated(cotangent, "mlp", by) for by in range(1, n_mlp)]

    activations = inputs.astype(f32)
    normed = layer_norm(activations, gain_one, bias_one).astype(bf16)
    zeros = jnp.zeros((D,), f32)
    qkv_bias = jnp.concatenate([qv_bias[0].astype(f32), zeros, qv_bias[1].astype(f32)])
    qkv = (dot(normed, attn_in) + qkv_bias).astype(bf16)
    rows = jnp.concatenate(
        [
            jnp.stack([attn_out_bias.astype(f32), gain_two, bias_two]),
            jnp.zeros((5, D), f32),
        ]
    )
    local, lse_local, mixture, middle, normed_two = local_attention(
        doc_lengths, qkv, attn_out, inputs, rows
    )
    steps = range(1, n_mlp)
    arrived_hi = [rotated(normed_two[HALF:], "mlp", by) for by in steps]

    tail_rows = tail[:HALF].astype(f32)
    normed_tail = layer_norm(tail_rows, gain_one, bias_one).astype(bf16)
    tail_kv = dot(normed_tail, attn_in[:, D:]).astype(bf16)
    reads = jnp.where(place == 0, 0, doc_lengths[:, :1])
    value_bias = jnp.broadcast_to(qv_bias[1].astype(f32), (8, D))
    tail_kv, *cotangents[1:] = fence((tail_kv, *cotangents[1:]))
    mixture, mem_k, mem_v, lse_mem, middle, normed_two, basis_t = memory_attention(
        reads,
        tail[HALF:],
        qkv,
        tail_kv,
        value_bias,
        local,
        attn_out,
        inputs,
        rows,
        mixture,
        middle,
        normed_two,
    )
    arrived_lo = [rotated(normed_two[:HALF], "mlp", by) for by in steps]

    bias_rows = jnp.broadcast_to(mlp_in_bias.astype(f32), (8, mlp_in.shape[1]))
    kept = ()
    d_mlp_in_bias = 0.0
    returned_y, returned_dx = [], []
    calls = [(by, part) for by in steps for part in (1, 0)]
    for by, part in calls:
        block = (arrived_lo, arrived_hi)[part][by - 1]
        hidden, d_pre, d_bias, y, dx = mlp_block(
            block, cotangents[by], part, mlp_in, bias_rows, mlp_out, n_mlp * L, 2 * by + part, kept
        )
        kept = (hidden, d_pre)
        d_mlp_in_bias = d_mlp_in_bias + d_bias[0]
        returned_dx.append(rotated(dx, "mlp", -by))
        returned_y.append(y)
    hidden, d_pre, d_bias, y_own, dx_own = mlp_block(
        normed_two, cotangent, 0, mlp_in, bias_rows, mlp_out, n_mlp * L, 0, kept
    )
    d_mlp_in_bias = d_mlp_in_bias + d_bias[0]
    over_rows = lambda a, b: lax.dot_general(
        a, b, (((0,), (0,)), ((), ())), preferred_element_type=f32
    )
    all_rows = jnp.concatenate(
        [normed_two] + [piece for pair in zip(arrived_lo, arrived_hi) for piece in pair], axis=0
    )
    d_mlp_in = over_rows(all_rows, d_pre).astype(bf16)
    d_mlp_out = over_rows(hidden, jnp.concatenate(cotangents, axis=0)).astype(bf16)

    hidden_count = mlp_in.shape[1]
    mlp_count = n_mlp.bit_length() - 1
    batch_count = lax.axis_size("batch").bit_length() - 1
    mlp_bits = list(range(mlp_count))
    core = [[mlp_count]]
    rest = list(range(mlp_count + 1, mlp_count + batch_count))
    groups = core + [mlp_bits[:1] + rest[:1]] + [[bit] for bit in mlp_bits[1:] + rest[1:]]

    halves = [dx_own[:HALF].astype(f32), dx_own[HALF:].astype(f32)]
    for (by, part), dx in zip(calls, returned_dx):
        halves[part] = halves[part] + dx.astype(f32)
    d_normed_two = jnp.concatenate(halves, axis=0)
    upstream = cotangent.astype(f32)
    d_out_bias = jnp.sum(upstream, axis=0)
    d_middle_norm, d_ln2_gain, d_ln2_bias = norm_backward(middle, gain_two, bias_two, d_normed_two)
    d_middle = upstream + d_middle_norm
    d_branch = d_middle.astype(bf16)
    d_attn_out_bias = jnp.sum(d_branch, axis=0, dtype=f32)

    d_branch, d_mlp_in, d_mlp_out = fence((d_branch, d_mlp_in, d_mlp_out))
    d_mlp_in, d_mlp_out = lax.psum((d_mlp_in, d_mlp_out), "batch")

    backward = lambda first, pairs, d: attention_backward(
        first, pairs, doc_lengths, qkv, mem_k, mem_v, d, attn_out, lse_local, lse_mem, basis_t
    )
    early = PAIRS // 3
    side = place_in(core[0]).reshape(1)
    d_one, d_tail_one, sums_one = backward(0, early, d_branch)
    d_attn_out = over_rows(mixture, d_branch).astype(bf16)
    chain_one = Chain(
        *weight_grads(normed, normed_tail, d_one, d_tail_one, d_attn_out, side), groups
    )
    chain_one.fly()
    chain_one.land()
    d_branch, chain_one.given = fence((d_branch, chain_one.given))
    chain_one.fly()
    d_two, d_tail_two, sums_two = backward(early, PAIRS - early, d_branch)
    d_two, d_tail_two, chain_one.got = fence((d_two, d_tail_two, chain_one.got))
    chain_one.land()
    d_two, d_tail_two, chain_one.given = fence((d_two, d_tail_two, chain_one.given))
    chain_one.fly()
    chain_two = Chain(*weight_grads(normed, normed_tail, d_two, d_tail_two, None, side), groups)
    chain_two.fly()
    chain_two.land()
    d_qkv, d_tail, sums, later, chain_two.given = fence(
        (
            (d_one, d_two),
            (d_tail_one, d_tail_two),
            (sums_one, sums_two),
            (d_mlp_in_bias, returned_y, y_own),
            chain_two.given,
        )
    )
    d_mlp_in_bias, returned_y, y_own = later
    chain_two.fly()
    returned_y = [rotated(y, "mlp", -by) for (by, part), y in zip(calls, returned_y)]

    token = chain_two.given
    flying = [chain_one, chain_two]
    events = 0
    while flying:
        for chain in list(flying):
            if events == MLP_DUE:
                chain.got, token, d_mlp_in, d_mlp_out = fence(
                    (chain.got, token, d_mlp_in, d_mlp_out)
                )
            else:
                chain.got, token = fence((chain.got, token))
            events += 1
            if chain.land():
                token = chain.given
                chain.fly()
            else:
                flying.remove(chain)

    d_qkv = jnp.concatenate(d_qkv, axis=2)
    d_tail = jnp.concatenate(d_tail, axis=2)
    sums = jnp.concatenate(sums, axis=1)
    columns = [attn_in[:, i * D : (i + 1) * D] for i in range(3)]
    d_tail_rows = dot_nt(d_tail[0], columns[1]) + dot_nt(d_tail[1], columns[2])
    from_next = rotated(d_tail_rows.astype(bf16), "mlp", -1)
    d_normed = (
        dot_nt(d_qkv[0], columns[0]) + dot_nt(d_qkv[1], columns[1]) + dot_nt(d_qkv[2], columns[2])
    )
    unused, d_ln1_gain, d_ln1_bias = norm_backward(activations, gain_one, bias_one, d_normed)
    unused, d_tail_gain, d_tail_bias = norm_backward(tail_rows, gain_one, bias_one, d_tail_rows)
    d_ln1_gain, d_ln1_bias = d_ln1_gain + d_tail_gain, d_ln1_bias + d_tail_bias

    placed_bias = lax.dynamic_update_slice(
        jnp.zeros((n_mlp * hidden_count,), f32), d_mlp_in_bias, (place * hidden_count,)
    )
    vectors = jnp.concatenate(
        [
            jnp.stack(
                [d_ln1_gain, d_ln1_bias, d_attn_out_bias, d_ln2_gain, d_ln2_bias, d_out_bias]
            ),
            sums[:2],
            placed_bias.reshape(-1, D),
        ],
        axis=0,
    )
    vectors = sum_small(vectors, groups)

    d_normed = jnp.concatenate(
        [d_normed[:HALF], d_normed[HALF:] + from_next.astype(f32)], axis=0
    )
    d_in_norm, unused, unused = norm_backward(activations, gain_one, bias_one, d_normed)
    input_grad = (d_middle + d_in_norm).astype(bf16)

    halves = [y_own[:HALF].astype(f32), y_own[HALF:].astype(f32)]
    for (by, part), y in zip(calls, returned_y):
        halves[part] = halves[part] + y.astype(f32)
    result = jnp.concatenate(halves, axis=0)
    layer_output = (middle + (result + mlp_out_bias)).astype(bf16)

    width = early * LANES
    rest = D - width
    d_attn_in = jnp.concatenate(
        [
            piece
            for i in range(3)
            for piece in (
                chain_one.value[:, i * width : (i + 1) * width],
                chain_two.value[:, i * rest : (i + 1) * rest],
            )
        ],
        axis=1,
    )
    return (
        layer_output,
        input_grad,
        vectors[0],
        vectors[1],
        d_attn_in.astype(f32),
        vectors[6:8],
        chain_one.value[:, 3 * width :].astype(f32),
        vectors[2],
        vectors[3],
        vectors[4],
        d_mlp_in.astype(f32),
        lax.dynamic_slice(vectors[8:].reshape(-1), (place * hidden_count,), (hidden_count,)),
        d_mlp_out.astype(f32),
        vectors[5],
    )


def solution(mesh):
    rows, whole = P(("batch", "mlp"), None), P()
    columns, hidden, depth = P(None, "mlp"), P("mlp"), P("mlp", None)
    return jax.shard_map(
        shards,
        mesh=mesh,
        in_specs=(rows, rows) + (whole,) * 8 + (columns, hidden, depth, whole, rows),
        out_specs=(rows, rows) + (whole,) * 8 + (columns, hidden, depth, whole),
        check_vma=False,
    )
```

```python
import jax
import jax.numpy as jnp
from jax import lax
from jax.experimental import pallas as pl
from jax.experimental.pallas import tpu as pltpu
from jax.sharding import PartitionSpec as P

D = 768
H = 12
HD = 64
NB = 512
L = 512
NDOC = 3
HALF = L // 2
PAIRS = H // 2
LANES = 2 * HD

LOG2E = 1.4426950408889634
SCORE_LOG2 = LOG2E * HD**-0.5
MASKED = -1e30

bf16 = jnp.bfloat16
f32 = jnp.float32


def dot(a, b):
    return jnp.dot(a, b, preferred_element_type=f32)


def dot_nt(a, b):
    return lax.dot_general(a, b, (((1,), (1,)), ((), ())), preferred_element_type=f32)


def layer_norm(matrix, gain_row, shift_row):
    center = jnp.mean(matrix, axis=-1, keepdims=True)
    centered = matrix - center
    spread = jnp.mean(centered * centered, axis=-1, keepdims=True)
    return centered * lax.rsqrt(spread + 1e-05) * gain_row + shift_row


def norm_backward(matrix, gain_row, shift_row, upstream):
    unused, pullback = jax.vjp(layer_norm, matrix, gain_row, shift_row)
    return pullback(upstream)


def head_lanes(matrix, head):
    lane = lax.broadcasted_iota(jnp.int32, (1, LANES), 1)
    return jnp.where(lane // HD == head, matrix, jnp.zeros_like(matrix))


def fill_mask(lens, mask):
    key = lax.broadcasted_iota(jnp.int32, (L, L), 0)
    query = lax.broadcasted_iota(jnp.int32, (L, L), 1)
    one = lens[0, 0]
    two = one + lens[0, 1]
    start = jnp.where(query >= two, two, jnp.where(query >= one, one, 0))
    mask[...] = jnp.where((key <= query) & (key >= start), 0.0, MASKED)


def local_kernel(
    lens,
    q_ref,
    k_ref,
    v_ref,
    wo_ref,
    x_ref,
    rows_ref,
    out_ref,
    lse_ref,
    mix_ref,
    middle_ref,
    normed_ref,
    mask,
    turned,
    acc,
):
    step = pl.program_id(0)

    @pl.when(step == 0)
    def _():
        fill_mask(lens, mask)
        acc[...] = jnp.zeros_like(acc)

    q, k = q_ref[...], k_ref[...]
    v_t = v_ref[...].T
    for head in range(2):
        q_head = head_lanes(q, head)
        rows = slice(head * HD, (head + 1) * HD)
        for part in range(2):
            keys = HALF * (part + 1)
            cols = slice(part * HALF, (part + 1) * HALF)
            s = dot_nt(k[:keys], q_head[cols]) * SCORE_LOG2 + mask[:keys, cols]
            top = jnp.max(s, axis=0, keepdims=True)
            e = jnp.exp2(s - top)
            total = jnp.sum(e, axis=0, keepdims=True)
            out = dot(v_t[rows, :keys], e.astype(bf16))
            turned[rows, cols] = out / total
            lse_ref[0, head : head + 1, cols] = top + jnp.log2(total)
    out_ref[...] = turned[:, :HALF].T
    mixed = turned[:, HALF:].T.astype(bf16)
    mix_ref[...] = mixed
    acc[...] += dot(mixed, wo_ref[...])

    @pl.when(step == PAIRS - 1)
    def _():
        finish_middle(x_ref, acc, rows_ref, middle_ref, normed_ref)


def finish_middle(x_ref, acc, rows_ref, middle_ref, normed_ref):
    middle = x_ref[...].astype(f32) + (acc[...] + rows_ref[0:1])
    middle_ref[...] = middle
    normed_ref[...] = layer_norm(middle, rows_ref[1:2], rows_ref[2:3]).astype(bf16)


def local_attention(lens, qkv, attn_out, inputs, rows):
    column = lambda k: pl.BlockSpec((L, LANES), lambda i: (0, k * PAIRS + i))
    upper = pl.BlockSpec((HALF, D), lambda i: (1, 0))
    return pl.pallas_call(
        local_kernel,
        grid=(PAIRS,),
        in_specs=[
            pl.BlockSpec(memory_space=pltpu.SMEM),
            column(0),
            column(1),
            column(2),
            pl.BlockSpec((LANES, D), lambda i: (i, 0)),
            upper,
            pl.BlockSpec((8, D), lambda i: (0, 0)),
        ],
        out_specs=[
            pl.BlockSpec((HALF, LANES), lambda i: (0, i)),
            pl.BlockSpec((1, 8, L), lambda i: (i, 0, 0)),
            pl.BlockSpec((HALF, LANES), lambda i: (1, i)),
            upper,
            upper,
        ],
        out_shape=[
            jax.ShapeDtypeStruct((HALF, D), f32),
            jax.ShapeDtypeStruct((PAIRS, 8, L), f32),
            jax.ShapeDtypeStruct((L, D), bf16),
            jax.ShapeDtypeStruct((L, D), f32),
            jax.ShapeDtypeStruct((L, D), bf16),
        ],
        scratch_shapes=[
            pltpu.VMEM((L, L), f32),
            pltpu.VMEM((LANES, L), f32),
            pltpu.VMEM((HALF, D), f32),
        ],
        cost_estimate=pl.CostEstimate(
            flops=H * 12 * HALF * HALF * 256, bytes_accessed=8 * L * D, transcendentals=H * L * L
        ),
        name="local_attention",
    )(lens, qkv, qkv, qkv, attn_out, inputs, rows)


def basis_rows(last_len, transposed):
    shape = (HALF, NB) if transposed else (NB, HALF)
    slot_dim, place_dim = (1, 0) if transposed else (0, 1)
    slot = lax.broadcasted_iota(jnp.int32, shape, slot_dim).astype(f32)
    place = lax.broadcasted_iota(jnp.int32, shape, place_dim).astype(f32)
    offsets = place - HALF + last_len + 0.5
    distances = (slot + 0.5) / NB * last_len - offsets
    weights = jnp.where(offsets > 0.0, jnp.exp(-0.5 * distances * distances), 0.0)
    return weights / jnp.sum(weights, axis=place_dim, keepdims=True)


def memory_kernel(
    reads,
    last_ref,
    q_ref,
    kt_ref,
    vt_ref,
    vb_ref,
    local_ref,
    wo_ref,
    x_ref,
    rows_ref,
    mix_whole,
    middle_whole,
    normed_whole,
    mix_ref,
    mk_ref,
    mv_ref,
    lse_ref,
    middle_ref,
    normed_ref,
    basis_t_ref,
    basis,
    turned,
    acc,
):
    step = pl.program_id(0)

    @pl.when(step == 0)
    def _():
        last_len = last_ref[0:1, 0:1]
        basis[...] = basis_rows(last_len, False).astype(bf16)
        basis_t_ref[...] = basis_rows(last_len, True).astype(bf16)
        acc[...] = jnp.zeros_like(acc)

    mem_k = dot(basis[...], kt_ref[...]).astype(bf16)
    mem_v = (dot(basis[...], vt_ref[...]) + vb_ref[0:1]).astype(bf16)
    mk_ref[...] = mem_k
    mv_ref[...] = mem_v
    v_t = mem_v.T
    query = lax.broadcasted_iota(jnp.int32, (1, HALF), 1)
    reading = query < reads[0, 0]
    q = q_ref[...]
    for head in range(2):
        rows = slice(head * HD, (head + 1) * HD)
        s = dot_nt(mem_k, head_lanes(q, head)) * SCORE_LOG2
        top = jnp.max(s, axis=0, keepdims=True)
        e = jnp.exp2(s - top)
        total = jnp.sum(e, axis=0, keepdims=True)
        out = dot(v_t[rows], e.astype(bf16))
        turned[rows, :] = jnp.where(reading, out / total, 0.0)
        lse_ref[0, head : head + 1, :] = jnp.where(reading, top + jnp.log2(total), -MASKED)
    mixed = (local_ref[...] + turned[...].T).astype(bf16)
    mix_ref[...] = mixed
    acc[...] += dot(mixed, wo_ref[...])

    @pl.when(step == PAIRS - 1)
    def _():
        finish_middle(x_ref, acc, rows_ref, middle_ref, normed_ref)


def memory_attention(
    reads, last_rows, qkv, tail_kv, value_bias, local, attn_out, inputs, rows, mixture, middle, normed
):
    whole = lambda shape: pl.BlockSpec(shape, lambda i: (0,) * len(shape))
    untouched = pl.BlockSpec(memory_space=pl.ANY)
    return pl.pallas_call(
        memory_kernel,
        grid=(PAIRS,),
        in_specs=[
            pl.BlockSpec(memory_space=pltpu.SMEM),
            whole((16, D)),
            pl.BlockSpec((HALF, LANES), lambda i: (0, i)),
            pl.BlockSpec((HALF, LANES), lambda i: (0, i)),
            pl.BlockSpec((HALF, LANES), lambda i: (0, PAIRS + i)),
            pl.BlockSpec((8, LANES), lambda i: (0, i)),
            pl.BlockSpec((HALF, LANES), lambda i: (0, i)),
            pl.BlockSpec((LANES, D), lambda i: (i, 0)),
            whole((HALF, D)),
            whole((8, D)),
            untouched,
            untouched,
            untouched,
        ],
        out_specs=[
            pl.BlockSpec((HALF, LANES), lambda i: (0, i)),
            pl.BlockSpec((NB, LANES), lambda i: (0, i)),
            pl.BlockSpec((NB, LANES), lambda i: (0, i)),
            pl.BlockSpec((1, 8, HALF), lambda i: (i, 0, 0)),
            whole((HALF, D)),
            whole((HALF, D)),
            whole((HALF, NB)),
        ],
        out_shape=[
            jax.ShapeDtypeStruct((L, D), bf16),
            jax.ShapeDtypeStruct((NB, D), bf16),
            jax.ShapeDtypeStruct((NB, D), bf16),
            jax.ShapeDtypeStruct((PAIRS, 8, HALF), f32),
            jax.ShapeDtypeStruct((L, D), f32),
            jax.ShapeDtypeStruct((L, D), bf16),
            jax.ShapeDtypeStruct((HALF, NB), bf16),
        ],
        scratch_shapes=[
            pltpu.VMEM((NB, HALF), bf16),
            pltpu.VMEM((LANES, HALF), f32),
            pltpu.VMEM((HALF, D), f32),
        ],
        input_output_aliases={10: 0, 11: 4, 12: 5},
        cost_estimate=pl.CostEstimate(
            flops=H * 16 * HALF * HALF * 256, bytes_accessed=16 * L * D, transcendentals=H * L * HALF
        ),
        name="memory_attention",
    )(
        reads,
        last_rows,
        qkv,
        tail_kv,
        tail_kv,
        value_bias,
        local,
        attn_out,
        inputs,
        rows,
        mixture,
        middle,
        normed,
    )


def mlp_kernel(x_ref, ct_ref, wi_ref, bi_ref, wo_ref, *refs):
    hid_ref, dpre_ref, bias_ref, y_ref, dx_ref, y_acc, dx_acc = refs[-7:]
    step = pl.program_id(0)
    pre = dot(x_ref[...], wi_ref[...]) + bi_ref[0:1]
    squared = pre * pre
    tanh = jnp.tanh(pre * (0.7978845608028654 + 0.7978845608028654 * 0.044715 * squared))
    half = 0.5 * pre
    hidden = (half + half * tanh).astype(bf16)
    slope = (
        0.5
        + 0.5 * tanh
        + half
        * (1.0 - tanh * tanh)
        * (0.7978845608028654 + 3 * 0.7978845608028654 * 0.044715 * squared)
    )
    d_pre = (slope * dot_nt(ct_ref[...], wo_ref[...])).astype(bf16)
    hid_ref[...] = hidden
    dpre_ref[...] = d_pre
    bias_ref[...] = jnp.broadcast_to(
        jnp.sum(d_pre.astype(f32), axis=0, keepdims=True), bias_ref.shape
    )
    y = dot(hidden, wo_ref[...])
    dx = dot_nt(d_pre, wi_ref[...])

    @pl.when(step == 0)
    def _():
        y_acc[...] = y
        dx_acc[...] = dx

    @pl.when(step > 0)
    def _():
        y_acc[...] += y
        dx_acc[...] += dx

    @pl.when(step == pl.num_programs(0) - 1)
    def _():
        y_ref[...] = y_acc[...].astype(bf16)
        dx_ref[...] = dx_acc[...].astype(bf16)


def mlp_block(rows, cotangent, part, mlp_in, bias_rows, mlp_out, total, place, kept):
    count, hidden = rows.shape[0], mlp_in.shape[1]
    tile = 256 if hidden % 256 == 0 else 128
    fixed = pl.BlockSpec((count, D), lambda i: (0, 0))
    across = pl.BlockSpec((count, tile), lambda i: (place, i))
    return pl.pallas_call(
        mlp_kernel,
        grid=(hidden // tile,),
        in_specs=[
            fixed,
            pl.BlockSpec((count, D), lambda i: (part, 0)),
            pl.BlockSpec((D, tile), lambda i: (0, i)),
            pl.BlockSpec((8, tile), lambda i: (0, i)),
            pl.BlockSpec((tile, D), lambda i: (i, 0)),
        ]
        + [pl.BlockSpec(memory_space=pl.ANY)] * len(kept),
        out_specs=[across, across, pl.BlockSpec((8, tile), lambda i: (0, i)), fixed, fixed],
        out_shape=[
            jax.ShapeDtypeStruct((total, hidden), bf16),
            jax.ShapeDtypeStruct((total, hidden), bf16),
            jax.ShapeDtypeStruct((8, hidden), f32),
            jax.ShapeDtypeStruct((count, D), bf16),
            jax.ShapeDtypeStruct((count, D), bf16),
        ],
        scratch_shapes=[pltpu.VMEM((count, D), f32), pltpu.VMEM((count, D), f32)],
        input_output_aliases={5 + i: i for i in range(len(kept))},
        cost_estimate=pl.CostEstimate(
            flops=8 * count * D * hidden,
            bytes_accessed=4 * D * hidden + 4 * count * hidden + 8 * count * D,
            transcendentals=count * hidden,
        ),
        name="mlp_block",
    )(rows, cotangent, mlp_in, bias_rows, mlp_out, *kept)


def backward_kernel(
    lens,
    q_ref,
    k_ref,
    v_ref,
    mk_ref,
    mv_ref,
    db_ref,
    wo_ref,
    ll_ref,
    lm_ref,
    bt_ref,
    dqkv_ref,
    dtail_ref,
    sums_ref,
    mask,
    turned,
    dk_acc,
    dv_acc,
):
    @pl.when(pl.program_id(0) == 0)
    def _():
        fill_mask(lens, mask)

    q, k, v = q_ref[...], k_ref[...], v_ref[...]
    mem_k, mem_v = mk_ref[...], mv_ref[...]
    d_mix = dot_nt(db_ref[...], wo_ref[...]).astype(bf16)
    k_t, mk_t = k.T, mem_k.T
    d_mem_k = d_mem_v = None

    def one(keys, values, q_part, d_part, lse, extra):
        s = dot_nt(keys, q_part) * SCORE_LOG2
        if extra is not None:
            s = s + extra
        weights = jnp.exp2(s - lse)
        d_weights = dot_nt(values, d_part)
        inner = jnp.sum(weights * d_weights, axis=0, keepdims=True)
        d_scores = (weights * (d_weights - inner)).astype(bf16)
        return d_scores, dot(d_scores, q_part), dot(weights.astype(bf16), d_part)

    for head in range(2):
        rows = slice(head * HD, (head + 1) * HD)
        q_head, d_head = head_lanes(q, head), head_lanes(d_mix, head)
        for part in range(2):
            keys = HALF * (part + 1)
            cols = slice(part * HALF, (part + 1) * HALF)
            ds, dk, dv = one(
                k[:keys],
                v[:keys],
                q_head[cols],
                d_head[cols],
                ll_ref[0, head : head + 1, cols],
                mask[:keys, cols],
            )
            dq = dot(k_t[rows, :keys], ds)
            if part == 0:
                ds, d_key, d_value = one(
                    mem_k, mem_v, q_head[cols], d_head[cols], lm_ref[0, head : head + 1, :], None
                )
                dq = dq + dot(mk_t[rows], ds)
                d_mem_k = d_key if d_mem_k is None else d_mem_k + d_key
                d_mem_v = d_value if d_mem_v is None else d_mem_v + d_value
            turned[rows, cols] = dq
            if head == 0 and part == 0:
                dk_acc[:HALF] = dk
                dv_acc[:HALF] = dv
            elif head == 0:
                dk_acc[:HALF] += dk[:HALF]
                dv_acc[:HALF] += dv[:HALF]
                dk_acc[HALF:] = dk[HALF:]
                dv_acc[HALF:] = dv[HALF:]
            else:
                dk_acc[:keys] += dk
                dv_acc[:keys] += dv
    scale = HD**-0.5
    d_q = (turned[...].T * scale).astype(bf16)
    d_v = dv_acc[...].astype(bf16)
    dqkv_ref[0] = d_q
    dqkv_ref[1] = (dk_acc[...] * scale).astype(bf16)
    dqkv_ref[2] = d_v
    d_mem_k = (d_mem_k * scale).astype(bf16)
    d_mem_v = d_mem_v.astype(bf16)
    dtail_ref[0] = dot(bt_ref[...], d_mem_k).astype(bf16)
    dtail_ref[1] = dot(bt_ref[...], d_mem_v).astype(bf16)
    sums_ref[0:1] = jnp.sum(d_q.astype(f32), axis=0, keepdims=True)
    sums_ref[1:2] = jnp.sum(d_v.astype(f32), axis=0, keepdims=True) + jnp.sum(
        d_mem_v.astype(f32), axis=0, keepdims=True
    )


HIDDEN = pl.CostEstimate(flops=1000, bytes_accessed=1000, transcendentals=0)


def attention_backward(
    first, pairs, lens, qkv, mem_k, mem_v, d_branch, attn_out, lse_local, lse_mem, basis_t
):
    column = lambda k: pl.BlockSpec((L, LANES), lambda i: (0, k * PAIRS + first + i))
    whole = lambda shape: pl.BlockSpec(shape, lambda i: (0,) * len(shape))
    width = pairs * LANES
    return pl.pallas_call(
        backward_kernel,
        grid=(pairs,),
        in_specs=[
            pl.BlockSpec(memory_space=pltpu.SMEM),
            column(0),
            column(1),
            column(2),
            column(0),
            column(0),
            whole((L, D)),
            pl.BlockSpec((LANES, D), lambda i: (first + i, 0)),
            pl.BlockSpec((1, 8, L), lambda i: (first + i, 0, 0)),
            pl.BlockSpec((1, 8, HALF), lambda i: (first + i, 0, 0)),
            whole((HALF, NB)),
        ],
        out_specs=[
            pl.BlockSpec((3, L, LANES), lambda i: (0, 0, i)),
            pl.BlockSpec((2, HALF, LANES), lambda i: (0, 0, i)),
            pl.BlockSpec((8, LANES), lambda i: (0, i)),
        ],
        out_shape=[
            jax.ShapeDtypeStruct((3, L, width), bf16),
            jax.ShapeDtypeStruct((2, HALF, width), bf16),
            jax.ShapeDtypeStruct((8, width), f32),
        ],
        scratch_shapes=[
            pltpu.VMEM((L, L), f32),
            pltpu.VMEM((LANES, L), f32),
            pltpu.VMEM((L, LANES), f32),
            pltpu.VMEM((L, LANES), f32),
        ],
        cost_estimate=pl.CostEstimate(
            flops=2 * pairs * 56 * HALF * HALF * 256,
            bytes_accessed=20 * L * width,
            transcendentals=2 * pairs * L * L,
        ),
        name="attention_backward",
    )(lens, qkv, qkv, qkv, mem_k, mem_v, d_branch, attn_out, lse_local, lse_mem, basis_t)


def rotated(value, axis, by):
    count = lax.axis_size(axis)
    return lax.ppermute(value, axis, [(i, (i + by) % count) for i in range(count)])


fence = lax.optimization_barrier
GRID = ("batch", "mlp")


def flipped(value, mask):
    count = lax.axis_size("batch") * lax.axis_size("mlp")
    return lax.ppermute(value, GRID, [(i, i ^ mask) for i in range(count)])


def place_in(bits):
    number = lax.axis_index(GRID)
    return sum(((number >> bit) & 1) << i for i, bit in enumerate(bits))


def peers(bits):
    return [sum(((q >> i) & 1) << bit for i, bit in enumerate(bits)) for q in range(1, 1 << len(bits))]


def grouped(bits):
    odd = len(bits) % 2
    return ([bits[:1]] if odd else []) + [bits[i : i + 2] for i in range(odd, len(bits), 2)]


class Chain:
    def __init__(self, kept, given, groups):
        self.stages = [(True, bits) for bits in groups] + [(False, bits) for bits in groups[::-1]]
        self.turn()
        self.kept, self.given = kept, [given]

    def turn(self):
        self.scatters, self.bits = self.stages.pop(0)
        self.place = place_in(self.bits)

    def prepare(self):
        self.turn()
        count = 1 << len(self.bits)
        if self.scatters:
            size = self.value.shape[0] // count
            piece = lambda i: lax.dynamic_slice_in_dim(self.value, i * size, size, 0)
            self.kept = piece(self.place)
            self.given = [piece(self.place ^ q) for q in range(1, count)]
        else:
            self.kept = self.value
            self.given = [self.value]

    def fly(self):
        masks = peers(self.bits)
        given = self.given if self.scatters else self.given * len(masks)
        self.got = [flipped(piece, mask) for piece, mask in zip(given, masks)]

    def land(self):
        if self.scatters:
            total = self.kept.astype(f32)
            for piece in self.got:
                total = total + piece.astype(f32)
            self.value = total.astype(self.kept.dtype)
        else:
            pieces = [self.kept] + self.got
            order = [
                lax.select_n(self.place ^ i, *pieces)
                if len(pieces) > 2
                else jnp.where(self.place == i, *pieces)
                for i in range(len(pieces))
            ]
            self.value = jnp.concatenate(order, axis=0)
        if self.stages:
            self.prepare()
            return True
        return False


def sum_small(value, groups):
    for bits in groups:
        value = value + sum(flipped(value, mask) for mask in peers(bits))
    return value


def weight_grads(normed, normed_tail, d, d_tail, ready, side):
    width = d.shape[2]
    tile = 256
    each = width // tile
    extra = 0 if ready is None else ready.shape[1] // tile
    half = D // 2

    def kernel(side_ref, n_ref, nt_ref, d_ref, dt_ref, *refs):
        kept_ref, given_ref, turned, tail_turned = refs[-4:]
        step = pl.program_id(0)

        @pl.when(step == 0)
        def _():
            turned[...] = n_ref[...].T
            tail_turned[...] = nt_ref[...].T

        def rows(which, ref):
            return ref[pl.ds(pl.multiple_of(which * half, half), half), :]

        for which, out_ref in ((side_ref[0], kept_ref), (1 - side_ref[0], given_ref)):

            @pl.when(step < each)
            def _():
                out_ref[...] = dot(rows(which, turned), d_ref[0]).astype(bf16)

            @pl.when((step >= each) & (step < 3 * each))
            def _():
                out_ref[...] = (
                    dot(rows(which, turned), d_ref[0]) + dot(rows(which, tail_turned), dt_ref[0])
                ).astype(bf16)

            if extra:

                @pl.when(step >= 3 * each)
                def _():
                    out_ref[...] = rows(which, refs[0])

    column = lambda i: jnp.where(i < 3 * each, i % each, each - 1)
    in_specs = [
        pl.BlockSpec(memory_space=pltpu.SMEM),
        pl.BlockSpec((L, D), lambda i: (0, 0)),
        pl.BlockSpec((HALF, D), lambda i: (0, 0)),
        pl.BlockSpec((1, L, tile), lambda i: (jnp.minimum(i // each, 2), 0, column(i))),
        pl.BlockSpec((1, HALF, tile), lambda i: (jnp.clip(i // each - 1, 0, 1), 0, column(i))),
    ]
    operands = [side, normed, normed_tail, d, d_tail]
    if extra:
        in_specs.append(pl.BlockSpec((D, tile), lambda i: (0, jnp.maximum(i - 3 * each, 0))))
        operands.append(ready)
    steps = 3 * each + extra
    return pl.pallas_call(
        kernel,
        grid=(steps,),
        in_specs=in_specs,
        out_specs=[pl.BlockSpec((half, tile), lambda i: (0, i))] * 2,
        out_shape=[jax.ShapeDtypeStruct((half, steps * tile), bf16)] * 2,
        scratch_shapes=[pltpu.VMEM((D, L), bf16), pltpu.VMEM((D, HALF), bf16)],
        cost_estimate=HIDDEN,
        name="weight_grads",
    )(*operands)


def shards(
    inputs,
    doc_lengths,
    ln1_gain,
    ln1_bias,
    attn_in,
    qv_bias,
    attn_out,
    attn_out_bias,
    ln2_gain,
    second_norm_bias,
    mlp_in,
    mlp_in_bias,
    mlp_out,
    mlp_out_bias,
    cotangent,
):
    n_mlp = lax.axis_size("mlp")
    place = lax.axis_index("mlp")
    gain_one = ln1_gain.astype(f32)
    bias_one = ln1_bias.astype(f32)
    gain_two = ln2_gain.astype(f32)
    bias_two = second_norm_bias.astype(f32)

    own_tail = jnp.concatenate(
        [
            inputs[HALF:],
            jnp.broadcast_to(doc_lengths[:, NDOC - 1 :].astype(bf16), (16, D)),
        ],
        axis=0,
    )
    tail = rotated(own_tail, "mlp", 1)
    cotangents = [cotangent] + [rotated(cotangent, "mlp", by) for by in range(1, n_mlp)]

    activations = inputs.astype(f32)
    normed = layer_norm(activations, gain_one, bias_one).astype(bf16)
    zeros = jnp.zeros((D,), f32)
    qkv_bias = jnp.concatenate([qv_bias[0].astype(f32), zeros, qv_bias[1].astype(f32)])
    qkv = (dot(normed, attn_in) + qkv_bias).astype(bf16)
    rows = jnp.concatenate(
        [
            jnp.stack([attn_out_bias.astype(f32), gain_two, bias_two]),
            jnp.zeros((5, D), f32),
        ]
    )
    local, lse_local, mixture, middle, normed_two = local_attention(
        doc_lengths, qkv, attn_out, inputs, rows
    )
    steps = range(1, n_mlp)
    arrived_hi = [rotated(normed_two[HALF:], "mlp", by) for by in steps]

    tail_rows = tail[:HALF].astype(f32)
    normed_tail = layer_norm(tail_rows, gain_one, bias_one).astype(bf16)
    tail_kv = dot(normed_tail, attn_in[:, D:]).astype(bf16)
    reads = jnp.where(place == 0, 0, doc_lengths[:, :1])
    value_bias = jnp.broadcast_to(qv_bias[1].astype(f32), (8, D))
    tail_kv, *cotangents[1:] = fence((tail_kv, *cotangents[1:]))
    mixture, mem_k, mem_v, lse_mem, middle, normed_two, basis_t = memory_attention(
        reads,
        tail[HALF:],
        qkv,
        tail_kv,
        value_bias,
        local,
        attn_out,
        inputs,
        rows,
        mixture,
        middle,
        normed_two,
    )
    arrived_lo = [rotated(normed_two[:HALF], "mlp", by) for by in steps]
    mem_k, arrived_hi = fence((mem_k, arrived_hi))

    bias_rows = jnp.broadcast_to(mlp_in_bias.astype(f32), (8, mlp_in.shape[1]))
    kept = ()
    d_mlp_in_bias = 0.0
    returned_y, returned_dx = [], []
    calls = [(by, part) for by in steps for part in (1, 0)]
    for by, part in calls:
        block = (arrived_lo, arrived_hi)[part][by - 1]
        hidden, d_pre, d_bias, y, dx = mlp_block(
            block, cotangents[by], part, mlp_in, bias_rows, mlp_out, n_mlp * L, 2 * by + part, kept
        )
        kept = (hidden, d_pre)
        d_mlp_in_bias = d_mlp_in_bias + d_bias[0]
        returned_dx.append(rotated(dx, "mlp", -by))
        returned_y.append(y)
    hidden, d_pre, d_bias, y_own, dx_own = mlp_block(
        normed_two, cotangent, 0, mlp_in, bias_rows, mlp_out, n_mlp * L, 0, kept
    )
    d_mlp_in_bias = d_mlp_in_bias + d_bias[0]
    hidden, d_pre, returned_dx = fence((hidden, d_pre, returned_dx))
    over_rows = lambda a, b: lax.dot_general(
        a, b, (((0,), (0,)), ((), ())), preferred_element_type=f32
    )
    all_rows = jnp.concatenate(
        [normed_two] + [piece for pair in zip(arrived_lo, arrived_hi) for piece in pair], axis=0
    )
    d_mlp_in = over_rows(all_rows, d_pre).astype(bf16)
    d_mlp_out = over_rows(hidden, jnp.concatenate(cotangents, axis=0)).astype(bf16)

    hidden_count = mlp_in.shape[1]
    mlp_count = n_mlp.bit_length() - 1
    batch_count = lax.axis_size("batch").bit_length() - 1
    mlp_bits = list(range(mlp_count))
    core = [[mlp_count]]
    rest = list(range(mlp_count + 1, mlp_count + batch_count))
    groups = core + [mlp_bits[:1] + rest[:1]] + [[bit] for bit in mlp_bits[1:] + rest[1:]]

    d_mlp_in, d_mlp_out = lax.psum((d_mlp_in, d_mlp_out), "batch")

    def finish():
        halves = [dx_own[:HALF].astype(f32), dx_own[HALF:].astype(f32)]
        for (by, part), dx in zip(calls, returned_dx):
            halves[part] = halves[part] + dx.astype(f32)
        d_normed_two = jnp.concatenate(halves, axis=0)
        upstream = cotangent.astype(f32)
        d_out_bias = jnp.sum(upstream, axis=0)
        d_middle_norm, d_ln2_gain, d_ln2_bias = norm_backward(middle, gain_two, bias_two, d_normed_two)
        d_middle = upstream + d_middle_norm
        d_branch = d_middle.astype(bf16)
        d_attn_out_bias = jnp.sum(d_branch, axis=0, dtype=f32)

        backward = lambda first, pairs, d: attention_backward(
            first, pairs, doc_lengths, qkv, mem_k, mem_v, d, attn_out, lse_local, lse_mem, basis_t
        )
        early = PAIRS // 3
        side = place_in(core[0]).reshape(1)
        d_one, d_tail_one, sums_one = backward(0, early, d_branch)
        d_attn_out = over_rows(mixture, d_branch).astype(bf16)
        chain_one = Chain(
            *weight_grads(normed, normed_tail, d_one, d_tail_one, d_attn_out, side), groups
        )
        chain_one.fly()
        chain_one.land()
        d_branch, chain_one.given = fence((d_branch, chain_one.given))
        chain_one.fly()
        d_two, d_tail_two, sums_two = backward(early, PAIRS - early, d_branch)
        d_two, d_tail_two, chain_one.got = fence((d_two, d_tail_two, chain_one.got))
        chain_one.land()
        d_two, d_tail_two, chain_one.given = fence((d_two, d_tail_two, chain_one.given))
        chain_one.fly()
        chain_two = Chain(*weight_grads(normed, normed_tail, d_two, d_tail_two, None, side), groups)
        chain_two.fly()
        chain_two.land()
        d_qkv, d_tail, sums, later, chain_two.given = fence(
            (
                (d_one, d_two),
                (d_tail_one, d_tail_two),
                (sums_one, sums_two),
                (d_mlp_in_bias, returned_y, y_own),
                chain_two.given,
            )
        )
        bias_grad, y_given, y_mine = later
        chain_two.fly()

        token = chain_two.given
        flying = [chain_one, chain_two]
        events = 0
        while flying:
            for chain in list(flying):
                chain.got, token = fence((chain.got, token))
                events += 1
                if events == 2:
                    chain.got, y_given = fence((chain.got, y_given))
                    returned = [rotated(y, "mlp", -by) for (by, part), y in zip(calls, y_given)]
                if events == 6:
                    chain.got, returned = fence((chain.got, returned))
                if chain.land():
                    token = chain.given
                    chain.fly()
                else:
                    flying.remove(chain)

        d_qkv = jnp.concatenate(d_qkv, axis=2)
        d_tail = jnp.concatenate(d_tail, axis=2)
        sums = jnp.concatenate(sums, axis=1)
        columns = [attn_in[:, i * D : (i + 1) * D] for i in range(3)]
        d_tail_rows = dot_nt(d_tail[0], columns[1]) + dot_nt(d_tail[1], columns[2])
        from_next = rotated(d_tail_rows.astype(bf16), "mlp", -1)
        d_normed = (
            dot_nt(d_qkv[0], columns[0]) + dot_nt(d_qkv[1], columns[1]) + dot_nt(d_qkv[2], columns[2])
        )
        unused, d_ln1_gain, d_ln1_bias = norm_backward(activations, gain_one, bias_one, d_normed)
        unused, d_tail_gain, d_tail_bias = norm_backward(tail_rows, gain_one, bias_one, d_tail_rows)
        d_ln1_gain, d_ln1_bias = d_ln1_gain + d_tail_gain, d_ln1_bias + d_tail_bias

        placed_bias = lax.dynamic_update_slice(
            jnp.zeros((n_mlp * hidden_count,), f32), bias_grad, (place * hidden_count,)
        )
        vectors = jnp.concatenate(
            [
                jnp.stack(
                    [d_ln1_gain, d_ln1_bias, d_attn_out_bias, d_ln2_gain, d_ln2_bias, d_out_bias]
                ),
                sums[:2],
                placed_bias.reshape(-1, D),
            ],
            axis=0,
        )
        vectors = sum_small(vectors, groups)

        d_normed = jnp.concatenate(
            [d_normed[:HALF], d_normed[HALF:] + from_next.astype(f32)], axis=0
        )
        d_in_norm, unused, unused = norm_backward(activations, gain_one, bias_one, d_normed)
        input_grad = (d_middle + d_in_norm).astype(bf16)

        halves = [y_mine[:HALF].astype(f32), y_mine[HALF:].astype(f32)]
        for (by, part), y in zip(calls, returned):
            halves[part] = halves[part] + y.astype(f32)
        result = jnp.concatenate(halves, axis=0)
        layer_output = (middle + (result + mlp_out_bias)).astype(bf16)

        width = early * LANES
        rest = D - width
        d_attn_in = jnp.concatenate(
            [
                piece
                for i in range(3)
                for piece in (
                    chain_one.value[:, i * width : (i + 1) * width],
                    chain_two.value[:, i * rest : (i + 1) * rest],
                )
            ],
            axis=1,
        )
        return (
            layer_output,
            input_grad,
            vectors[0],
            vectors[1],
            d_attn_in.astype(f32),
            vectors[6:8],
            chain_one.value[:, 3 * width :].astype(f32),
            vectors[2],
            vectors[3],
            vectors[4],
            lax.dynamic_slice(vectors[8:].reshape(-1), (place * hidden_count,), (hidden_count,)),
            vectors[5],
        )

    shapes = jax.eval_shape(finish)
    done = lax.cond(
        doc_lengths[0, 0] > 0,
        finish,
        lambda: jax.tree.map(lambda leaf: jnp.zeros(leaf.shape, leaf.dtype), shapes),
    )
    return (*done[:10], d_mlp_in.astype(f32), done[10], d_mlp_out.astype(f32), done[11])


def solution(mesh):
    rows, whole = P(("batch", "mlp"), None), P()
    columns, hidden, depth = P(None, "mlp"), P("mlp"), P("mlp", None)
    return jax.shard_map(
        shards,
        mesh=mesh,
        in_specs=(rows, rows) + (whole,) * 8 + (columns, hidden, depth, whole, rows),
        out_specs=(rows, rows) + (whole,) * 8 + (columns, hidden, depth, whole),
        check_vma=False,
    )
```

```python
import jax
import jax.numpy as jnp
from jax import lax
from jax.experimental import pallas as pl
from jax.experimental.pallas import tpu as pltpu
from jax.sharding import PartitionSpec as P

D = 768
H = 12
HD = 64
NB = 512
L = 512
NDOC = 3
HALF = L // 2
PAIRS = H // 2
LANES = 2 * HD

LOG2E = 1.4426950408889634
SCORE_LOG2 = LOG2E * HD**-0.5
MASKED = -1e30

bf16 = jnp.bfloat16
f32 = jnp.float32


def dot(a, b):
    return jnp.dot(a, b, preferred_element_type=f32)


def dot_nt(a, b):
    return lax.dot_general(a, b, (((1,), (1,)), ((), ())), preferred_element_type=f32)


def layer_norm(matrix, gain_row, shift_row):
    center = jnp.mean(matrix, axis=-1, keepdims=True)
    centered = matrix - center
    spread = jnp.mean(centered * centered, axis=-1, keepdims=True)
    return centered * lax.rsqrt(spread + 1e-05) * gain_row + shift_row


def head_lanes(matrix, head):
    lane = lax.broadcasted_iota(jnp.int32, (1, LANES), 1)
    return jnp.where(lane // HD == head, matrix, jnp.zeros_like(matrix))


def fill_mask(lens, mask):
    key = lax.broadcasted_iota(jnp.int32, (L, L), 0)
    query = lax.broadcasted_iota(jnp.int32, (L, L), 1)
    one = lens[0, 0]
    two = one + lens[0, 1]
    start = jnp.where(query >= two, two, jnp.where(query >= one, one, 0))
    mask[...] = jnp.where((key <= query) & (key >= start), 0.0, MASKED)


def local_kernel(
    lens,
    q_ref,
    k_ref,
    v_ref,
    wo_ref,
    x_ref,
    rows_ref,
    out_ref,
    lse_ref,
    mix_ref,
    middle_ref,
    normed_ref,
    sent_ref,
    mask,
    turned,
    acc,
):
    step = pl.program_id(0)

    @pl.when(step == 0)
    def _():
        fill_mask(lens, mask)
        acc[...] = jnp.zeros_like(acc)

    q, k = q_ref[...], k_ref[...]
    v_t = v_ref[...].T
    for head in range(2):
        q_head = head_lanes(q, head)
        rows = slice(head * HD, (head + 1) * HD)
        for part in range(2):
            keys = HALF * (part + 1)
            cols = slice(part * HALF, (part + 1) * HALF)
            s = dot_nt(k[:keys], q_head[cols]) * SCORE_LOG2 + mask[:keys, cols]
            top = jnp.max(s, axis=0, keepdims=True)
            e = jnp.exp2(s - top)
            total = jnp.sum(e, axis=0, keepdims=True)
            out = dot(v_t[rows, :keys], e.astype(bf16))
            turned[rows, cols] = out / total
            lse_ref[0, head : head + 1, cols] = top + jnp.log2(total)
    out_ref[...] = turned[:, :HALF].T
    mixed = turned[:, HALF:].T.astype(bf16)
    mix_ref[...] = mixed
    acc[...] += dot(mixed, wo_ref[...])

    @pl.when(step == PAIRS - 1)
    def _():
        finish_middle(x_ref, acc, rows_ref, middle_ref, normed_ref, sent_ref)


def finish_middle(x_ref, acc, rows_ref, middle_ref, normed_ref, sent_ref):
    middle = x_ref[...].astype(f32) + (acc[...] + rows_ref[0:1])
    middle_ref[...] = middle
    normed = layer_norm(middle, rows_ref[1:2], rows_ref[2:3]).astype(bf16)
    normed_ref[...] = normed
    sent_ref[...] = normed


def local_attention(lens, qkv, attn_out, inputs, rows):
    column = lambda k: pl.BlockSpec((L, LANES), lambda i: (0, k * PAIRS + i))
    upper = pl.BlockSpec((HALF, D), lambda i: (1, 0))
    return pl.pallas_call(
        local_kernel,
        grid=(PAIRS,),
        in_specs=[
            pl.BlockSpec(memory_space=pltpu.SMEM),
            column(0),
            column(1),
            column(2),
            pl.BlockSpec((LANES, D), lambda i: (i, 0)),
            upper,
            pl.BlockSpec((8, D), lambda i: (0, 0)),
        ],
        out_specs=[
            pl.BlockSpec((HALF, LANES), lambda i: (0, i)),
            pl.BlockSpec((1, 8, L), lambda i: (i, 0, 0)),
            pl.BlockSpec((HALF, LANES), lambda i: (1, i)),
            upper,
            upper,
            pl.BlockSpec((HALF, D), lambda i: (0, 0)),
        ],
        out_shape=[
            jax.ShapeDtypeStruct((HALF, D), f32),
            jax.ShapeDtypeStruct((PAIRS, 8, L), f32),
            jax.ShapeDtypeStruct((L, D), bf16),
            jax.ShapeDtypeStruct((L, D), f32),
            jax.ShapeDtypeStruct((L, D), bf16),
            jax.ShapeDtypeStruct((HALF, D), bf16),
        ],
        scratch_shapes=[
            pltpu.VMEM((L, L), f32),
            pltpu.VMEM((LANES, L), f32),
            pltpu.VMEM((HALF, D), f32),
        ],
        cost_estimate=pl.CostEstimate(
            flops=H * 12 * HALF * HALF * 256, bytes_accessed=8 * L * D, transcendentals=H * L * L
        ),
        name="local_attention",
    )(lens, qkv, qkv, qkv, attn_out, inputs, rows)


def basis_rows(last_len, transposed):
    shape = (HALF, NB) if transposed else (NB, HALF)
    slot_dim, place_dim = (1, 0) if transposed else (0, 1)
    slot = lax.broadcasted_iota(jnp.int32, shape, slot_dim).astype(f32)
    place = lax.broadcasted_iota(jnp.int32, shape, place_dim).astype(f32)
    offsets = place - HALF + last_len + 0.5
    distances = (slot + 0.5) / NB * last_len - offsets
    weights = jnp.where(offsets > 0.0, jnp.exp(-0.5 * distances * distances), 0.0)
    return weights / jnp.sum(weights, axis=place_dim, keepdims=True)


def memory_kernel(
    reads,
    last_ref,
    q_ref,
    kt_ref,
    vt_ref,
    vb_ref,
    local_ref,
    wo_ref,
    x_ref,
    rows_ref,
    mix_whole,
    middle_whole,
    normed_whole,
    mix_ref,
    mk_ref,
    mv_ref,
    lse_ref,
    middle_ref,
    normed_ref,
    basis_t_ref,
    sent_ref,
    basis,
    turned,
    acc,
):
    step = pl.program_id(0)

    @pl.when(step == 0)
    def _():
        last_len = last_ref[0:1, 0:1]
        basis[...] = basis_rows(last_len, False).astype(bf16)
        basis_t_ref[...] = basis_rows(last_len, True).astype(bf16)
        acc[...] = jnp.zeros_like(acc)

    mem_k = dot(basis[...], kt_ref[...]).astype(bf16)
    mem_v = (dot(basis[...], vt_ref[...]) + vb_ref[0:1]).astype(bf16)
    mk_ref[...] = mem_k
    mv_ref[...] = mem_v
    v_t = mem_v.T
    query = lax.broadcasted_iota(jnp.int32, (1, HALF), 1)
    reading = query < reads[0, 0]
    q = q_ref[...]
    for head in range(2):
        rows = slice(head * HD, (head + 1) * HD)
        s = dot_nt(mem_k, head_lanes(q, head)) * SCORE_LOG2
        top = jnp.max(s, axis=0, keepdims=True)
        e = jnp.exp2(s - top)
        total = jnp.sum(e, axis=0, keepdims=True)
        out = dot(v_t[rows], e.astype(bf16))
        turned[rows, :] = jnp.where(reading, out / total, 0.0)
        lse_ref[0, head : head + 1, :] = jnp.where(reading, top + jnp.log2(total), -MASKED)
    mixed = (local_ref[...] + turned[...].T).astype(bf16)
    mix_ref[...] = mixed
    acc[...] += dot(mixed, wo_ref[...])

    @pl.when(step == PAIRS - 1)
    def _():
        finish_middle(x_ref, acc, rows_ref, middle_ref, normed_ref, sent_ref)


def memory_attention(
    reads, last_rows, qkv, tail_kv, value_bias, local, attn_out, inputs, rows, mixture, middle, normed
):
    whole = lambda shape: pl.BlockSpec(shape, lambda i: (0,) * len(shape))
    untouched = pl.BlockSpec(memory_space=pl.ANY)
    return pl.pallas_call(
        memory_kernel,
        grid=(PAIRS,),
        in_specs=[
            pl.BlockSpec(memory_space=pltpu.SMEM),
            whole((16, D)),
            pl.BlockSpec((HALF, LANES), lambda i: (0, i)),
            pl.BlockSpec((HALF, LANES), lambda i: (0, i)),
            pl.BlockSpec((HALF, LANES), lambda i: (0, PAIRS + i)),
            pl.BlockSpec((8, LANES), lambda i: (0, i)),
            pl.BlockSpec((HALF, LANES), lambda i: (0, i)),
            pl.BlockSpec((LANES, D), lambda i: (i, 0)),
            whole((HALF, D)),
            whole((8, D)),
            untouched,
            untouched,
            untouched,
        ],
        out_specs=[
            pl.BlockSpec((HALF, LANES), lambda i: (0, i)),
            pl.BlockSpec((NB, LANES), lambda i: (0, i)),
            pl.BlockSpec((NB, LANES), lambda i: (0, i)),
            pl.BlockSpec((1, 8, HALF), lambda i: (i, 0, 0)),
            whole((HALF, D)),
            whole((HALF, D)),
            whole((HALF, NB)),
            whole((HALF, D)),
        ],
        out_shape=[
            jax.ShapeDtypeStruct((L, D), bf16),
            jax.ShapeDtypeStruct((NB, D), bf16),
            jax.ShapeDtypeStruct((NB, D), bf16),
            jax.ShapeDtypeStruct((PAIRS, 8, HALF), f32),
            jax.ShapeDtypeStruct((L, D), f32),
            jax.ShapeDtypeStruct((L, D), bf16),
            jax.ShapeDtypeStruct((HALF, NB), bf16),
            jax.ShapeDtypeStruct((HALF, D), bf16),
        ],
        scratch_shapes=[
            pltpu.VMEM((NB, HALF), bf16),
            pltpu.VMEM((LANES, HALF), f32),
            pltpu.VMEM((HALF, D), f32),
        ],
        input_output_aliases={10: 0, 11: 4, 12: 5},
        cost_estimate=pl.CostEstimate(
            flops=H * 16 * HALF * HALF * 256, bytes_accessed=16 * L * D, transcendentals=H * L * HALF
        ),
        name="memory_attention",
    )(
        reads,
        last_rows,
        qkv,
        tail_kv,
        tail_kv,
        value_bias,
        local,
        attn_out,
        inputs,
        rows,
        mixture,
        middle,
        normed,
    )


def mlp_kernel(x_ref, ct_ref, wi_ref, bi_ref, wo_ref, *refs):
    hid_ref, dpre_ref, bias_ref, y_ref, dx_ref, y_acc, dx_acc = refs[-7:]
    step = pl.program_id(0)
    pre = dot(x_ref[...], wi_ref[...]) + bi_ref[0:1]
    squared = pre * pre
    tanh = jnp.tanh(pre * (0.7978845608028654 + 0.7978845608028654 * 0.044715 * squared))
    half = 0.5 * pre
    hidden = (half + half * tanh).astype(bf16)
    slope = (
        0.5
        + 0.5 * tanh
        + half
        * (1.0 - tanh * tanh)
        * (0.7978845608028654 + 3 * 0.7978845608028654 * 0.044715 * squared)
    )
    d_pre = (slope * dot_nt(ct_ref[...], wo_ref[...])).astype(bf16)
    hid_ref[...] = hidden
    dpre_ref[...] = d_pre
    bias_ref[...] = jnp.broadcast_to(
        jnp.sum(d_pre.astype(f32), axis=0, keepdims=True), bias_ref.shape
    )
    y = dot(hidden, wo_ref[...])
    dx = dot_nt(d_pre, wi_ref[...])

    @pl.when(step == 0)
    def _():
        y_acc[...] = y
        dx_acc[...] = dx

    @pl.when(step > 0)
    def _():
        y_acc[...] += y
        dx_acc[...] += dx

    @pl.when(step == pl.num_programs(0) - 1)
    def _():
        y_ref[...] = y_acc[...].astype(bf16)
        dx_ref[...] = dx_acc[...].astype(bf16)


def mlp_block(rows, cotangent, part, mlp_in, bias_rows, mlp_out, total, place, kept):
    count, hidden = rows.shape[0], mlp_in.shape[1]
    tile = 256 if hidden % 256 == 0 else 128
    fixed = pl.BlockSpec((count, D), lambda i: (0, 0))
    across = pl.BlockSpec((count, tile), lambda i: (place, i))
    return pl.pallas_call(
        mlp_kernel,
        grid=(hidden // tile,),
        in_specs=[
            fixed,
            pl.BlockSpec((count, D), lambda i: (part, 0)),
            pl.BlockSpec((D, tile), lambda i: (0, i)),
            pl.BlockSpec((8, tile), lambda i: (0, i)),
            pl.BlockSpec((tile, D), lambda i: (i, 0)),
        ]
        + [pl.BlockSpec(memory_space=pl.ANY)] * len(kept),
        out_specs=[across, across, pl.BlockSpec((8, tile), lambda i: (0, i)), fixed, fixed],
        out_shape=[
            jax.ShapeDtypeStruct((total, hidden), bf16),
            jax.ShapeDtypeStruct((total, hidden), bf16),
            jax.ShapeDtypeStruct((8, hidden), f32),
            jax.ShapeDtypeStruct((count, D), bf16),
            jax.ShapeDtypeStruct((count, D), bf16),
        ],
        scratch_shapes=[pltpu.VMEM((count, D), f32), pltpu.VMEM((count, D), f32)],
        input_output_aliases={5 + i: i for i in range(len(kept))},
        cost_estimate=pl.CostEstimate(
            flops=8 * count * D * hidden,
            bytes_accessed=4 * D * hidden + 4 * count * hidden + 8 * count * D,
            transcendentals=count * hidden,
        ),
        name="mlp_block",
    )(rows, cotangent, mlp_in, bias_rows, mlp_out, *kept)


def backward_kernel(
    lens,
    q_ref,
    k_ref,
    v_ref,
    mk_ref,
    mv_ref,
    db_ref,
    wo_ref,
    ll_ref,
    lm_ref,
    bt_ref,
    dqkv_ref,
    dtail_ref,
    sums_ref,
    mask,
    turned,
    dk_acc,
    dv_acc,
):
    @pl.when(pl.program_id(0) == 0)
    def _():
        fill_mask(lens, mask)

    q, k, v = q_ref[...], k_ref[...], v_ref[...]
    mem_k, mem_v = mk_ref[...], mv_ref[...]
    d_mix = dot_nt(db_ref[...], wo_ref[...]).astype(bf16)
    k_t, mk_t = k.T, mem_k.T
    d_mem_k = d_mem_v = None

    def one(keys, values, q_part, d_part, lse, extra):
        s = dot_nt(keys, q_part) * SCORE_LOG2
        if extra is not None:
            s = s + extra
        weights = jnp.exp2(s - lse)
        d_weights = dot_nt(values, d_part)
        inner = jnp.sum(weights * d_weights, axis=0, keepdims=True)
        d_scores = (weights * (d_weights - inner)).astype(bf16)
        return d_scores, dot(d_scores, q_part), dot(weights.astype(bf16), d_part)

    for head in range(2):
        rows = slice(head * HD, (head + 1) * HD)
        q_head, d_head = head_lanes(q, head), head_lanes(d_mix, head)
        for part in range(2):
            keys = HALF * (part + 1)
            cols = slice(part * HALF, (part + 1) * HALF)
            ds, dk, dv = one(
                k[:keys],
                v[:keys],
                q_head[cols],
                d_head[cols],
                ll_ref[0, head : head + 1, cols],
                mask[:keys, cols],
            )
            dq = dot(k_t[rows, :keys], ds)
            if part == 0:
                ds, d_key, d_value = one(
                    mem_k, mem_v, q_head[cols], d_head[cols], lm_ref[0, head : head + 1, :], None
                )
                dq = dq + dot(mk_t[rows], ds)
                d_mem_k = d_key if d_mem_k is None else d_mem_k + d_key
                d_mem_v = d_value if d_mem_v is None else d_mem_v + d_value
            turned[rows, cols] = dq
            if head == 0 and part == 0:
                dk_acc[:HALF] = dk
                dv_acc[:HALF] = dv
            elif head == 0:
                dk_acc[:HALF] += dk[:HALF]
                dv_acc[:HALF] += dv[:HALF]
                dk_acc[HALF:] = dk[HALF:]
                dv_acc[HALF:] = dv[HALF:]
            else:
                dk_acc[:keys] += dk
                dv_acc[:keys] += dv
    scale = HD**-0.5
    d_q = (turned[...].T * scale).astype(bf16)
    d_v = dv_acc[...].astype(bf16)
    dqkv_ref[0] = d_q
    dqkv_ref[1] = (dk_acc[...] * scale).astype(bf16)
    dqkv_ref[2] = d_v
    d_mem_k = (d_mem_k * scale).astype(bf16)
    d_mem_v = d_mem_v.astype(bf16)
    dtail_ref[0] = dot(bt_ref[...], d_mem_k).astype(bf16)
    dtail_ref[1] = dot(bt_ref[...], d_mem_v).astype(bf16)
    sums_ref[0:1] = jnp.sum(d_q.astype(f32), axis=0, keepdims=True)
    sums_ref[1:2] = jnp.sum(d_v.astype(f32), axis=0, keepdims=True) + jnp.sum(
        d_mem_v.astype(f32), axis=0, keepdims=True
    )


HIDDEN = pl.CostEstimate(flops=1000, bytes_accessed=1000, transcendentals=0)


def attention_backward(
    first, pairs, lens, qkv, mem_k, mem_v, d_branch, attn_out, lse_local, lse_mem, basis_t
):
    column = lambda k: pl.BlockSpec((L, LANES), lambda i: (0, k * PAIRS + first + i))
    whole = lambda shape: pl.BlockSpec(shape, lambda i: (0,) * len(shape))
    width = pairs * LANES
    return pl.pallas_call(
        backward_kernel,
        grid=(pairs,),
        in_specs=[
            pl.BlockSpec(memory_space=pltpu.SMEM),
            column(0),
            column(1),
            column(2),
            column(0),
            column(0),
            whole((L, D)),
            pl.BlockSpec((LANES, D), lambda i: (first + i, 0)),
            pl.BlockSpec((1, 8, L), lambda i: (first + i, 0, 0)),
            pl.BlockSpec((1, 8, HALF), lambda i: (first + i, 0, 0)),
            whole((HALF, NB)),
        ],
        out_specs=[
            pl.BlockSpec((3, L, LANES), lambda i: (0, 0, i)),
            pl.BlockSpec((2, HALF, LANES), lambda i: (0, 0, i)),
            pl.BlockSpec((8, LANES), lambda i: (0, i)),
        ],
        out_shape=[
            jax.ShapeDtypeStruct((3, L, width), bf16),
            jax.ShapeDtypeStruct((2, HALF, width), bf16),
            jax.ShapeDtypeStruct((8, width), f32),
        ],
        scratch_shapes=[
            pltpu.VMEM((L, L), f32),
            pltpu.VMEM((LANES, L), f32),
            pltpu.VMEM((L, LANES), f32),
            pltpu.VMEM((L, LANES), f32),
        ],
        cost_estimate=pl.CostEstimate(
            flops=2 * pairs * 56 * HALF * HALF * 256,
            bytes_accessed=20 * L * width,
            transcendentals=2 * pairs * L * L,
        ),
        name="attention_backward",
    )(lens, qkv, qkv, qkv, mem_k, mem_v, d_branch, attn_out, lse_local, lse_mem, basis_t)


def normalized(matrix):
    centered = matrix - jnp.mean(matrix, axis=-1, keepdims=True)
    scale = lax.rsqrt(jnp.mean(centered * centered, axis=-1, keepdims=True) + 1e-05)
    return centered * scale, scale


def norm_slope(unit, scale, grown):
    inner = jnp.mean(grown * unit, axis=-1, keepdims=True)
    return (grown - jnp.mean(grown, axis=-1, keepdims=True) - unit * inner) * scale


def column_sum(matrix):
    return jnp.sum(matrix, axis=0, keepdims=True)


def middle_backward(d_own, returned, cotangent, middle, rows):
    count = len(returned[0])

    def kernel(d_ref, ct_ref, middle_ref, rows_ref, *refs):
        shares = refs[: 2 * count]
        d_middle_ref, d_branch_ref, sums_ref = refs[2 * count :]
        part = pl.program_id(0)
        total = d_ref[...].astype(f32)
        for i in range(count):
            total = total + jnp.where(part == 0, shares[i][...], shares[count + i][...]).astype(f32)
        upstream = ct_ref[...].astype(f32)
        unit, scale = normalized(middle_ref[...])
        d_middle = upstream + norm_slope(unit, scale, total * rows_ref[1:2])
        d_branch = d_middle.astype(bf16)
        d_middle_ref[...] = d_middle
        d_branch_ref[...] = d_branch
        sums = jnp.concatenate(
            [
                column_sum(d_branch.astype(f32)),
                column_sum(total * unit),
                column_sum(total),
                column_sum(upstream),
                jnp.zeros((4, D), f32),
            ],
            axis=0,
        )

        @pl.when(part == 0)
        def _():
            sums_ref[...] = sums

        @pl.when(part > 0)
        def _():
            sums_ref[...] += sums

    half = pl.BlockSpec((HALF, D), lambda i: (i, 0))
    fixed = pl.BlockSpec((HALF, D), lambda i: (0, 0))
    eight = pl.BlockSpec((8, D), lambda i: (0, 0))
    return pl.pallas_call(
        kernel,
        grid=(2,),
        in_specs=[half, half, half, eight] + [fixed] * (2 * count),
        out_specs=[half, half, eight],
        out_shape=[
            jax.ShapeDtypeStruct((L, D), f32),
            jax.ShapeDtypeStruct((L, D), bf16),
            jax.ShapeDtypeStruct((8, D), f32),
        ],
        cost_estimate=pl.CostEstimate(
            flops=20 * L * D, bytes_accessed=14 * L * D, transcendentals=0
        ),
        name="middle_backward",
    )(d_own, cotangent, middle, rows, *returned[0], *returned[1])


def qkv_backward(d_one, d_two, d_tail_one, d_tail_two, attn_in, inputs, tail_rows):
    cut = d_one.shape[2]

    def kernel(
        one_ref, two_ref, t_one_ref, t_two_ref, w_ref, x_ref, xt_ref, dn_ref, dt_ref, sums_ref, tail
    ):
        step = pl.program_id(0)
        left, right = w_ref[:, :cut], w_ref[:, cut:]
        part = dot_nt(one_ref[0], left) + dot_nt(two_ref[0], right)

        @pl.when(step == 0)
        def _():
            dn_ref[...] = part
            tail[...] = jnp.zeros_like(tail)

        @pl.when(step > 0)
        def _():
            dn_ref[...] += part
            tail[...] += dot_nt(t_one_ref[0], left) + dot_nt(t_two_ref[0], right)

        @pl.when(step == 2)
        def _():
            dt_ref[...] = tail[...].astype(bf16)
            unit, unused = normalized(x_ref[...].astype(f32))
            tail_unit, unused = normalized(xt_ref[...].astype(f32))
            sums_ref[0:1] = column_sum(dn_ref[...] * unit) + column_sum(tail[...] * tail_unit)
            sums_ref[1:2] = column_sum(dn_ref[...]) + column_sum(tail[...])

    fixed = lambda count: pl.BlockSpec((count, D), lambda i: (0, 0))
    return pl.pallas_call(
        kernel,
        grid=(3,),
        in_specs=[
            pl.BlockSpec((1, L, cut), lambda i: (i, 0, 0)),
            pl.BlockSpec((1, L, D - cut), lambda i: (i, 0, 0)),
            pl.BlockSpec((1, HALF, cut), lambda i: (jnp.maximum(i - 1, 0), 0, 0)),
            pl.BlockSpec((1, HALF, D - cut), lambda i: (jnp.maximum(i - 1, 0), 0, 0)),
            pl.BlockSpec((D, D), lambda i: (0, i)),
            fixed(L),
            fixed(HALF),
        ],
        out_specs=[fixed(L), fixed(HALF), fixed(8)],
        out_shape=[
            jax.ShapeDtypeStruct((L, D), f32),
            jax.ShapeDtypeStruct((HALF, D), bf16),
            jax.ShapeDtypeStruct((8, D), f32),
        ],
        scratch_shapes=[pltpu.VMEM((HALF, D), f32)],
        cost_estimate=pl.CostEstimate(
            flops=8 * L * D * D, bytes_accessed=20 * L * D, transcendentals=0
        ),
        name="qkv_backward",
    )(d_one, d_two, d_tail_one, d_tail_two, attn_in, inputs, tail_rows)


def input_backward(d_normed, from_next, inputs, d_middle, gain):
    def kernel(dn_ref, next_ref, x_ref, dm_ref, gain_ref, out_ref):
        unit, scale = normalized(x_ref[...].astype(f32))
        shared = jnp.where(pl.program_id(0) == 0, 0.0, next_ref[...].astype(f32))
        grown = (dn_ref[...] + shared) * gain_ref[0:1]
        out_ref[...] = (dm_ref[...] + norm_slope(unit, scale, grown)).astype(bf16)

    half = pl.BlockSpec((HALF, D), lambda i: (i, 0))
    return pl.pallas_call(
        kernel,
        grid=(2,),
        in_specs=[
            half,
            pl.BlockSpec((HALF, D), lambda i: (0, 0)),
            half,
            half,
            pl.BlockSpec((8, D), lambda i: (0, 0)),
        ],
        out_specs=half,
        out_shape=jax.ShapeDtypeStruct((L, D), bf16),
        cost_estimate=pl.CostEstimate(
            flops=20 * L * D, bytes_accessed=12 * L * D, transcendentals=0
        ),
        name="input_backward",
    )(d_normed, from_next, inputs, d_middle, gain)


def widened(first, second):
    steps = 6

    def kernel(a_ref, b_ref, a_out, b_out):
        a_out[...] = a_ref[...].astype(f32)
        b_out[...] = b_ref[...].astype(f32)

    specs = [
        pl.BlockSpec((matrix.shape[0] // steps, matrix.shape[1]), lambda i: (i, 0))
        for matrix in (first, second)
    ]
    return pl.pallas_call(
        kernel,
        grid=(steps,),
        in_specs=specs,
        out_specs=specs,
        out_shape=[jax.ShapeDtypeStruct(matrix.shape, f32) for matrix in (first, second)],
        cost_estimate=pl.CostEstimate(
            flops=0, bytes_accessed=6 * (first.size + second.size), transcendentals=0
        ),
        name="widened",
    )(first, second)


def rotated(value, axis, by):
    count = lax.axis_size(axis)
    return lax.ppermute(value, axis, [(i, (i + by) % count) for i in range(count)])


fence = lax.optimization_barrier
GRID = ("batch", "mlp")


def flipped(value, mask):
    count = lax.axis_size("batch") * lax.axis_size("mlp")
    return lax.ppermute(value, GRID, [(i, i ^ mask) for i in range(count)])


def place_in(bits):
    number = lax.axis_index(GRID)
    return sum(((number >> bit) & 1) << i for i, bit in enumerate(bits))


def peers(bits):
    return [sum(((q >> i) & 1) << bit for i, bit in enumerate(bits)) for q in range(1, 1 << len(bits))]


def grouped(bits):
    odd = len(bits) % 2
    return ([bits[:1]] if odd else []) + [bits[i : i + 2] for i in range(odd, len(bits), 2)]


class Chain:
    def __init__(self, kept, given, groups):
        self.stages = [(True, bits) for bits in groups] + [(False, bits) for bits in groups[::-1]]
        self.turn()
        self.kept, self.given = kept, [given]

    def turn(self):
        self.scatters, self.bits = self.stages.pop(0)
        self.place = place_in(self.bits)

    def prepare(self):
        self.turn()
        count = 1 << len(self.bits)
        if self.scatters:
            size = self.value.shape[0] // count
            piece = lambda i: lax.dynamic_slice_in_dim(self.value, i * size, size, 0)
            self.kept = piece(self.place)
            self.given = [piece(self.place ^ q) for q in range(1, count)]
        else:
            self.kept = self.value
            self.given = [self.value]

    def fly(self):
        masks = peers(self.bits)
        given = self.given if self.scatters else self.given * len(masks)
        self.got = [flipped(piece, mask) for piece, mask in zip(given, masks)]

    def land(self):
        if self.scatters:
            total = self.kept.astype(f32)
            for piece in self.got:
                total = total + piece.astype(f32)
            self.value = total.astype(self.kept.dtype)
        else:
            pieces = [self.kept] + self.got
            order = [
                lax.select_n(self.place ^ i, *pieces)
                if len(pieces) > 2
                else jnp.where(self.place == i, *pieces)
                for i in range(len(pieces))
            ]
            self.value = jnp.concatenate(order, axis=0)
        if self.stages:
            self.prepare()
            return True
        return False


class Total:
    def __init__(self, value, bits):
        self.value, self.bits = value, list(bits)

    def fly(self):
        self.got = flipped(self.value, 1 << self.bits.pop(0))

    def land(self):
        self.value = self.value + self.got
        self.given = [self.value]
        return bool(self.bits)


def weight_grads(normed, normed_tail, d, d_tail, ready, side):
    width = d.shape[2]
    tile = 256
    each = width // tile
    extra = 0 if ready is None else ready.shape[1] // tile
    half = D // 2

    def kernel(side_ref, n_ref, nt_ref, d_ref, dt_ref, *refs):
        kept_ref, given_ref, turned, tail_turned = refs[-4:]
        step = pl.program_id(0)

        @pl.when(step == 0)
        def _():
            turned[...] = n_ref[...].T
            tail_turned[...] = nt_ref[...].T

        def rows(which, ref):
            return ref[pl.ds(pl.multiple_of(which * half, half), half), :]

        for which, out_ref in ((side_ref[0], kept_ref), (1 - side_ref[0], given_ref)):

            @pl.when(step < each)
            def _():
                out_ref[...] = dot(rows(which, turned), d_ref[0]).astype(bf16)

            @pl.when((step >= each) & (step < 3 * each))
            def _():
                out_ref[...] = (
                    dot(rows(which, turned), d_ref[0]) + dot(rows(which, tail_turned), dt_ref[0])
                ).astype(bf16)

            if extra:

                @pl.when(step >= 3 * each)
                def _():
                    out_ref[...] = rows(which, refs[0])

    column = lambda i: jnp.where(i < 3 * each, i % each, each - 1)
    in_specs = [
        pl.BlockSpec(memory_space=pltpu.SMEM),
        pl.BlockSpec((L, D), lambda i: (0, 0)),
        pl.BlockSpec((HALF, D), lambda i: (0, 0)),
        pl.BlockSpec((1, L, tile), lambda i: (jnp.minimum(i // each, 2), 0, column(i))),
        pl.BlockSpec((1, HALF, tile), lambda i: (jnp.clip(i // each - 1, 0, 1), 0, column(i))),
    ]
    operands = [side, normed, normed_tail, d, d_tail]
    if extra:
        in_specs.append(pl.BlockSpec((D, tile), lambda i: (0, jnp.maximum(i - 3 * each, 0))))
        operands.append(ready)
    steps = 3 * each + extra
    return pl.pallas_call(
        kernel,
        grid=(steps,),
        in_specs=in_specs,
        out_specs=[pl.BlockSpec((half, tile), lambda i: (0, i))] * 2,
        out_shape=[jax.ShapeDtypeStruct((half, steps * tile), bf16)] * 2,
        scratch_shapes=[pltpu.VMEM((D, L), bf16), pltpu.VMEM((D, HALF), bf16)],
        cost_estimate=HIDDEN,
        name="weight_grads",
    )(*operands)


def shards(
    inputs,
    doc_lengths,
    ln1_gain,
    ln1_bias,
    attn_in,
    qv_bias,
    attn_out,
    attn_out_bias,
    ln2_gain,
    second_norm_bias,
    mlp_in,
    mlp_in_bias,
    mlp_out,
    mlp_out_bias,
    cotangent,
):
    n_mlp = lax.axis_size("mlp")
    place = lax.axis_index("mlp")
    gain_one = ln1_gain.astype(f32)
    bias_one = ln1_bias.astype(f32)
    gain_two = ln2_gain.astype(f32)
    bias_two = second_norm_bias.astype(f32)

    own_tail = jnp.concatenate(
        [
            inputs[HALF:],
            jnp.broadcast_to(doc_lengths[:, NDOC - 1 :].astype(bf16), (16, D)),
        ],
        axis=0,
    )
    tail = rotated(own_tail, "mlp", 1)
    cotangents = [cotangent] + [rotated(cotangent, "mlp", by) for by in range(1, n_mlp)]

    activations = inputs.astype(f32)
    normed = layer_norm(activations, gain_one, bias_one).astype(bf16)
    zeros = jnp.zeros((D,), f32)
    qkv_bias = jnp.concatenate([qv_bias[0].astype(f32), zeros, qv_bias[1].astype(f32)])
    qkv = (dot(normed, attn_in) + qkv_bias).astype(bf16)
    rows = jnp.concatenate(
        [
            jnp.stack([attn_out_bias.astype(f32), gain_two, bias_two]),
            jnp.zeros((5, D), f32),
        ]
    )
    local, lse_local, mixture, middle, normed_two, sent = local_attention(
        doc_lengths, qkv, attn_out, inputs, rows
    )
    steps = range(1, n_mlp)
    arrived_hi = [rotated(sent, "mlp", by) for by in steps]

    tail_rows = tail[:HALF].astype(f32)
    normed_tail = layer_norm(tail_rows, gain_one, bias_one).astype(bf16)
    tail_kv = dot(normed_tail, attn_in[:, D:]).astype(bf16)
    reads = jnp.where(place == 0, 0, doc_lengths[:, :1])
    value_bias = jnp.broadcast_to(qv_bias[1].astype(f32), (8, D))
    tail_kv, *cotangents[1:] = fence((tail_kv, *cotangents[1:]))
    mixture, mem_k, mem_v, lse_mem, middle, normed_two, basis_t, sent = memory_attention(
        reads,
        tail[HALF:],
        qkv,
        tail_kv,
        value_bias,
        local,
        attn_out,
        inputs,
        rows,
        mixture,
        middle,
        normed_two,
    )
    arrived_lo = [rotated(sent, "mlp", by) for by in steps]
    mem_k, arrived_hi = fence((mem_k, arrived_hi))

    bias_rows = jnp.broadcast_to(mlp_in_bias.astype(f32), (8, mlp_in.shape[1]))
    kept = ()
    d_mlp_in_bias = 0.0
    returned_y, returned_dx = [], []
    calls = [(by, part) for by in steps for part in (1, 0)]
    for by, part in calls:
        block = (arrived_lo, arrived_hi)[part][by - 1]
        hidden, d_pre, d_bias, y, dx = mlp_block(
            block, cotangents[by], part, mlp_in, bias_rows, mlp_out, n_mlp * L, 2 * by + part, kept
        )
        kept = (hidden, d_pre)
        d_mlp_in_bias = d_mlp_in_bias + d_bias[0]
        returned_dx.append(rotated(dx, "mlp", -by))
        returned_y.append(y)
    hidden, d_pre, d_bias, y_own, dx_own = mlp_block(
        normed_two, cotangent, 0, mlp_in, bias_rows, mlp_out, n_mlp * L, 0, kept
    )
    d_mlp_in_bias = d_mlp_in_bias + d_bias[0]
    hidden, d_pre, returned_dx = fence((hidden, d_pre, returned_dx))
    over_rows = lambda a, b: lax.dot_general(
        a, b, (((0,), (0,)), ((), ())), preferred_element_type=f32
    )
    all_rows = jnp.concatenate(
        [normed_two] + [piece for pair in zip(arrived_lo, arrived_hi) for piece in pair], axis=0
    )
    d_mlp_in = over_rows(all_rows, d_pre).astype(bf16)
    d_mlp_out = over_rows(hidden, jnp.concatenate(cotangents, axis=0)).astype(bf16)

    hidden_count = mlp_in.shape[1]
    mlp_count = n_mlp.bit_length() - 1
    batch_count = lax.axis_size("batch").bit_length() - 1
    mlp_bits = list(range(mlp_count))
    core = [[mlp_count]]
    rest = list(range(mlp_count + 1, mlp_count + batch_count))
    groups = core + [mlp_bits[:1] + rest[:1]] + [[bit] for bit in mlp_bits[1:] + rest[1:]]

    d_mlp_in, d_mlp_out = lax.psum((d_mlp_in, d_mlp_out), "batch")

    def finish():
        shares = [[dx for (by, part), dx in zip(calls, returned_dx) if part == half] for half in (0, 1)]
        d_middle, d_branch, middle_sums = middle_backward(dx_own, shares, cotangent, middle, rows)
        backward = lambda first, pairs, d: attention_backward(
            first, pairs, doc_lengths, qkv, mem_k, mem_v, d, attn_out, lse_local, lse_mem, basis_t
        )
        early = PAIRS // 3
        side = place_in(core[0]).reshape(1)
        d_one, d_tail_one, sums_one = backward(0, early, d_branch)
        d_attn_out = over_rows(mixture, d_branch).astype(bf16)
        chain_one = Chain(
            *weight_grads(normed, normed_tail, d_one, d_tail_one, d_attn_out, side), groups
        )
        chain_one.fly()
        chain_one.land()
        d_branch, chain_one.given = fence((d_branch, chain_one.given))
        chain_one.fly()
        d_two, d_tail_two, sums_two = backward(early, PAIRS - early, d_branch)
        d_two, d_tail_two, chain_one.got = fence((d_two, d_tail_two, chain_one.got))
        chain_one.land()
        d_two, d_tail_two, chain_one.given = fence((d_two, d_tail_two, chain_one.given))
        chain_one.fly()
        chain_two = Chain(*weight_grads(normed, normed_tail, d_two, d_tail_two, None, side), groups)
        chain_two.fly()
        chain_two.land()
        d_one, d_two, d_tails, sums, later, chain_two.given = fence(
            (
                d_one,
                d_two,
                (d_tail_one, d_tail_two),
                (sums_one, sums_two),
                (d_mlp_in_bias, returned_y, y_own),
                chain_two.given,
            )
        )
        bias_grad, y_given, y_mine = later
        chain_two.fly()
        d_normed, d_tail_rows, input_sums = qkv_backward(
            d_one, d_two, *d_tails, attn_in, inputs, tail[:HALF]
        )
        chain_one.got, d_normed, d_tail_rows, input_sums = fence(
            (chain_one.got, d_normed, d_tail_rows, input_sums)
        )
        chain_one.land()
        chain_one.fly()
        from_next = rotated(d_tail_rows, "mlp", -1)
        placed_bias = lax.dynamic_update_slice(
            jnp.zeros((n_mlp * hidden_count,), f32), bias_grad, (place * hidden_count,)
        )
        vectors = Total(
            jnp.concatenate(
                [
                    input_sums[:2],
                    middle_sums[:4],
                    jnp.concatenate(sums, axis=1)[:2],
                    placed_bias.reshape(-1, D),
                ],
                axis=0,
            ),
            core[0] + mlp_bits + rest,
        )
        vectors.fly()

        token = chain_one.given
        flying = [chain_one, chain_two, vectors]
        turns = 0
        while flying:
            for chain in list(flying):
                chain.got, token = fence((chain.got, token))
                if chain is chain_two:
                    turns += 1
                    if turns == 1:
                        chain.got, y_given = fence((chain.got, y_given))
                        returned = [
                            rotated(y, "mlp", -by) for (by, part), y in zip(calls, y_given)
                        ]
                    if turns == 3:
                        chain.got, returned = fence((chain.got, returned))
                if chain.land():
                    token = chain.given
                    chain.fly()
                else:
                    flying.remove(chain)

        gain = jnp.broadcast_to(gain_one, (8, D))
        input_grad = input_backward(d_normed, from_next, inputs, d_middle, gain)

        halves = [y_mine[:HALF].astype(f32), y_mine[HALF:].astype(f32)]
        for (by, part), y in zip(calls, returned):
            halves[part] = halves[part] + y.astype(f32)
        result = jnp.concatenate(halves, axis=0)
        layer_output = (middle + (result + mlp_out_bias)).astype(bf16)

        width = early * LANES
        late = D - width
        d_attn_in = jnp.concatenate(
            [
                piece
                for i in range(3)
                for piece in (
                    chain_one.value[:, i * width : (i + 1) * width],
                    chain_two.value[:, i * late : (i + 1) * late],
                )
            ],
            axis=1,
        )
        summed = vectors.value
        return (
            layer_output,
            input_grad,
            summed[0],
            summed[1],
            d_attn_in.astype(f32),
            summed[6:8],
            chain_one.value[:, 3 * width :].astype(f32),
            summed[2],
            summed[3],
            summed[4],
            lax.dynamic_slice(summed[8:].reshape(-1), (place * hidden_count,), (hidden_count,)),
            summed[5],
        )


    shapes = jax.eval_shape(finish)
    done = lax.cond(
        doc_lengths[0, 0] > 0,
        finish,
        lambda: jax.tree.map(lambda leaf: jnp.zeros(leaf.shape, leaf.dtype), shapes),
    )
    d_mlp_in, d_mlp_out = widened(d_mlp_in, d_mlp_out)
    return (*done[:10], d_mlp_in, done[10], d_mlp_out, done[11])


def solution(mesh):
    rows, whole = P(("batch", "mlp"), None), P()
    columns, hidden, depth = P(None, "mlp"), P("mlp"), P("mlp", None)
    return jax.shard_map(
        shards,
        mesh=mesh,
        in_specs=(rows, rows) + (whole,) * 8 + (columns, hidden, depth, whole, rows),
        out_specs=(rows, rows) + (whole,) * 8 + (columns, hidden, depth, whole),
        check_vma=False,
    )
```

```python
import jax
import jax.numpy as jnp
from jax import lax
from jax.experimental import pallas as pl
from jax.experimental.pallas import tpu as pltpu
from jax.sharding import PartitionSpec as P

D = 768
H = 12
HD = 64
NB = 512
L = 512
NDOC = 3
HALF = L // 2
PAIRS = H // 2
LANES = 2 * HD

LOG2E = 1.4426950408889634
SCORE_LOG2 = LOG2E * HD**-0.5
MASKED = -1e30

bf16 = jnp.bfloat16
f32 = jnp.float32


def dot(a, b):
    return jnp.dot(a, b, preferred_element_type=f32)


def dot_nt(a, b):
    return lax.dot_general(a, b, (((1,), (1,)), ((), ())), preferred_element_type=f32)


def layer_norm(matrix, gain_row, shift_row):
    center = jnp.mean(matrix, axis=-1, keepdims=True)
    centered = matrix - center
    spread = jnp.mean(centered * centered, axis=-1, keepdims=True)
    return centered * lax.rsqrt(spread + 1e-05) * gain_row + shift_row


def head_lanes(matrix, head):
    lane = lax.broadcasted_iota(jnp.int32, (1, LANES), 1)
    return jnp.where(lane // HD == head, matrix, jnp.zeros_like(matrix))


def fill_mask(lens, mask):
    key = lax.broadcasted_iota(jnp.int32, (L, L), 0)
    query = lax.broadcasted_iota(jnp.int32, (L, L), 1)
    one = lens[0, 0]
    two = one + lens[0, 1]
    start = jnp.where(query >= two, two, jnp.where(query >= one, one, 0))
    mask[...] = jnp.where((key <= query) & (key >= start), 0.0, MASKED)


def local_kernel(
    lens,
    q_ref,
    k_ref,
    v_ref,
    wo_ref,
    x_ref,
    rows_ref,
    out_ref,
    lse_ref,
    mix_ref,
    middle_ref,
    normed_ref,
    sent_ref,
    mask,
    turned,
    acc,
):
    step = pl.program_id(0)

    @pl.when(step == 0)
    def _():
        fill_mask(lens, mask)
        acc[...] = jnp.zeros_like(acc)

    q, k = q_ref[...], k_ref[...]
    v_t = v_ref[...].T
    for head in range(2):
        q_head = head_lanes(q, head)
        rows = slice(head * HD, (head + 1) * HD)
        for part in range(2):
            keys = HALF * (part + 1)
            cols = slice(part * HALF, (part + 1) * HALF)
            s = dot_nt(k[:keys], q_head[cols]) * SCORE_LOG2 + mask[:keys, cols]
            top = jnp.max(s, axis=0, keepdims=True)
            e = jnp.exp2(s - top)
            total = jnp.sum(e, axis=0, keepdims=True)
            out = dot(v_t[rows, :keys], e.astype(bf16))
            turned[rows, cols] = out / total
            lse_ref[0, head : head + 1, cols] = top + jnp.log2(total)
    out_ref[...] = turned[:, :HALF].T
    mixed = turned[:, HALF:].T.astype(bf16)
    mix_ref[...] = mixed
    acc[...] += dot(mixed, wo_ref[...])

    @pl.when(step == PAIRS - 1)
    def _():
        finish_middle(x_ref, acc, rows_ref, middle_ref, normed_ref, sent_ref)


def finish_middle(x_ref, acc, rows_ref, middle_ref, normed_ref, sent_ref):
    middle = x_ref[...].astype(f32) + (acc[...] + rows_ref[0:1])
    middle_ref[...] = middle
    normed = layer_norm(middle, rows_ref[1:2], rows_ref[2:3]).astype(bf16)
    normed_ref[...] = normed
    sent_ref[...] = normed


def local_attention(lens, qkv, attn_out, inputs, rows):
    column = lambda k: pl.BlockSpec((L, LANES), lambda i: (0, k * PAIRS + i))
    upper = pl.BlockSpec((HALF, D), lambda i: (1, 0))
    return pl.pallas_call(
        local_kernel,
        grid=(PAIRS,),
        in_specs=[
            pl.BlockSpec(memory_space=pltpu.SMEM),
            column(0),
            column(1),
            column(2),
            pl.BlockSpec((LANES, D), lambda i: (i, 0)),
            upper,
            pl.BlockSpec((8, D), lambda i: (0, 0)),
        ],
        out_specs=[
            pl.BlockSpec((HALF, LANES), lambda i: (0, i)),
            pl.BlockSpec((1, 8, L), lambda i: (i, 0, 0)),
            pl.BlockSpec((HALF, LANES), lambda i: (1, i)),
            upper,
            upper,
            pl.BlockSpec((HALF, D), lambda i: (0, 0)),
        ],
        out_shape=[
            jax.ShapeDtypeStruct((HALF, D), f32),
            jax.ShapeDtypeStruct((PAIRS, 8, L), f32),
            jax.ShapeDtypeStruct((L, D), bf16),
            jax.ShapeDtypeStruct((L, D), f32),
            jax.ShapeDtypeStruct((L, D), bf16),
            jax.ShapeDtypeStruct((HALF, D), bf16),
        ],
        scratch_shapes=[
            pltpu.VMEM((L, L), f32),
            pltpu.VMEM((LANES, L), f32),
            pltpu.VMEM((HALF, D), f32),
        ],
        cost_estimate=pl.CostEstimate(
            flops=H * 12 * HALF * HALF * 256, bytes_accessed=8 * L * D, transcendentals=H * L * L
        ),
        name="local_attention",
    )(lens, qkv, qkv, qkv, attn_out, inputs, rows)


def basis_rows(last_len, transposed):
    shape = (HALF, NB) if transposed else (NB, HALF)
    slot_dim, place_dim = (1, 0) if transposed else (0, 1)
    slot = lax.broadcasted_iota(jnp.int32, shape, slot_dim).astype(f32)
    place = lax.broadcasted_iota(jnp.int32, shape, place_dim).astype(f32)
    offsets = place - HALF + last_len + 0.5
    distances = (slot + 0.5) / NB * last_len - offsets
    weights = jnp.where(offsets > 0.0, jnp.exp(-0.5 * distances * distances), 0.0)
    return weights / jnp.sum(weights, axis=place_dim, keepdims=True)


def tail_projection(tail, first_rows, attn_in):
    tile = D // 2

    def kernel(x_ref, rows_ref, w_ref, normed_ref, kv_ref):
        @pl.when(pl.program_id(0) == 0)
        def _():
            normed_ref[...] = layer_norm(
                x_ref[...].astype(f32), rows_ref[0:1], rows_ref[1:2]
            ).astype(bf16)

        kv_ref[...] = dot(normed_ref[...], w_ref[...]).astype(bf16)

    fixed = lambda count: pl.BlockSpec((count, D), lambda i: (0, 0))
    return pl.pallas_call(
        kernel,
        grid=(4,),
        in_specs=[fixed(HALF), fixed(8), pl.BlockSpec((D, tile), lambda i: (0, 2 + i))],
        out_specs=[fixed(HALF), pl.BlockSpec((HALF, tile), lambda i: (0, i))],
        out_shape=[
            jax.ShapeDtypeStruct((HALF, D), bf16),
            jax.ShapeDtypeStruct((HALF, 2 * D), bf16),
        ],
        cost_estimate=pl.CostEstimate(
            flops=4 * HALF * D * D, bytes_accessed=4 * D * D, transcendentals=0
        ),
        name="tail_projection",
    )(tail, first_rows, attn_in)


def memory_kernel(
    reads,
    last_ref,
    q_ref,
    kt_ref,
    vt_ref,
    vb_ref,
    local_ref,
    wo_ref,
    x_ref,
    rows_ref,
    mix_whole,
    middle_whole,
    normed_whole,
    mix_ref,
    mk_ref,
    mv_ref,
    lse_ref,
    middle_ref,
    normed_ref,
    basis_t_ref,
    sent_ref,
    basis,
    turned,
    acc,
):
    step = pl.program_id(0)

    @pl.when(step == 0)
    def _():
        last_len = last_ref[0:1, 0:1]
        basis[...] = basis_rows(last_len, False).astype(bf16)
        basis_t_ref[...] = basis_rows(last_len, True).astype(bf16)
        acc[...] = jnp.zeros_like(acc)

    mem_k = dot(basis[...], kt_ref[...]).astype(bf16)
    mem_v = (dot(basis[...], vt_ref[...]) + vb_ref[0:1]).astype(bf16)
    mk_ref[...] = mem_k
    mv_ref[...] = mem_v
    v_t = mem_v.T
    query = lax.broadcasted_iota(jnp.int32, (1, HALF), 1)
    reading = query < reads[0, 0]
    q = q_ref[...]
    for head in range(2):
        rows = slice(head * HD, (head + 1) * HD)
        s = dot_nt(mem_k, head_lanes(q, head)) * SCORE_LOG2
        top = jnp.max(s, axis=0, keepdims=True)
        e = jnp.exp2(s - top)
        total = jnp.sum(e, axis=0, keepdims=True)
        out = dot(v_t[rows], e.astype(bf16))
        turned[rows, :] = jnp.where(reading, out / total, 0.0)
        lse_ref[0, head : head + 1, :] = jnp.where(reading, top + jnp.log2(total), -MASKED)
    mixed = (local_ref[...] + turned[...].T).astype(bf16)
    mix_ref[...] = mixed
    acc[...] += dot(mixed, wo_ref[...])

    @pl.when(step == PAIRS - 1)
    def _():
        finish_middle(x_ref, acc, rows_ref, middle_ref, normed_ref, sent_ref)


def memory_attention(
    reads, last_rows, qkv, tail_kv, value_bias, local, attn_out, inputs, rows, mixture, middle, normed
):
    whole = lambda shape: pl.BlockSpec(shape, lambda i: (0,) * len(shape))
    untouched = pl.BlockSpec(memory_space=pl.ANY)
    return pl.pallas_call(
        memory_kernel,
        grid=(PAIRS,),
        in_specs=[
            pl.BlockSpec(memory_space=pltpu.SMEM),
            whole((16, LANES)),
            pl.BlockSpec((HALF, LANES), lambda i: (0, i)),
            pl.BlockSpec((HALF, LANES), lambda i: (0, i)),
            pl.BlockSpec((HALF, LANES), lambda i: (0, PAIRS + i)),
            pl.BlockSpec((8, LANES), lambda i: (0, i)),
            pl.BlockSpec((HALF, LANES), lambda i: (0, i)),
            pl.BlockSpec((LANES, D), lambda i: (i, 0)),
            whole((HALF, D)),
            whole((8, D)),
            untouched,
            untouched,
            untouched,
        ],
        out_specs=[
            pl.BlockSpec((HALF, LANES), lambda i: (0, i)),
            pl.BlockSpec((NB, LANES), lambda i: (0, i)),
            pl.BlockSpec((NB, LANES), lambda i: (0, i)),
            pl.BlockSpec((1, 8, HALF), lambda i: (i, 0, 0)),
            whole((HALF, D)),
            whole((HALF, D)),
            whole((HALF, NB)),
            whole((HALF, D)),
        ],
        out_shape=[
            jax.ShapeDtypeStruct((L, D), bf16),
            jax.ShapeDtypeStruct((NB, D), bf16),
            jax.ShapeDtypeStruct((NB, D), bf16),
            jax.ShapeDtypeStruct((PAIRS, 8, HALF), f32),
            jax.ShapeDtypeStruct((L, D), f32),
            jax.ShapeDtypeStruct((L, D), bf16),
            jax.ShapeDtypeStruct((HALF, NB), bf16),
            jax.ShapeDtypeStruct((HALF, D), bf16),
        ],
        scratch_shapes=[
            pltpu.VMEM((NB, HALF), bf16),
            pltpu.VMEM((LANES, HALF), f32),
            pltpu.VMEM((HALF, D), f32),
        ],
        input_output_aliases={10: 0, 11: 4, 12: 5},
        cost_estimate=pl.CostEstimate(
            flops=H * 16 * HALF * HALF * 256, bytes_accessed=16 * L * D, transcendentals=H * L * HALF
        ),
        name="memory_attention",
    )(
        reads,
        last_rows,
        qkv,
        tail_kv,
        tail_kv,
        value_bias,
        local,
        attn_out,
        inputs,
        rows,
        mixture,
        middle,
        normed,
    )


def mlp_kernel(x_ref, ct_ref, wi_ref, bi_ref, wo_ref, *refs):
    hid_ref, dpre_ref, bias_ref, y_ref, dx_ref, y_acc, dx_acc = refs[-7:]
    step = pl.program_id(0)
    pre = dot(x_ref[...], wi_ref[...]) + bi_ref[0:1]
    squared = pre * pre
    tanh = jnp.tanh(pre * (0.7978845608028654 + 0.7978845608028654 * 0.044715 * squared))
    half = 0.5 * pre
    hidden = (half + half * tanh).astype(bf16)
    slope = (
        0.5
        + 0.5 * tanh
        + half
        * (1.0 - tanh * tanh)
        * (0.7978845608028654 + 3 * 0.7978845608028654 * 0.044715 * squared)
    )
    d_pre = (slope * dot_nt(ct_ref[...], wo_ref[...])).astype(bf16)
    hid_ref[...] = hidden
    dpre_ref[...] = d_pre
    bias_ref[...] = jnp.broadcast_to(
        jnp.sum(d_pre.astype(f32), axis=0, keepdims=True), bias_ref.shape
    )
    y = dot(hidden, wo_ref[...])
    dx = dot_nt(d_pre, wi_ref[...])

    @pl.when(step == 0)
    def _():
        y_acc[...] = y
        dx_acc[...] = dx

    @pl.when(step > 0)
    def _():
        y_acc[...] += y
        dx_acc[...] += dx

    @pl.when(step == pl.num_programs(0) - 1)
    def _():
        y_ref[...] = y_acc[...].astype(bf16)
        dx_ref[...] = dx_acc[...].astype(bf16)


def mlp_block(rows, cotangent, part, mlp_in, bias_rows, mlp_out, total, place, kept):
    count, hidden = rows.shape[0], mlp_in.shape[1]
    tile = 256 if hidden % 256 == 0 else 128
    fixed = pl.BlockSpec((count, D), lambda i: (0, 0))
    across = pl.BlockSpec((count, tile), lambda i: (place, i))
    return pl.pallas_call(
        mlp_kernel,
        grid=(hidden // tile,),
        in_specs=[
            fixed,
            pl.BlockSpec((count, D), lambda i: (part, 0)),
            pl.BlockSpec((D, tile), lambda i: (0, i)),
            pl.BlockSpec((8, tile), lambda i: (0, i)),
            pl.BlockSpec((tile, D), lambda i: (i, 0)),
        ]
        + [pl.BlockSpec(memory_space=pl.ANY)] * len(kept),
        out_specs=[across, across, pl.BlockSpec((8, tile), lambda i: (0, i)), fixed, fixed],
        out_shape=[
            jax.ShapeDtypeStruct((total, hidden), bf16),
            jax.ShapeDtypeStruct((total, hidden), bf16),
            jax.ShapeDtypeStruct((8, hidden), f32),
            jax.ShapeDtypeStruct((count, D), bf16),
            jax.ShapeDtypeStruct((count, D), bf16),
        ],
        scratch_shapes=[pltpu.VMEM((count, D), f32), pltpu.VMEM((count, D), f32)],
        input_output_aliases={5 + i: i for i in range(len(kept))},
        cost_estimate=pl.CostEstimate(
            flops=8 * count * D * hidden,
            bytes_accessed=4 * D * hidden + 4 * count * hidden + 8 * count * D,
            transcendentals=count * hidden,
        ),
        name="mlp_block",
    )(rows, cotangent, mlp_in, bias_rows, mlp_out, *kept)


def backward_kernel(
    lens,
    q_ref,
    k_ref,
    v_ref,
    mk_ref,
    mv_ref,
    db_ref,
    wo_ref,
    ll_ref,
    lm_ref,
    bt_ref,
    dqkv_ref,
    dtail_ref,
    sums_ref,
    mask,
    turned,
    dk_acc,
    dv_acc,
):
    @pl.when(pl.program_id(0) == 0)
    def _():
        fill_mask(lens, mask)

    q, k, v = q_ref[...], k_ref[...], v_ref[...]
    mem_k, mem_v = mk_ref[...], mv_ref[...]
    d_mix = dot_nt(db_ref[...], wo_ref[...]).astype(bf16)
    k_t, mk_t = k.T, mem_k.T
    d_mem_k = d_mem_v = None

    def one(keys, values, q_part, d_part, lse, extra):
        s = dot_nt(keys, q_part) * SCORE_LOG2
        if extra is not None:
            s = s + extra
        weights = jnp.exp2(s - lse)
        d_weights = dot_nt(values, d_part)
        inner = jnp.sum(weights * d_weights, axis=0, keepdims=True)
        d_scores = (weights * (d_weights - inner)).astype(bf16)
        return d_scores, dot(d_scores, q_part), dot(weights.astype(bf16), d_part)

    for head in range(2):
        rows = slice(head * HD, (head + 1) * HD)
        q_head, d_head = head_lanes(q, head), head_lanes(d_mix, head)
        for part in range(2):
            keys = HALF * (part + 1)
            cols = slice(part * HALF, (part + 1) * HALF)
            ds, dk, dv = one(
                k[:keys],
                v[:keys],
                q_head[cols],
                d_head[cols],
                ll_ref[0, head : head + 1, cols],
                mask[:keys, cols],
            )
            dq = dot(k_t[rows, :keys], ds)
            if part == 0:
                ds, d_key, d_value = one(
                    mem_k, mem_v, q_head[cols], d_head[cols], lm_ref[0, head : head + 1, :], None
                )
                dq = dq + dot(mk_t[rows], ds)
                d_mem_k = d_key if d_mem_k is None else d_mem_k + d_key
                d_mem_v = d_value if d_mem_v is None else d_mem_v + d_value
            turned[rows, cols] = dq
            if head == 0 and part == 0:
                dk_acc[:HALF] = dk
                dv_acc[:HALF] = dv
            elif head == 0:
                dk_acc[:HALF] += dk[:HALF]
                dv_acc[:HALF] += dv[:HALF]
                dk_acc[HALF:] = dk[HALF:]
                dv_acc[HALF:] = dv[HALF:]
            else:
                dk_acc[:keys] += dk
                dv_acc[:keys] += dv
    scale = HD**-0.5
    d_q = (turned[...].T * scale).astype(bf16)
    d_v = dv_acc[...].astype(bf16)
    dqkv_ref[0] = d_q
    dqkv_ref[1] = (dk_acc[...] * scale).astype(bf16)
    dqkv_ref[2] = d_v
    d_mem_k = (d_mem_k * scale).astype(bf16)
    d_mem_v = d_mem_v.astype(bf16)
    dtail_ref[0] = dot(bt_ref[...], d_mem_k).astype(bf16)
    dtail_ref[1] = dot(bt_ref[...], d_mem_v).astype(bf16)
    sums_ref[0:1] = jnp.sum(d_q.astype(f32), axis=0, keepdims=True)
    sums_ref[1:2] = jnp.sum(d_v.astype(f32), axis=0, keepdims=True) + jnp.sum(
        d_mem_v.astype(f32), axis=0, keepdims=True
    )


HIDDEN = pl.CostEstimate(flops=1000, bytes_accessed=1000, transcendentals=0)


def attention_backward(
    first, pairs, lens, qkv, mem_k, mem_v, d_branch, attn_out, lse_local, lse_mem, basis_t
):
    column = lambda k: pl.BlockSpec((L, LANES), lambda i: (0, k * PAIRS + first + i))
    whole = lambda shape: pl.BlockSpec(shape, lambda i: (0,) * len(shape))
    width = pairs * LANES
    return pl.pallas_call(
        backward_kernel,
        grid=(pairs,),
        in_specs=[
            pl.BlockSpec(memory_space=pltpu.SMEM),
            column(0),
            column(1),
            column(2),
            column(0),
            column(0),
            whole((L, D)),
            pl.BlockSpec((LANES, D), lambda i: (first + i, 0)),
            pl.BlockSpec((1, 8, L), lambda i: (first + i, 0, 0)),
            pl.BlockSpec((1, 8, HALF), lambda i: (first + i, 0, 0)),
            whole((HALF, NB)),
        ],
        out_specs=[
            pl.BlockSpec((3, L, LANES), lambda i: (0, 0, i)),
            pl.BlockSpec((2, HALF, LANES), lambda i: (0, 0, i)),
            pl.BlockSpec((8, LANES), lambda i: (0, i)),
        ],
        out_shape=[
            jax.ShapeDtypeStruct((3, L, width), bf16),
            jax.ShapeDtypeStruct((2, HALF, width), bf16),
            jax.ShapeDtypeStruct((8, width), f32),
        ],
        scratch_shapes=[
            pltpu.VMEM((L, L), f32),
            pltpu.VMEM((LANES, L), f32),
            pltpu.VMEM((L, LANES), f32),
            pltpu.VMEM((L, LANES), f32),
        ],
        cost_estimate=pl.CostEstimate(
            flops=2 * pairs * 56 * HALF * HALF * 256,
            bytes_accessed=20 * L * width,
            transcendentals=2 * pairs * L * L,
        ),
        name="attention_backward",
    )(lens, qkv, qkv, qkv, mem_k, mem_v, d_branch, attn_out, lse_local, lse_mem, basis_t)


def normalized(matrix):
    centered = matrix - jnp.mean(matrix, axis=-1, keepdims=True)
    scale = lax.rsqrt(jnp.mean(centered * centered, axis=-1, keepdims=True) + 1e-05)
    return centered * scale, scale


def norm_slope(unit, scale, grown):
    inner = jnp.mean(grown * unit, axis=-1, keepdims=True)
    return (grown - jnp.mean(grown, axis=-1, keepdims=True) - unit * inner) * scale


def column_sum(matrix):
    return jnp.sum(matrix, axis=0, keepdims=True)


def middle_backward(d_own, returned, cotangent, middle, rows):
    count = len(returned[0])

    def kernel(d_ref, ct_ref, middle_ref, rows_ref, *refs):
        shares = refs[: 2 * count]
        d_middle_ref, d_branch_ref, sums_ref = refs[2 * count :]
        part = pl.program_id(0)
        total = d_ref[...].astype(f32)
        for i in range(count):
            total = total + jnp.where(part == 0, shares[i][...], shares[count + i][...]).astype(f32)
        upstream = ct_ref[...].astype(f32)
        unit, scale = normalized(middle_ref[...])
        d_middle = upstream + norm_slope(unit, scale, total * rows_ref[1:2])
        d_branch = d_middle.astype(bf16)
        d_middle_ref[...] = d_middle
        d_branch_ref[...] = d_branch
        sums = jnp.concatenate(
            [
                column_sum(d_branch.astype(f32)),
                column_sum(total * unit),
                column_sum(total),
                column_sum(upstream),
                jnp.zeros((4, D), f32),
            ],
            axis=0,
        )

        @pl.when(part == 0)
        def _():
            sums_ref[...] = sums

        @pl.when(part > 0)
        def _():
            sums_ref[...] += sums

    half = pl.BlockSpec((HALF, D), lambda i: (i, 0))
    fixed = pl.BlockSpec((HALF, D), lambda i: (0, 0))
    eight = pl.BlockSpec((8, D), lambda i: (0, 0))
    return pl.pallas_call(
        kernel,
        grid=(2,),
        in_specs=[half, half, half, eight] + [fixed] * (2 * count),
        out_specs=[half, half, eight],
        out_shape=[
            jax.ShapeDtypeStruct((L, D), f32),
            jax.ShapeDtypeStruct((L, D), bf16),
            jax.ShapeDtypeStruct((8, D), f32),
        ],
        cost_estimate=pl.CostEstimate(
            flops=20 * L * D, bytes_accessed=14 * L * D, transcendentals=0
        ),
        name="middle_backward",
    )(d_own, cotangent, middle, rows, *returned[0], *returned[1])


def qkv_backward(d_one, d_two, d_tail_one, d_tail_two, attn_in, inputs, tail_rows):
    cut = d_one.shape[2]

    def kernel(
        one_ref, two_ref, t_one_ref, t_two_ref, w_ref, x_ref, xt_ref, dn_ref, dt_ref, sums_ref, tail
    ):
        step = pl.program_id(0)
        left, right = w_ref[:, :cut], w_ref[:, cut:]
        part = dot_nt(one_ref[0], left) + dot_nt(two_ref[0], right)

        @pl.when(step == 0)
        def _():
            dn_ref[...] = part
            tail[...] = jnp.zeros_like(tail)

        @pl.when(step > 0)
        def _():
            dn_ref[...] += part
            tail[...] += dot_nt(t_one_ref[0], left) + dot_nt(t_two_ref[0], right)

        @pl.when(step == 2)
        def _():
            dt_ref[...] = tail[...].astype(bf16)
            unit, unused = normalized(x_ref[...].astype(f32))
            tail_unit, unused = normalized(xt_ref[...].astype(f32))
            sums_ref[0:1] = column_sum(dn_ref[...] * unit) + column_sum(tail[...] * tail_unit)
            sums_ref[1:2] = column_sum(dn_ref[...]) + column_sum(tail[...])

    fixed = lambda count: pl.BlockSpec((count, D), lambda i: (0, 0))
    return pl.pallas_call(
        kernel,
        grid=(3,),
        in_specs=[
            pl.BlockSpec((1, L, cut), lambda i: (i, 0, 0)),
            pl.BlockSpec((1, L, D - cut), lambda i: (i, 0, 0)),
            pl.BlockSpec((1, HALF, cut), lambda i: (jnp.maximum(i - 1, 0), 0, 0)),
            pl.BlockSpec((1, HALF, D - cut), lambda i: (jnp.maximum(i - 1, 0), 0, 0)),
            pl.BlockSpec((D, D), lambda i: (0, i)),
            fixed(L),
            fixed(HALF),
        ],
        out_specs=[fixed(L), fixed(HALF), fixed(8)],
        out_shape=[
            jax.ShapeDtypeStruct((L, D), f32),
            jax.ShapeDtypeStruct((HALF, D), bf16),
            jax.ShapeDtypeStruct((8, D), f32),
        ],
        scratch_shapes=[pltpu.VMEM((HALF, D), f32)],
        cost_estimate=pl.CostEstimate(
            flops=8 * L * D * D, bytes_accessed=20 * L * D, transcendentals=0
        ),
        name="qkv_backward",
    )(d_one, d_two, d_tail_one, d_tail_two, attn_in, inputs, tail_rows)


def input_backward(d_normed, from_next, inputs, d_middle, gain):
    def kernel(dn_ref, next_ref, x_ref, dm_ref, gain_ref, out_ref):
        unit, scale = normalized(x_ref[...].astype(f32))
        shared = jnp.where(pl.program_id(0) == 0, 0.0, next_ref[...].astype(f32))
        grown = (dn_ref[...] + shared) * gain_ref[0:1]
        out_ref[...] = (dm_ref[...] + norm_slope(unit, scale, grown)).astype(bf16)

    half = pl.BlockSpec((HALF, D), lambda i: (i, 0))
    return pl.pallas_call(
        kernel,
        grid=(2,),
        in_specs=[
            half,
            pl.BlockSpec((HALF, D), lambda i: (0, 0)),
            half,
            half,
            pl.BlockSpec((8, D), lambda i: (0, 0)),
        ],
        out_specs=half,
        out_shape=jax.ShapeDtypeStruct((L, D), bf16),
        cost_estimate=pl.CostEstimate(
            flops=20 * L * D, bytes_accessed=12 * L * D, transcendentals=0
        ),
        name="input_backward",
    )(d_normed, from_next, inputs, d_middle, gain)


def widened(first, second):
    steps = 6

    def kernel(a_ref, b_ref, a_out, b_out):
        a_out[...] = a_ref[...].astype(f32)
        b_out[...] = b_ref[...].astype(f32)

    specs = [
        pl.BlockSpec((matrix.shape[0] // steps, matrix.shape[1]), lambda i: (i, 0))
        for matrix in (first, second)
    ]
    return pl.pallas_call(
        kernel,
        grid=(steps,),
        in_specs=specs,
        out_specs=specs,
        out_shape=[jax.ShapeDtypeStruct(matrix.shape, f32) for matrix in (first, second)],
        cost_estimate=pl.CostEstimate(
            flops=0, bytes_accessed=6 * (first.size + second.size), transcendentals=0
        ),
        name="widened",
    )(first, second)


def rotated(value, axis, by):
    count = lax.axis_size(axis)
    return lax.ppermute(value, axis, [(i, (i + by) % count) for i in range(count)])


fence = lax.optimization_barrier
GRID = ("batch", "mlp")


def flipped(value, mask):
    count = lax.axis_size("batch") * lax.axis_size("mlp")
    return lax.ppermute(value, GRID, [(i, i ^ mask) for i in range(count)])


def place_in(bits):
    number = lax.axis_index(GRID)
    return sum(((number >> bit) & 1) << i for i, bit in enumerate(bits))


def peers(bits):
    return [sum(((q >> i) & 1) << bit for i, bit in enumerate(bits)) for q in range(1, 1 << len(bits))]


def grouped(bits):
    odd = len(bits) % 2
    return ([bits[:1]] if odd else []) + [bits[i : i + 2] for i in range(odd, len(bits), 2)]


class Chain:
    def __init__(self, kept, given, groups):
        self.stages = [(True, bits) for bits in groups] + [(False, bits) for bits in groups[::-1]]
        self.turn()
        self.kept, self.given = kept, [given]

    def left(self):
        return len(self.stages) + 1

    def turn(self):
        self.scatters, self.bits = self.stages.pop(0)
        self.place = place_in(self.bits)

    def prepare(self):
        self.turn()
        count = 1 << len(self.bits)
        if self.scatters:
            size = self.value.shape[0] // count
            piece = lambda i: lax.dynamic_slice_in_dim(self.value, i * size, size, 0)
            self.kept = piece(self.place)
            self.given = [piece(self.place ^ q) for q in range(1, count)]
        else:
            self.kept = self.value
            self.given = [self.value]

    def fly(self):
        masks = peers(self.bits)
        given = self.given if self.scatters else self.given * len(masks)
        self.got = [flipped(piece, mask) for piece, mask in zip(given, masks)]

    @classmethod
    def gathering(cls, value, groups):
        chain = cls.__new__(cls)
        chain.stages = [(False, bits) for bits in groups]
        chain.turn()
        chain.kept, chain.given = value, [value]
        return chain

    def land(self):
        if self.scatters and self.stages[0][0] and len(self.stages[0][1]) > 1:
            kept, got = self.kept, self.got[0]
            self.turn()
            self.kept, *self.given = split_sum(kept, got, self.place, 1 << len(self.bits))
            return True
        if self.scatters:
            total = self.kept.astype(f32)
            for piece in self.got:
                total = total + piece.astype(f32)
            self.value = total.astype(self.kept.dtype)
        else:
            pieces = [self.kept] + self.got
            order = [
                lax.select_n(self.place ^ i, *pieces)
                if len(pieces) > 2
                else jnp.where(self.place == i, *pieces)
                for i in range(len(pieces))
            ]
            self.value = jnp.concatenate(order, axis=0)
        if self.stages:
            self.prepare()
            return True
        return False


class Total:
    def __init__(self, value, bits):
        self.value, self.bits = value, list(bits)

    def fly(self):
        self.got = flipped(self.value, 1 << self.bits.pop(0))

    def land(self):
        self.value = self.value + self.got
        self.given = [self.value]

    def left(self):
        return len(self.bits)


def weight_grads(turned, d, d_tail, ready, side):
    width = d.shape[2]
    tile = width if ready is None else 256
    each = width // tile
    extra = 0 if ready is None else ready.shape[1] // tile
    half = D // 2
    fresh = turned[0].shape[0] == L

    def kernel(side_ref, n_ref, nt_ref, d_ref, dt_ref, *refs):
        step = pl.program_id(0)
        kept_ref, given_ref = refs[extra > 0 : (extra > 0) + 2]
        if fresh:
            turn_refs = refs[-2:]

            @pl.when(step == 0)
            def _():
                turn_refs[0][...] = n_ref[...].T
                turn_refs[1][...] = nt_ref[...].T

        else:
            turn_refs = (n_ref, nt_ref)

        def rows(which, ref):
            return ref[pl.ds(pl.multiple_of(which * half, half), half), :]

        for which, out_ref in ((side_ref[0], kept_ref), (1 - side_ref[0], given_ref)):

            @pl.when(step < each)
            def _():
                out_ref[...] = dot(rows(which, turn_refs[0]), d_ref[0]).astype(bf16)

            @pl.when((step >= each) & (step < 3 * each))
            def _():
                out_ref[...] = (
                    dot(rows(which, turn_refs[0]), d_ref[0])
                    + dot(rows(which, turn_refs[1]), dt_ref[0])
                ).astype(bf16)

            if extra:

                @pl.when(step >= 3 * each)
                def _():
                    out_ref[...] = rows(which, refs[0])

    column = lambda i: jnp.where(i < 3 * each, i % each, each - 1)
    fixed = lambda matrix: pl.BlockSpec(matrix.shape, lambda i: (0, 0))
    in_specs = [
        pl.BlockSpec(memory_space=pltpu.SMEM),
        fixed(turned[0]),
        fixed(turned[1]),
        pl.BlockSpec((1, L, tile), lambda i: (jnp.minimum(i // each, 2), 0, column(i))),
        pl.BlockSpec((1, HALF, tile), lambda i: (jnp.clip(i // each - 1, 0, 1), 0, column(i))),
    ]
    operands = [side, *turned, d, d_tail]
    if extra:
        in_specs.append(pl.BlockSpec((D, tile), lambda i: (0, jnp.maximum(i - 3 * each, 0))))
        operands.append(ready)
    steps = 3 * each + extra
    shapes = [jax.ShapeDtypeStruct((half, steps * tile), bf16)] * 2
    specs = [pl.BlockSpec((half, tile), lambda i: (0, i))] * 2
    if fresh:
        turns = [jax.ShapeDtypeStruct((D, L), bf16), jax.ShapeDtypeStruct((D, HALF), bf16)]
        shapes, specs = shapes + turns, specs + [fixed(turn) for turn in turns]
    kept, given, *turns = pl.pallas_call(
        kernel,
        grid=(steps,),
        in_specs=in_specs,
        out_specs=specs,
        out_shape=shapes,
        cost_estimate=HIDDEN,
        name="weight_grads",
    )(*operands)
    return kept, given, turns or turned


def split_sum(kept, got, number, count):
    size = kept.shape[0] // count

    def kernel(number_ref, kept_ref, got_ref, *outs):
        for q, out_ref in enumerate(outs):
            rows = pl.ds(pl.multiple_of((number_ref[0] ^ q) * size, size), size)
            out_ref[...] = (kept_ref[rows, :].astype(f32) + got_ref[rows, :].astype(f32)).astype(
                out_ref.dtype
            )

    whole = lambda matrix: pl.BlockSpec(matrix.shape, lambda: (0, 0))
    out = jax.ShapeDtypeStruct((size, kept.shape[1]), kept.dtype)
    return pl.pallas_call(
        kernel,
        in_specs=[pl.BlockSpec(memory_space=pltpu.SMEM), whole(kept), whole(got)],
        out_specs=[whole(out)] * count,
        out_shape=[out] * count,
        cost_estimate=HIDDEN,
        name="split_sum",
    )(number.reshape(1), kept, got)


def shards(
    inputs,
    doc_lengths,
    ln1_gain,
    ln1_bias,
    attn_in,
    qv_bias,
    attn_out,
    attn_out_bias,
    ln2_gain,
    second_norm_bias,
    mlp_in,
    mlp_in_bias,
    mlp_out,
    mlp_out_bias,
    cotangent,
):
    n_mlp = lax.axis_size("mlp")
    place = lax.axis_index("mlp")
    gain_one = ln1_gain.astype(f32)
    bias_one = ln1_bias.astype(f32)
    gain_two = ln2_gain.astype(f32)
    bias_two = second_norm_bias.astype(f32)

    tail = rotated(inputs[HALF:], "mlp", 1)
    last_len = rotated(
        jnp.broadcast_to(doc_lengths[:, NDOC - 1 :].astype(bf16), (16, LANES)), "mlp", 1
    )
    cotangents = [cotangent] + [rotated(cotangent, "mlp", by) for by in range(1, n_mlp)]

    activations = inputs.astype(f32)
    normed = layer_norm(activations, gain_one, bias_one).astype(bf16)
    first_rows = jnp.concatenate([jnp.stack([gain_one, bias_one]), jnp.zeros((6, D), f32)])
    zeros = jnp.zeros((D,), f32)
    qkv_bias = jnp.concatenate([qv_bias[0].astype(f32), zeros, qv_bias[1].astype(f32)])
    qkv = (dot(normed, attn_in) + qkv_bias).astype(bf16)
    rows = jnp.concatenate(
        [
            jnp.stack([attn_out_bias.astype(f32), gain_two, bias_two]),
            jnp.zeros((5, D), f32),
        ]
    )
    local, lse_local, mixture, middle, normed_two, sent = local_attention(
        doc_lengths, qkv, attn_out, inputs, rows
    )
    steps = range(1, n_mlp)
    arrived_hi = [rotated(sent, "mlp", by) for by in steps]

    normed_tail, tail_kv = tail_projection(tail, first_rows, attn_in)
    reads = jnp.where(place == 0, 0, doc_lengths[:, :1])
    value_bias = jnp.broadcast_to(qv_bias[1].astype(f32), (8, D))
    tail_kv, *cotangents[1:] = fence((tail_kv, *cotangents[1:]))
    mixture, mem_k, mem_v, lse_mem, middle, normed_two, basis_t, sent = memory_attention(
        reads,
        last_len,
        qkv,
        tail_kv,
        value_bias,
        local,
        attn_out,
        inputs,
        rows,
        mixture,
        middle,
        normed_two,
    )
    arrived_lo = [rotated(sent, "mlp", by) for by in steps]
    mem_k, arrived_hi = fence((mem_k, arrived_hi))

    bias_rows = jnp.broadcast_to(mlp_in_bias.astype(f32), (8, mlp_in.shape[1]))
    kept = ()
    d_mlp_in_bias = 0.0
    returned_y, returned_dx = [], []
    calls = [(by, part) for by in steps for part in (1, 0)]
    for by, part in calls:
        block = (arrived_lo, arrived_hi)[part][by - 1]
        hidden, d_pre, d_bias, y, dx = mlp_block(
            block, cotangents[by], part, mlp_in, bias_rows, mlp_out, n_mlp * L, 2 * by + part, kept
        )
        kept = (hidden, d_pre)
        d_mlp_in_bias = d_mlp_in_bias + d_bias[0]
        returned_dx.append(rotated(dx, "mlp", -by))
        returned_y.append(y)
    hidden, d_pre, d_bias, y_own, dx_own = mlp_block(
        normed_two, cotangent, 0, mlp_in, bias_rows, mlp_out, n_mlp * L, 0, kept
    )
    d_mlp_in_bias = d_mlp_in_bias + d_bias[0]
    hidden, d_pre, returned_dx = fence((hidden, d_pre, returned_dx))
    over_rows = lambda a, b: lax.dot_general(
        a, b, (((0,), (0,)), ((), ())), preferred_element_type=f32
    )
    all_rows = jnp.concatenate(
        [normed_two] + [piece for pair in zip(arrived_lo, arrived_hi) for piece in pair], axis=0
    )
    d_mlp_in = over_rows(all_rows, d_pre).astype(bf16)
    d_mlp_out = over_rows(hidden, jnp.concatenate(cotangents, axis=0)).astype(bf16)

    hidden_count = mlp_in.shape[1]
    mlp_count = n_mlp.bit_length() - 1
    batch_count = lax.axis_size("batch").bit_length() - 1
    mlp_bits = list(range(mlp_count))
    core = [[mlp_count]]
    rest = list(range(mlp_count + 1, mlp_count + batch_count))
    groups = core + [mlp_bits[:1] + rest[:1]] + [[bit] for bit in mlp_bits[1:] + rest[1:]]

    d_mlp_in, d_mlp_out = lax.psum((d_mlp_in, d_mlp_out), "batch")

    def finish():
        shares = [[dx for (by, part), dx in zip(calls, returned_dx) if part == half] for half in (0, 1)]
        d_middle, d_branch, middle_sums = middle_backward(dx_own, shares, cotangent, middle, rows)
        backward = lambda first, pairs, d: attention_backward(
            first, pairs, doc_lengths, qkv, mem_k, mem_v, d, attn_out, lse_local, lse_mem, basis_t
        )
        early = PAIRS // 3
        side = place_in(core[0]).reshape(1)
        d_one, d_tail_one, sums_one = backward(0, early, d_branch)
        d_attn_out = over_rows(mixture, d_branch).astype(bf16)
        kept, given, turned = weight_grads(
            (normed, normed_tail), d_one, d_tail_one, d_attn_out, side
        )
        chain_one = Chain(kept, given, groups)
        chain_one.fly()
        chain_one.land()
        d_branch, chain_one.given = fence((d_branch, chain_one.given))
        chain_one.fly()
        d_two, d_tail_two, sums_two = backward(early, PAIRS - early, d_branch)
        d_two, d_tail_two, chain_one.got = fence((d_two, d_tail_two, chain_one.got))
        chain_one.land()
        d_two, d_tail_two, chain_one.given = fence((d_two, d_tail_two, chain_one.given))
        chain_one.fly()
        kept, given, turned = weight_grads(turned, d_two, d_tail_two, None, side)
        chain_two = Chain(kept, given, groups)
        chain_two.fly()
        chain_two.land()
        d_one, d_two, d_tails, sums, later, chain_two.given = fence(
            (
                d_one,
                d_two,
                (d_tail_one, d_tail_two),
                (sums_one, sums_two),
                (d_mlp_in_bias, returned_y, y_own),
                chain_two.given,
            )
        )
        bias_grad, y_given, y_mine = later
        chain_two.fly()
        d_normed, d_tail_rows, input_sums = qkv_backward(
            d_one, d_two, *d_tails, attn_in, inputs, tail
        )
        chain_one.got, chain_two.got[0], d_normed, d_tail_rows, input_sums = fence(
            (chain_one.got, chain_two.got[0], d_normed, d_tail_rows, input_sums)
        )
        chain_one.land()
        chain_one.fly()
        from_next = rotated(d_tail_rows, "mlp", -1)
        placed_bias = lax.dynamic_update_slice(
            jnp.zeros((n_mlp * hidden_count,), f32), bias_grad, (place * hidden_count,)
        )
        vectors = Total(
            jnp.concatenate(
                [
                    input_sums[:2],
                    middle_sums[:4],
                    jnp.concatenate(sums, axis=1)[:2],
                    placed_bias.reshape(-1, D),
                ],
                axis=0,
            ),
            core[0] + mlp_bits + rest,
        )
        vectors.fly()

        token = chain_one.given
        flying = [chain_one, chain_two, vectors]
        held = {chain_one: 1, chain_two: 2, vectors: 1}
        turns = 0
        while flying:
            for chain in list(flying):
                chain.got, token = fence((chain.got, token))
                if chain is chain_two:
                    turns += 1
                    if turns == 1:
                        chain.got, y_given = fence((chain.got, y_given))
                        returned = [
                            rotated(y, "mlp", -by) for (by, part), y in zip(calls, y_given)
                        ]
                    if turns == 3:
                        chain.got, returned = fence((chain.got, returned))
                chain.land()
                token = chain.given
                if chain.left() > held[chain]:
                    chain.fly()
                else:
                    flying.remove(chain)

        return (
            chain_one.value,
            chain_two.value,
            vectors.value,
            (d_normed, from_next, d_middle),
            (y_mine, returned),
        )

    shapes = jax.eval_shape(finish)
    done = lax.cond(
        doc_lengths[0, 0] > 0,
        finish,
        lambda: jax.tree.map(lambda leaf: jnp.zeros(leaf.shape, leaf.dtype), shapes),
    )
    one, two, summed, (d_normed, from_next, d_middle), (y_own, returned) = done
    chain_two = Chain.gathering(two, [groups[1], core[0]])
    chain_two.fly()
    chain_one = Chain.gathering(one, core)
    chain_one.fly()
    vectors = Total(summed, (core[0] + mlp_bits + rest)[-1:])
    vectors.fly()

    gain = jnp.broadcast_to(gain_one, (8, D))
    input_grad = input_backward(d_normed, from_next, inputs, d_middle, gain)
    halves = [y_own[:HALF].astype(f32), y_own[HALF:].astype(f32)]
    for (by, part), y in zip(calls, returned):
        halves[part] = halves[part] + y.astype(f32)
    result = jnp.concatenate(halves, axis=0)
    layer_output = (middle + (result + mlp_out_bias)).astype(bf16)
    d_mlp_in, d_mlp_out = widened(d_mlp_in, d_mlp_out)
    chain_two.got, vectors.got, layer_output, input_grad, d_mlp_in, d_mlp_out = fence(
        (chain_two.got, vectors.got, layer_output, input_grad, d_mlp_in, d_mlp_out)
    )
    chain_two.land()
    chain_two.fly()
    chain_one.land()
    chain_two.land()
    vectors.land()
    summed = vectors.value

    width = PAIRS // 3 * LANES
    late = D - width
    d_attn_in = jnp.concatenate(
        [
            piece
            for i in range(3)
            for piece in (
                chain_one.value[:, i * width : (i + 1) * width],
                chain_two.value[:, i * late : (i + 1) * late],
            )
        ],
        axis=1,
    )
    return (
        layer_output,
        input_grad,
        summed[0],
        summed[1],
        d_attn_in.astype(f32),
        summed[6:8],
        chain_one.value[:, 3 * width :].astype(f32),
        summed[2],
        summed[3],
        summed[4],
        d_mlp_in,
        lax.dynamic_slice(summed[8:].reshape(-1), (place * hidden_count,), (hidden_count,)),
        d_mlp_out,
        summed[5],
    )


def solution(mesh):
    rows, whole = P(("batch", "mlp"), None), P()
    columns, hidden, depth = P(None, "mlp"), P("mlp"), P("mlp", None)
    return jax.shard_map(
        shards,
        mesh=mesh,
        in_specs=(rows, rows) + (whole,) * 8 + (columns, hidden, depth, whole, rows),
        out_specs=(rows, rows) + (whole,) * 8 + (columns, hidden, depth, whole),
        check_vma=False,
    )
```

```python
import jax
import jax.numpy as jnp
from jax import lax
from jax.experimental import pallas as pl
from jax.experimental.pallas import tpu as pltpu
from jax.sharding import PartitionSpec as P

D = 768
H = 12
HD = 64
NB = 512
L = 512
NDOC = 3
HALF = L // 2
PAIRS = H // 2
LANES = 2 * HD

LOG2E = 1.4426950408889634
SCORE_LOG2 = LOG2E * HD**-0.5
MASKED = -1e30

bf16 = jnp.bfloat16
f32 = jnp.float32


def dot(a, b):
    return jnp.dot(a, b, preferred_element_type=f32)


def dot_nt(a, b):
    return lax.dot_general(a, b, (((1,), (1,)), ((), ())), preferred_element_type=f32)


def layer_norm(matrix, gain_row, shift_row):
    center = jnp.mean(matrix, axis=-1, keepdims=True)
    centered = matrix - center
    spread = jnp.mean(centered * centered, axis=-1, keepdims=True)
    return centered * lax.rsqrt(spread + 1e-05) * gain_row + shift_row


def head_lanes(matrix, head):
    lane = lax.broadcasted_iota(jnp.int32, (1, LANES), 1)
    return jnp.where(lane // HD == head, matrix, jnp.zeros_like(matrix))


def fill_mask(lens, mask):
    key = lax.broadcasted_iota(jnp.int32, (L, L), 0)
    query = lax.broadcasted_iota(jnp.int32, (L, L), 1)
    one = lens[0, 0]
    two = one + lens[0, 1]
    start = jnp.where(query >= two, two, jnp.where(query >= one, one, 0))
    mask[...] = jnp.where((key <= query) & (key >= start), 0.0, MASKED)


def local_kernel(
    lens,
    q_ref,
    k_ref,
    v_ref,
    wo_ref,
    x_ref,
    rows_ref,
    out_ref,
    lse_ref,
    mix_ref,
    middle_ref,
    normed_ref,
    sent_ref,
    mask,
    turned,
    acc,
):
    step = pl.program_id(0)

    @pl.when(step == 0)
    def _():
        fill_mask(lens, mask)
        acc[...] = jnp.zeros_like(acc)

    q, k = q_ref[...], k_ref[...]
    v_t = v_ref[...].T
    for head in range(2):
        q_head = head_lanes(q, head)
        rows = slice(head * HD, (head + 1) * HD)
        for part in range(2):
            keys = HALF * (part + 1)
            cols = slice(part * HALF, (part + 1) * HALF)
            s = dot_nt(k[:keys], q_head[cols]) * SCORE_LOG2 + mask[:keys, cols]
            top = jnp.max(s, axis=0, keepdims=True)
            e = jnp.exp2(s - top)
            total = jnp.sum(e, axis=0, keepdims=True)
            out = dot(v_t[rows, :keys], e.astype(bf16))
            turned[rows, cols] = out / total
            lse_ref[0, head : head + 1, cols] = top + jnp.log2(total)
    out_ref[...] = turned[:, :HALF].T
    mixed = turned[:, HALF:].T.astype(bf16)
    mix_ref[...] = mixed
    acc[...] += dot(mixed, wo_ref[...])

    @pl.when(step == PAIRS - 1)
    def _():
        finish_middle(x_ref, acc, rows_ref, middle_ref, normed_ref, sent_ref)


def finish_middle(x_ref, acc, rows_ref, middle_ref, normed_ref, sent_ref):
    middle = x_ref[...].astype(f32) + (acc[...] + rows_ref[0:1])
    middle_ref[...] = middle
    normed = layer_norm(middle, rows_ref[1:2], rows_ref[2:3]).astype(bf16)
    normed_ref[...] = normed
    sent_ref[...] = normed


def local_attention(lens, qkv, attn_out, inputs, rows):
    column = lambda k: pl.BlockSpec((L, LANES), lambda i: (0, k * PAIRS + i))
    upper = pl.BlockSpec((HALF, D), lambda i: (1, 0))
    return pl.pallas_call(
        local_kernel,
        grid=(PAIRS,),
        in_specs=[
            pl.BlockSpec(memory_space=pltpu.SMEM),
            column(0),
            column(1),
            column(2),
            pl.BlockSpec((LANES, D), lambda i: (i, 0)),
            upper,
            pl.BlockSpec((8, D), lambda i: (0, 0)),
        ],
        out_specs=[
            pl.BlockSpec((HALF, LANES), lambda i: (0, i)),
            pl.BlockSpec((1, 8, L), lambda i: (i, 0, 0)),
            pl.BlockSpec((HALF, LANES), lambda i: (1, i)),
            upper,
            upper,
            pl.BlockSpec((HALF, D), lambda i: (0, 0)),
        ],
        out_shape=[
            jax.ShapeDtypeStruct((HALF, D), f32),
            jax.ShapeDtypeStruct((PAIRS, 8, L), f32),
            jax.ShapeDtypeStruct((L, D), bf16),
            jax.ShapeDtypeStruct((L, D), f32),
            jax.ShapeDtypeStruct((L, D), bf16),
            jax.ShapeDtypeStruct((HALF, D), bf16),
        ],
        scratch_shapes=[
            pltpu.VMEM((L, L), f32),
            pltpu.VMEM((LANES, L), f32),
            pltpu.VMEM((HALF, D), f32),
        ],
        cost_estimate=pl.CostEstimate(
            flops=H * 12 * HALF * HALF * 256, bytes_accessed=8 * L * D, transcendentals=H * L * L
        ),
        name="local_attention",
    )(lens, qkv, qkv, qkv, attn_out, inputs, rows)


def basis_rows(last_len, transposed):
    shape = (HALF, NB) if transposed else (NB, HALF)
    slot_dim, place_dim = (1, 0) if transposed else (0, 1)
    slot = lax.broadcasted_iota(jnp.int32, shape, slot_dim).astype(f32)
    place = lax.broadcasted_iota(jnp.int32, shape, place_dim).astype(f32)
    offsets = place - HALF + last_len + 0.5
    distances = (slot + 0.5) / NB * last_len - offsets
    weights = jnp.where(offsets > 0.0, jnp.exp(-0.5 * distances * distances), 0.0)
    return weights / jnp.sum(weights, axis=place_dim, keepdims=True)


def tail_projection(tail, rows, attn_in):
    tile = D // 2

    def kernel(x_ref, rows_ref, w_ref, normed_ref, kv_ref):
        @pl.when(pl.program_id(0) == 0)
        def _():
            normed_ref[...] = layer_norm(
                x_ref[...].astype(f32), rows_ref[3:4], rows_ref[4:5]
            ).astype(bf16)

        kv_ref[...] = dot(normed_ref[...], w_ref[...]).astype(bf16)

    fixed = lambda count: pl.BlockSpec((count, D), lambda i: (0, 0))
    return pl.pallas_call(
        kernel,
        grid=(4,),
        in_specs=[fixed(HALF), fixed(8), pl.BlockSpec((D, tile), lambda i: (0, 2 + i))],
        out_specs=[fixed(HALF), pl.BlockSpec((HALF, tile), lambda i: (0, i))],
        out_shape=[
            jax.ShapeDtypeStruct((HALF, D), bf16),
            jax.ShapeDtypeStruct((HALF, 2 * D), bf16),
        ],
        cost_estimate=pl.CostEstimate(
            flops=4 * HALF * D * D, bytes_accessed=4 * D * D, transcendentals=0
        ),
        name="tail_projection",
    )(tail, rows, attn_in)


def memory_kernel(
    reads,
    last_ref,
    q_ref,
    kt_ref,
    vt_ref,
    vb_ref,
    local_ref,
    wo_ref,
    x_ref,
    rows_ref,
    mix_whole,
    middle_whole,
    normed_whole,
    mix_ref,
    mk_ref,
    mv_ref,
    lse_ref,
    middle_ref,
    normed_ref,
    basis_t_ref,
    sent_ref,
    basis,
    turned,
    acc,
):
    step = pl.program_id(0)

    @pl.when(step == 0)
    def _():
        last_len = last_ref[0:1, 0:1]
        basis[...] = basis_rows(last_len, False).astype(bf16)
        basis_t_ref[...] = basis_rows(last_len, True).astype(bf16)
        acc[...] = jnp.zeros_like(acc)

    mem_k = dot(basis[...], kt_ref[...]).astype(bf16)
    mem_v = (dot(basis[...], vt_ref[...]) + vb_ref[5:6]).astype(bf16)
    mk_ref[...] = mem_k
    mv_ref[...] = mem_v
    v_t = mem_v.T
    query = lax.broadcasted_iota(jnp.int32, (1, HALF), 1)
    reading = query < reads[0, 0]
    q = q_ref[...]
    for head in range(2):
        rows = slice(head * HD, (head + 1) * HD)
        s = dot_nt(mem_k, head_lanes(q, head)) * SCORE_LOG2
        top = jnp.max(s, axis=0, keepdims=True)
        e = jnp.exp2(s - top)
        total = jnp.sum(e, axis=0, keepdims=True)
        out = dot(v_t[rows], e.astype(bf16))
        turned[rows, :] = jnp.where(reading, out / total, 0.0)
        lse_ref[0, head : head + 1, :] = jnp.where(reading, top + jnp.log2(total), -MASKED)
    mixed = (local_ref[...] + turned[...].T).astype(bf16)
    mix_ref[...] = mixed
    acc[...] += dot(mixed, wo_ref[...])

    @pl.when(step == PAIRS - 1)
    def _():
        finish_middle(x_ref, acc, rows_ref, middle_ref, normed_ref, sent_ref)


def memory_attention(
    reads, last_rows, qkv, tail_kv, value_bias, local, attn_out, inputs, rows, mixture, middle, normed
):
    whole = lambda shape: pl.BlockSpec(shape, lambda i: (0,) * len(shape))
    untouched = pl.BlockSpec(memory_space=pl.ANY)
    return pl.pallas_call(
        memory_kernel,
        grid=(PAIRS,),
        in_specs=[
            pl.BlockSpec(memory_space=pltpu.SMEM),
            whole((16, LANES)),
            pl.BlockSpec((HALF, LANES), lambda i: (0, i)),
            pl.BlockSpec((HALF, LANES), lambda i: (0, i)),
            pl.BlockSpec((HALF, LANES), lambda i: (0, PAIRS + i)),
            pl.BlockSpec((8, LANES), lambda i: (0, i)),
            pl.BlockSpec((HALF, LANES), lambda i: (0, i)),
            pl.BlockSpec((LANES, D), lambda i: (i, 0)),
            whole((HALF, D)),
            whole((8, D)),
            untouched,
            untouched,
            untouched,
        ],
        out_specs=[
            pl.BlockSpec((HALF, LANES), lambda i: (0, i)),
            pl.BlockSpec((NB, LANES), lambda i: (0, i)),
            pl.BlockSpec((NB, LANES), lambda i: (0, i)),
            pl.BlockSpec((1, 8, HALF), lambda i: (i, 0, 0)),
            whole((HALF, D)),
            whole((HALF, D)),
            whole((HALF, NB)),
            whole((HALF, D)),
        ],
        out_shape=[
            jax.ShapeDtypeStruct((L, D), bf16),
            jax.ShapeDtypeStruct((NB, D), bf16),
            jax.ShapeDtypeStruct((NB, D), bf16),
            jax.ShapeDtypeStruct((PAIRS, 8, HALF), f32),
            jax.ShapeDtypeStruct((L, D), f32),
            jax.ShapeDtypeStruct((L, D), bf16),
            jax.ShapeDtypeStruct((HALF, NB), bf16),
            jax.ShapeDtypeStruct((HALF, D), bf16),
        ],
        scratch_shapes=[
            pltpu.VMEM((NB, HALF), bf16),
            pltpu.VMEM((LANES, HALF), f32),
            pltpu.VMEM((HALF, D), f32),
        ],
        input_output_aliases={10: 0, 11: 4, 12: 5},
        cost_estimate=pl.CostEstimate(
            flops=H * 16 * HALF * HALF * 256, bytes_accessed=16 * L * D, transcendentals=H * L * HALF
        ),
        name="memory_attention",
    )(
        reads,
        last_rows,
        qkv,
        tail_kv,
        tail_kv,
        value_bias,
        local,
        attn_out,
        inputs,
        rows,
        mixture,
        middle,
        normed,
    )


def mlp_kernel(x_ref, ct_ref, wi_ref, bi_ref, wo_ref, *refs):
    hid_ref, dpre_ref, bias_ref, y_ref, dx_ref, y_acc, dx_acc = refs[-7:]
    step = pl.program_id(0)
    pre = dot(x_ref[...], wi_ref[...]) + bi_ref[0:1]
    squared = pre * pre
    tanh = jnp.tanh(pre * (0.7978845608028654 + 0.7978845608028654 * 0.044715 * squared))
    half = 0.5 * pre
    hidden = (half + half * tanh).astype(bf16)
    slope = (
        0.5
        + 0.5 * tanh
        + half
        * (1.0 - tanh * tanh)
        * (0.7978845608028654 + 3 * 0.7978845608028654 * 0.044715 * squared)
    )
    d_pre = (slope * dot_nt(ct_ref[...], wo_ref[...])).astype(bf16)
    hid_ref[...] = hidden
    dpre_ref[...] = d_pre
    bias_ref[...] = jnp.broadcast_to(
        jnp.sum(d_pre.astype(f32), axis=0, keepdims=True), bias_ref.shape
    )
    y = dot(hidden, wo_ref[...])
    dx = dot_nt(d_pre, wi_ref[...])

    @pl.when(step == 0)
    def _():
        y_acc[...] = y
        dx_acc[...] = dx

    @pl.when(step > 0)
    def _():
        y_acc[...] += y
        dx_acc[...] += dx

    @pl.when(step == pl.num_programs(0) - 1)
    def _():
        y_ref[...] = y_acc[...].astype(bf16)
        dx_ref[...] = dx_acc[...].astype(bf16)


def mlp_block(rows, cotangent, part, mlp_in, bias_rows, mlp_out, total, place, kept):
    count, hidden = rows.shape[0], mlp_in.shape[1]
    tile = next(t for t in (768 if count <= HALF else 512, 384, 256, 128) if hidden % t == 0)
    fixed = pl.BlockSpec((count, D), lambda i: (0, 0))
    across = pl.BlockSpec((count, tile), lambda i: (place, i))
    return pl.pallas_call(
        mlp_kernel,
        grid=(hidden // tile,),
        in_specs=[
            fixed,
            pl.BlockSpec((count, D), lambda i: (part, 0)),
            pl.BlockSpec((D, tile), lambda i: (0, i)),
            pl.BlockSpec((8, tile), lambda i: (0, i)),
            pl.BlockSpec((tile, D), lambda i: (i, 0)),
        ]
        + [pl.BlockSpec(memory_space=pl.ANY)] * len(kept),
        out_specs=[across, across, pl.BlockSpec((8, tile), lambda i: (0, i)), fixed, fixed],
        out_shape=[
            jax.ShapeDtypeStruct((total, hidden), bf16),
            jax.ShapeDtypeStruct((total, hidden), bf16),
            jax.ShapeDtypeStruct((8, hidden), f32),
            jax.ShapeDtypeStruct((count, D), bf16),
            jax.ShapeDtypeStruct((count, D), bf16),
        ],
        scratch_shapes=[pltpu.VMEM((count, D), f32), pltpu.VMEM((count, D), f32)],
        input_output_aliases={5 + i: i for i in range(len(kept))},
        cost_estimate=pl.CostEstimate(
            flops=8 * count * D * hidden,
            bytes_accessed=4 * D * hidden + 4 * count * hidden + 8 * count * D,
            transcendentals=count * hidden,
        ),
        name="mlp_block",
    )(rows, cotangent, mlp_in, bias_rows, mlp_out, *kept)


def backward_kernel(
    lens,
    q_ref,
    k_ref,
    v_ref,
    mk_ref,
    mv_ref,
    db_ref,
    wo_ref,
    ll_ref,
    lm_ref,
    bt_ref,
    dqkv_ref,
    dtail_ref,
    sums_ref,
    mask,
    turned,
    dk_acc,
    dv_acc,
):
    @pl.when(pl.program_id(0) == 0)
    def _():
        fill_mask(lens, mask)

    q, k, v = q_ref[...], k_ref[...], v_ref[...]
    mem_k, mem_v = mk_ref[...], mv_ref[...]
    d_mix = dot_nt(db_ref[...], wo_ref[...]).astype(bf16)
    k_t, mk_t = k.T, mem_k.T
    d_mem_k = d_mem_v = None

    def one(keys, values, q_part, d_part, lse, extra):
        s = dot_nt(keys, q_part) * SCORE_LOG2
        if extra is not None:
            s = s + extra
        weights = jnp.exp2(s - lse)
        d_weights = dot_nt(values, d_part)
        inner = jnp.sum(weights * d_weights, axis=0, keepdims=True)
        d_scores = (weights * (d_weights - inner)).astype(bf16)
        return d_scores, dot(d_scores, q_part), dot(weights.astype(bf16), d_part)

    for head in range(2):
        rows = slice(head * HD, (head + 1) * HD)
        q_head, d_head = head_lanes(q, head), head_lanes(d_mix, head)
        for part in range(2):
            keys = HALF * (part + 1)
            cols = slice(part * HALF, (part + 1) * HALF)
            ds, dk, dv = one(
                k[:keys],
                v[:keys],
                q_head[cols],
                d_head[cols],
                ll_ref[0, head : head + 1, cols],
                mask[:keys, cols],
            )
            dq = dot(k_t[rows, :keys], ds)
            if part == 0:
                ds, d_key, d_value = one(
                    mem_k, mem_v, q_head[cols], d_head[cols], lm_ref[0, head : head + 1, :], None
                )
                dq = dq + dot(mk_t[rows], ds)
                d_mem_k = d_key if d_mem_k is None else d_mem_k + d_key
                d_mem_v = d_value if d_mem_v is None else d_mem_v + d_value
            turned[rows, cols] = dq
            if head == 0 and part == 0:
                dk_acc[:HALF] = dk
                dv_acc[:HALF] = dv
            elif head == 0:
                dk_acc[:HALF] += dk[:HALF]
                dv_acc[:HALF] += dv[:HALF]
                dk_acc[HALF:] = dk[HALF:]
                dv_acc[HALF:] = dv[HALF:]
            else:
                dk_acc[:keys] += dk
                dv_acc[:keys] += dv
    scale = HD**-0.5
    d_q = (turned[...].T * scale).astype(bf16)
    d_v = dv_acc[...].astype(bf16)
    dqkv_ref[0] = d_q
    dqkv_ref[1] = (dk_acc[...] * scale).astype(bf16)
    dqkv_ref[2] = d_v
    d_mem_k = (d_mem_k * scale).astype(bf16)
    d_mem_v = d_mem_v.astype(bf16)
    dtail_ref[0] = dot(bt_ref[...], d_mem_k).astype(bf16)
    dtail_ref[1] = dot(bt_ref[...], d_mem_v).astype(bf16)
    sums_ref[0:1] = jnp.sum(d_q.astype(f32), axis=0, keepdims=True)
    sums_ref[1:2] = jnp.sum(d_v.astype(f32), axis=0, keepdims=True) + jnp.sum(
        d_mem_v.astype(f32), axis=0, keepdims=True
    )


HIDDEN = pl.CostEstimate(flops=1000, bytes_accessed=1000, transcendentals=0)


def attention_backward(
    first, pairs, lens, qkv, mem_k, mem_v, d_branch, attn_out, lse_local, lse_mem, basis_t
):
    column = lambda k: pl.BlockSpec((L, LANES), lambda i: (0, k * PAIRS + first + i))
    whole = lambda shape: pl.BlockSpec(shape, lambda i: (0,) * len(shape))
    width = pairs * LANES
    return pl.pallas_call(
        backward_kernel,
        grid=(pairs,),
        in_specs=[
            pl.BlockSpec(memory_space=pltpu.SMEM),
            column(0),
            column(1),
            column(2),
            column(0),
            column(0),
            whole((L, D)),
            pl.BlockSpec((LANES, D), lambda i: (first + i, 0)),
            pl.BlockSpec((1, 8, L), lambda i: (first + i, 0, 0)),
            pl.BlockSpec((1, 8, HALF), lambda i: (first + i, 0, 0)),
            whole((HALF, NB)),
        ],
        out_specs=[
            pl.BlockSpec((3, L, LANES), lambda i: (0, 0, i)),
            pl.BlockSpec((2, HALF, LANES), lambda i: (0, 0, i)),
            pl.BlockSpec((8, LANES), lambda i: (0, i)),
        ],
        out_shape=[
            jax.ShapeDtypeStruct((3, L, width), bf16),
            jax.ShapeDtypeStruct((2, HALF, width), bf16),
            jax.ShapeDtypeStruct((8, width), f32),
        ],
        scratch_shapes=[
            pltpu.VMEM((L, L), f32),
            pltpu.VMEM((LANES, L), f32),
            pltpu.VMEM((L, LANES), f32),
            pltpu.VMEM((L, LANES), f32),
        ],
        cost_estimate=pl.CostEstimate(
            flops=2 * pairs * 56 * HALF * HALF * 256,
            bytes_accessed=20 * L * width,
            transcendentals=2 * pairs * L * L,
        ),
        name="attention_backward",
    )(lens, qkv, qkv, qkv, mem_k, mem_v, d_branch, attn_out, lse_local, lse_mem, basis_t)


def normalized(matrix):
    centered = matrix - jnp.mean(matrix, axis=-1, keepdims=True)
    scale = lax.rsqrt(jnp.mean(centered * centered, axis=-1, keepdims=True) + 1e-05)
    return centered * scale, scale


def norm_slope(unit, scale, grown):
    inner = jnp.mean(grown * unit, axis=-1, keepdims=True)
    return (grown - jnp.mean(grown, axis=-1, keepdims=True) - unit * inner) * scale


def column_sum(matrix):
    return jnp.sum(matrix, axis=0, keepdims=True)


def middle_backward(d_own, returned, cotangent, middle, rows):
    count = len(returned[0])

    def kernel(d_ref, ct_ref, middle_ref, rows_ref, *refs):
        shares = refs[: 2 * count]
        d_middle_ref, d_branch_ref, sums_ref = refs[2 * count :]
        part = pl.program_id(0)
        total = d_ref[...].astype(f32)
        for i in range(count):
            total = total + jnp.where(part == 0, shares[i][...], shares[count + i][...]).astype(f32)
        upstream = ct_ref[...].astype(f32)
        unit, scale = normalized(middle_ref[...])
        d_middle = upstream + norm_slope(unit, scale, total * rows_ref[1:2])
        d_branch = d_middle.astype(bf16)
        d_middle_ref[...] = d_middle
        d_branch_ref[...] = d_branch
        sums = jnp.concatenate(
            [
                column_sum(d_branch.astype(f32)),
                column_sum(total * unit),
                column_sum(total),
                column_sum(upstream),
                jnp.zeros((4, D), f32),
            ],
            axis=0,
        )

        @pl.when(part == 0)
        def _():
            sums_ref[...] = sums

        @pl.when(part > 0)
        def _():
            sums_ref[...] += sums

    half = pl.BlockSpec((HALF, D), lambda i: (i, 0))
    fixed = pl.BlockSpec((HALF, D), lambda i: (0, 0))
    eight = pl.BlockSpec((8, D), lambda i: (0, 0))
    return pl.pallas_call(
        kernel,
        grid=(2,),
        in_specs=[half, half, half, eight] + [fixed] * (2 * count),
        out_specs=[half, half, eight],
        out_shape=[
            jax.ShapeDtypeStruct((L, D), f32),
            jax.ShapeDtypeStruct((L, D), bf16),
            jax.ShapeDtypeStruct((8, D), f32),
        ],
        cost_estimate=pl.CostEstimate(
            flops=20 * L * D, bytes_accessed=14 * L * D, transcendentals=0
        ),
        name="middle_backward",
    )(d_own, cotangent, middle, rows, *returned[0], *returned[1])


def qkv_backward(d_one, d_two, d_tail_one, d_tail_two, attn_in, inputs, tail_rows):
    cut = d_one.shape[2]

    def kernel(
        one_ref, two_ref, t_one_ref, t_two_ref, w_ref, x_ref, xt_ref, dn_ref, dt_ref, sums_ref, tail
    ):
        step = pl.program_id(0)
        left, right = w_ref[:, :cut], w_ref[:, cut:]
        part = dot_nt(one_ref[0], left) + dot_nt(two_ref[0], right)

        @pl.when(step == 0)
        def _():
            dn_ref[...] = part
            tail[...] = jnp.zeros_like(tail)

        @pl.when(step > 0)
        def _():
            dn_ref[...] += part
            tail[...] += dot_nt(t_one_ref[0], left) + dot_nt(t_two_ref[0], right)

        @pl.when(step == 2)
        def _():
            dt_ref[...] = tail[...].astype(bf16)
            unit, unused = normalized(x_ref[...].astype(f32))
            tail_unit, unused = normalized(xt_ref[...].astype(f32))
            sums_ref[0:1] = column_sum(dn_ref[...] * unit) + column_sum(tail[...] * tail_unit)
            sums_ref[1:2] = column_sum(dn_ref[...]) + column_sum(tail[...])

    fixed = lambda count: pl.BlockSpec((count, D), lambda i: (0, 0))
    return pl.pallas_call(
        kernel,
        grid=(3,),
        in_specs=[
            pl.BlockSpec((1, L, cut), lambda i: (i, 0, 0)),
            pl.BlockSpec((1, L, D - cut), lambda i: (i, 0, 0)),
            pl.BlockSpec((1, HALF, cut), lambda i: (jnp.maximum(i - 1, 0), 0, 0)),
            pl.BlockSpec((1, HALF, D - cut), lambda i: (jnp.maximum(i - 1, 0), 0, 0)),
            pl.BlockSpec((D, D), lambda i: (0, i)),
            fixed(L),
            fixed(HALF),
        ],
        out_specs=[fixed(L), fixed(HALF), fixed(8)],
        out_shape=[
            jax.ShapeDtypeStruct((L, D), f32),
            jax.ShapeDtypeStruct((HALF, D), bf16),
            jax.ShapeDtypeStruct((8, D), f32),
        ],
        scratch_shapes=[pltpu.VMEM((HALF, D), f32)],
        cost_estimate=pl.CostEstimate(
            flops=8 * L * D * D, bytes_accessed=20 * L * D, transcendentals=0
        ),
        name="qkv_backward",
    )(d_one, d_two, d_tail_one, d_tail_two, attn_in, inputs, tail_rows)


def input_backward(d_normed, from_next, inputs, d_middle, rows):
    def kernel(dn_ref, next_ref, x_ref, dm_ref, rows_ref, out_ref):
        unit, scale = normalized(x_ref[...].astype(f32))
        shared = jnp.where(pl.program_id(0) == 0, 0.0, next_ref[...].astype(f32))
        grown = (dn_ref[...] + shared) * rows_ref[3:4]
        out_ref[...] = (dm_ref[...] + norm_slope(unit, scale, grown)).astype(bf16)

    half = pl.BlockSpec((HALF, D), lambda i: (i, 0))
    return pl.pallas_call(
        kernel,
        grid=(2,),
        in_specs=[
            half,
            pl.BlockSpec((HALF, D), lambda i: (0, 0)),
            half,
            half,
            pl.BlockSpec((8, D), lambda i: (0, 0)),
        ],
        out_specs=half,
        out_shape=jax.ShapeDtypeStruct((L, D), bf16),
        cost_estimate=pl.CostEstimate(
            flops=20 * L * D, bytes_accessed=12 * L * D, transcendentals=0
        ),
        name="input_backward",
    )(d_normed, from_next, inputs, d_middle, rows)


def widened(first, second):
    steps = 6

    def kernel(a_ref, b_ref, a_out, b_out):
        a_out[...] = a_ref[...].astype(f32)
        b_out[...] = b_ref[...].astype(f32)

    specs = [
        pl.BlockSpec((matrix.shape[0] // steps, matrix.shape[1]), lambda i: (i, 0))
        for matrix in (first, second)
    ]
    return pl.pallas_call(
        kernel,
        grid=(steps,),
        in_specs=specs,
        out_specs=specs,
        out_shape=[jax.ShapeDtypeStruct(matrix.shape, f32) for matrix in (first, second)],
        cost_estimate=pl.CostEstimate(
            flops=0, bytes_accessed=6 * (first.size + second.size), transcendentals=0
        ),
        name="widened",
    )(first, second)


def rotated(value, axis, by):
    count = lax.axis_size(axis)
    return lax.ppermute(value, axis, [(i, (i + by) % count) for i in range(count)])


fence = lax.optimization_barrier
GRID = ("batch", "mlp")


def flipped(value, mask):
    count = lax.axis_size("batch") * lax.axis_size("mlp")
    return lax.ppermute(value, GRID, [(i, i ^ mask) for i in range(count)])


def place_in(bits):
    number = lax.axis_index(GRID)
    return sum(((number >> bit) & 1) << i for i, bit in enumerate(bits))


def peers(bits):
    return [sum(((q >> i) & 1) << bit for i, bit in enumerate(bits)) for q in range(1, 1 << len(bits))]


def grouped(bits):
    odd = len(bits) % 2
    return ([bits[:1]] if odd else []) + [bits[i : i + 2] for i in range(odd, len(bits), 2)]


class Chain:
    def __init__(self, kept, given, groups):
        self.stages = [(True, bits) for bits in groups] + [(False, bits) for bits in groups[::-1]]
        self.turn()
        self.kept, self.given = kept, [given]

    def left(self):
        return len(self.stages) + 1

    def turn(self):
        self.scatters, self.bits = self.stages.pop(0)
        self.place = place_in(self.bits)

    def prepare(self):
        self.turn()
        count = 1 << len(self.bits)
        if self.scatters:
            size = self.value.shape[0] // count
            piece = lambda i: lax.dynamic_slice_in_dim(self.value, i * size, size, 0)
            self.kept = piece(self.place)
            self.given = [piece(self.place ^ q) for q in range(1, count)]
        else:
            self.kept = self.value
            self.given = [self.value]

    def fly(self):
        masks = peers(self.bits)
        given = self.given if self.scatters else self.given * len(masks)
        self.got = [flipped(piece, mask) for piece, mask in zip(given, masks)]

    @classmethod
    def gathering(cls, value, groups):
        chain = cls.__new__(cls)
        chain.stages = [(False, bits) for bits in groups]
        chain.turn()
        chain.kept, chain.given = value, [value]
        return chain

    def land(self):
        if self.scatters and self.stages[0][0] and len(self.stages[0][1]) > 1:
            kept, got = self.kept, self.got[0]
            self.turn()
            self.kept, *self.given = split_sum(kept, got, self.place, 1 << len(self.bits))
            return True
        if self.scatters:
            total = self.kept.astype(f32)
            for piece in self.got:
                total = total + piece.astype(f32)
            self.value = total.astype(self.kept.dtype)
        else:
            pieces = [self.kept] + self.got
            order = [
                lax.select_n(self.place ^ i, *pieces)
                if len(pieces) > 2
                else jnp.where(self.place == i, *pieces)
                for i in range(len(pieces))
            ]
            self.value = jnp.concatenate(order, axis=0)
        if self.stages:
            self.prepare()
            return True
        return False


class Total:
    def __init__(self, value, bits):
        self.value, self.bits = value, list(bits)

    def fly(self):
        self.got = flipped(self.value, 1 << self.bits.pop(0))

    def land(self):
        self.value = self.value + self.got
        self.given = [self.value]

    def left(self):
        return len(self.bits)


def weight_grads(turned, d, d_tail, ready, side):
    width = d.shape[2]
    tile = width if ready is None else 256
    each = width // tile
    extra = 0 if ready is None else ready.shape[1] // tile
    half = D // 2
    fresh = turned[0].shape[0] == L

    def kernel(side_ref, n_ref, nt_ref, d_ref, dt_ref, *refs):
        step = pl.program_id(0)
        kept_ref, given_ref = refs[extra > 0 : (extra > 0) + 2]
        if fresh:
            turn_refs = refs[-2:]

            @pl.when(step == 0)
            def _():
                turn_refs[0][...] = n_ref[...].T
                turn_refs[1][...] = nt_ref[...].T

        else:
            turn_refs = (n_ref, nt_ref)

        def rows(which, ref):
            return ref[pl.ds(pl.multiple_of(which * half, half), half), :]

        for which, out_ref in ((side_ref[0], kept_ref), (1 - side_ref[0], given_ref)):

            @pl.when(step < each)
            def _():
                out_ref[...] = dot(rows(which, turn_refs[0]), d_ref[0]).astype(bf16)

            @pl.when((step >= each) & (step < 3 * each))
            def _():
                out_ref[...] = (
                    dot(rows(which, turn_refs[0]), d_ref[0])
                    + dot(rows(which, turn_refs[1]), dt_ref[0])
                ).astype(bf16)

            if extra:

                @pl.when(step >= 3 * each)
                def _():
                    out_ref[...] = rows(which, refs[0])

    column = lambda i: jnp.where(i < 3 * each, i % each, each - 1)
    fixed = lambda matrix: pl.BlockSpec(matrix.shape, lambda i: (0, 0))
    in_specs = [
        pl.BlockSpec(memory_space=pltpu.SMEM),
        fixed(turned[0]),
        fixed(turned[1]),
        pl.BlockSpec((1, L, tile), lambda i: (jnp.minimum(i // each, 2), 0, column(i))),
        pl.BlockSpec((1, HALF, tile), lambda i: (jnp.clip(i // each - 1, 0, 1), 0, column(i))),
    ]
    operands = [side, *turned, d, d_tail]
    if extra:
        in_specs.append(pl.BlockSpec((D, tile), lambda i: (0, jnp.maximum(i - 3 * each, 0))))
        operands.append(ready)
    steps = 3 * each + extra
    shapes = [jax.ShapeDtypeStruct((half, steps * tile), bf16)] * 2
    specs = [pl.BlockSpec((half, tile), lambda i: (0, i))] * 2
    if fresh:
        turns = [jax.ShapeDtypeStruct((D, L), bf16), jax.ShapeDtypeStruct((D, HALF), bf16)]
        shapes, specs = shapes + turns, specs + [fixed(turn) for turn in turns]
    kept, given, *turns = pl.pallas_call(
        kernel,
        grid=(steps,),
        in_specs=in_specs,
        out_specs=specs,
        out_shape=shapes,
        cost_estimate=pl.CostEstimate(
            flops=8 * L * D * width, bytes_accessed=8 * D * width, transcendentals=0
        ),
        name="weight_grads",
    )(*operands)
    return kept, given, turns or turned


def split_sum(kept, got, number, count):
    size = kept.shape[0] // count

    def kernel(number_ref, kept_ref, got_ref, *outs):
        for q, out_ref in enumerate(outs):
            rows = pl.ds(pl.multiple_of((number_ref[0] ^ q) * size, size), size)
            out_ref[...] = (kept_ref[rows, :].astype(f32) + got_ref[rows, :].astype(f32)).astype(
                out_ref.dtype
            )

    whole = lambda matrix: pl.BlockSpec(matrix.shape, lambda: (0, 0))
    out = jax.ShapeDtypeStruct((size, kept.shape[1]), kept.dtype)
    return pl.pallas_call(
        kernel,
        in_specs=[pl.BlockSpec(memory_space=pltpu.SMEM), whole(kept), whole(got)],
        out_specs=[whole(out)] * count,
        out_shape=[out] * count,
        cost_estimate=HIDDEN,
        name="split_sum",
    )(number.reshape(1), kept, got)


def shards(
    inputs,
    doc_lengths,
    ln1_gain,
    ln1_bias,
    attn_in,
    qv_bias,
    attn_out,
    attn_out_bias,
    ln2_gain,
    second_norm_bias,
    mlp_in,
    mlp_in_bias,
    mlp_out,
    mlp_out_bias,
    cotangent,
):
    n_mlp = lax.axis_size("mlp")
    place = lax.axis_index("mlp")
    gain_one = ln1_gain.astype(f32)
    bias_one = ln1_bias.astype(f32)
    gain_two = ln2_gain.astype(f32)
    bias_two = second_norm_bias.astype(f32)

    tail = rotated(inputs[HALF:], "mlp", 1)
    cotangents = [cotangent] + [rotated(cotangent, "mlp", by) for by in range(1, n_mlp)]

    activations = inputs.astype(f32)
    normed = layer_norm(activations, gain_one, bias_one).astype(bf16)
    zeros = jnp.zeros((D,), f32)
    qkv_bias = jnp.concatenate([qv_bias[0].astype(f32), zeros, qv_bias[1].astype(f32)])
    qkv = (dot(normed, attn_in) + qkv_bias).astype(bf16)
    rows = jnp.concatenate(
        [
            jnp.stack(
                [
                    attn_out_bias.astype(f32),
                    gain_two,
                    bias_two,
                    gain_one,
                    bias_one,
                    qv_bias[1].astype(f32),
                ]
            ),
            jnp.zeros((2, D), f32),
        ]
    )
    local, lse_local, mixture, middle, normed_two, sent = local_attention(
        doc_lengths, qkv, attn_out, inputs, rows
    )
    steps = range(1, n_mlp)
    arrived_hi = [rotated(sent, "mlp", by) for by in steps]

    own_len, local = fence((doc_lengths[:, NDOC - 1 :], local))
    last_len = rotated(jnp.broadcast_to(own_len.astype(bf16), (16, LANES)), "mlp", 1)
    normed_tail, tail_kv = tail_projection(tail, rows, attn_in)
    reads = jnp.where(place == 0, 0, doc_lengths[:, :1])
    tail_kv, *cotangents[1:] = fence((tail_kv, *cotangents[1:]))
    mixture, mem_k, mem_v, lse_mem, middle, normed_two, basis_t, sent = memory_attention(
        reads,
        last_len,
        qkv,
        tail_kv,
        rows,
        local,
        attn_out,
        inputs,
        rows,
        mixture,
        middle,
        normed_two,
    )
    arrived_lo = [rotated(sent, "mlp", by) for by in steps]
    mem_k, arrived_hi = fence((mem_k, arrived_hi))

    bias_rows = jnp.broadcast_to(mlp_in_bias.astype(f32), (8, mlp_in.shape[1]))
    kept = ()
    d_mlp_in_bias = 0.0
    returned_y, returned_dx = [], []
    calls = [(by, part) for by in steps for part in (1, 0)]
    for by, part in calls:
        block = (arrived_lo, arrived_hi)[part][by - 1]
        hidden, d_pre, d_bias, y, dx = mlp_block(
            block, cotangents[by], part, mlp_in, bias_rows, mlp_out, n_mlp * L, 2 * by + part, kept
        )
        kept = (hidden, d_pre)
        d_mlp_in_bias = d_mlp_in_bias + d_bias[0]
        returned_dx.append(rotated(dx, "mlp", -by))
        returned_y.append(y)
    hidden, d_pre, d_bias, y_own, dx_own = mlp_block(
        normed_two, cotangent, 0, mlp_in, bias_rows, mlp_out, n_mlp * L, 0, kept
    )
    d_mlp_in_bias = d_mlp_in_bias + d_bias[0]
    hidden, d_pre, returned_dx = fence((hidden, d_pre, returned_dx))
    over_rows = lambda a, b: lax.dot_general(
        a, b, (((0,), (0,)), ((), ())), preferred_element_type=f32
    )
    all_rows = jnp.concatenate(
        [normed_two] + [piece for pair in zip(arrived_lo, arrived_hi) for piece in pair], axis=0
    )
    d_mlp_in = over_rows(all_rows, d_pre).astype(bf16)
    d_mlp_out = over_rows(hidden, jnp.concatenate(cotangents, axis=0)).astype(bf16)

    hidden_count = mlp_in.shape[1]
    mlp_count = n_mlp.bit_length() - 1
    batch_count = lax.axis_size("batch").bit_length() - 1
    mlp_bits = list(range(mlp_count))
    core = [[mlp_count]]
    rest = list(range(mlp_count + 1, mlp_count + batch_count))
    groups = core + [mlp_bits[:1] + rest[:1]] + [[bit] for bit in mlp_bits[1:] + rest[1:]]

    d_mlp_in, d_mlp_out = lax.psum((d_mlp_in, d_mlp_out), "batch")

    def finish():
        shares = [[dx for (by, part), dx in zip(calls, returned_dx) if part == half] for half in (0, 1)]
        d_middle, d_branch, middle_sums = middle_backward(dx_own, shares, cotangent, middle, rows)
        backward = lambda first, pairs, d: attention_backward(
            first, pairs, doc_lengths, qkv, mem_k, mem_v, d, attn_out, lse_local, lse_mem, basis_t
        )
        early = PAIRS // 3
        side = place_in(core[0]).reshape(1)
        d_one, d_tail_one, sums_one = backward(0, early, d_branch)
        d_attn_out = over_rows(mixture, d_branch).astype(bf16)
        kept, given, turned = weight_grads(
            (normed, normed_tail), d_one, d_tail_one, d_attn_out, side
        )
        chain_one = Chain(kept, given, groups)
        chain_one.fly()
        chain_one.land()
        d_branch, chain_one.given = fence((d_branch, chain_one.given))
        chain_one.fly()
        d_two, d_tail_two, sums_two = backward(early, PAIRS - early, d_branch)
        d_two, d_tail_two, chain_one.got = fence((d_two, d_tail_two, chain_one.got))
        chain_one.land()
        d_two, d_tail_two, chain_one.given = fence((d_two, d_tail_two, chain_one.given))
        chain_one.fly()
        kept, given, turned = weight_grads(turned, d_two, d_tail_two, None, side)
        chain_two = Chain(kept, given, groups)
        chain_two.fly()
        chain_two.land()
        d_one, d_two, d_tails, sums, later, chain_two.given = fence(
            (
                d_one,
                d_two,
                (d_tail_one, d_tail_two),
                (sums_one, sums_two),
                (d_mlp_in_bias, returned_y, y_own),
                chain_two.given,
            )
        )
        bias_grad, y_given, y_mine = later
        chain_two.fly()
        chain_one.got, unused = fence((chain_one.got, chain_two.given))
        chain_one.land()
        d_one, chain_one.given = fence((d_one, chain_one.given))
        chain_one.fly()
        d_normed, d_tail_rows, input_sums = qkv_backward(
            d_one, d_two, *d_tails, attn_in, inputs, tail
        )
        chain_one.got, chain_two.got, d_normed, d_tail_rows, input_sums = fence(
            (chain_one.got, chain_two.got, d_normed, d_tail_rows, input_sums)
        )
        chain_one.land()
        chain_one.fly()
        chain_two.land()
        chain_two.fly()
        y_given, unused = fence((y_given, chain_two.given))
        shares = [
            jnp.concatenate([y for (by, part), y in zip(calls, y_given) if by == step][::-1], axis=0)
            for step in steps
        ]
        returned = [rotated(y, "mlp", -step) for step, y in zip(steps, shares)]
        from_next = rotated(d_tail_rows, "mlp", -1)
        placed_bias = lax.dynamic_update_slice(
            jnp.zeros((n_mlp * hidden_count,), f32), bias_grad, (place * hidden_count,)
        )
        vectors = Total(
            jnp.concatenate(
                [
                    input_sums[:2],
                    middle_sums[:4],
                    jnp.concatenate(sums, axis=1)[:2],
                    placed_bias.reshape(-1, D),
                ],
                axis=0,
            ),
            core[0] + mlp_bits + rest,
        )
        vectors.fly()

        chains = {"one": chain_one, "two": chain_two, "all": vectors}
        held = {"one": 1, "two": 2, "all": 1}
        order = ["two", "one", "all"] * 2 + ["two", "all"] * 2 + ["one"]
        token = chain_two.given
        input_grad = layer_output = None
        turns = 0
        while any(chains[name].left() > held[name] or name in order for name in chains):
            for name in order:
                chain = chains[name]
                chain.got, token = fence((chain.got, token))
                turns += 1
                if turns == 7:
                    chain.got, returned = fence((chain.got, returned))
                if turns == 9:
                    input_grad = input_backward(d_normed, from_next, inputs, d_middle, rows)
                    chain.got, input_grad = fence((chain.got, input_grad))
                if turns == 11:
                    result = y_mine.astype(f32)
                    for y in returned:
                        result = result + y.astype(f32)
                    layer_output = (middle + (result + mlp_out_bias)).astype(bf16)
                    chain.got, layer_output = fence((chain.got, layer_output))
                chain.land()
                token = chain.given
                if chain.left() > held[name]:
                    chain.fly()
            order = [name for name in chains if chains[name].left() > held[name]]

        return chain_one.value, chain_two.value, vectors.value, input_grad, layer_output

    shapes = jax.eval_shape(finish)
    done = lax.cond(
        doc_lengths[0, 0] > 0,
        finish,
        lambda: jax.tree.map(lambda leaf: jnp.zeros(leaf.shape, leaf.dtype), shapes),
    )
    one, two, summed, input_grad, layer_output = done
    chain_two = Chain.gathering(two, [groups[1], core[0]])
    chain_two.fly()
    chain_one = Chain.gathering(one, core)
    chain_one.fly()
    vectors = Total(summed, (core[0] + mlp_bits + rest)[-1:])
    vectors.fly()
    vectors.land()
    bias_grad = lax.dynamic_slice(
        vectors.value[8:].reshape(-1), (place * hidden_count,), (hidden_count,)
    )
    summed = [vectors.value[i] for i in range(6)] + [vectors.value[6:8], bias_grad]
    d_mlp_in, d_mlp_out = widened(d_mlp_in, d_mlp_out)
    chain_two.got, summed, d_mlp_in, d_mlp_out = fence(
        (chain_two.got, summed, d_mlp_in, d_mlp_out)
    )
    chain_two.land()
    chain_two.fly()
    chain_one.land()
    chain_two.land()

    width = PAIRS // 3 * LANES
    late = D - width
    d_attn_in = jnp.concatenate(
        [
            piece
            for i in range(3)
            for piece in (
                chain_one.value[:, i * width : (i + 1) * width],
                chain_two.value[:, i * late : (i + 1) * late],
            )
        ],
        axis=1,
    )
    return (
        layer_output,
        input_grad,
        summed[0],
        summed[1],
        d_attn_in.astype(f32),
        summed[6],
        chain_one.value[:, 3 * width :].astype(f32),
        summed[2],
        summed[3],
        summed[4],
        d_mlp_in,
        summed[7],
        d_mlp_out,
        summed[5],
    )


def solution(mesh):
    rows, whole = P(("batch", "mlp"), None), P()
    columns, hidden, depth = P(None, "mlp"), P("mlp"), P("mlp", None)
    return jax.shard_map(
        shards,
        mesh=mesh,
        in_specs=(rows, rows) + (whole,) * 8 + (columns, hidden, depth, whole, rows),
        out_specs=(rows, rows) + (whole,) * 8 + (columns, hidden, depth, whole),
        check_vma=False,
    )
```

```python
import jax
import jax.numpy as jnp
from jax import lax
from jax.experimental import pallas as pl
from jax.experimental.pallas import tpu as pltpu
from jax.sharding import PartitionSpec as P

D = 768
H = 12
HD = 64
NB = 512
L = 512
NDOC = 3
HALF = L // 2
PAIRS = H // 2
LANES = 2 * HD

LOG2E = 1.4426950408889634
SCORE_LOG2 = LOG2E * HD**-0.5
MASKED = -1e30

bf16 = jnp.bfloat16
f32 = jnp.float32


def dot(a, b):
    return jnp.dot(a, b, preferred_element_type=f32)


def dot_nt(a, b):
    return lax.dot_general(a, b, (((1,), (1,)), ((), ())), preferred_element_type=f32)


def layer_norm(matrix, gain_row, shift_row):
    center = jnp.mean(matrix, axis=-1, keepdims=True)
    centered = matrix - center
    spread = jnp.mean(centered * centered, axis=-1, keepdims=True)
    return centered * lax.rsqrt(spread + 1e-05) * gain_row + shift_row


def head_lanes(matrix, head):
    lane = lax.broadcasted_iota(jnp.int32, (1, LANES), 1)
    return jnp.where(lane // HD == head, matrix, jnp.zeros_like(matrix))


def fill_mask(lens, mask):
    key = lax.broadcasted_iota(jnp.int32, (L, L), 0)
    query = lax.broadcasted_iota(jnp.int32, (L, L), 1)
    one = lens[0, 0]
    two = one + lens[0, 1]
    start = jnp.where(query >= two, two, jnp.where(query >= one, one, 0))
    mask[...] = jnp.where((key <= query) & (key >= start), 0.0, MASKED)


def local_kernel(
    lens,
    q_ref,
    k_ref,
    v_ref,
    wo_ref,
    x_ref,
    rows_ref,
    out_ref,
    lse_ref,
    mix_ref,
    middle_ref,
    normed_ref,
    sent_ref,
    mask,
    turned,
    acc,
):
    step = pl.program_id(0)

    @pl.when(step == 0)
    def _():
        fill_mask(lens, mask)
        acc[...] = jnp.zeros_like(acc)

    q, k = q_ref[...], k_ref[...]
    v_t = v_ref[...].T
    for head in range(2):
        q_head = head_lanes(q, head)
        rows = slice(head * HD, (head + 1) * HD)
        for part in range(2):
            keys = HALF * (part + 1)
            cols = slice(part * HALF, (part + 1) * HALF)
            s = dot_nt(k[:keys], q_head[cols]) * SCORE_LOG2 + mask[:keys, cols]
            top = jnp.max(s, axis=0, keepdims=True)
            e = jnp.exp2(s - top)
            total = jnp.sum(e, axis=0, keepdims=True)
            out = dot(v_t[rows, :keys], e.astype(bf16))
            turned[rows, cols] = out / total
            lse_ref[0, head : head + 1, cols] = top + jnp.log2(total)
    out_ref[...] = turned[:, :HALF].T
    mixed = turned[:, HALF:].T.astype(bf16)
    mix_ref[...] = mixed
    acc[...] += dot(mixed, wo_ref[...])

    @pl.when(step == PAIRS - 1)
    def _():
        finish_middle(x_ref, acc, rows_ref, middle_ref, normed_ref, sent_ref)


def finish_middle(x_ref, acc, rows_ref, middle_ref, normed_ref, sent_ref):
    middle = x_ref[...].astype(f32) + (acc[...] + rows_ref[0:1])
    middle_ref[...] = middle
    normed = layer_norm(middle, rows_ref[1:2], rows_ref[2:3]).astype(bf16)
    normed_ref[...] = normed
    sent_ref[...] = normed


def local_attention(lens, qkv, attn_out, inputs, rows):
    column = lambda k: pl.BlockSpec((L, LANES), lambda i: (0, k * PAIRS + i))
    upper = pl.BlockSpec((HALF, D), lambda i: (1, 0))
    return pl.pallas_call(
        local_kernel,
        grid=(PAIRS,),
        in_specs=[
            pl.BlockSpec(memory_space=pltpu.SMEM),
            column(0),
            column(1),
            column(2),
            pl.BlockSpec((LANES, D), lambda i: (i, 0)),
            upper,
            pl.BlockSpec((8, D), lambda i: (0, 0)),
        ],
        out_specs=[
            pl.BlockSpec((HALF, LANES), lambda i: (0, i)),
            pl.BlockSpec((1, 8, L), lambda i: (i, 0, 0)),
            pl.BlockSpec((HALF, LANES), lambda i: (1, i)),
            upper,
            upper,
            pl.BlockSpec((HALF, D), lambda i: (0, 0)),
        ],
        out_shape=[
            jax.ShapeDtypeStruct((HALF, D), f32),
            jax.ShapeDtypeStruct((PAIRS, 8, L), f32),
            jax.ShapeDtypeStruct((L, D), bf16),
            jax.ShapeDtypeStruct((L, D), f32),
            jax.ShapeDtypeStruct((L, D), bf16),
            jax.ShapeDtypeStruct((HALF, D), bf16),
        ],
        scratch_shapes=[
            pltpu.VMEM((L, L), f32),
            pltpu.VMEM((LANES, L), f32),
            pltpu.VMEM((HALF, D), f32),
        ],
        cost_estimate=pl.CostEstimate(
            flops=H * 12 * HALF * HALF * 256, bytes_accessed=8 * L * D, transcendentals=H * L * L
        ),
        name="local_attention",
    )(lens, qkv, qkv, qkv, attn_out, inputs, rows)


def basis_rows(last_len, transposed):
    shape = (HALF, NB) if transposed else (NB, HALF)
    slot_dim, place_dim = (1, 0) if transposed else (0, 1)
    slot = lax.broadcasted_iota(jnp.int32, shape, slot_dim).astype(f32)
    place = lax.broadcasted_iota(jnp.int32, shape, place_dim).astype(f32)
    offsets = place - HALF + last_len + 0.5
    distances = (slot + 0.5) / NB * last_len - offsets
    weights = jnp.where(offsets > 0.0, jnp.exp(-0.5 * distances * distances), 0.0)
    return weights / jnp.sum(weights, axis=place_dim, keepdims=True)


def tail_projection(tail, rows, attn_in):
    tile = D // 2

    def kernel(x_ref, rows_ref, w_ref, normed_ref, kv_ref):
        @pl.when(pl.program_id(0) == 0)
        def _():
            normed_ref[...] = layer_norm(
                x_ref[...].astype(f32), rows_ref[3:4], rows_ref[4:5]
            ).astype(bf16)

        kv_ref[...] = dot(normed_ref[...], w_ref[...]).astype(bf16)

    fixed = lambda count: pl.BlockSpec((count, D), lambda i: (0, 0))
    return pl.pallas_call(
        kernel,
        grid=(4,),
        in_specs=[fixed(HALF), fixed(8), pl.BlockSpec((D, tile), lambda i: (0, 2 + i))],
        out_specs=[fixed(HALF), pl.BlockSpec((HALF, tile), lambda i: (0, i))],
        out_shape=[
            jax.ShapeDtypeStruct((HALF, D), bf16),
            jax.ShapeDtypeStruct((HALF, 2 * D), bf16),
        ],
        cost_estimate=pl.CostEstimate(
            flops=4 * HALF * D * D, bytes_accessed=4 * D * D, transcendentals=0
        ),
        name="tail_projection",
    )(tail, rows, attn_in)


def memory_kernel(
    reads,
    tail_lengths,
    q_ref,
    kt_ref,
    vt_ref,
    vb_ref,
    local_ref,
    wo_ref,
    x_ref,
    rows_ref,
    mix_whole,
    middle_whole,
    normed_whole,
    mix_ref,
    mk_ref,
    mv_ref,
    lse_ref,
    middle_ref,
    normed_ref,
    basis_t_ref,
    sent_ref,
    basis,
    turned,
    acc,
):
    step = pl.program_id(0)

    @pl.when(step == 0)
    def _():
        last_len = tail_lengths[0, NDOC - 1].astype(f32)
        basis[...] = basis_rows(last_len, False).astype(bf16)
        basis_t_ref[...] = basis_rows(last_len, True).astype(bf16)
        acc[...] = jnp.zeros_like(acc)

    mem_k = dot(basis[...], kt_ref[...]).astype(bf16)
    mem_v = (dot(basis[...], vt_ref[...]) + vb_ref[5:6]).astype(bf16)
    mk_ref[...] = mem_k
    mv_ref[...] = mem_v
    v_t = mem_v.T
    query = lax.broadcasted_iota(jnp.int32, (1, HALF), 1)
    reading = query < reads[0, 0]
    q = q_ref[...]
    for head in range(2):
        rows = slice(head * HD, (head + 1) * HD)
        s = dot_nt(mem_k, head_lanes(q, head)) * SCORE_LOG2
        top = jnp.max(s, axis=0, keepdims=True)
        e = jnp.exp2(s - top)
        total = jnp.sum(e, axis=0, keepdims=True)
        out = dot(v_t[rows], e.astype(bf16))
        turned[rows, :] = jnp.where(reading, out / total, 0.0)
        lse_ref[0, head : head + 1, :] = jnp.where(reading, top + jnp.log2(total), -MASKED)
    mixed = (local_ref[...] + turned[...].T).astype(bf16)
    mix_ref[...] = mixed
    acc[...] += dot(mixed, wo_ref[...])

    @pl.when(step == PAIRS - 1)
    def _():
        finish_middle(x_ref, acc, rows_ref, middle_ref, normed_ref, sent_ref)


def memory_attention(
    reads, tail_lengths, qkv, tail_kv, value_bias, local, attn_out, inputs, rows, mixture, middle, normed
):
    whole = lambda shape: pl.BlockSpec(shape, lambda i: (0,) * len(shape))
    untouched = pl.BlockSpec(memory_space=pl.ANY)
    return pl.pallas_call(
        memory_kernel,
        grid=(PAIRS,),
        in_specs=[
            pl.BlockSpec(memory_space=pltpu.SMEM),
            pl.BlockSpec(memory_space=pltpu.SMEM),
            pl.BlockSpec((HALF, LANES), lambda i: (0, i)),
            pl.BlockSpec((HALF, LANES), lambda i: (0, i)),
            pl.BlockSpec((HALF, LANES), lambda i: (0, PAIRS + i)),
            pl.BlockSpec((8, LANES), lambda i: (0, i)),
            pl.BlockSpec((HALF, LANES), lambda i: (0, i)),
            pl.BlockSpec((LANES, D), lambda i: (i, 0)),
            whole((HALF, D)),
            whole((8, D)),
            untouched,
            untouched,
            untouched,
        ],
        out_specs=[
            pl.BlockSpec((HALF, LANES), lambda i: (0, i)),
            pl.BlockSpec((NB, LANES), lambda i: (0, i)),
            pl.BlockSpec((NB, LANES), lambda i: (0, i)),
            pl.BlockSpec((1, 8, HALF), lambda i: (i, 0, 0)),
            whole((HALF, D)),
            whole((HALF, D)),
            whole((HALF, NB)),
            whole((HALF, D)),
        ],
        out_shape=[
            jax.ShapeDtypeStruct((L, D), bf16),
            jax.ShapeDtypeStruct((NB, D), bf16),
            jax.ShapeDtypeStruct((NB, D), bf16),
            jax.ShapeDtypeStruct((PAIRS, 8, HALF), f32),
            jax.ShapeDtypeStruct((L, D), f32),
            jax.ShapeDtypeStruct((L, D), bf16),
            jax.ShapeDtypeStruct((HALF, NB), bf16),
            jax.ShapeDtypeStruct((HALF, D), bf16),
        ],
        scratch_shapes=[
            pltpu.VMEM((NB, HALF), bf16),
            pltpu.VMEM((LANES, HALF), f32),
            pltpu.VMEM((HALF, D), f32),
        ],
        input_output_aliases={10: 0, 11: 4, 12: 5},
        cost_estimate=pl.CostEstimate(
            flops=H * 16 * HALF * HALF * 256, bytes_accessed=16 * L * D, transcendentals=H * L * HALF
        ),
        name="memory_attention",
    )(
        reads,
        tail_lengths,
        qkv,
        tail_kv,
        tail_kv,
        value_bias,
        local,
        attn_out,
        inputs,
        rows,
        mixture,
        middle,
        normed,
    )


def mlp_kernel(x_ref, ct_ref, wi_ref, bi_ref, wo_ref, *refs):
    hid_ref, dpre_ref, bias_ref, y_ref, dx_ref, y_acc, dx_acc = refs[-7:]
    step = pl.program_id(0)
    pre = dot(x_ref[...], wi_ref[...]) + bi_ref[0:1]
    squared = pre * pre
    tanh = jnp.tanh(pre * (0.7978845608028654 + 0.7978845608028654 * 0.044715 * squared))
    half = 0.5 * pre
    hidden = (half + half * tanh).astype(bf16)
    slope = (
        0.5
        + 0.5 * tanh
        + half
        * (1.0 - tanh * tanh)
        * (0.7978845608028654 + 3 * 0.7978845608028654 * 0.044715 * squared)
    )
    d_pre = (slope * dot_nt(ct_ref[...], wo_ref[...])).astype(bf16)
    hid_ref[...] = hidden
    dpre_ref[...] = d_pre
    bias_ref[...] = jnp.broadcast_to(
        jnp.sum(d_pre.astype(f32), axis=0, keepdims=True), bias_ref.shape
    )
    y = dot(hidden, wo_ref[...])
    dx = dot_nt(d_pre, wi_ref[...])

    @pl.when(step == 0)
    def _():
        y_acc[...] = y
        dx_acc[...] = dx

    @pl.when(step > 0)
    def _():
        y_acc[...] += y
        dx_acc[...] += dx

    @pl.when(step == pl.num_programs(0) - 1)
    def _():
        y_ref[...] = y_acc[...].astype(bf16)
        dx_ref[...] = dx_acc[...].astype(bf16)


def mlp_block(rows, cotangent, part, mlp_in, bias_rows, mlp_out, total, place, kept):
    count, hidden = rows.shape[0], mlp_in.shape[1]
    tile = next(t for t in (768 if count <= HALF else 512, 384, 256, 128) if hidden % t == 0)
    fixed = pl.BlockSpec((count, D), lambda i: (0, 0))
    across = pl.BlockSpec((count, tile), lambda i: (place, i))
    return pl.pallas_call(
        mlp_kernel,
        grid=(hidden // tile,),
        in_specs=[
            fixed,
            pl.BlockSpec((count, D), lambda i: (part, 0)),
            pl.BlockSpec((D, tile), lambda i: (0, i)),
            pl.BlockSpec((8, tile), lambda i: (0, i)),
            pl.BlockSpec((tile, D), lambda i: (i, 0)),
        ]
        + [pl.BlockSpec(memory_space=pl.ANY)] * len(kept),
        out_specs=[across, across, pl.BlockSpec((8, tile), lambda i: (0, i)), fixed, fixed],
        out_shape=[
            jax.ShapeDtypeStruct((total, hidden), bf16),
            jax.ShapeDtypeStruct((total, hidden), bf16),
            jax.ShapeDtypeStruct((8, hidden), f32),
            jax.ShapeDtypeStruct((count, D), bf16),
            jax.ShapeDtypeStruct((count, D), bf16),
        ],
        scratch_shapes=[pltpu.VMEM((count, D), f32), pltpu.VMEM((count, D), f32)],
        input_output_aliases={5 + i: i for i in range(len(kept))},
        cost_estimate=pl.CostEstimate(
            flops=8 * count * D * hidden,
            bytes_accessed=4 * D * hidden + 4 * count * hidden + 8 * count * D,
            transcendentals=count * hidden,
        ),
        name="mlp_block",
    )(rows, cotangent, mlp_in, bias_rows, mlp_out, *kept)


def backward_kernel(
    lens,
    q_ref,
    k_ref,
    v_ref,
    mk_ref,
    mv_ref,
    db_ref,
    wo_ref,
    ll_ref,
    lm_ref,
    bt_ref,
    dqkv_ref,
    dtail_ref,
    sums_ref,
    mask,
    turned,
    dk_acc,
    dv_acc,
):
    @pl.when(pl.program_id(0) == 0)
    def _():
        fill_mask(lens, mask)

    q, k, v = q_ref[...], k_ref[...], v_ref[...]
    mem_k, mem_v = mk_ref[...], mv_ref[...]
    d_mix = dot_nt(db_ref[...], wo_ref[...]).astype(bf16)
    k_t, mk_t = k.T, mem_k.T
    d_mem_k = d_mem_v = None

    def one(keys, values, q_part, d_part, lse, extra):
        s = dot_nt(keys, q_part) * SCORE_LOG2
        if extra is not None:
            s = s + extra
        weights = jnp.exp2(s - lse)
        d_weights = dot_nt(values, d_part)
        inner = jnp.sum(weights * d_weights, axis=0, keepdims=True)
        d_scores = (weights * (d_weights - inner)).astype(bf16)
        return d_scores, dot(d_scores, q_part), dot(weights.astype(bf16), d_part)

    for head in range(2):
        rows = slice(head * HD, (head + 1) * HD)
        q_head, d_head = head_lanes(q, head), head_lanes(d_mix, head)
        for part in range(2):
            keys = HALF * (part + 1)
            cols = slice(part * HALF, (part + 1) * HALF)
            ds, dk, dv = one(
                k[:keys],
                v[:keys],
                q_head[cols],
                d_head[cols],
                ll_ref[0, head : head + 1, cols],
                mask[:keys, cols],
            )
            dq = dot(k_t[rows, :keys], ds)
            if part == 0:
                ds, d_key, d_value = one(
                    mem_k, mem_v, q_head[cols], d_head[cols], lm_ref[0, head : head + 1, :], None
                )
                dq = dq + dot(mk_t[rows], ds)
                d_mem_k = d_key if d_mem_k is None else d_mem_k + d_key
                d_mem_v = d_value if d_mem_v is None else d_mem_v + d_value
            turned[rows, cols] = dq
            if head == 0 and part == 0:
                dk_acc[:HALF] = dk
                dv_acc[:HALF] = dv
            elif head == 0:
                dk_acc[:HALF] += dk[:HALF]
                dv_acc[:HALF] += dv[:HALF]
                dk_acc[HALF:] = dk[HALF:]
                dv_acc[HALF:] = dv[HALF:]
            else:
                dk_acc[:keys] += dk
                dv_acc[:keys] += dv
    scale = HD**-0.5
    d_q = (turned[...].T * scale).astype(bf16)
    d_v = dv_acc[...].astype(bf16)
    dqkv_ref[0] = d_q
    dqkv_ref[1] = (dk_acc[...] * scale).astype(bf16)
    dqkv_ref[2] = d_v
    d_mem_k = (d_mem_k * scale).astype(bf16)
    d_mem_v = d_mem_v.astype(bf16)
    dtail_ref[0] = dot(bt_ref[...], d_mem_k).astype(bf16)
    dtail_ref[1] = dot(bt_ref[...], d_mem_v).astype(bf16)
    sums_ref[0:1] = jnp.sum(d_q.astype(f32), axis=0, keepdims=True)
    sums_ref[1:2] = jnp.sum(d_v.astype(f32), axis=0, keepdims=True) + jnp.sum(
        d_mem_v.astype(f32), axis=0, keepdims=True
    )


HIDDEN = pl.CostEstimate(flops=1000, bytes_accessed=1000, transcendentals=0)


def attention_backward(
    first, pairs, lens, qkv, mem_k, mem_v, d_branch, attn_out, lse_local, lse_mem, basis_t
):
    column = lambda k: pl.BlockSpec((L, LANES), lambda i: (0, k * PAIRS + first + i))
    whole = lambda shape: pl.BlockSpec(shape, lambda i: (0,) * len(shape))
    width = pairs * LANES
    return pl.pallas_call(
        backward_kernel,
        grid=(pairs,),
        in_specs=[
            pl.BlockSpec(memory_space=pltpu.SMEM),
            column(0),
            column(1),
            column(2),
            column(0),
            column(0),
            whole((L, D)),
            pl.BlockSpec((LANES, D), lambda i: (first + i, 0)),
            pl.BlockSpec((1, 8, L), lambda i: (first + i, 0, 0)),
            pl.BlockSpec((1, 8, HALF), lambda i: (first + i, 0, 0)),
            whole((HALF, NB)),
        ],
        out_specs=[
            pl.BlockSpec((3, L, LANES), lambda i: (0, 0, i)),
            pl.BlockSpec((2, HALF, LANES), lambda i: (0, 0, i)),
            pl.BlockSpec((8, LANES), lambda i: (0, i)),
        ],
        out_shape=[
            jax.ShapeDtypeStruct((3, L, width), bf16),
            jax.ShapeDtypeStruct((2, HALF, width), bf16),
            jax.ShapeDtypeStruct((8, width), f32),
        ],
        scratch_shapes=[
            pltpu.VMEM((L, L), f32),
            pltpu.VMEM((LANES, L), f32),
            pltpu.VMEM((L, LANES), f32),
            pltpu.VMEM((L, LANES), f32),
        ],
        cost_estimate=pl.CostEstimate(
            flops=2 * pairs * 56 * HALF * HALF * 256,
            bytes_accessed=20 * L * width,
            transcendentals=2 * pairs * L * L,
        ),
        name="attention_backward",
    )(lens, qkv, qkv, qkv, mem_k, mem_v, d_branch, attn_out, lse_local, lse_mem, basis_t)


def normalized(matrix):
    centered = matrix - jnp.mean(matrix, axis=-1, keepdims=True)
    scale = lax.rsqrt(jnp.mean(centered * centered, axis=-1, keepdims=True) + 1e-05)
    return centered * scale, scale


def norm_slope(unit, scale, grown):
    inner = jnp.mean(grown * unit, axis=-1, keepdims=True)
    return (grown - jnp.mean(grown, axis=-1, keepdims=True) - unit * inner) * scale


def column_sum(matrix):
    return jnp.sum(matrix, axis=0, keepdims=True)


def middle_backward(d_own, returned, cotangent, middle, rows):
    count = len(returned[0])

    def kernel(d_ref, ct_ref, middle_ref, rows_ref, *refs):
        shares = refs[: 2 * count]
        d_middle_ref, d_branch_ref, sums_ref = refs[2 * count :]
        part = pl.program_id(0)
        total = d_ref[...].astype(f32)
        for i in range(count):
            total = total + jnp.where(part == 0, shares[i][...], shares[count + i][...]).astype(f32)
        upstream = ct_ref[...].astype(f32)
        unit, scale = normalized(middle_ref[...])
        d_middle = upstream + norm_slope(unit, scale, total * rows_ref[1:2])
        d_branch = d_middle.astype(bf16)
        d_middle_ref[...] = d_middle
        d_branch_ref[...] = d_branch
        sums = jnp.concatenate(
            [
                column_sum(d_branch.astype(f32)),
                column_sum(total * unit),
                column_sum(total),
                column_sum(upstream),
                jnp.zeros((4, D), f32),
            ],
            axis=0,
        )

        @pl.when(part == 0)
        def _():
            sums_ref[...] = sums

        @pl.when(part > 0)
        def _():
            sums_ref[...] += sums

    half = pl.BlockSpec((HALF, D), lambda i: (i, 0))
    fixed = pl.BlockSpec((HALF, D), lambda i: (0, 0))
    eight = pl.BlockSpec((8, D), lambda i: (0, 0))
    return pl.pallas_call(
        kernel,
        grid=(2,),
        in_specs=[half, half, half, eight] + [fixed] * (2 * count),
        out_specs=[half, half, eight],
        out_shape=[
            jax.ShapeDtypeStruct((L, D), f32),
            jax.ShapeDtypeStruct((L, D), bf16),
            jax.ShapeDtypeStruct((8, D), f32),
        ],
        cost_estimate=pl.CostEstimate(
            flops=20 * L * D, bytes_accessed=14 * L * D, transcendentals=0
        ),
        name="middle_backward",
    )(d_own, cotangent, middle, rows, *returned[0], *returned[1])


def qkv_backward(d_one, d_two, d_tail_one, d_tail_two, attn_in, inputs, tail_rows):
    cut = d_one.shape[2]

    def kernel(
        one_ref, two_ref, t_one_ref, t_two_ref, w_ref, x_ref, xt_ref, dn_ref, dt_ref, sums_ref, tail
    ):
        step = pl.program_id(0)
        left, right = w_ref[:, :cut], w_ref[:, cut:]
        part = dot_nt(one_ref[0], left) + dot_nt(two_ref[0], right)

        @pl.when(step == 0)
        def _():
            dn_ref[...] = part
            tail[...] = jnp.zeros_like(tail)

        @pl.when(step > 0)
        def _():
            dn_ref[...] += part
            tail[...] += dot_nt(t_one_ref[0], left) + dot_nt(t_two_ref[0], right)

        @pl.when(step == 2)
        def _():
            dt_ref[...] = tail[...].astype(bf16)
            unit, unused = normalized(x_ref[...].astype(f32))
            tail_unit, unused = normalized(xt_ref[...].astype(f32))
            sums_ref[0:1] = column_sum(dn_ref[...] * unit) + column_sum(tail[...] * tail_unit)
            sums_ref[1:2] = column_sum(dn_ref[...]) + column_sum(tail[...])

    fixed = lambda count: pl.BlockSpec((count, D), lambda i: (0, 0))
    return pl.pallas_call(
        kernel,
        grid=(3,),
        in_specs=[
            pl.BlockSpec((1, L, cut), lambda i: (i, 0, 0)),
            pl.BlockSpec((1, L, D - cut), lambda i: (i, 0, 0)),
            pl.BlockSpec((1, HALF, cut), lambda i: (jnp.maximum(i - 1, 0), 0, 0)),
            pl.BlockSpec((1, HALF, D - cut), lambda i: (jnp.maximum(i - 1, 0), 0, 0)),
            pl.BlockSpec((D, D), lambda i: (0, i)),
            fixed(L),
            fixed(HALF),
        ],
        out_specs=[fixed(L), fixed(HALF), fixed(8)],
        out_shape=[
            jax.ShapeDtypeStruct((L, D), f32),
            jax.ShapeDtypeStruct((HALF, D), bf16),
            jax.ShapeDtypeStruct((8, D), f32),
        ],
        scratch_shapes=[pltpu.VMEM((HALF, D), f32)],
        cost_estimate=pl.CostEstimate(
            flops=8 * L * D * D, bytes_accessed=20 * L * D, transcendentals=0
        ),
        name="qkv_backward",
    )(d_one, d_two, d_tail_one, d_tail_two, attn_in, inputs, tail_rows)


def input_backward(d_normed, from_next, inputs, d_middle, rows):
    def kernel(dn_ref, next_ref, x_ref, dm_ref, rows_ref, out_ref):
        unit, scale = normalized(x_ref[...].astype(f32))
        shared = jnp.where(pl.program_id(0) == 0, 0.0, next_ref[...].astype(f32))
        grown = (dn_ref[...] + shared) * rows_ref[3:4]
        out_ref[...] = (dm_ref[...] + norm_slope(unit, scale, grown)).astype(bf16)

    half = pl.BlockSpec((HALF, D), lambda i: (i, 0))
    return pl.pallas_call(
        kernel,
        grid=(2,),
        in_specs=[
            half,
            pl.BlockSpec((HALF, D), lambda i: (0, 0)),
            half,
            half,
            pl.BlockSpec((8, D), lambda i: (0, 0)),
        ],
        out_specs=half,
        out_shape=jax.ShapeDtypeStruct((L, D), bf16),
        cost_estimate=pl.CostEstimate(
            flops=20 * L * D, bytes_accessed=12 * L * D, transcendentals=0
        ),
        name="input_backward",
    )(d_normed, from_next, inputs, d_middle, rows)


def widened(first, second):
    steps = 6

    def kernel(a_ref, b_ref, a_out, b_out):
        a_out[...] = a_ref[...].astype(f32)
        b_out[...] = b_ref[...].astype(f32)

    specs = [
        pl.BlockSpec((matrix.shape[0] // steps, matrix.shape[1]), lambda i: (i, 0))
        for matrix in (first, second)
    ]
    return pl.pallas_call(
        kernel,
        grid=(steps,),
        in_specs=specs,
        out_specs=specs,
        out_shape=[jax.ShapeDtypeStruct(matrix.shape, f32) for matrix in (first, second)],
        cost_estimate=pl.CostEstimate(
            flops=0, bytes_accessed=6 * (first.size + second.size), transcendentals=0
        ),
        name="widened",
    )(first, second)


def rotated(value, axis, by):
    count = lax.axis_size(axis)
    return lax.ppermute(value, axis, [(i, (i + by) % count) for i in range(count)])


fence = lax.optimization_barrier
GRID = ("batch", "mlp")


def flipped(value, mask):
    count = lax.axis_size("batch") * lax.axis_size("mlp")
    return lax.ppermute(value, GRID, [(i, i ^ mask) for i in range(count)])


def place_in(bits):
    number = lax.axis_index(GRID)
    return sum(((number >> bit) & 1) << i for i, bit in enumerate(bits))


def peers(bits):
    return [sum(((q >> i) & 1) << bit for i, bit in enumerate(bits)) for q in range(1, 1 << len(bits))]


def grouped(bits):
    odd = len(bits) % 2
    return ([bits[:1]] if odd else []) + [bits[i : i + 2] for i in range(odd, len(bits), 2)]


class Chain:
    def __init__(self, kept, given, groups):
        self.stages = [(True, bits) for bits in groups] + [(False, bits) for bits in groups[::-1]]
        self.turn()
        self.kept, self.given = kept, [given]

    def left(self):
        return len(self.stages) + 1

    def turn(self):
        self.scatters, self.bits = self.stages.pop(0)
        self.place = place_in(self.bits)

    def prepare(self):
        self.turn()
        count = 1 << len(self.bits)
        if self.scatters:
            size = self.value.shape[0] // count
            piece = lambda i: lax.dynamic_slice_in_dim(self.value, i * size, size, 0)
            self.kept = piece(self.place)
            self.given = [piece(self.place ^ q) for q in range(1, count)]
        else:
            self.kept = self.value
            self.given = [self.value]

    def fly(self):
        masks = peers(self.bits)
        given = self.given if self.scatters else self.given * len(masks)
        self.got = [flipped(piece, mask) for piece, mask in zip(given, masks)]

    @classmethod
    def gathering(cls, value, groups):
        chain = cls.__new__(cls)
        chain.stages = [(False, bits) for bits in groups]
        chain.turn()
        chain.kept, chain.given = value, [value]
        return chain

    def land(self):
        if self.scatters and self.stages[0][0] and len(self.stages[0][1]) > 1:
            kept, got = self.kept, self.got[0]
            self.turn()
            self.kept, *self.given = split_sum(kept, got, self.place, 1 << len(self.bits))
            return True
        if self.scatters:
            total = self.kept.astype(f32)
            for piece in self.got:
                total = total + piece.astype(f32)
            self.value = total.astype(self.kept.dtype)
        else:
            pieces = [self.kept] + self.got
            order = [
                lax.select_n(self.place ^ i, *pieces)
                if len(pieces) > 2
                else jnp.where(self.place == i, *pieces)
                for i in range(len(pieces))
            ]
            self.value = jnp.concatenate(order, axis=0)
        if self.stages:
            self.prepare()
            return True
        return False


class Total:
    def __init__(self, value, bits):
        self.value, self.bits = value, list(bits)

    def fly(self):
        self.got = flipped(self.value, 1 << self.bits.pop(0))

    def land(self):
        self.value = self.value + self.got
        self.given = [self.value]

    def left(self):
        return len(self.bits)


def weight_grads(turned, d, d_tail, pair, side):
    width = d.shape[2]
    tile = width if pair is None else 256
    each = width // tile
    extra = 0 if pair is None else pair[1].shape[1] // tile
    paired = 2 if extra else 0
    half = D // 2
    fresh = turned[0].shape[0] == L

    def kernel(side_ref, n_ref, nt_ref, d_ref, dt_ref, *refs):
        step = pl.program_id(0)
        kept_ref, given_ref = refs[paired : paired + 2]
        if extra:

            @pl.when(step == 0)
            def _():
                refs[-1][...] = refs[0][...].T

        if fresh:
            turn_refs = refs[paired + 2 : paired + 4]

            @pl.when(step == 0)
            def _():
                turn_refs[0][...] = n_ref[...].T
                turn_refs[1][...] = nt_ref[...].T

        else:
            turn_refs = (n_ref, nt_ref)

        def rows(which, ref):
            return ref[pl.ds(pl.multiple_of(which * half, half), half), :]

        for which, out_ref in ((side_ref[0], kept_ref), (1 - side_ref[0], given_ref)):

            @pl.when(step < each)
            def _():
                out_ref[...] = dot(rows(which, turn_refs[0]), d_ref[0]).astype(bf16)

            @pl.when((step >= each) & (step < 3 * each))
            def _():
                out_ref[...] = (
                    dot(rows(which, turn_refs[0]), d_ref[0])
                    + dot(rows(which, turn_refs[1]), dt_ref[0])
                ).astype(bf16)

            if extra:

                @pl.when(step >= 3 * each)
                def _():
                    out_ref[...] = dot(rows(which, refs[-1]), refs[1][...]).astype(bf16)

    column = lambda i: jnp.where(i < 3 * each, i % each, each - 1)
    fixed = lambda matrix: pl.BlockSpec(matrix.shape, lambda i: (0, 0))
    in_specs = [
        pl.BlockSpec(memory_space=pltpu.SMEM),
        fixed(turned[0]),
        fixed(turned[1]),
        pl.BlockSpec((1, L, tile), lambda i: (jnp.minimum(i // each, 2), 0, column(i))),
        pl.BlockSpec((1, HALF, tile), lambda i: (jnp.clip(i // each - 1, 0, 1), 0, column(i))),
    ]
    operands = [side, *turned, d, d_tail]
    if extra:
        in_specs.append(fixed(pair[0]))
        in_specs.append(pl.BlockSpec((L, tile), lambda i: (0, jnp.maximum(i - 3 * each, 0))))
        operands += pair
    steps = 3 * each + extra
    shapes = [jax.ShapeDtypeStruct((half, steps * tile), bf16)] * 2
    specs = [pl.BlockSpec((half, tile), lambda i: (0, i))] * 2
    if fresh:
        turns = [jax.ShapeDtypeStruct((D, L), bf16), jax.ShapeDtypeStruct((D, HALF), bf16)]
        shapes, specs = shapes + turns, specs + [fixed(turn) for turn in turns]
    kept, given, *turns = pl.pallas_call(
        kernel,
        grid=(steps,),
        in_specs=in_specs,
        out_specs=specs,
        out_shape=shapes,
        scratch_shapes=[pltpu.VMEM((D, L), bf16)] if extra else [],
        cost_estimate=pl.CostEstimate(
            flops=8 * L * D * width, bytes_accessed=8 * D * width, transcendentals=0
        ),
        name="weight_grads",
    )(*operands)
    return kept, given, turns or turned


def split_sum(kept, got, number, count):
    size = kept.shape[0] // count

    def kernel(number_ref, kept_ref, got_ref, *outs):
        for q, out_ref in enumerate(outs):
            rows = pl.ds(pl.multiple_of((number_ref[0] ^ q) * size, size), size)
            out_ref[...] = (kept_ref[rows, :].astype(f32) + got_ref[rows, :].astype(f32)).astype(
                out_ref.dtype
            )

    whole = lambda matrix: pl.BlockSpec(matrix.shape, lambda: (0, 0))
    out = jax.ShapeDtypeStruct((size, kept.shape[1]), kept.dtype)
    return pl.pallas_call(
        kernel,
        in_specs=[pl.BlockSpec(memory_space=pltpu.SMEM), whole(kept), whole(got)],
        out_specs=[whole(out)] * count,
        out_shape=[out] * count,
        cost_estimate=HIDDEN,
        name="split_sum",
    )(number.reshape(1), kept, got)


def shards(
    inputs,
    doc_lengths,
    ln1_gain,
    ln1_bias,
    attn_in,
    qv_bias,
    attn_out,
    attn_out_bias,
    ln2_gain,
    second_norm_bias,
    mlp_in,
    mlp_in_bias,
    mlp_out,
    mlp_out_bias,
    cotangent,
):
    n_mlp = lax.axis_size("mlp")
    place = lax.axis_index("mlp")
    gain_one = ln1_gain.astype(f32)
    bias_one = ln1_bias.astype(f32)
    gain_two = ln2_gain.astype(f32)
    bias_two = second_norm_bias.astype(f32)

    tail = rotated(inputs[HALF:], "mlp", 1)
    tail_lengths = rotated(doc_lengths, "mlp", 1)
    cotangents = [cotangent] + [rotated(cotangent, "mlp", by) for by in range(1, n_mlp)]

    activations = inputs.astype(f32)
    normed = layer_norm(activations, gain_one, bias_one).astype(bf16)
    zeros = jnp.zeros((D,), f32)
    qkv_bias = jnp.concatenate([qv_bias[0].astype(f32), zeros, qv_bias[1].astype(f32)])
    qkv = (dot(normed, attn_in) + qkv_bias).astype(bf16)
    rows = jnp.concatenate(
        [
            jnp.stack(
                [
                    attn_out_bias.astype(f32),
                    gain_two,
                    bias_two,
                    gain_one,
                    bias_one,
                    qv_bias[1].astype(f32),
                ]
            ),
            jnp.zeros((2, D), f32),
        ]
    )
    local, lse_local, mixture, middle, normed_two, sent = local_attention(
        doc_lengths, qkv, attn_out, inputs, rows
    )
    steps = range(1, n_mlp)
    arrived_hi = [rotated(sent, "mlp", by) for by in steps]

    normed_tail, tail_kv = tail_projection(tail, rows, attn_in)
    reads = jnp.where(place == 0, 0, doc_lengths[:, :1])
    tail_kv, *cotangents[1:] = fence((tail_kv, *cotangents[1:]))
    mixture, mem_k, mem_v, lse_mem, middle, normed_two, basis_t, sent = memory_attention(
        reads,
        tail_lengths,
        qkv,
        tail_kv,
        rows,
        local,
        attn_out,
        inputs,
        rows,
        mixture,
        middle,
        normed_two,
    )
    arrived_lo = [rotated(sent, "mlp", by) for by in steps]
    mem_k, arrived_hi = fence((mem_k, arrived_hi))

    bias_rows = jnp.broadcast_to(mlp_in_bias.astype(f32), (8, mlp_in.shape[1]))
    kept = ()
    d_mlp_in_bias = 0.0
    returned_y, returned_dx = [], []
    calls = [(by, part) for by in steps for part in (1, 0)]
    for by, part in calls:
        block = (arrived_lo, arrived_hi)[part][by - 1]
        hidden, d_pre, d_bias, y, dx = mlp_block(
            block, cotangents[by], part, mlp_in, bias_rows, mlp_out, n_mlp * L, 2 * by + part, kept
        )
        kept = (hidden, d_pre)
        d_mlp_in_bias = d_mlp_in_bias + d_bias[0]
        returned_dx.append(rotated(dx, "mlp", -by))
        returned_y.append(y)
    hidden, d_pre, d_bias, y_own, dx_own = mlp_block(
        normed_two, cotangent, 0, mlp_in, bias_rows, mlp_out, n_mlp * L, 0, kept
    )
    d_mlp_in_bias = d_mlp_in_bias + d_bias[0]
    hidden, d_pre, returned_dx = fence((hidden, d_pre, returned_dx))
    over_rows = lambda a, b: lax.dot_general(
        a, b, (((0,), (0,)), ((), ())), preferred_element_type=f32
    )
    all_rows = jnp.concatenate(
        [normed_two] + [piece for pair in zip(arrived_lo, arrived_hi) for piece in pair], axis=0
    )
    d_mlp_in = over_rows(all_rows, d_pre).astype(bf16)
    d_mlp_out = over_rows(hidden, jnp.concatenate(cotangents, axis=0)).astype(bf16)

    hidden_count = mlp_in.shape[1]
    mlp_count = n_mlp.bit_length() - 1
    batch_count = lax.axis_size("batch").bit_length() - 1
    mlp_bits = list(range(mlp_count))
    core = [[mlp_count]]
    rest = list(range(mlp_count + 1, mlp_count + batch_count))
    groups = core + [mlp_bits[:1] + rest[:1]] + [[bit] for bit in mlp_bits[1:] + rest[1:]]

    d_mlp_in, d_mlp_out = lax.psum((d_mlp_in, d_mlp_out), "batch")

    def finish():
        shares = [[dx for (by, part), dx in zip(calls, returned_dx) if part == half] for half in (0, 1)]
        d_middle, d_branch, middle_sums = middle_backward(dx_own, shares, cotangent, middle, rows)
        backward = lambda first, pairs, d: attention_backward(
            first, pairs, doc_lengths, qkv, mem_k, mem_v, d, attn_out, lse_local, lse_mem, basis_t
        )
        early = PAIRS // 3
        side = place_in(core[0]).reshape(1)
        d_one, d_tail_one, sums_one = backward(0, early, d_branch)
        kept, given, turned = weight_grads(
            (normed, normed_tail), d_one, d_tail_one, (mixture, d_branch), side
        )
        chain_one = Chain(kept, given, groups)
        chain_one.fly()
        chain_one.land()
        d_branch, chain_one.given = fence((d_branch, chain_one.given))
        chain_one.fly()
        d_two, d_tail_two, sums_two = backward(early, PAIRS - early, d_branch)
        d_two, d_tail_two, chain_one.got = fence((d_two, d_tail_two, chain_one.got))
        chain_one.land()
        d_two, d_tail_two, chain_one.given = fence((d_two, d_tail_two, chain_one.given))
        chain_one.fly()
        kept, given, turned = weight_grads(turned, d_two, d_tail_two, None, side)
        chain_two = Chain(kept, given, groups)
        chain_two.fly()
        chain_two.land()
        d_one, d_two, d_tails, sums, later, chain_two.given = fence(
            (
                d_one,
                d_two,
                (d_tail_one, d_tail_two),
                (sums_one, sums_two),
                (d_mlp_in_bias, returned_y, y_own),
                chain_two.given,
            )
        )
        bias_grad, y_given, y_mine = later
        chain_two.fly()
        chain_one.got, unused = fence((chain_one.got, chain_two.given))
        chain_one.land()
        d_one, chain_one.given = fence((d_one, chain_one.given))
        chain_one.fly()
        d_normed, d_tail_rows, input_sums = qkv_backward(
            d_one, d_two, *d_tails, attn_in, inputs, tail
        )
        chain_one.got, chain_two.got, d_normed, d_tail_rows, input_sums = fence(
            (chain_one.got, chain_two.got, d_normed, d_tail_rows, input_sums)
        )
        chain_one.land()
        chain_one.fly()
        chain_two.land()
        chain_two.fly()
        y_given, unused = fence((y_given, chain_two.given))
        shares = [
            jnp.concatenate([y for (by, part), y in zip(calls, y_given) if by == step][::-1], axis=0)
            for step in steps
        ]
        returned = [rotated(y, "mlp", -step) for step, y in zip(steps, shares)]
        from_next = rotated(d_tail_rows, "mlp", -1)
        placed_bias = lax.dynamic_update_slice(
            jnp.zeros((n_mlp * hidden_count,), f32), bias_grad, (place * hidden_count,)
        )
        vectors = Total(
            jnp.concatenate(
                [
                    input_sums[:2],
                    middle_sums[:4],
                    jnp.concatenate(sums, axis=1)[:2],
                    placed_bias.reshape(-1, D),
                ],
                axis=0,
            ),
            core[0] + rest + mlp_bits,
        )
        vectors.fly()

        chains = {"one": chain_one, "two": chain_two, "all": vectors}
        held = {"one": 1, "two": 2, "all": 1}
        order = ["two", "one", "all"] * 2 + ["two", "all"] * 2 + ["one"]
        token = chain_two.given
        input_grad = layer_output = None
        turns = 0
        while any(chains[name].left() > held[name] or name in order for name in chains):
            for name in order:
                chain = chains[name]
                chain.got, token = fence((chain.got, token))
                turns += 1
                if turns == 7:
                    chain.got, returned = fence((chain.got, returned))
                if turns == 9:
                    input_grad = input_backward(d_normed, from_next, inputs, d_middle, rows)
                    chain.got, input_grad = fence((chain.got, input_grad))
                if turns == 11:
                    result = y_mine.astype(f32)
                    for y in returned:
                        result = result + y.astype(f32)
                    layer_output = (middle + (result + mlp_out_bias)).astype(bf16)
                    chain.got, layer_output = fence((chain.got, layer_output))
                chain.land()
                token = chain.given
                if chain.left() > held[name]:
                    chain.fly()
            order = [name for name in chains if chains[name].left() > held[name]]

        return chain_one.value, chain_two.value, vectors.value, input_grad, layer_output

    shapes = jax.eval_shape(finish)
    done = lax.cond(
        doc_lengths[0, 0] > 0,
        finish,
        lambda: jax.tree.map(lambda leaf: jnp.zeros(leaf.shape, leaf.dtype), shapes),
    )
    one, two, summed, input_grad, layer_output = done
    chain_two = Chain.gathering(two, [groups[1], core[0]])
    chain_two.fly()
    chain_one = Chain.gathering(one, core)
    chain_one.fly()
    vectors = Total(summed, mlp_bits[-1:])
    vectors.fly()
    vectors.land()
    bias_grad = lax.dynamic_slice(
        vectors.value[8:].reshape(-1), (place * hidden_count,), (hidden_count,)
    )
    summed = [vectors.value[i] for i in range(6)] + [vectors.value[6:8], bias_grad]
    d_mlp_in, d_mlp_out = widened(d_mlp_in, d_mlp_out)
    chain_two.got, summed, d_mlp_in, d_mlp_out = fence(
        (chain_two.got, summed, d_mlp_in, d_mlp_out)
    )
    chain_two.land()
    chain_two.fly()
    chain_one.land()
    chain_two.land()

    width = PAIRS // 3 * LANES
    late = D - width
    d_attn_in = jnp.concatenate(
        [
            piece
            for i in range(3)
            for piece in (
                chain_one.value[:, i * width : (i + 1) * width],
                chain_two.value[:, i * late : (i + 1) * late],
            )
        ],
        axis=1,
    )
    return (
        layer_output,
        input_grad,
        summed[0],
        summed[1],
        d_attn_in.astype(f32),
        summed[6],
        chain_one.value[:, 3 * width :].astype(f32),
        summed[2],
        summed[3],
        summed[4],
        d_mlp_in,
        summed[7],
        d_mlp_out,
        summed[5],
    )


def solution(mesh):
    rows, whole = P(("batch", "mlp"), None), P()
    columns, hidden, depth = P(None, "mlp"), P("mlp"), P("mlp", None)
    return jax.shard_map(
        shards,
        mesh=mesh,
        in_specs=(rows, rows) + (whole,) * 8 + (columns, hidden, depth, whole, rows),
        out_specs=(rows, rows) + (whole,) * 8 + (columns, hidden, depth, whole),
        check_vma=False,
    )
```

```python
import jax
import jax.numpy as jnp
from jax import lax
from jax.experimental import pallas as pl
from jax.experimental.pallas import tpu as pltpu
from jax.sharding import PartitionSpec as P

D = 768
H = 12
HD = 64
NB = 512
L = 512
NDOC = 3
HALF = L // 2
PAIRS = H // 2
LANES = 2 * HD

LOG2E = 1.4426950408889634
SCORE_LOG2 = LOG2E * HD**-0.5
MASKED = -1e30

bf16 = jnp.bfloat16
f32 = jnp.float32


def dot(a, b):
    return jnp.dot(a, b, preferred_element_type=f32)


def dot_nt(a, b):
    return lax.dot_general(a, b, (((1,), (1,)), ((), ())), preferred_element_type=f32)


def layer_norm(matrix, gain_row, shift_row):
    center = jnp.mean(matrix, axis=-1, keepdims=True)
    centered = matrix - center
    spread = jnp.mean(centered * centered, axis=-1, keepdims=True)
    return centered * lax.rsqrt(spread + 1e-05) * gain_row + shift_row


def head_lanes(matrix, head):
    lane = lax.broadcasted_iota(jnp.int32, (1, LANES), 1)
    return jnp.where(lane // HD == head, matrix, jnp.zeros_like(matrix))


def fill_mask(lens, mask):
    key = lax.broadcasted_iota(jnp.int32, (L, L), 0)
    query = lax.broadcasted_iota(jnp.int32, (L, L), 1)
    one = lens[0, 0]
    two = one + lens[0, 1]
    start = jnp.where(query >= two, two, jnp.where(query >= one, one, 0))
    mask[...] = jnp.where((key <= query) & (key >= start), 0.0, MASKED)


def local_kernel(
    lens,
    q_ref,
    k_ref,
    v_ref,
    wo_ref,
    x_ref,
    rows_ref,
    out_ref,
    lse_ref,
    mix_ref,
    middle_ref,
    normed_ref,
    sent_ref,
    mask,
    turned,
    acc,
):
    step = pl.program_id(0)

    @pl.when(step == 0)
    def _():
        fill_mask(lens, mask)
        acc[...] = jnp.zeros_like(acc)

    q, k = q_ref[...], k_ref[...]
    v_t = v_ref[...].T
    for head in range(2):
        q_head = head_lanes(q, head)
        rows = slice(head * HD, (head + 1) * HD)
        for part in range(2):
            keys = HALF * (part + 1)
            cols = slice(part * HALF, (part + 1) * HALF)
            s = dot_nt(k[:keys], q_head[cols]) * SCORE_LOG2 + mask[:keys, cols]
            top = jnp.max(s, axis=0, keepdims=True)
            e = jnp.exp2(s - top)
            total = jnp.sum(e, axis=0, keepdims=True)
            out = dot(v_t[rows, :keys], e.astype(bf16))
            turned[rows, cols] = out / total
            lse_ref[0, head : head + 1, cols] = top + jnp.log2(total)
    out_ref[...] = turned[:, :HALF].T
    mixed = turned[:, HALF:].T.astype(bf16)
    mix_ref[...] = mixed
    acc[...] += dot(mixed, wo_ref[...])

    @pl.when(step == PAIRS - 1)
    def _():
        finish_middle(x_ref, acc, rows_ref, middle_ref, normed_ref, sent_ref)


def finish_middle(x_ref, acc, rows_ref, middle_ref, normed_ref, sent_ref):
    middle = x_ref[...].astype(f32) + (acc[...] + rows_ref[0:1])
    middle_ref[...] = middle
    normed = layer_norm(middle, rows_ref[1:2], rows_ref[2:3]).astype(bf16)
    normed_ref[...] = normed
    sent_ref[...] = normed


def local_attention(lens, qkv, attn_out, inputs, rows):
    column = lambda k: pl.BlockSpec((L, LANES), lambda i: (0, k * PAIRS + i))
    upper = pl.BlockSpec((HALF, D), lambda i: (1, 0))
    return pl.pallas_call(
        local_kernel,
        grid=(PAIRS,),
        in_specs=[
            pl.BlockSpec(memory_space=pltpu.SMEM),
            column(0),
            column(1),
            column(2),
            pl.BlockSpec((LANES, D), lambda i: (i, 0)),
            upper,
            pl.BlockSpec((8, D), lambda i: (0, 0)),
        ],
        out_specs=[
            pl.BlockSpec((HALF, LANES), lambda i: (0, i)),
            pl.BlockSpec((1, 8, L), lambda i: (i, 0, 0)),
            pl.BlockSpec((HALF, LANES), lambda i: (1, i)),
            upper,
            upper,
            pl.BlockSpec((HALF, D), lambda i: (0, 0)),
        ],
        out_shape=[
            jax.ShapeDtypeStruct((HALF, D), f32),
            jax.ShapeDtypeStruct((PAIRS, 8, L), f32),
            jax.ShapeDtypeStruct((L, D), bf16),
            jax.ShapeDtypeStruct((L, D), f32),
            jax.ShapeDtypeStruct((L, D), bf16),
            jax.ShapeDtypeStruct((HALF, D), bf16),
        ],
        scratch_shapes=[
            pltpu.VMEM((L, L), f32),
            pltpu.VMEM((LANES, L), f32),
            pltpu.VMEM((HALF, D), f32),
        ],
        cost_estimate=pl.CostEstimate(
            flops=H * 12 * HALF * HALF * 256, bytes_accessed=8 * L * D, transcendentals=H * L * L
        ),
        name="local_attention",
    )(lens, qkv, qkv, qkv, attn_out, inputs, rows)


def basis_rows(last_len, transposed):
    shape = (HALF, NB) if transposed else (NB, HALF)
    slot_dim, place_dim = (1, 0) if transposed else (0, 1)
    slot = lax.broadcasted_iota(jnp.int32, shape, slot_dim).astype(f32)
    place = lax.broadcasted_iota(jnp.int32, shape, place_dim).astype(f32)
    offsets = place - HALF + last_len + 0.5
    distances = (slot + 0.5) / NB * last_len - offsets
    weights = jnp.where(offsets > 0.0, jnp.exp(-0.5 * distances * distances), 0.0)
    return weights / jnp.sum(weights, axis=place_dim, keepdims=True)


def tail_projection(tail, rows, attn_in):
    tile = D // 2

    def kernel(x_ref, rows_ref, w_ref, normed_ref, kv_ref):
        @pl.when(pl.program_id(0) == 0)
        def _():
            normed_ref[...] = layer_norm(
                x_ref[...].astype(f32), rows_ref[3:4], rows_ref[4:5]
            ).astype(bf16)

        kv_ref[...] = dot(normed_ref[...], w_ref[...]).astype(bf16)

    fixed = lambda count: pl.BlockSpec((count, D), lambda i: (0, 0))
    return pl.pallas_call(
        kernel,
        grid=(4,),
        in_specs=[fixed(HALF), fixed(8), pl.BlockSpec((D, tile), lambda i: (0, 2 + i))],
        out_specs=[fixed(HALF), pl.BlockSpec((HALF, tile), lambda i: (0, i))],
        out_shape=[
            jax.ShapeDtypeStruct((HALF, D), bf16),
            jax.ShapeDtypeStruct((HALF, 2 * D), bf16),
        ],
        cost_estimate=pl.CostEstimate(
            flops=4 * HALF * D * D, bytes_accessed=4 * D * D, transcendentals=0
        ),
        name="tail_projection",
    )(tail, rows, attn_in)


def memory_kernel(
    reads,
    tail_lengths,
    q_ref,
    kt_ref,
    vt_ref,
    vb_ref,
    local_ref,
    wo_ref,
    x_ref,
    rows_ref,
    mix_whole,
    middle_whole,
    normed_whole,
    mix_ref,
    mk_ref,
    mv_ref,
    lse_ref,
    middle_ref,
    normed_ref,
    basis_t_ref,
    sent_ref,
    basis,
    turned,
    acc,
):
    step = pl.program_id(0)

    @pl.when(step == 0)
    def _():
        last_len = tail_lengths[0, NDOC - 1].astype(f32)
        basis[...] = basis_rows(last_len, False).astype(bf16)
        basis_t_ref[...] = basis_rows(last_len, True).astype(bf16)
        acc[...] = jnp.zeros_like(acc)

    mem_k = dot(basis[...], kt_ref[...]).astype(bf16)
    mem_v = (dot(basis[...], vt_ref[...]) + vb_ref[5:6]).astype(bf16)
    mk_ref[...] = mem_k
    mv_ref[...] = mem_v
    v_t = mem_v.T
    query = lax.broadcasted_iota(jnp.int32, (1, HALF), 1)
    reading = query < reads[0, 0]
    q = q_ref[...]
    for head in range(2):
        rows = slice(head * HD, (head + 1) * HD)
        s = dot_nt(mem_k, head_lanes(q, head)) * SCORE_LOG2
        top = jnp.max(s, axis=0, keepdims=True)
        e = jnp.exp2(s - top)
        total = jnp.sum(e, axis=0, keepdims=True)
        out = dot(v_t[rows], e.astype(bf16))
        turned[rows, :] = jnp.where(reading, out / total, 0.0)
        lse_ref[0, head : head + 1, :] = jnp.where(reading, top + jnp.log2(total), -MASKED)
    mixed = (local_ref[...] + turned[...].T).astype(bf16)
    mix_ref[...] = mixed
    acc[...] += dot(mixed, wo_ref[...])

    @pl.when(step == PAIRS - 1)
    def _():
        finish_middle(x_ref, acc, rows_ref, middle_ref, normed_ref, sent_ref)


def memory_attention(
    reads, tail_lengths, qkv, tail_kv, value_bias, local, attn_out, inputs, rows, mixture, middle, normed
):
    whole = lambda shape: pl.BlockSpec(shape, lambda i: (0,) * len(shape))
    untouched = pl.BlockSpec(memory_space=pl.ANY)
    return pl.pallas_call(
        memory_kernel,
        grid=(PAIRS,),
        in_specs=[
            pl.BlockSpec(memory_space=pltpu.SMEM),
            pl.BlockSpec(memory_space=pltpu.SMEM),
            pl.BlockSpec((HALF, LANES), lambda i: (0, i)),
            pl.BlockSpec((HALF, LANES), lambda i: (0, i)),
            pl.BlockSpec((HALF, LANES), lambda i: (0, PAIRS + i)),
            pl.BlockSpec((8, LANES), lambda i: (0, i)),
            pl.BlockSpec((HALF, LANES), lambda i: (0, i)),
            pl.BlockSpec((LANES, D), lambda i: (i, 0)),
            whole((HALF, D)),
            whole((8, D)),
            untouched,
            untouched,
            untouched,
        ],
        out_specs=[
            pl.BlockSpec((HALF, LANES), lambda i: (0, i)),
            pl.BlockSpec((NB, LANES), lambda i: (0, i)),
            pl.BlockSpec((NB, LANES), lambda i: (0, i)),
            pl.BlockSpec((1, 8, HALF), lambda i: (i, 0, 0)),
            whole((HALF, D)),
            whole((HALF, D)),
            whole((HALF, NB)),
            whole((HALF, D)),
        ],
        out_shape=[
            jax.ShapeDtypeStruct((L, D), bf16),
            jax.ShapeDtypeStruct((NB, D), bf16),
            jax.ShapeDtypeStruct((NB, D), bf16),
            jax.ShapeDtypeStruct((PAIRS, 8, HALF), f32),
            jax.ShapeDtypeStruct((L, D), f32),
            jax.ShapeDtypeStruct((L, D), bf16),
            jax.ShapeDtypeStruct((HALF, NB), bf16),
            jax.ShapeDtypeStruct((HALF, D), bf16),
        ],
        scratch_shapes=[
            pltpu.VMEM((NB, HALF), bf16),
            pltpu.VMEM((LANES, HALF), f32),
            pltpu.VMEM((HALF, D), f32),
        ],
        input_output_aliases={10: 0, 11: 4, 12: 5},
        cost_estimate=pl.CostEstimate(
            flops=H * 16 * HALF * HALF * 256, bytes_accessed=16 * L * D, transcendentals=H * L * HALF
        ),
        name="memory_attention",
    )(
        reads,
        tail_lengths,
        qkv,
        tail_kv,
        tail_kv,
        value_bias,
        local,
        attn_out,
        inputs,
        rows,
        mixture,
        middle,
        normed,
    )


def mlp_kernel(x_ref, ct_ref, wi_ref, bi_ref, wo_ref, *refs):
    hid_ref, dpre_ref, bias_ref, y_ref, dx_ref, y_acc, dx_acc = refs[-7:]
    step = pl.program_id(0)
    pre = dot(x_ref[...], wi_ref[...]) + bi_ref[0:1]
    squared = pre * pre
    tanh = jnp.tanh(pre * (0.7978845608028654 + 0.7978845608028654 * 0.044715 * squared))
    half = 0.5 * pre
    hidden = (half + half * tanh).astype(bf16)
    slope = (
        0.5
        + 0.5 * tanh
        + half
        * (1.0 - tanh * tanh)
        * (0.7978845608028654 + 3 * 0.7978845608028654 * 0.044715 * squared)
    )
    d_pre = (slope * dot_nt(ct_ref[...], wo_ref[...])).astype(bf16)
    hid_ref[...] = hidden
    dpre_ref[...] = d_pre
    bias_ref[...] = jnp.broadcast_to(
        jnp.sum(d_pre.astype(f32), axis=0, keepdims=True), bias_ref.shape
    )
    y = dot(hidden, wo_ref[...])
    dx = dot_nt(d_pre, wi_ref[...])

    @pl.when(step == 0)
    def _():
        y_acc[...] = y
        dx_acc[...] = dx

    @pl.when(step > 0)
    def _():
        y_acc[...] += y
        dx_acc[...] += dx

    @pl.when(step == pl.num_programs(0) - 1)
    def _():
        y_ref[...] = y_acc[...].astype(bf16)
        dx_ref[...] = dx_acc[...].astype(bf16)


def mlp_block(rows, cotangent, part, mlp_in, bias_rows, mlp_out, total, place, kept):
    count, hidden = rows.shape[0], mlp_in.shape[1]
    tile = next(t for t in (768 if count <= HALF else 512, 384, 256, 128) if hidden % t == 0)
    fixed = pl.BlockSpec((count, D), lambda i: (0, 0))
    across = pl.BlockSpec((count, tile), lambda i: (place, i))
    return pl.pallas_call(
        mlp_kernel,
        grid=(hidden // tile,),
        in_specs=[
            fixed,
            pl.BlockSpec((count, D), lambda i: (part, 0)),
            pl.BlockSpec((D, tile), lambda i: (0, i)),
            pl.BlockSpec((8, tile), lambda i: (0, i)),
            pl.BlockSpec((tile, D), lambda i: (i, 0)),
        ]
        + [pl.BlockSpec(memory_space=pl.ANY)] * len(kept),
        out_specs=[across, across, pl.BlockSpec((8, tile), lambda i: (0, i)), fixed, fixed],
        out_shape=[
            jax.ShapeDtypeStruct((total, hidden), bf16),
            jax.ShapeDtypeStruct((total, hidden), bf16),
            jax.ShapeDtypeStruct((8, hidden), f32),
            jax.ShapeDtypeStruct((count, D), bf16),
            jax.ShapeDtypeStruct((count, D), bf16),
        ],
        scratch_shapes=[pltpu.VMEM((count, D), f32), pltpu.VMEM((count, D), f32)],
        input_output_aliases={5 + i: i for i in range(len(kept))},
        cost_estimate=pl.CostEstimate(
            flops=8 * count * D * hidden,
            bytes_accessed=4 * D * hidden + 4 * count * hidden + 8 * count * D,
            transcendentals=count * hidden,
        ),
        name="mlp_block",
    )(rows, cotangent, mlp_in, bias_rows, mlp_out, *kept)


def backward_kernel(
    lens,
    q_ref,
    k_ref,
    v_ref,
    mk_ref,
    mv_ref,
    db_ref,
    wo_ref,
    ll_ref,
    lm_ref,
    bt_ref,
    dqkv_ref,
    dtail_ref,
    sums_ref,
    mask,
    turned,
    dk_acc,
    dv_acc,
):
    @pl.when(pl.program_id(0) == 0)
    def _():
        fill_mask(lens, mask)

    q, k, v = q_ref[...], k_ref[...], v_ref[...]
    mem_k, mem_v = mk_ref[...], mv_ref[...]
    d_mix = dot_nt(db_ref[...], wo_ref[...]).astype(bf16)
    k_t, mk_t = k.T, mem_k.T
    d_mem_k = d_mem_v = None

    def one(keys, values, q_part, d_part, lse, extra):
        s = dot_nt(keys, q_part) * SCORE_LOG2
        if extra is not None:
            s = s + extra
        weights = jnp.exp2(s - lse)
        d_weights = dot_nt(values, d_part)
        inner = jnp.sum(weights * d_weights, axis=0, keepdims=True)
        d_scores = (weights * (d_weights - inner)).astype(bf16)
        return d_scores, dot(d_scores, q_part), dot(weights.astype(bf16), d_part)

    for head in range(2):
        rows = slice(head * HD, (head + 1) * HD)
        q_head, d_head = head_lanes(q, head), head_lanes(d_mix, head)
        for part in range(2):
            keys = HALF * (part + 1)
            cols = slice(part * HALF, (part + 1) * HALF)
            ds, dk, dv = one(
                k[:keys],
                v[:keys],
                q_head[cols],
                d_head[cols],
                ll_ref[0, head : head + 1, cols],
                mask[:keys, cols],
            )
            dq = dot(k_t[rows, :keys], ds)
            if part == 0:
                ds, d_key, d_value = one(
                    mem_k, mem_v, q_head[cols], d_head[cols], lm_ref[0, head : head + 1, :], None
                )
                dq = dq + dot(mk_t[rows], ds)
                d_mem_k = d_key if d_mem_k is None else d_mem_k + d_key
                d_mem_v = d_value if d_mem_v is None else d_mem_v + d_value
            turned[rows, cols] = dq
            if head == 0 and part == 0:
                dk_acc[:HALF] = dk
                dv_acc[:HALF] = dv
            elif head == 0:
                dk_acc[:HALF] += dk[:HALF]
                dv_acc[:HALF] += dv[:HALF]
                dk_acc[HALF:] = dk[HALF:]
                dv_acc[HALF:] = dv[HALF:]
            else:
                dk_acc[:keys] += dk
                dv_acc[:keys] += dv
    scale = HD**-0.5
    d_q = (turned[...].T * scale).astype(bf16)
    d_v = dv_acc[...].astype(bf16)
    dqkv_ref[0] = d_q
    dqkv_ref[1] = (dk_acc[...] * scale).astype(bf16)
    dqkv_ref[2] = d_v
    d_mem_k = (d_mem_k * scale).astype(bf16)
    d_mem_v = d_mem_v.astype(bf16)
    dtail_ref[0] = dot(bt_ref[...], d_mem_k).astype(bf16)
    dtail_ref[1] = dot(bt_ref[...], d_mem_v).astype(bf16)
    sums_ref[0:1] = jnp.sum(d_q.astype(f32), axis=0, keepdims=True)
    sums_ref[1:2] = jnp.sum(d_v.astype(f32), axis=0, keepdims=True) + jnp.sum(
        d_mem_v.astype(f32), axis=0, keepdims=True
    )


HIDDEN = pl.CostEstimate(flops=1000, bytes_accessed=1000, transcendentals=0)


def attention_backward(
    first, pairs, lens, qkv, mem_k, mem_v, d_branch, attn_out, lse_local, lse_mem, basis_t
):
    column = lambda k: pl.BlockSpec((L, LANES), lambda i: (0, k * PAIRS + first + i))
    whole = lambda shape: pl.BlockSpec(shape, lambda i: (0,) * len(shape))
    width = pairs * LANES
    return pl.pallas_call(
        backward_kernel,
        grid=(pairs,),
        in_specs=[
            pl.BlockSpec(memory_space=pltpu.SMEM),
            column(0),
            column(1),
            column(2),
            column(0),
            column(0),
            whole((L, D)),
            pl.BlockSpec((LANES, D), lambda i: (first + i, 0)),
            pl.BlockSpec((1, 8, L), lambda i: (first + i, 0, 0)),
            pl.BlockSpec((1, 8, HALF), lambda i: (first + i, 0, 0)),
            whole((HALF, NB)),
        ],
        out_specs=[
            pl.BlockSpec((3, L, LANES), lambda i: (0, 0, i)),
            pl.BlockSpec((2, HALF, LANES), lambda i: (0, 0, i)),
            pl.BlockSpec((8, LANES), lambda i: (0, i)),
        ],
        out_shape=[
            jax.ShapeDtypeStruct((3, L, width), bf16),
            jax.ShapeDtypeStruct((2, HALF, width), bf16),
            jax.ShapeDtypeStruct((8, width), f32),
        ],
        scratch_shapes=[
            pltpu.VMEM((L, L), f32),
            pltpu.VMEM((LANES, L), f32),
            pltpu.VMEM((L, LANES), f32),
            pltpu.VMEM((L, LANES), f32),
        ],
        cost_estimate=pl.CostEstimate(
            flops=2 * pairs * 56 * HALF * HALF * 256,
            bytes_accessed=20 * L * width,
            transcendentals=2 * pairs * L * L,
        ),
        name="attention_backward",
    )(lens, qkv, qkv, qkv, mem_k, mem_v, d_branch, attn_out, lse_local, lse_mem, basis_t)


def normalized(matrix):
    centered = matrix - jnp.mean(matrix, axis=-1, keepdims=True)
    scale = lax.rsqrt(jnp.mean(centered * centered, axis=-1, keepdims=True) + 1e-05)
    return centered * scale, scale


def norm_slope(unit, scale, grown):
    inner = jnp.mean(grown * unit, axis=-1, keepdims=True)
    return (grown - jnp.mean(grown, axis=-1, keepdims=True) - unit * inner) * scale


def column_sum(matrix):
    return jnp.sum(matrix, axis=0, keepdims=True)


def middle_backward(d_own, returned, cotangent, middle, rows):
    count = len(returned[0])

    def kernel(d_ref, ct_ref, middle_ref, rows_ref, *refs):
        shares = refs[: 2 * count]
        d_middle_ref, d_branch_ref, sums_ref = refs[2 * count :]
        part = pl.program_id(0)
        total = d_ref[...].astype(f32)
        for i in range(count):
            total = total + jnp.where(part == 0, shares[i][...], shares[count + i][...]).astype(f32)
        upstream = ct_ref[...].astype(f32)
        unit, scale = normalized(middle_ref[...])
        d_middle = upstream + norm_slope(unit, scale, total * rows_ref[1:2])
        d_branch = d_middle.astype(bf16)
        d_middle_ref[...] = d_middle
        d_branch_ref[...] = d_branch
        sums = jnp.concatenate(
            [
                column_sum(d_branch.astype(f32)),
                column_sum(total * unit),
                column_sum(total),
                column_sum(upstream),
                jnp.zeros((4, D), f32),
            ],
            axis=0,
        )

        @pl.when(part == 0)
        def _():
            sums_ref[...] = sums

        @pl.when(part > 0)
        def _():
            sums_ref[...] += sums

    half = pl.BlockSpec((HALF, D), lambda i: (i, 0))
    fixed = pl.BlockSpec((HALF, D), lambda i: (0, 0))
    eight = pl.BlockSpec((8, D), lambda i: (0, 0))
    return pl.pallas_call(
        kernel,
        grid=(2,),
        in_specs=[half, half, half, eight] + [fixed] * (2 * count),
        out_specs=[half, half, eight],
        out_shape=[
            jax.ShapeDtypeStruct((L, D), f32),
            jax.ShapeDtypeStruct((L, D), bf16),
            jax.ShapeDtypeStruct((8, D), f32),
        ],
        cost_estimate=pl.CostEstimate(
            flops=20 * L * D, bytes_accessed=14 * L * D, transcendentals=0
        ),
        name="middle_backward",
    )(d_own, cotangent, middle, rows, *returned[0], *returned[1])


def qkv_backward(d_one, d_two, d_tail_one, d_tail_two, attn_in, inputs, tail_rows):
    cut = d_one.shape[2]

    def kernel(
        one_ref, two_ref, t_one_ref, t_two_ref, w_ref, x_ref, xt_ref, dn_ref, dt_ref, sums_ref, tail
    ):
        step = pl.program_id(0)
        left, right = w_ref[:, :cut], w_ref[:, cut:]
        part = dot_nt(one_ref[0], left) + dot_nt(two_ref[0], right)

        @pl.when(step == 0)
        def _():
            dn_ref[...] = part
            tail[...] = jnp.zeros_like(tail)

        @pl.when(step > 0)
        def _():
            dn_ref[...] += part
            tail[...] += dot_nt(t_one_ref[0], left) + dot_nt(t_two_ref[0], right)

        @pl.when(step == 2)
        def _():
            dt_ref[...] = tail[...].astype(bf16)
            unit, unused = normalized(x_ref[...].astype(f32))
            tail_unit, unused = normalized(xt_ref[...].astype(f32))
            sums_ref[0:1] = column_sum(dn_ref[...] * unit) + column_sum(tail[...] * tail_unit)
            sums_ref[1:2] = column_sum(dn_ref[...]) + column_sum(tail[...])

    fixed = lambda count: pl.BlockSpec((count, D), lambda i: (0, 0))
    return pl.pallas_call(
        kernel,
        grid=(3,),
        in_specs=[
            pl.BlockSpec((1, L, cut), lambda i: (i, 0, 0)),
            pl.BlockSpec((1, L, D - cut), lambda i: (i, 0, 0)),
            pl.BlockSpec((1, HALF, cut), lambda i: (jnp.maximum(i - 1, 0), 0, 0)),
            pl.BlockSpec((1, HALF, D - cut), lambda i: (jnp.maximum(i - 1, 0), 0, 0)),
            pl.BlockSpec((D, D), lambda i: (0, i)),
            fixed(L),
            fixed(HALF),
        ],
        out_specs=[fixed(L), fixed(HALF), fixed(8)],
        out_shape=[
            jax.ShapeDtypeStruct((L, D), f32),
            jax.ShapeDtypeStruct((HALF, D), bf16),
            jax.ShapeDtypeStruct((8, D), f32),
        ],
        scratch_shapes=[pltpu.VMEM((HALF, D), f32)],
        cost_estimate=pl.CostEstimate(
            flops=8 * L * D * D, bytes_accessed=20 * L * D, transcendentals=0
        ),
        name="qkv_backward",
    )(d_one, d_two, d_tail_one, d_tail_two, attn_in, inputs, tail_rows)


def input_backward(d_normed, from_next, inputs, d_middle, rows):
    def kernel(dn_ref, next_ref, x_ref, dm_ref, rows_ref, out_ref):
        unit, scale = normalized(x_ref[...].astype(f32))
        shared = jnp.where(pl.program_id(0) == 0, 0.0, next_ref[...].astype(f32))
        grown = (dn_ref[...] + shared) * rows_ref[3:4]
        out_ref[...] = (dm_ref[...] + norm_slope(unit, scale, grown)).astype(bf16)

    half = pl.BlockSpec((HALF, D), lambda i: (i, 0))
    return pl.pallas_call(
        kernel,
        grid=(2,),
        in_specs=[
            half,
            pl.BlockSpec((HALF, D), lambda i: (0, 0)),
            half,
            half,
            pl.BlockSpec((8, D), lambda i: (0, 0)),
        ],
        out_specs=half,
        out_shape=jax.ShapeDtypeStruct((L, D), bf16),
        cost_estimate=pl.CostEstimate(
            flops=20 * L * D, bytes_accessed=12 * L * D, transcendentals=0
        ),
        name="input_backward",
    )(d_normed, from_next, inputs, d_middle, rows)


def widened(first, second):
    steps = 6

    def kernel(a_ref, b_ref, a_out, b_out):
        a_out[...] = a_ref[...].astype(f32)
        b_out[...] = b_ref[...].astype(f32)

    specs = [
        pl.BlockSpec((matrix.shape[0] // steps, matrix.shape[1]), lambda i: (i, 0))
        for matrix in (first, second)
    ]
    return pl.pallas_call(
        kernel,
        grid=(steps,),
        in_specs=specs,
        out_specs=specs,
        out_shape=[jax.ShapeDtypeStruct(matrix.shape, f32) for matrix in (first, second)],
        cost_estimate=pl.CostEstimate(
            flops=0, bytes_accessed=6 * (first.size + second.size), transcendentals=0
        ),
        name="widened",
    )(first, second)


def rotated(value, axis, by):
    count = lax.axis_size(axis)
    return lax.ppermute(value, axis, [(i, (i + by) % count) for i in range(count)])


fence = lax.optimization_barrier
GRID = ("batch", "mlp")


def flipped(value, mask):
    count = lax.axis_size("batch") * lax.axis_size("mlp")
    return lax.ppermute(value, GRID, [(i, i ^ mask) for i in range(count)])


def place_in(bits):
    number = lax.axis_index(GRID)
    return sum(((number >> bit) & 1) << i for i, bit in enumerate(bits))


def peers(bits):
    return [sum(((q >> i) & 1) << bit for i, bit in enumerate(bits)) for q in range(1, 1 << len(bits))]


def grouped(bits):
    odd = len(bits) % 2
    return ([bits[:1]] if odd else []) + [bits[i : i + 2] for i in range(odd, len(bits), 2)]


class Chain:
    def __init__(self, kept, given, groups):
        self.stages = [(True, bits) for bits in groups] + [(False, bits) for bits in groups[::-1]]
        self.turn()
        self.kept, self.given = kept, [given]

    def left(self):
        return len(self.stages) + 1

    def turn(self):
        self.scatters, self.bits = self.stages.pop(0)
        self.place = place_in(self.bits)

    def prepare(self):
        self.turn()
        count = 1 << len(self.bits)
        if self.scatters:
            size = self.value.shape[0] // count
            piece = lambda i: lax.dynamic_slice_in_dim(self.value, i * size, size, 0)
            self.kept = piece(self.place)
            self.given = [piece(self.place ^ q) for q in range(1, count)]
        else:
            self.kept = self.value
            self.given = [self.value]

    def fly(self):
        masks = peers(self.bits)
        given = self.given if self.scatters else self.given * len(masks)
        self.got = [flipped(piece, mask) for piece, mask in zip(given, masks)]

    @classmethod
    def gathering(cls, value, groups):
        chain = cls.__new__(cls)
        chain.stages = [(False, bits) for bits in groups]
        chain.turn()
        chain.kept, chain.given = value, [value]
        return chain

    def land(self):
        if self.scatters and self.stages[0][0] and len(self.stages[0][1]) > 1:
            kept, got = self.kept, self.got[0]
            self.turn()
            self.kept, *self.given = split_sum(kept, got, self.place, 1 << len(self.bits))
            return True
        if self.scatters:
            total = self.kept.astype(f32)
            for piece in self.got:
                total = total + piece.astype(f32)
            self.value = total.astype(self.kept.dtype)
        else:
            pieces = [self.kept] + self.got
            order = [
                lax.select_n(self.place ^ i, *pieces)
                if len(pieces) > 2
                else jnp.where(self.place == i, *pieces)
                for i in range(len(pieces))
            ]
            self.value = jnp.concatenate(order, axis=0)
        if self.stages:
            self.prepare()
            return True
        return False


class Total:
    def __init__(self, value, bits):
        self.value, self.bits = value, list(bits)

    def fly(self):
        self.got = flipped(self.value, 1 << self.bits.pop(0))

    def land(self):
        self.value = self.value + self.got
        self.given = [self.value]

    def left(self):
        return len(self.bits)


def weight_grads(turned, d, d_tail, pair, side):
    width = d.shape[2]
    tile = width if pair is None else 256
    each = width // tile
    extra = 0 if pair is None else pair[1].shape[1] // tile
    paired = 2 if extra else 0
    half = D // 2
    fresh = turned[0].shape[0] == L

    def kernel(side_ref, n_ref, nt_ref, d_ref, dt_ref, *refs):
        step = pl.program_id(0)
        kept_ref, given_ref = refs[paired : paired + 2]
        if extra:

            @pl.when(step == 0)
            def _():
                refs[-1][...] = refs[0][...].T

        if fresh:
            turn_refs = refs[paired + 2 : paired + 4]

            @pl.when(step == 0)
            def _():
                turn_refs[0][...] = n_ref[...].T
                turn_refs[1][...] = nt_ref[...].T

        else:
            turn_refs = (n_ref, nt_ref)

        def rows(which, ref):
            return ref[pl.ds(pl.multiple_of(which * half, half), half), :]

        for which, out_ref in ((side_ref[0], kept_ref), (1 - side_ref[0], given_ref)):

            @pl.when(step < each)
            def _():
                out_ref[...] = dot(rows(which, turn_refs[0]), d_ref[0]).astype(bf16)

            @pl.when((step >= each) & (step < 3 * each))
            def _():
                out_ref[...] = (
                    dot(rows(which, turn_refs[0]), d_ref[0])
                    + dot(rows(which, turn_refs[1]), dt_ref[0])
                ).astype(bf16)

            if extra:

                @pl.when(step >= 3 * each)
                def _():
                    out_ref[...] = dot(rows(which, refs[-1]), refs[1][...]).astype(bf16)

    column = lambda i: jnp.where(i < 3 * each, i % each, each - 1)
    fixed = lambda matrix: pl.BlockSpec(matrix.shape, lambda i: (0, 0))
    in_specs = [
        pl.BlockSpec(memory_space=pltpu.SMEM),
        fixed(turned[0]),
        fixed(turned[1]),
        pl.BlockSpec((1, L, tile), lambda i: (jnp.minimum(i // each, 2), 0, column(i))),
        pl.BlockSpec((1, HALF, tile), lambda i: (jnp.clip(i // each - 1, 0, 1), 0, column(i))),
    ]
    operands = [side, *turned, d, d_tail]
    if extra:
        in_specs.append(fixed(pair[0]))
        in_specs.append(pl.BlockSpec((L, tile), lambda i: (0, jnp.maximum(i - 3 * each, 0))))
        operands += pair
    steps = 3 * each + extra
    shapes = [jax.ShapeDtypeStruct((half, steps * tile), bf16)] * 2
    specs = [pl.BlockSpec((half, tile), lambda i: (0, i))] * 2
    if fresh:
        turns = [jax.ShapeDtypeStruct((D, L), bf16), jax.ShapeDtypeStruct((D, HALF), bf16)]
        shapes, specs = shapes + turns, specs + [fixed(turn) for turn in turns]
    kept, given, *turns = pl.pallas_call(
        kernel,
        grid=(steps,),
        in_specs=in_specs,
        out_specs=specs,
        out_shape=shapes,
        scratch_shapes=[pltpu.VMEM((D, L), bf16)] if extra else [],
        cost_estimate=pl.CostEstimate(
            flops=8 * L * D * width, bytes_accessed=8 * D * width, transcendentals=0
        ),
        name="weight_grads",
    )(*operands)
    return kept, given, turns or turned


def split_sum(kept, got, number, count):
    size = kept.shape[0] // count

    def kernel(number_ref, kept_ref, got_ref, *outs):
        for q, out_ref in enumerate(outs):
            rows = pl.ds(pl.multiple_of((number_ref[0] ^ q) * size, size), size)
            out_ref[...] = (kept_ref[rows, :].astype(f32) + got_ref[rows, :].astype(f32)).astype(
                out_ref.dtype
            )

    whole = lambda matrix: pl.BlockSpec(matrix.shape, lambda: (0, 0))
    out = jax.ShapeDtypeStruct((size, kept.shape[1]), kept.dtype)
    return pl.pallas_call(
        kernel,
        in_specs=[pl.BlockSpec(memory_space=pltpu.SMEM), whole(kept), whole(got)],
        out_specs=[whole(out)] * count,
        out_shape=[out] * count,
        cost_estimate=HIDDEN,
        name="split_sum",
    )(number.reshape(1), kept, got)


def shards(
    inputs,
    doc_lengths,
    ln1_gain,
    ln1_bias,
    attn_in,
    qv_bias,
    attn_out,
    attn_out_bias,
    ln2_gain,
    second_norm_bias,
    mlp_in,
    mlp_in_bias,
    mlp_out,
    mlp_out_bias,
    cotangent,
):
    n_mlp = lax.axis_size("mlp")
    place = lax.axis_index("mlp")
    gain_one = ln1_gain.astype(f32)
    bias_one = ln1_bias.astype(f32)
    gain_two = ln2_gain.astype(f32)
    bias_two = second_norm_bias.astype(f32)

    tail = rotated(inputs[HALF:], "mlp", 1)
    tail_lengths = rotated(doc_lengths, "mlp", 1)
    cotangents = [cotangent] + [rotated(cotangent, "mlp", by) for by in range(1, n_mlp)]

    activations = inputs.astype(f32)
    normed = layer_norm(activations, gain_one, bias_one).astype(bf16)
    zeros = jnp.zeros((D,), f32)
    qkv_bias = jnp.concatenate([qv_bias[0].astype(f32), zeros, qv_bias[1].astype(f32)])
    qkv = (dot(normed, attn_in) + qkv_bias).astype(bf16)
    rows = jnp.concatenate(
        [
            jnp.stack(
                [
                    attn_out_bias.astype(f32),
                    gain_two,
                    bias_two,
                    gain_one,
                    bias_one,
                    qv_bias[1].astype(f32),
                ]
            ),
            jnp.zeros((2, D), f32),
        ]
    )
    local, lse_local, mixture, middle, normed_two, sent = local_attention(
        doc_lengths, qkv, attn_out, inputs, rows
    )
    steps = range(1, n_mlp)
    arrived_hi = [rotated(sent, "mlp", by) for by in steps]

    normed_tail, tail_kv = tail_projection(tail, rows, attn_in)
    reads = jnp.where(place == 0, 0, doc_lengths[:, :1])
    tail_kv, *cotangents[1:] = fence((tail_kv, *cotangents[1:]))
    mixture, mem_k, mem_v, lse_mem, middle, normed_two, basis_t, sent = memory_attention(
        reads,
        tail_lengths,
        qkv,
        tail_kv,
        rows,
        local,
        attn_out,
        inputs,
        rows,
        mixture,
        middle,
        normed_two,
    )
    arrived_lo = [rotated(sent, "mlp", by) for by in steps]
    mem_k, arrived_hi = fence((mem_k, arrived_hi))

    bias_rows = jnp.broadcast_to(mlp_in_bias.astype(f32), (8, mlp_in.shape[1]))
    kept = ()
    d_mlp_in_bias = 0.0
    returned_y, returned_dx = [], []
    calls = [(by, part) for by in steps for part in (1, 0)]
    for by, part in calls:
        block = (arrived_lo, arrived_hi)[part][by - 1]
        hidden, d_pre, d_bias, y, dx = mlp_block(
            block, cotangents[by], part, mlp_in, bias_rows, mlp_out, n_mlp * L, 2 * by + part, kept
        )
        kept = (hidden, d_pre)
        d_mlp_in_bias = d_mlp_in_bias + d_bias[0]
        returned_dx.append(rotated(dx, "mlp", -by))
        returned_y.append(y)
    hidden, d_pre, d_bias, y_own, dx_own = mlp_block(
        normed_two, cotangent, 0, mlp_in, bias_rows, mlp_out, n_mlp * L, 0, kept
    )
    d_mlp_in_bias = d_mlp_in_bias + d_bias[0]
    hidden, d_pre, returned_dx = fence((hidden, d_pre, returned_dx))
    over_rows = lambda a, b: lax.dot_general(
        a, b, (((0,), (0,)), ((), ())), preferred_element_type=f32
    )
    all_rows = jnp.concatenate(
        [normed_two] + [piece for pair in zip(arrived_lo, arrived_hi) for piece in pair], axis=0
    )
    d_mlp_in = over_rows(all_rows, d_pre).astype(bf16)
    d_mlp_out = over_rows(hidden, jnp.concatenate(cotangents, axis=0)).astype(bf16)

    hidden_count = mlp_in.shape[1]
    mlp_count = n_mlp.bit_length() - 1
    batch_count = lax.axis_size("batch").bit_length() - 1
    mlp_bits = list(range(mlp_count))
    core = [[mlp_count]]
    rest = list(range(mlp_count + 1, mlp_count + batch_count))
    groups = core + [mlp_bits[:1] + rest[:1]] + [[bit] for bit in mlp_bits[1:] + rest[1:]]

    d_mlp_in, d_mlp_out = lax.psum((d_mlp_in, d_mlp_out), "batch")

    def finish():
        shares = [[dx for (by, part), dx in zip(calls, returned_dx) if part == half] for half in (0, 1)]
        d_middle, d_branch, middle_sums = middle_backward(dx_own, shares, cotangent, middle, rows)
        backward = lambda first, pairs, d: attention_backward(
            first, pairs, doc_lengths, qkv, mem_k, mem_v, d, attn_out, lse_local, lse_mem, basis_t
        )
        early = PAIRS // 3
        side = place_in(core[0]).reshape(1)
        d_one, d_tail_one, sums_one = backward(0, early, d_branch)
        kept, given, turned = weight_grads(
            (normed, normed_tail), d_one, d_tail_one, (mixture, d_branch), side
        )
        chain_one = Chain(kept, given, groups)
        chain_one.fly()
        chain_one.land()
        d_branch, chain_one.given = fence((d_branch, chain_one.given))
        chain_one.fly()
        d_two, d_tail_two, sums_two = backward(early, PAIRS - early, d_branch)
        d_two, d_tail_two, chain_one.got = fence((d_two, d_tail_two, chain_one.got))
        chain_one.land()
        d_two, d_tail_two, chain_one.given = fence((d_two, d_tail_two, chain_one.given))
        chain_one.fly()
        kept, given, turned = weight_grads(turned, d_two, d_tail_two, None, side)
        chain_two = Chain(kept, given, groups)
        chain_two.fly()
        chain_two.land()
        d_one, d_two, d_tails, sums, later, chain_two.given = fence(
            (
                d_one,
                d_two,
                (d_tail_one, d_tail_two),
                (sums_one, sums_two),
                (d_mlp_in_bias, returned_y, y_own),
                chain_two.given,
            )
        )
        bias_grad, y_given, y_mine = later
        chain_two.fly()
        chain_one.got, unused = fence((chain_one.got, chain_two.given))
        chain_one.land()
        d_one, chain_one.given = fence((d_one, chain_one.given))
        chain_one.fly()
        d_normed, d_tail_rows, input_sums = qkv_backward(
            d_one, d_two, *d_tails, attn_in, inputs, tail
        )
        chain_one.got, chain_two.got, d_normed, d_tail_rows, input_sums = fence(
            (chain_one.got, chain_two.got, d_normed, d_tail_rows, input_sums)
        )
        chain_one.land()
        chain_one.fly()
        chain_two.land()
        chain_two.fly()
        shares = [
            jnp.concatenate([y for (by, part), y in zip(calls, y_given) if by == step][::-1], axis=0)
            for step in steps
        ]
        shares, unused = fence((shares, chain_two.given))
        returned = [rotated(y, "mlp", -step) for step, y in zip(steps, shares)]
        from_next = rotated(d_tail_rows, "mlp", -1)
        placed_bias = lax.dynamic_update_slice(
            jnp.zeros((n_mlp * hidden_count,), f32), bias_grad, (place * hidden_count,)
        )
        vectors = Total(
            jnp.concatenate(
                [
                    input_sums[:2],
                    middle_sums[:4],
                    jnp.concatenate(sums, axis=1)[:2],
                    placed_bias.reshape(-1, D),
                ],
                axis=0,
            ),
            core[0] + rest + mlp_bits,
        )
        vectors.fly()

        chains = {"one": chain_one, "two": chain_two, "all": vectors}
        held = {"one": 1, "two": 2, "all": 1}
        order = ["two", "one", "all"] * 2 + ["two", "all"] * 2 + ["one"]
        token = chain_two.given
        input_grad = layer_output = None
        turns = 0
        while any(chains[name].left() > held[name] or name in order for name in chains):
            for name in order:
                chain = chains[name]
                chain.got, token = fence((chain.got, token))
                turns += 1
                if turns == 7:
                    chain.got, returned = fence((chain.got, returned))
                if turns == 9:
                    input_grad = input_backward(d_normed, from_next, inputs, d_middle, rows)
                    chain.got, input_grad = fence((chain.got, input_grad))
                if turns == 11:
                    result = y_mine.astype(f32)
                    for y in returned:
                        result = result + y.astype(f32)
                    layer_output = (middle + (result + mlp_out_bias)).astype(bf16)
                    chain.got, layer_output = fence((chain.got, layer_output))
                chain.land()
                token = chain.given
                if chain.left() > held[name]:
                    chain.fly()
            order = [name for name in chains if chains[name].left() > held[name]]

        return chain_one.value, chain_two.value, vectors.value, input_grad, layer_output

    shapes = jax.eval_shape(finish)
    done = lax.cond(
        doc_lengths[0, 0] > 0,
        finish,
        lambda: jax.tree.map(lambda leaf: jnp.zeros(leaf.shape, leaf.dtype), shapes),
    )
    one, two, summed, input_grad, layer_output = done
    chain_two = Chain.gathering(two, [groups[1], core[0]])
    chain_two.fly()
    chain_one = Chain.gathering(one, core)
    chain_one.fly()
    vectors = Total(summed, mlp_bits[-1:])
    vectors.fly()
    d_mlp_in, d_mlp_out = widened(d_mlp_in, d_mlp_out)
    vectors.got, d_mlp_in, d_mlp_out = fence((vectors.got, d_mlp_in, d_mlp_out))
    vectors.land()
    bias_grad = lax.dynamic_slice(
        vectors.value[8:].reshape(-1), (place * hidden_count,), (hidden_count,)
    )
    summed = [vectors.value[i] for i in range(6)] + [vectors.value[6:8], bias_grad]
    chain_two.got, summed, d_mlp_in, d_mlp_out = fence(
        (chain_two.got, summed, d_mlp_in, d_mlp_out)
    )
    chain_two.land()
    chain_two.fly()
    chain_one.land()
    chain_two.land()

    width = PAIRS // 3 * LANES
    late = D - width
    d_attn_in = jnp.concatenate(
        [
            piece
            for i in range(3)
            for piece in (
                chain_one.value[:, i * width : (i + 1) * width],
                chain_two.value[:, i * late : (i + 1) * late],
            )
        ],
        axis=1,
    )
    return (
        layer_output,
        input_grad,
        summed[0],
        summed[1],
        d_attn_in.astype(f32),
        summed[6],
        chain_one.value[:, 3 * width :].astype(f32),
        summed[2],
        summed[3],
        summed[4],
        d_mlp_in,
        summed[7],
        d_mlp_out,
        summed[5],
    )


def solution(mesh):
    rows, whole = P(("batch", "mlp"), None), P()
    columns, hidden, depth = P(None, "mlp"), P("mlp"), P("mlp", None)
    return jax.shard_map(
        shards,
        mesh=mesh,
        in_specs=(rows, rows) + (whole,) * 8 + (columns, hidden, depth, whole, rows),
        out_specs=(rows, rows) + (whole,) * 8 + (columns, hidden, depth, whole),
        check_vma=False,
    )
```

```python
import jax
import jax.numpy as jnp
from jax import lax
from jax.experimental import pallas as pl
from jax.experimental.pallas import tpu as pltpu
from jax.sharding import PartitionSpec as P

D = 768
H = 12
HD = 64
NB = 512
L = 512
NDOC = 3
HALF = L // 2
PAIRS = H // 2
LANES = 2 * HD

LOG2E = 1.4426950408889634
SCORE_LOG2 = LOG2E * HD**-0.5
MASKED = -1e30

bf16 = jnp.bfloat16
f32 = jnp.float32


def dot(a, b):
    return jnp.dot(a, b, preferred_element_type=f32)


def dot_nt(a, b):
    return lax.dot_general(a, b, (((1,), (1,)), ((), ())), preferred_element_type=f32)


def layer_norm(matrix, gain_row, shift_row):
    center = jnp.mean(matrix, axis=-1, keepdims=True)
    centered = matrix - center
    spread = jnp.mean(centered * centered, axis=-1, keepdims=True)
    return centered * lax.rsqrt(spread + 1e-05) * gain_row + shift_row


def head_lanes(matrix, head):
    lane = lax.broadcasted_iota(jnp.int32, (1, LANES), 1)
    return jnp.where(lane // HD == head, matrix, jnp.zeros_like(matrix))


def fill_mask(lens, mask):
    key = lax.broadcasted_iota(jnp.int32, (L, L), 0)
    query = lax.broadcasted_iota(jnp.int32, (L, L), 1)
    one = lens[0, 0]
    two = one + lens[0, 1]
    start = jnp.where(query >= two, two, jnp.where(query >= one, one, 0))
    mask[...] = jnp.where((key <= query) & (key >= start), 0.0, MASKED)


def local_kernel(
    lens,
    q_ref,
    k_ref,
    v_ref,
    wo_ref,
    x_ref,
    rows_ref,
    out_ref,
    lse_ref,
    mix_ref,
    middle_ref,
    normed_ref,
    sent_ref,
    mask,
    turned,
    acc,
):
    step = pl.program_id(0)

    @pl.when(step == 0)
    def _():
        fill_mask(lens, mask)
        acc[...] = jnp.zeros_like(acc)

    q, k = q_ref[...], k_ref[...]
    v_t = v_ref[...].T
    for head in range(2):
        q_head = head_lanes(q, head)
        rows = slice(head * HD, (head + 1) * HD)
        for part in range(2):
            keys = HALF * (part + 1)
            cols = slice(part * HALF, (part + 1) * HALF)
            s = dot_nt(k[:keys], q_head[cols]) * SCORE_LOG2 + mask[:keys, cols]
            top = jnp.max(s, axis=0, keepdims=True)
            e = jnp.exp2(s - top)
            total = jnp.sum(e, axis=0, keepdims=True)
            out = dot(v_t[rows, :keys], e.astype(bf16))
            turned[rows, cols] = out / total
            lse_ref[0, head : head + 1, cols] = top + jnp.log2(total)
    out_ref[...] = turned[:, :HALF].T
    mixed = turned[:, HALF:].T.astype(bf16)
    mix_ref[...] = mixed
    acc[...] += dot(mixed, wo_ref[...])

    @pl.when(step == PAIRS - 1)
    def _():
        finish_middle(x_ref, acc, rows_ref, middle_ref, normed_ref, sent_ref)


def finish_middle(x_ref, acc, rows_ref, middle_ref, normed_ref, sent_ref):
    middle = x_ref[...].astype(f32) + (acc[...] + rows_ref[0:1])
    middle_ref[...] = middle
    normed = layer_norm(middle, rows_ref[1:2], rows_ref[2:3]).astype(bf16)
    normed_ref[...] = normed
    sent_ref[...] = normed


def local_attention(lens, qkv, attn_out, inputs, rows):
    column = lambda k: pl.BlockSpec((L, LANES), lambda i: (0, k * PAIRS + i))
    upper = pl.BlockSpec((HALF, D), lambda i: (1, 0))
    return pl.pallas_call(
        local_kernel,
        grid=(PAIRS,),
        in_specs=[
            pl.BlockSpec(memory_space=pltpu.SMEM),
            column(0),
            column(1),
            column(2),
            pl.BlockSpec((LANES, D), lambda i: (i, 0)),
            upper,
            pl.BlockSpec((8, D), lambda i: (0, 0)),
        ],
        out_specs=[
            pl.BlockSpec((HALF, LANES), lambda i: (0, i)),
            pl.BlockSpec((1, 8, L), lambda i: (i, 0, 0)),
            pl.BlockSpec((HALF, LANES), lambda i: (1, i)),
            upper,
            upper,
            pl.BlockSpec((HALF, D), lambda i: (0, 0)),
        ],
        out_shape=[
            jax.ShapeDtypeStruct((HALF, D), f32),
            jax.ShapeDtypeStruct((PAIRS, 8, L), f32),
            jax.ShapeDtypeStruct((L, D), bf16),
            jax.ShapeDtypeStruct((L, D), f32),
            jax.ShapeDtypeStruct((L, D), bf16),
            jax.ShapeDtypeStruct((HALF, D), bf16),
        ],
        scratch_shapes=[
            pltpu.VMEM((L, L), f32),
            pltpu.VMEM((LANES, L), f32),
            pltpu.VMEM((HALF, D), f32),
        ],
        cost_estimate=pl.CostEstimate(
            flops=H * 12 * HALF * HALF * 256, bytes_accessed=8 * L * D, transcendentals=H * L * L
        ),
        name="local_attention",
    )(lens, qkv, qkv, qkv, attn_out, inputs, rows)


def basis_rows(last_len, transposed):
    shape = (HALF, NB) if transposed else (NB, HALF)
    slot_dim, place_dim = (1, 0) if transposed else (0, 1)
    slot = lax.broadcasted_iota(jnp.int32, shape, slot_dim).astype(f32)
    place = lax.broadcasted_iota(jnp.int32, shape, place_dim).astype(f32)
    offsets = place - HALF + last_len + 0.5
    distances = (slot + 0.5) / NB * last_len - offsets
    weights = jnp.where(offsets > 0.0, jnp.exp(-0.5 * distances * distances), 0.0)
    return weights / jnp.sum(weights, axis=place_dim, keepdims=True)


def tail_projection(tail, rows, attn_in):
    tile = D // 2

    def kernel(x_ref, rows_ref, w_ref, normed_ref, kv_ref):
        @pl.when(pl.program_id(0) == 0)
        def _():
            normed_ref[...] = layer_norm(
                x_ref[...].astype(f32), rows_ref[3:4], rows_ref[4:5]
            ).astype(bf16)

        kv_ref[...] = dot(normed_ref[...], w_ref[...]).astype(bf16)

    fixed = lambda count: pl.BlockSpec((count, D), lambda i: (0, 0))
    return pl.pallas_call(
        kernel,
        grid=(4,),
        in_specs=[fixed(HALF), fixed(8), pl.BlockSpec((D, tile), lambda i: (0, 2 + i))],
        out_specs=[fixed(HALF), pl.BlockSpec((HALF, tile), lambda i: (0, i))],
        out_shape=[
            jax.ShapeDtypeStruct((HALF, D), bf16),
            jax.ShapeDtypeStruct((HALF, 2 * D), bf16),
        ],
        cost_estimate=pl.CostEstimate(
            flops=4 * HALF * D * D, bytes_accessed=4 * D * D, transcendentals=0
        ),
        name="tail_projection",
    )(tail, rows, attn_in)


def memory_kernel(
    reads,
    tail_lengths,
    q_ref,
    kt_ref,
    vt_ref,
    vb_ref,
    local_ref,
    wo_ref,
    x_ref,
    rows_ref,
    mix_whole,
    middle_whole,
    normed_whole,
    mix_ref,
    mk_ref,
    mv_ref,
    lse_ref,
    middle_ref,
    normed_ref,
    basis_t_ref,
    sent_ref,
    basis,
    turned,
    acc,
):
    step = pl.program_id(0)

    @pl.when(step == 0)
    def _():
        last_len = tail_lengths[0, NDOC - 1].astype(f32)
        basis[...] = basis_rows(last_len, False).astype(bf16)
        basis_t_ref[...] = basis_rows(last_len, True).astype(bf16)
        acc[...] = jnp.zeros_like(acc)

    mem_k = dot(basis[...], kt_ref[...]).astype(bf16)
    mem_v = (dot(basis[...], vt_ref[...]) + vb_ref[5:6]).astype(bf16)
    mk_ref[...] = mem_k
    mv_ref[...] = mem_v
    v_t = mem_v.T
    query = lax.broadcasted_iota(jnp.int32, (1, HALF), 1)
    reading = query < reads[0, 0]
    q = q_ref[...]
    for head in range(2):
        rows = slice(head * HD, (head + 1) * HD)
        s = dot_nt(mem_k, head_lanes(q, head)) * SCORE_LOG2
        top = jnp.max(s, axis=0, keepdims=True)
        e = jnp.exp2(s - top)
        total = jnp.sum(e, axis=0, keepdims=True)
        out = dot(v_t[rows], e.astype(bf16))
        turned[rows, :] = jnp.where(reading, out / total, 0.0)
        lse_ref[0, head : head + 1, :] = jnp.where(reading, top + jnp.log2(total), -MASKED)
    mixed = (local_ref[...] + turned[...].T).astype(bf16)
    mix_ref[...] = mixed
    acc[...] += dot(mixed, wo_ref[...])

    @pl.when(step == PAIRS - 1)
    def _():
        finish_middle(x_ref, acc, rows_ref, middle_ref, normed_ref, sent_ref)


def memory_attention(
    reads, tail_lengths, qkv, tail_kv, value_bias, local, attn_out, inputs, rows, mixture, middle, normed
):
    whole = lambda shape: pl.BlockSpec(shape, lambda i: (0,) * len(shape))
    untouched = pl.BlockSpec(memory_space=pl.ANY)
    return pl.pallas_call(
        memory_kernel,
        grid=(PAIRS,),
        in_specs=[
            pl.BlockSpec(memory_space=pltpu.SMEM),
            pl.BlockSpec(memory_space=pltpu.SMEM),
            pl.BlockSpec((HALF, LANES), lambda i: (0, i)),
            pl.BlockSpec((HALF, LANES), lambda i: (0, i)),
            pl.BlockSpec((HALF, LANES), lambda i: (0, PAIRS + i)),
            pl.BlockSpec((8, LANES), lambda i: (0, i)),
            pl.BlockSpec((HALF, LANES), lambda i: (0, i)),
            pl.BlockSpec((LANES, D), lambda i: (i, 0)),
            whole((HALF, D)),
            whole((8, D)),
            untouched,
            untouched,
            untouched,
        ],
        out_specs=[
            pl.BlockSpec((HALF, LANES), lambda i: (0, i)),
            pl.BlockSpec((NB, LANES), lambda i: (0, i)),
            pl.BlockSpec((NB, LANES), lambda i: (0, i)),
            pl.BlockSpec((1, 8, HALF), lambda i: (i, 0, 0)),
            whole((HALF, D)),
            whole((HALF, D)),
            whole((HALF, NB)),
            whole((HALF, D)),
        ],
        out_shape=[
            jax.ShapeDtypeStruct((L, D), bf16),
            jax.ShapeDtypeStruct((NB, D), bf16),
            jax.ShapeDtypeStruct((NB, D), bf16),
            jax.ShapeDtypeStruct((PAIRS, 8, HALF), f32),
            jax.ShapeDtypeStruct((L, D), f32),
            jax.ShapeDtypeStruct((L, D), bf16),
            jax.ShapeDtypeStruct((HALF, NB), bf16),
            jax.ShapeDtypeStruct((HALF, D), bf16),
        ],
        scratch_shapes=[
            pltpu.VMEM((NB, HALF), bf16),
            pltpu.VMEM((LANES, HALF), f32),
            pltpu.VMEM((HALF, D), f32),
        ],
        input_output_aliases={10: 0, 11: 4, 12: 5},
        cost_estimate=pl.CostEstimate(
            flops=H * 16 * HALF * HALF * 256, bytes_accessed=16 * L * D, transcendentals=H * L * HALF
        ),
        name="memory_attention",
    )(
        reads,
        tail_lengths,
        qkv,
        tail_kv,
        tail_kv,
        value_bias,
        local,
        attn_out,
        inputs,
        rows,
        mixture,
        middle,
        normed,
    )


def mlp_kernel(x_ref, ct_ref, wi_ref, bi_ref, wo_ref, *refs):
    hid_ref, dpre_ref, bias_ref, y_ref, dx_ref, y_acc, dx_acc = refs[-7:]
    step = pl.program_id(0)
    pre = dot(x_ref[...], wi_ref[...]) + bi_ref[0:1]
    squared = pre * pre
    tanh = jnp.tanh(pre * (0.7978845608028654 + 0.7978845608028654 * 0.044715 * squared))
    half = 0.5 * pre
    hidden = (half + half * tanh).astype(bf16)
    slope = (
        0.5
        + 0.5 * tanh
        + half
        * (1.0 - tanh * tanh)
        * (0.7978845608028654 + 3 * 0.7978845608028654 * 0.044715 * squared)
    )
    d_pre = (slope * dot_nt(ct_ref[...], wo_ref[...])).astype(bf16)
    hid_ref[...] = hidden
    dpre_ref[...] = d_pre
    bias_ref[...] = jnp.broadcast_to(
        jnp.sum(d_pre.astype(f32), axis=0, keepdims=True), bias_ref.shape
    )
    y = dot(hidden, wo_ref[...])
    dx = dot_nt(d_pre, wi_ref[...])

    @pl.when(step == 0)
    def _():
        y_acc[...] = y
        dx_acc[...] = dx

    @pl.when(step > 0)
    def _():
        y_acc[...] += y
        dx_acc[...] += dx

    @pl.when(step == pl.num_programs(0) - 1)
    def _():
        y_ref[...] = y_acc[...].astype(bf16)
        dx_ref[...] = dx_acc[...].astype(bf16)


def mlp_block(rows, cotangent, part, mlp_in, bias_rows, mlp_out, total, place, kept):
    count, hidden = rows.shape[0], mlp_in.shape[1]
    tile = next(t for t in (768 if count <= HALF else 512, 384, 256, 128) if hidden % t == 0)
    fixed = pl.BlockSpec((count, D), lambda i: (0, 0))
    across = pl.BlockSpec((count, tile), lambda i: (place, i))
    return pl.pallas_call(
        mlp_kernel,
        grid=(hidden // tile,),
        in_specs=[
            fixed,
            pl.BlockSpec((count, D), lambda i: (part, 0)),
            pl.BlockSpec((D, tile), lambda i: (0, i)),
            pl.BlockSpec((8, tile), lambda i: (0, i)),
            pl.BlockSpec((tile, D), lambda i: (i, 0)),
        ]
        + [pl.BlockSpec(memory_space=pl.ANY)] * len(kept),
        out_specs=[across, across, pl.BlockSpec((8, tile), lambda i: (0, i)), fixed, fixed],
        out_shape=[
            jax.ShapeDtypeStruct((total, hidden), bf16),
            jax.ShapeDtypeStruct((total, hidden), bf16),
            jax.ShapeDtypeStruct((8, hidden), f32),
            jax.ShapeDtypeStruct((count, D), bf16),
            jax.ShapeDtypeStruct((count, D), bf16),
        ],
        scratch_shapes=[pltpu.VMEM((count, D), f32), pltpu.VMEM((count, D), f32)],
        input_output_aliases={5 + i: i for i in range(len(kept))},
        cost_estimate=pl.CostEstimate(
            flops=8 * count * D * hidden,
            bytes_accessed=4 * D * hidden + 4 * count * hidden + 8 * count * D,
            transcendentals=count * hidden,
        ),
        name="mlp_block",
    )(rows, cotangent, mlp_in, bias_rows, mlp_out, *kept)


def backward_kernel(
    lens,
    q_ref,
    k_ref,
    v_ref,
    mk_ref,
    mv_ref,
    db_ref,
    wo_ref,
    ll_ref,
    lm_ref,
    bt_ref,
    dqkv_ref,
    dtail_ref,
    sums_ref,
    mask,
    turned,
    dk_acc,
    dv_acc,
):
    @pl.when(pl.program_id(0) == 0)
    def _():
        fill_mask(lens, mask)

    q, k, v = q_ref[...], k_ref[...], v_ref[...]
    mem_k, mem_v = mk_ref[...], mv_ref[...]
    d_mix = dot_nt(db_ref[...], wo_ref[...]).astype(bf16)
    k_t, mk_t = k.T, mem_k.T
    d_mem_k = d_mem_v = None

    def one(keys, values, q_part, d_part, lse, extra):
        s = dot_nt(keys, q_part) * SCORE_LOG2
        if extra is not None:
            s = s + extra
        weights = jnp.exp2(s - lse)
        d_weights = dot_nt(values, d_part)
        inner = jnp.sum(weights * d_weights, axis=0, keepdims=True)
        d_scores = (weights * (d_weights - inner)).astype(bf16)
        return d_scores, dot(d_scores, q_part), dot(weights.astype(bf16), d_part)

    for head in range(2):
        rows = slice(head * HD, (head + 1) * HD)
        q_head, d_head = head_lanes(q, head), head_lanes(d_mix, head)
        for part in range(2):
            keys = HALF * (part + 1)
            cols = slice(part * HALF, (part + 1) * HALF)
            ds, dk, dv = one(
                k[:keys],
                v[:keys],
                q_head[cols],
                d_head[cols],
                ll_ref[0, head : head + 1, cols],
                mask[:keys, cols],
            )
            dq = dot(k_t[rows, :keys], ds)
            if part == 0:
                ds, d_key, d_value = one(
                    mem_k, mem_v, q_head[cols], d_head[cols], lm_ref[0, head : head + 1, :], None
                )
                dq = dq + dot(mk_t[rows], ds)
                d_mem_k = d_key if d_mem_k is None else d_mem_k + d_key
                d_mem_v = d_value if d_mem_v is None else d_mem_v + d_value
            turned[rows, cols] = dq
            if head == 0 and part == 0:
                dk_acc[:HALF] = dk
                dv_acc[:HALF] = dv
            elif head == 0:
                dk_acc[:HALF] += dk[:HALF]
                dv_acc[:HALF] += dv[:HALF]
                dk_acc[HALF:] = dk[HALF:]
                dv_acc[HALF:] = dv[HALF:]
            else:
                dk_acc[:keys] += dk
                dv_acc[:keys] += dv
    scale = HD**-0.5
    d_q = (turned[...].T * scale).astype(bf16)
    d_v = dv_acc[...].astype(bf16)
    dqkv_ref[0] = d_q
    dqkv_ref[1] = (dk_acc[...] * scale).astype(bf16)
    dqkv_ref[2] = d_v
    d_mem_k = (d_mem_k * scale).astype(bf16)
    d_mem_v = d_mem_v.astype(bf16)
    dtail_ref[0] = dot(bt_ref[...], d_mem_k).astype(bf16)
    dtail_ref[1] = dot(bt_ref[...], d_mem_v).astype(bf16)
    sums_ref[0:1] = jnp.sum(d_q.astype(f32), axis=0, keepdims=True)
    sums_ref[1:2] = jnp.sum(d_v.astype(f32), axis=0, keepdims=True) + jnp.sum(
        d_mem_v.astype(f32), axis=0, keepdims=True
    )


HIDDEN = pl.CostEstimate(flops=1000, bytes_accessed=1000, transcendentals=0)


def attention_backward(
    first, pairs, lens, qkv, mem_k, mem_v, d_branch, attn_out, lse_local, lse_mem, basis_t
):
    column = lambda k: pl.BlockSpec((L, LANES), lambda i: (0, k * PAIRS + first + i))
    whole = lambda shape: pl.BlockSpec(shape, lambda i: (0,) * len(shape))
    width = pairs * LANES
    return pl.pallas_call(
        backward_kernel,
        grid=(pairs,),
        in_specs=[
            pl.BlockSpec(memory_space=pltpu.SMEM),
            column(0),
            column(1),
            column(2),
            column(0),
            column(0),
            whole((L, D)),
            pl.BlockSpec((LANES, D), lambda i: (first + i, 0)),
            pl.BlockSpec((1, 8, L), lambda i: (first + i, 0, 0)),
            pl.BlockSpec((1, 8, HALF), lambda i: (first + i, 0, 0)),
            whole((HALF, NB)),
        ],
        out_specs=[
            pl.BlockSpec((3, L, LANES), lambda i: (0, 0, i)),
            pl.BlockSpec((2, HALF, LANES), lambda i: (0, 0, i)),
            pl.BlockSpec((8, LANES), lambda i: (0, i)),
        ],
        out_shape=[
            jax.ShapeDtypeStruct((3, L, width), bf16),
            jax.ShapeDtypeStruct((2, HALF, width), bf16),
            jax.ShapeDtypeStruct((8, width), f32),
        ],
        scratch_shapes=[
            pltpu.VMEM((L, L), f32),
            pltpu.VMEM((LANES, L), f32),
            pltpu.VMEM((L, LANES), f32),
            pltpu.VMEM((L, LANES), f32),
        ],
        cost_estimate=pl.CostEstimate(
            flops=2 * pairs * 56 * HALF * HALF * 256,
            bytes_accessed=20 * L * width,
            transcendentals=2 * pairs * L * L,
        ),
        name="attention_backward",
    )(lens, qkv, qkv, qkv, mem_k, mem_v, d_branch, attn_out, lse_local, lse_mem, basis_t)


def normalized(matrix):
    centered = matrix - jnp.mean(matrix, axis=-1, keepdims=True)
    scale = lax.rsqrt(jnp.mean(centered * centered, axis=-1, keepdims=True) + 1e-05)
    return centered * scale, scale


def norm_slope(unit, scale, grown):
    inner = jnp.mean(grown * unit, axis=-1, keepdims=True)
    return (grown - jnp.mean(grown, axis=-1, keepdims=True) - unit * inner) * scale


def column_sum(matrix):
    return jnp.sum(matrix, axis=0, keepdims=True)


def middle_backward(d_own, returned, cotangent, middle, rows):
    count = len(returned[0])

    def kernel(d_ref, ct_ref, middle_ref, rows_ref, *refs):
        shares = refs[: 2 * count]
        d_middle_ref, d_branch_ref, sums_ref = refs[2 * count :]
        part = pl.program_id(0)
        total = d_ref[...].astype(f32)
        for i in range(count):
            total = total + jnp.where(part == 0, shares[i][...], shares[count + i][...]).astype(f32)
        upstream = ct_ref[...].astype(f32)
        unit, scale = normalized(middle_ref[...])
        d_middle = upstream + norm_slope(unit, scale, total * rows_ref[1:2])
        d_branch = d_middle.astype(bf16)
        d_middle_ref[...] = d_middle
        d_branch_ref[...] = d_branch
        sums = jnp.concatenate(
            [
                column_sum(d_branch.astype(f32)),
                column_sum(total * unit),
                column_sum(total),
                column_sum(upstream),
                jnp.zeros((4, D), f32),
            ],
            axis=0,
        )

        @pl.when(part == 0)
        def _():
            sums_ref[...] = sums

        @pl.when(part > 0)
        def _():
            sums_ref[...] += sums

    half = pl.BlockSpec((HALF, D), lambda i: (i, 0))
    fixed = pl.BlockSpec((HALF, D), lambda i: (0, 0))
    eight = pl.BlockSpec((8, D), lambda i: (0, 0))
    return pl.pallas_call(
        kernel,
        grid=(2,),
        in_specs=[half, half, half, eight] + [fixed] * (2 * count),
        out_specs=[half, half, eight],
        out_shape=[
            jax.ShapeDtypeStruct((L, D), f32),
            jax.ShapeDtypeStruct((L, D), bf16),
            jax.ShapeDtypeStruct((8, D), f32),
        ],
        cost_estimate=pl.CostEstimate(
            flops=20 * L * D, bytes_accessed=14 * L * D, transcendentals=0
        ),
        name="middle_backward",
    )(d_own, cotangent, middle, rows, *returned[0], *returned[1])


def qkv_backward(d_one, d_two, d_tail_one, d_tail_two, attn_in, inputs, tail_rows):
    cut = d_one.shape[2]

    def kernel(
        one_ref, two_ref, t_one_ref, t_two_ref, w_ref, x_ref, xt_ref, dn_ref, dt_ref, sums_ref, tail
    ):
        step = pl.program_id(0)
        left, right = w_ref[:, :cut], w_ref[:, cut:]
        part = dot_nt(one_ref[0], left) + dot_nt(two_ref[0], right)

        @pl.when(step == 0)
        def _():
            dn_ref[...] = part
            tail[...] = jnp.zeros_like(tail)

        @pl.when(step > 0)
        def _():
            dn_ref[...] += part
            tail[...] += dot_nt(t_one_ref[0], left) + dot_nt(t_two_ref[0], right)

        @pl.when(step == 2)
        def _():
            dt_ref[...] = tail[...].astype(bf16)
            unit, unused = normalized(x_ref[...].astype(f32))
            tail_unit, unused = normalized(xt_ref[...].astype(f32))
            sums_ref[0:1] = column_sum(dn_ref[...] * unit) + column_sum(tail[...] * tail_unit)
            sums_ref[1:2] = column_sum(dn_ref[...]) + column_sum(tail[...])

    fixed = lambda count: pl.BlockSpec((count, D), lambda i: (0, 0))
    return pl.pallas_call(
        kernel,
        grid=(3,),
        in_specs=[
            pl.BlockSpec((1, L, cut), lambda i: (i, 0, 0)),
            pl.BlockSpec((1, L, D - cut), lambda i: (i, 0, 0)),
            pl.BlockSpec((1, HALF, cut), lambda i: (jnp.maximum(i - 1, 0), 0, 0)),
            pl.BlockSpec((1, HALF, D - cut), lambda i: (jnp.maximum(i - 1, 0), 0, 0)),
            pl.BlockSpec((D, D), lambda i: (0, i)),
            fixed(L),
            fixed(HALF),
        ],
        out_specs=[fixed(L), fixed(HALF), fixed(8)],
        out_shape=[
            jax.ShapeDtypeStruct((L, D), f32),
            jax.ShapeDtypeStruct((HALF, D), bf16),
            jax.ShapeDtypeStruct((8, D), f32),
        ],
        scratch_shapes=[pltpu.VMEM((HALF, D), f32)],
        cost_estimate=pl.CostEstimate(
            flops=8 * L * D * D, bytes_accessed=20 * L * D, transcendentals=0
        ),
        name="qkv_backward",
    )(d_one, d_two, d_tail_one, d_tail_two, attn_in, inputs, tail_rows)


def input_backward(d_normed, from_next, inputs, d_middle, rows):
    def kernel(dn_ref, next_ref, x_ref, dm_ref, rows_ref, out_ref):
        unit, scale = normalized(x_ref[...].astype(f32))
        shared = jnp.where(pl.program_id(0) == 0, 0.0, next_ref[...].astype(f32))
        grown = (dn_ref[...] + shared) * rows_ref[3:4]
        out_ref[...] = (dm_ref[...] + norm_slope(unit, scale, grown)).astype(bf16)

    half = pl.BlockSpec((HALF, D), lambda i: (i, 0))
    return pl.pallas_call(
        kernel,
        grid=(2,),
        in_specs=[
            half,
            pl.BlockSpec((HALF, D), lambda i: (0, 0)),
            half,
            half,
            pl.BlockSpec((8, D), lambda i: (0, 0)),
        ],
        out_specs=half,
        out_shape=jax.ShapeDtypeStruct((L, D), bf16),
        cost_estimate=pl.CostEstimate(
            flops=20 * L * D, bytes_accessed=12 * L * D, transcendentals=0
        ),
        name="input_backward",
    )(d_normed, from_next, inputs, d_middle, rows)


def widened(first, second):
    steps = 6

    def kernel(a_ref, b_ref, a_out, b_out):
        a_out[...] = a_ref[...].astype(f32)
        b_out[...] = b_ref[...].astype(f32)

    specs = [
        pl.BlockSpec((matrix.shape[0] // steps, matrix.shape[1]), lambda i: (i, 0))
        for matrix in (first, second)
    ]
    return pl.pallas_call(
        kernel,
        grid=(steps,),
        in_specs=specs,
        out_specs=specs,
        out_shape=[jax.ShapeDtypeStruct(matrix.shape, f32) for matrix in (first, second)],
        cost_estimate=pl.CostEstimate(
            flops=0, bytes_accessed=6 * (first.size + second.size), transcendentals=0
        ),
        name="widened",
    )(first, second)


def rotated(value, axis, by):
    count = lax.axis_size(axis)
    return lax.ppermute(value, axis, [(i, (i + by) % count) for i in range(count)])


fence = lax.optimization_barrier
GRID = ("batch", "mlp")


def flipped(value, mask):
    count = lax.axis_size("batch") * lax.axis_size("mlp")
    return lax.ppermute(value, GRID, [(i, i ^ mask) for i in range(count)])


def place_in(bits):
    number = lax.axis_index(GRID)
    return sum(((number >> bit) & 1) << i for i, bit in enumerate(bits))


def peers(bits):
    return [sum(((q >> i) & 1) << bit for i, bit in enumerate(bits)) for q in range(1, 1 << len(bits))]


def grouped(bits):
    odd = len(bits) % 2
    return ([bits[:1]] if odd else []) + [bits[i : i + 2] for i in range(odd, len(bits), 2)]


class Chain:
    def __init__(self, kept, given, groups):
        self.stages = [(True, bits) for bits in groups] + [(False, bits) for bits in groups[::-1]]
        self.turn()
        self.kept, self.given = kept, [given]

    def left(self):
        return len(self.stages) + 1

    def turn(self):
        self.scatters, self.bits = self.stages.pop(0)
        self.place = place_in(self.bits)

    def prepare(self):
        self.turn()
        count = 1 << len(self.bits)
        if self.scatters:
            size = self.value.shape[0] // count
            piece = lambda i: lax.dynamic_slice_in_dim(self.value, i * size, size, 0)
            self.kept = piece(self.place)
            self.given = [piece(self.place ^ q) for q in range(1, count)]
        else:
            self.kept = self.value
            self.given = [self.value]

    def fly(self):
        masks = peers(self.bits)
        given = self.given if self.scatters else self.given * len(masks)
        self.got = [flipped(piece, mask) for piece, mask in zip(given, masks)]

    @classmethod
    def gathering(cls, value, groups):
        chain = cls.__new__(cls)
        chain.stages = [(False, bits) for bits in groups]
        chain.turn()
        chain.kept, chain.given = value, [value]
        return chain

    def land(self):
        if self.scatters and self.stages[0][0] and len(self.stages[0][1]) > 1:
            kept, got = self.kept, self.got[0]
            self.turn()
            self.kept, *self.given = split_sum(kept, got, self.place, 1 << len(self.bits))
            return True
        if self.scatters:
            total = self.kept.astype(f32)
            for piece in self.got:
                total = total + piece.astype(f32)
            self.value = total.astype(self.kept.dtype)
        else:
            pieces = [self.kept] + self.got
            order = [
                lax.select_n(self.place ^ i, *pieces)
                if len(pieces) > 2
                else jnp.where(self.place == i, *pieces)
                for i in range(len(pieces))
            ]
            self.value = jnp.concatenate(order, axis=0)
        if self.stages:
            self.prepare()
            return True
        return False


class Total:
    def __init__(self, value, bits):
        self.value, self.bits = value, list(bits)

    def fly(self):
        self.got = flipped(self.value, 1 << self.bits.pop(0))

    def land(self):
        self.value = self.value + self.got
        self.given = [self.value]

    def left(self):
        return len(self.bits)


def weight_grads(turned, d, d_tail, pair, side):
    width = d.shape[2]
    tile = width if pair is None else 256
    each = width // tile
    extra = 0 if pair is None else pair[1].shape[1] // tile
    paired = 2 if extra else 0
    half = D // 2
    fresh = turned[0].shape[0] == L

    def kernel(side_ref, n_ref, nt_ref, d_ref, dt_ref, *refs):
        step = pl.program_id(0)
        kept_ref, given_ref = refs[paired : paired + 2]
        if extra:

            @pl.when(step == 0)
            def _():
                refs[-1][...] = refs[0][...].T

        if fresh:
            turn_refs = refs[paired + 2 : paired + 4]

            @pl.when(step == 0)
            def _():
                turn_refs[0][...] = n_ref[...].T
                turn_refs[1][...] = nt_ref[...].T

        else:
            turn_refs = (n_ref, nt_ref)

        def rows(which, ref):
            return ref[pl.ds(pl.multiple_of(which * half, half), half), :]

        for which, out_ref in ((side_ref[0], kept_ref), (1 - side_ref[0], given_ref)):

            @pl.when(step < each)
            def _():
                out_ref[...] = dot(rows(which, turn_refs[0]), d_ref[0]).astype(bf16)

            @pl.when((step >= each) & (step < 3 * each))
            def _():
                out_ref[...] = (
                    dot(rows(which, turn_refs[0]), d_ref[0])
                    + dot(rows(which, turn_refs[1]), dt_ref[0])
                ).astype(bf16)

            if extra:

                @pl.when(step >= 3 * each)
                def _():
                    out_ref[...] = dot(rows(which, refs[-1]), refs[1][...]).astype(bf16)

    column = lambda i: jnp.where(i < 3 * each, i % each, each - 1)
    fixed = lambda matrix: pl.BlockSpec(matrix.shape, lambda i: (0, 0))
    in_specs = [
        pl.BlockSpec(memory_space=pltpu.SMEM),
        fixed(turned[0]),
        fixed(turned[1]),
        pl.BlockSpec((1, L, tile), lambda i: (jnp.minimum(i // each, 2), 0, column(i))),
        pl.BlockSpec((1, HALF, tile), lambda i: (jnp.clip(i // each - 1, 0, 1), 0, column(i))),
    ]
    operands = [side, *turned, d, d_tail]
    if extra:
        in_specs.append(fixed(pair[0]))
        in_specs.append(pl.BlockSpec((L, tile), lambda i: (0, jnp.maximum(i - 3 * each, 0))))
        operands += pair
    steps = 3 * each + extra
    shapes = [jax.ShapeDtypeStruct((half, steps * tile), bf16)] * 2
    specs = [pl.BlockSpec((half, tile), lambda i: (0, i))] * 2
    if fresh:
        turns = [jax.ShapeDtypeStruct((D, L), bf16), jax.ShapeDtypeStruct((D, HALF), bf16)]
        shapes, specs = shapes + turns, specs + [fixed(turn) for turn in turns]
    kept, given, *turns = pl.pallas_call(
        kernel,
        grid=(steps,),
        in_specs=in_specs,
        out_specs=specs,
        out_shape=shapes,
        scratch_shapes=[pltpu.VMEM((D, L), bf16)] if extra else [],
        cost_estimate=pl.CostEstimate(
            flops=8 * L * D * width, bytes_accessed=8 * D * width, transcendentals=0
        ),
        name="weight_grads",
    )(*operands)
    return kept, given, turns or turned


def split_sum(kept, got, number, count):
    size = kept.shape[0] // count

    def kernel(number_ref, kept_ref, got_ref, *outs):
        for q, out_ref in enumerate(outs):
            rows = pl.ds(pl.multiple_of((number_ref[0] ^ q) * size, size), size)
            out_ref[...] = (kept_ref[rows, :].astype(f32) + got_ref[rows, :].astype(f32)).astype(
                out_ref.dtype
            )

    whole = lambda matrix: pl.BlockSpec(matrix.shape, lambda: (0, 0))
    out = jax.ShapeDtypeStruct((size, kept.shape[1]), kept.dtype)
    return pl.pallas_call(
        kernel,
        in_specs=[pl.BlockSpec(memory_space=pltpu.SMEM), whole(kept), whole(got)],
        out_specs=[whole(out)] * count,
        out_shape=[out] * count,
        cost_estimate=HIDDEN,
        name="split_sum",
    )(number.reshape(1), kept, got)


def shards(
    inputs,
    doc_lengths,
    ln1_gain,
    ln1_bias,
    attn_in,
    qv_bias,
    attn_out,
    attn_out_bias,
    ln2_gain,
    second_norm_bias,
    mlp_in,
    mlp_in_bias,
    mlp_out,
    mlp_out_bias,
    cotangent,
):
    n_mlp = lax.axis_size("mlp")
    place = lax.axis_index("mlp")
    gain_one = ln1_gain.astype(f32)
    bias_one = ln1_bias.astype(f32)
    gain_two = ln2_gain.astype(f32)
    bias_two = second_norm_bias.astype(f32)

    tail = rotated(inputs[HALF:], "mlp", 1)
    tail_lengths = rotated(doc_lengths, "mlp", 1)
    cotangents = [cotangent] + [rotated(cotangent, "mlp", by) for by in range(1, n_mlp)]

    activations = inputs.astype(f32)
    normed = layer_norm(activations, gain_one, bias_one).astype(bf16)
    zeros = jnp.zeros((D,), f32)
    qkv_bias = jnp.concatenate([qv_bias[0].astype(f32), zeros, qv_bias[1].astype(f32)])
    qkv = (dot(normed, attn_in) + qkv_bias).astype(bf16)
    rows = jnp.concatenate(
        [
            jnp.stack(
                [
                    attn_out_bias.astype(f32),
                    gain_two,
                    bias_two,
                    gain_one,
                    bias_one,
                    qv_bias[1].astype(f32),
                ]
            ),
            jnp.zeros((2, D), f32),
        ]
    )
    local, lse_local, mixture, middle, normed_two, sent = local_attention(
        doc_lengths, qkv, attn_out, inputs, rows
    )
    steps = range(1, n_mlp)
    arrived_hi = [rotated(sent, "mlp", by) for by in steps]

    normed_tail, tail_kv = tail_projection(tail, rows, attn_in)
    reads = jnp.where(place == 0, 0, doc_lengths[:, :1])
    tail_kv, *cotangents[1:] = fence((tail_kv, *cotangents[1:]))
    mixture, mem_k, mem_v, lse_mem, middle, normed_two, basis_t, sent = memory_attention(
        reads,
        tail_lengths,
        qkv,
        tail_kv,
        rows,
        local,
        attn_out,
        inputs,
        rows,
        mixture,
        middle,
        normed_two,
    )
    arrived_lo = [rotated(sent, "mlp", by) for by in steps]
    mem_k, arrived_hi = fence((mem_k, arrived_hi))

    bias_rows = jnp.broadcast_to(mlp_in_bias.astype(f32), (8, mlp_in.shape[1]))
    kept = ()
    d_mlp_in_bias = 0.0
    returned_y, returned_dx = [], []
    calls = [(by, part) for by in steps for part in (1, 0)]
    for by, part in calls:
        block = (arrived_lo, arrived_hi)[part][by - 1]
        hidden, d_pre, d_bias, y, dx = mlp_block(
            block, cotangents[by], part, mlp_in, bias_rows, mlp_out, n_mlp * L, 2 * by + part, kept
        )
        kept = (hidden, d_pre)
        d_mlp_in_bias = d_mlp_in_bias + d_bias[0]
        returned_dx.append(rotated(dx, "mlp", -by))
        returned_y.append(y)
    hidden, d_pre, d_bias, y_own, dx_own = mlp_block(
        normed_two, cotangent, 0, mlp_in, bias_rows, mlp_out, n_mlp * L, 0, kept
    )
    d_mlp_in_bias = d_mlp_in_bias + d_bias[0]
    hidden, d_pre, returned_dx = fence((hidden, d_pre, returned_dx))
    over_rows = lambda a, b: lax.dot_general(
        a, b, (((0,), (0,)), ((), ())), preferred_element_type=f32
    )
    all_rows = jnp.concatenate(
        [normed_two] + [piece for pair in zip(arrived_lo, arrived_hi) for piece in pair], axis=0
    )
    d_mlp_in = over_rows(all_rows, d_pre).astype(bf16)
    d_mlp_out = over_rows(hidden, jnp.concatenate(cotangents, axis=0)).astype(bf16)

    hidden_count = mlp_in.shape[1]
    mlp_count = n_mlp.bit_length() - 1
    batch_count = lax.axis_size("batch").bit_length() - 1
    mlp_bits = list(range(mlp_count))
    core = [[mlp_count]]
    rest = list(range(mlp_count + 1, mlp_count + batch_count))
    groups = core + [mlp_bits[:1] + rest[:1]] + [[bit] for bit in mlp_bits[1:] + rest[1:]]

    d_mlp_in, d_mlp_out = lax.psum((d_mlp_in, d_mlp_out), "batch")

    def finish():
        shares = [[dx for (by, part), dx in zip(calls, returned_dx) if part == half] for half in (0, 1)]
        d_middle, d_branch, middle_sums = middle_backward(dx_own, shares, cotangent, middle, rows)
        backward = lambda first, pairs, d: attention_backward(
            first, pairs, doc_lengths, qkv, mem_k, mem_v, d, attn_out, lse_local, lse_mem, basis_t
        )
        early = PAIRS // 3
        side = place_in(core[0]).reshape(1)
        d_one, d_tail_one, sums_one = backward(0, early, d_branch)
        kept, given, turned = weight_grads(
            (normed, normed_tail), d_one, d_tail_one, (mixture, d_branch), side
        )
        chain_one = Chain(kept, given, groups)
        chain_one.fly()
        chain_one.land()
        d_branch, chain_one.given = fence((d_branch, chain_one.given))
        chain_one.fly()
        d_two, d_tail_two, sums_two = backward(early, PAIRS - early, d_branch)
        d_two, d_tail_two, chain_one.got = fence((d_two, d_tail_two, chain_one.got))
        chain_one.land()
        d_two, d_tail_two, chain_one.given = fence((d_two, d_tail_two, chain_one.given))
        chain_one.fly()
        kept, given, turned = weight_grads(turned, d_two, d_tail_two, None, side)
        chain_two = Chain(kept, given, groups)
        chain_two.fly()
        chain_two.land()
        d_one, d_two, d_tails, sums, later, chain_two.given = fence(
            (
                d_one,
                d_two,
                (d_tail_one, d_tail_two),
                (sums_one, sums_two),
                (d_mlp_in_bias, returned_y, y_own),
                chain_two.given,
            )
        )
        bias_grad, y_given, y_mine = later
        chain_two.fly()
        chain_one.got, unused = fence((chain_one.got, chain_two.given))
        chain_one.land()
        d_one, chain_one.given = fence((d_one, chain_one.given))
        chain_one.fly()
        d_normed, d_tail_rows, input_sums = qkv_backward(
            d_one, d_two, *d_tails, attn_in, inputs, tail
        )
        chain_one.got, chain_two.got, d_normed, d_tail_rows, input_sums = fence(
            (chain_one.got, chain_two.got, d_normed, d_tail_rows, input_sums)
        )
        chain_one.land()
        chain_one.fly()
        chain_two.land()
        chain_two.fly()
        y_given, unused = fence((y_given, chain_two.given))
        shares = [
            jnp.concatenate([y for (by, part), y in zip(calls, y_given) if by == step][::-1], axis=0)
            for step in steps
        ]
        returned = [rotated(y, "mlp", -step) for step, y in zip(steps, shares)]
        from_next = rotated(d_tail_rows, "mlp", -1)
        placed_bias = lax.dynamic_update_slice(
            jnp.zeros((n_mlp * hidden_count,), f32), bias_grad, (place * hidden_count,)
        )
        vectors = Total(
            jnp.concatenate(
                [
                    input_sums[:2],
                    middle_sums[:4],
                    jnp.concatenate(sums, axis=1)[:2],
                    placed_bias.reshape(-1, D),
                ],
                axis=0,
            ),
            core[0] + rest + mlp_bits,
        )
        vectors.fly()

        chains = {"one": chain_one, "two": chain_two, "all": vectors}
        held = {"one": 1, "two": 2, "all": 1}
        order = ["two", "one", "all"] * 2 + ["two", "all"] * 2 + ["one"]
        token = chain_two.given
        input_grad = layer_output = None
        turns = 0
        while any(chains[name].left() > held[name] or name in order for name in chains):
            for name in order:
                chain = chains[name]
                chain.got, token = fence((chain.got, token))
                turns += 1
                if turns == 7:
                    chain.got, returned = fence((chain.got, returned))
                if turns == 9:
                    input_grad = input_backward(d_normed, from_next, inputs, d_middle, rows)
                    chain.got, input_grad = fence((chain.got, input_grad))
                if turns == 11:
                    result = y_mine.astype(f32)
                    for y in returned:
                        result = result + y.astype(f32)
                    layer_output = (middle + (result + mlp_out_bias)).astype(bf16)
                    chain.got, layer_output = fence((chain.got, layer_output))
                chain.land()
                token = chain.given
                if chain.left() > held[name]:
                    chain.fly()
            order = [name for name in chains if chains[name].left() > held[name]]

        return chain_one.value, chain_two.value, vectors.value, input_grad, layer_output

    shapes = jax.eval_shape(finish)
    done = lax.cond(
        doc_lengths[0, 0] > 0,
        finish,
        lambda: jax.tree.map(lambda leaf: jnp.zeros(leaf.shape, leaf.dtype), shapes),
    )
    one, two, summed, input_grad, layer_output = done
    chain_two = Chain.gathering(two, [groups[1], core[0]])
    chain_two.fly()
    chain_one = Chain.gathering(one, core)
    chain_one.fly()
    vectors = Total(summed, mlp_bits[-1:])
    vectors.fly()
    d_mlp_in, d_mlp_out = widened(d_mlp_in, d_mlp_out)
    vectors.got, d_mlp_in, d_mlp_out = fence((vectors.got, d_mlp_in, d_mlp_out))
    vectors.land()
    bias_grad = lax.dynamic_slice(
        vectors.value[8:].reshape(-1), (place * hidden_count,), (hidden_count,)
    )
    summed = [vectors.value[i] for i in range(6)] + [vectors.value[6:8], bias_grad]
    chain_two.got, summed, d_mlp_in, d_mlp_out = fence(
        (chain_two.got, summed, d_mlp_in, d_mlp_out)
    )
    chain_two.land()
    chain_two.fly()
    chain_one.land()
    chain_two.land()

    width = PAIRS // 3 * LANES
    late = D - width
    d_attn_in = jnp.concatenate(
        [
            piece
            for i in range(3)
            for piece in (
                chain_one.value[:, i * width : (i + 1) * width],
                chain_two.value[:, i * late : (i + 1) * late],
            )
        ],
        axis=1,
    )
    return (
        layer_output,
        input_grad,
        summed[0],
        summed[1],
        d_attn_in.astype(f32),
        summed[6],
        chain_one.value[:, 3 * width :].astype(f32),
        summed[2],
        summed[3],
        summed[4],
        d_mlp_in,
        summed[7],
        d_mlp_out,
        summed[5],
    )


def solution(mesh):
    rows, whole = P(("batch", "mlp"), None), P()
    columns, hidden, depth = P(None, "mlp"), P("mlp"), P("mlp", None)
    return jax.shard_map(
        shards,
        mesh=mesh,
        in_specs=(rows, rows) + (whole,) * 8 + (columns, hidden, depth, whole, rows),
        out_specs=(rows, rows) + (whole,) * 8 + (columns, hidden, depth, whole),
        check_vma=False,
    )
```

```python
import jax
import jax.numpy as jnp
from jax import lax
from jax.experimental import pallas as pl
from jax.experimental.pallas import tpu as pltpu
from jax.sharding import PartitionSpec as P

D = 768
H = 12
HD = 64
NB = 512
L = 512
NDOC = 3
HALF = L // 2
PAIRS = H // 2
LANES = 2 * HD

LOG2E = 1.4426950408889634
SCORE_LOG2 = LOG2E * HD**-0.5
MASKED = -1e30

bf16 = jnp.bfloat16
f32 = jnp.float32


def dot(a, b):
    return jnp.dot(a, b, preferred_element_type=f32)


def dot_nt(a, b):
    return lax.dot_general(a, b, (((1,), (1,)), ((), ())), preferred_element_type=f32)


def layer_norm(matrix, gain_row, shift_row):
    center = jnp.mean(matrix, axis=-1, keepdims=True)
    centered = matrix - center
    spread = jnp.mean(centered * centered, axis=-1, keepdims=True)
    return centered * lax.rsqrt(spread + 1e-05) * gain_row + shift_row


def head_lanes(matrix, head):
    lane = lax.broadcasted_iota(jnp.int32, (1, LANES), 1)
    return jnp.where(lane // HD == head, matrix, jnp.zeros_like(matrix))


def fill_mask(lens, mask):
    key = lax.broadcasted_iota(jnp.int32, (L, L), 0)
    query = lax.broadcasted_iota(jnp.int32, (L, L), 1)
    one = lens[0, 0]
    two = one + lens[0, 1]
    start = jnp.where(query >= two, two, jnp.where(query >= one, one, 0))
    mask[...] = jnp.where((key <= query) & (key >= start), 0.0, MASKED)


def local_kernel(
    lens,
    q_ref,
    k_ref,
    v_ref,
    wo_ref,
    x_ref,
    rows_ref,
    out_ref,
    lse_ref,
    mix_ref,
    middle_ref,
    normed_ref,
    sent_ref,
    mask,
    turned,
    acc,
):
    step = pl.program_id(0)

    @pl.when(step == 0)
    def _():
        fill_mask(lens, mask)
        acc[...] = jnp.zeros_like(acc)

    q, k = q_ref[...], k_ref[...]
    v_t = v_ref[...].T
    for head in range(2):
        q_head = head_lanes(q, head)
        rows = slice(head * HD, (head + 1) * HD)
        for part in range(2):
            keys = HALF * (part + 1)
            cols = slice(part * HALF, (part + 1) * HALF)
            s = dot_nt(k[:keys], q_head[cols]) * SCORE_LOG2 + mask[:keys, cols]
            top = jnp.max(s, axis=0, keepdims=True)
            e = jnp.exp2(s - top)
            total = jnp.sum(e, axis=0, keepdims=True)
            out = dot(v_t[rows, :keys], e.astype(bf16))
            turned[rows, cols] = out / total
            lse_ref[0, head : head + 1, cols] = top + jnp.log2(total)
    out_ref[...] = turned[:, :HALF].T
    mixed = turned[:, HALF:].T.astype(bf16)
    mix_ref[...] = mixed
    acc[...] += dot(mixed, wo_ref[...])

    @pl.when(step == PAIRS - 1)
    def _():
        finish_middle(x_ref, acc, rows_ref, middle_ref, normed_ref, sent_ref)


def finish_middle(x_ref, acc, rows_ref, middle_ref, normed_ref, sent_ref):
    middle = x_ref[...].astype(f32) + (acc[...] + rows_ref[0:1])
    middle_ref[...] = middle
    normed = layer_norm(middle, rows_ref[1:2], rows_ref[2:3]).astype(bf16)
    normed_ref[...] = normed
    sent_ref[...] = normed


def local_attention(lens, qkv, attn_out, inputs, rows):
    column = lambda k: pl.BlockSpec((L, LANES), lambda i: (0, k * PAIRS + i))
    upper = pl.BlockSpec((HALF, D), lambda i: (1, 0))
    return pl.pallas_call(
        local_kernel,
        grid=(PAIRS,),
        in_specs=[
            pl.BlockSpec(memory_space=pltpu.SMEM),
            column(0),
            column(1),
            column(2),
            pl.BlockSpec((LANES, D), lambda i: (i, 0)),
            upper,
            pl.BlockSpec((8, D), lambda i: (0, 0)),
        ],
        out_specs=[
            pl.BlockSpec((HALF, LANES), lambda i: (0, i)),
            pl.BlockSpec((1, 8, L), lambda i: (i, 0, 0)),
            pl.BlockSpec((HALF, LANES), lambda i: (1, i)),
            upper,
            upper,
            pl.BlockSpec((HALF, D), lambda i: (0, 0)),
        ],
        out_shape=[
            jax.ShapeDtypeStruct((HALF, D), f32),
            jax.ShapeDtypeStruct((PAIRS, 8, L), f32),
            jax.ShapeDtypeStruct((L, D), bf16),
            jax.ShapeDtypeStruct((L, D), f32),
            jax.ShapeDtypeStruct((L, D), bf16),
            jax.ShapeDtypeStruct((HALF, D), bf16),
        ],
        scratch_shapes=[
            pltpu.VMEM((L, L), f32),
            pltpu.VMEM((LANES, L), f32),
            pltpu.VMEM((HALF, D), f32),
        ],
        cost_estimate=pl.CostEstimate(
            flops=H * 12 * HALF * HALF * 256, bytes_accessed=8 * L * D, transcendentals=H * L * L
        ),
        name="local_attention",
    )(lens, qkv, qkv, qkv, attn_out, inputs, rows)


def basis_rows(last_len, transposed):
    shape = (HALF, NB) if transposed else (NB, HALF)
    slot_dim, place_dim = (1, 0) if transposed else (0, 1)
    slot = lax.broadcasted_iota(jnp.int32, shape, slot_dim).astype(f32)
    place = lax.broadcasted_iota(jnp.int32, shape, place_dim).astype(f32)
    offsets = place - HALF + last_len + 0.5
    distances = (slot + 0.5) / NB * last_len - offsets
    weights = jnp.where(offsets > 0.0, jnp.exp(-0.5 * distances * distances), 0.0)
    return weights / jnp.sum(weights, axis=place_dim, keepdims=True)


def tail_projection(tail, rows, attn_in):
    tile = D // 2

    def kernel(x_ref, rows_ref, w_ref, normed_ref, kv_ref):
        @pl.when(pl.program_id(0) == 0)
        def _():
            normed_ref[...] = layer_norm(
                x_ref[...].astype(f32), rows_ref[3:4], rows_ref[4:5]
            ).astype(bf16)

        kv_ref[...] = dot(normed_ref[...], w_ref[...]).astype(bf16)

    fixed = lambda count: pl.BlockSpec((count, D), lambda i: (0, 0))
    return pl.pallas_call(
        kernel,
        grid=(4,),
        in_specs=[fixed(HALF), fixed(8), pl.BlockSpec((D, tile), lambda i: (0, 2 + i))],
        out_specs=[fixed(HALF), pl.BlockSpec((HALF, tile), lambda i: (0, i))],
        out_shape=[
            jax.ShapeDtypeStruct((HALF, D), bf16),
            jax.ShapeDtypeStruct((HALF, 2 * D), bf16),
        ],
        cost_estimate=pl.CostEstimate(
            flops=4 * HALF * D * D, bytes_accessed=4 * D * D, transcendentals=0
        ),
        name="tail_projection",
    )(tail, rows, attn_in)


def memory_kernel(
    reads,
    tail_lengths,
    q_ref,
    kt_ref,
    vt_ref,
    vb_ref,
    local_ref,
    wo_ref,
    x_ref,
    rows_ref,
    mix_whole,
    middle_whole,
    normed_whole,
    mix_ref,
    mk_ref,
    mv_ref,
    lse_ref,
    middle_ref,
    normed_ref,
    basis_t_ref,
    sent_ref,
    basis,
    turned,
    acc,
):
    step = pl.program_id(0)

    @pl.when(step == 0)
    def _():
        last_len = tail_lengths[0, NDOC - 1].astype(f32)
        basis[...] = basis_rows(last_len, False).astype(bf16)
        basis_t_ref[...] = basis_rows(last_len, True).astype(bf16)
        acc[...] = jnp.zeros_like(acc)

    mem_k = dot(basis[...], kt_ref[...]).astype(bf16)
    mem_v = (dot(basis[...], vt_ref[...]) + vb_ref[5:6]).astype(bf16)
    mk_ref[...] = mem_k
    mv_ref[...] = mem_v
    v_t = mem_v.T
    query = lax.broadcasted_iota(jnp.int32, (1, HALF), 1)
    reading = query < reads[0, 0]
    q = q_ref[...]
    for head in range(2):
        rows = slice(head * HD, (head + 1) * HD)
        s = dot_nt(mem_k, head_lanes(q, head)) * SCORE_LOG2
        top = jnp.max(s, axis=0, keepdims=True)
        e = jnp.exp2(s - top)
        total = jnp.sum(e, axis=0, keepdims=True)
        out = dot(v_t[rows], e.astype(bf16))
        turned[rows, :] = jnp.where(reading, out / total, 0.0)
        lse_ref[0, head : head + 1, :] = jnp.where(reading, top + jnp.log2(total), -MASKED)
    mixed = (local_ref[...] + turned[...].T).astype(bf16)
    mix_ref[...] = mixed
    acc[...] += dot(mixed, wo_ref[...])

    @pl.when(step == PAIRS - 1)
    def _():
        finish_middle(x_ref, acc, rows_ref, middle_ref, normed_ref, sent_ref)


def memory_attention(
    reads, tail_lengths, qkv, tail_kv, value_bias, local, attn_out, inputs, rows, mixture, middle, normed
):
    whole = lambda shape: pl.BlockSpec(shape, lambda i: (0,) * len(shape))
    untouched = pl.BlockSpec(memory_space=pl.ANY)
    return pl.pallas_call(
        memory_kernel,
        grid=(PAIRS,),
        in_specs=[
            pl.BlockSpec(memory_space=pltpu.SMEM),
            pl.BlockSpec(memory_space=pltpu.SMEM),
            pl.BlockSpec((HALF, LANES), lambda i: (0, i)),
            pl.BlockSpec((HALF, LANES), lambda i: (0, i)),
            pl.BlockSpec((HALF, LANES), lambda i: (0, PAIRS + i)),
            pl.BlockSpec((8, LANES), lambda i: (0, i)),
            pl.BlockSpec((HALF, LANES), lambda i: (0, i)),
            pl.BlockSpec((LANES, D), lambda i: (i, 0)),
            whole((HALF, D)),
            whole((8, D)),
            untouched,
            untouched,
            untouched,
        ],
        out_specs=[
            pl.BlockSpec((HALF, LANES), lambda i: (0, i)),
            pl.BlockSpec((NB, LANES), lambda i: (0, i)),
            pl.BlockSpec((NB, LANES), lambda i: (0, i)),
            pl.BlockSpec((1, 8, HALF), lambda i: (i, 0, 0)),
            whole((HALF, D)),
            whole((HALF, D)),
            whole((HALF, NB)),
            whole((HALF, D)),
        ],
        out_shape=[
            jax.ShapeDtypeStruct((L, D), bf16),
            jax.ShapeDtypeStruct((NB, D), bf16),
            jax.ShapeDtypeStruct((NB, D), bf16),
            jax.ShapeDtypeStruct((PAIRS, 8, HALF), f32),
            jax.ShapeDtypeStruct((L, D), f32),
            jax.ShapeDtypeStruct((L, D), bf16),
            jax.ShapeDtypeStruct((HALF, NB), bf16),
            jax.ShapeDtypeStruct((HALF, D), bf16),
        ],
        scratch_shapes=[
            pltpu.VMEM((NB, HALF), bf16),
            pltpu.VMEM((LANES, HALF), f32),
            pltpu.VMEM((HALF, D), f32),
        ],
        input_output_aliases={10: 0, 11: 4, 12: 5},
        cost_estimate=pl.CostEstimate(
            flops=H * 16 * HALF * HALF * 256, bytes_accessed=16 * L * D, transcendentals=H * L * HALF
        ),
        name="memory_attention",
    )(
        reads,
        tail_lengths,
        qkv,
        tail_kv,
        tail_kv,
        value_bias,
        local,
        attn_out,
        inputs,
        rows,
        mixture,
        middle,
        normed,
    )


def mlp_kernel(x_ref, ct_ref, wi_ref, bi_ref, wo_ref, *refs):
    hid_ref, dpre_ref, bias_ref, y_ref, dx_ref, y_acc, dx_acc = refs[-7:]
    step = pl.program_id(0)
    pre = dot(x_ref[...], wi_ref[...]) + bi_ref[0:1]
    squared = pre * pre
    tanh = jnp.tanh(pre * (0.7978845608028654 + 0.7978845608028654 * 0.044715 * squared))
    half = 0.5 * pre
    hidden = (half + half * tanh).astype(bf16)
    slope = (
        0.5
        + 0.5 * tanh
        + half
        * (1.0 - tanh * tanh)
        * (0.7978845608028654 + 3 * 0.7978845608028654 * 0.044715 * squared)
    )
    d_pre = (slope * dot_nt(ct_ref[...], wo_ref[...])).astype(bf16)
    hid_ref[...] = hidden
    dpre_ref[...] = d_pre
    bias_ref[...] = jnp.broadcast_to(
        jnp.sum(d_pre.astype(f32), axis=0, keepdims=True), bias_ref.shape
    )
    y = dot(hidden, wo_ref[...])
    dx = dot_nt(d_pre, wi_ref[...])

    @pl.when(step == 0)
    def _():
        y_acc[...] = y
        dx_acc[...] = dx

    @pl.when(step > 0)
    def _():
        y_acc[...] += y
        dx_acc[...] += dx

    @pl.when(step == pl.num_programs(0) - 1)
    def _():
        y_ref[...] = y_acc[...].astype(bf16)
        dx_ref[...] = dx_acc[...].astype(bf16)


def mlp_block(rows, cotangent, part, mlp_in, bias_rows, mlp_out, total, place, kept):
    count, hidden = rows.shape[0], mlp_in.shape[1]
    tile = next(t for t in (768 if count <= HALF else 512, 384, 256, 128) if hidden % t == 0)
    fixed = pl.BlockSpec((count, D), lambda i: (0, 0))
    across = pl.BlockSpec((count, tile), lambda i: (place, i))
    return pl.pallas_call(
        mlp_kernel,
        grid=(hidden // tile,),
        in_specs=[
            fixed,
            pl.BlockSpec((count, D), lambda i: (part, 0)),
            pl.BlockSpec((D, tile), lambda i: (0, i)),
            pl.BlockSpec((8, tile), lambda i: (0, i)),
            pl.BlockSpec((tile, D), lambda i: (i, 0)),
        ]
        + [pl.BlockSpec(memory_space=pl.ANY)] * len(kept),
        out_specs=[across, across, pl.BlockSpec((8, tile), lambda i: (0, i)), fixed, fixed],
        out_shape=[
            jax.ShapeDtypeStruct((total, hidden), bf16),
            jax.ShapeDtypeStruct((total, hidden), bf16),
            jax.ShapeDtypeStruct((8, hidden), f32),
            jax.ShapeDtypeStruct((count, D), bf16),
            jax.ShapeDtypeStruct((count, D), bf16),
        ],
        scratch_shapes=[pltpu.VMEM((count, D), f32), pltpu.VMEM((count, D), f32)],
        input_output_aliases={5 + i: i for i in range(len(kept))},
        cost_estimate=pl.CostEstimate(
            flops=8 * count * D * hidden,
            bytes_accessed=4 * D * hidden + 4 * count * hidden + 8 * count * D,
            transcendentals=count * hidden,
        ),
        name="mlp_block",
    )(rows, cotangent, mlp_in, bias_rows, mlp_out, *kept)


def backward_kernel(
    lens,
    q_ref,
    k_ref,
    v_ref,
    mk_ref,
    mv_ref,
    db_ref,
    wo_ref,
    ll_ref,
    lm_ref,
    bt_ref,
    dqkv_ref,
    dtail_ref,
    sums_ref,
    mask,
    turned,
    dk_acc,
    dv_acc,
):
    @pl.when(pl.program_id(0) == 0)
    def _():
        fill_mask(lens, mask)

    q, k, v = q_ref[...], k_ref[...], v_ref[...]
    mem_k, mem_v = mk_ref[...], mv_ref[...]
    d_mix = dot_nt(db_ref[...], wo_ref[...]).astype(bf16)
    k_t, mk_t = k.T, mem_k.T
    d_mem_k = d_mem_v = None

    def one(keys, values, q_part, d_part, lse, extra):
        s = dot_nt(keys, q_part) * SCORE_LOG2
        if extra is not None:
            s = s + extra
        weights = jnp.exp2(s - lse)
        d_weights = dot_nt(values, d_part)
        inner = jnp.sum(weights * d_weights, axis=0, keepdims=True)
        d_scores = (weights * (d_weights - inner)).astype(bf16)
        return d_scores, dot(d_scores, q_part), dot(weights.astype(bf16), d_part)

    for head in range(2):
        rows = slice(head * HD, (head + 1) * HD)
        q_head, d_head = head_lanes(q, head), head_lanes(d_mix, head)
        for part in range(2):
            keys = HALF * (part + 1)
            cols = slice(part * HALF, (part + 1) * HALF)
            ds, dk, dv = one(
                k[:keys],
                v[:keys],
                q_head[cols],
                d_head[cols],
                ll_ref[0, head : head + 1, cols],
                mask[:keys, cols],
            )
            dq = dot(k_t[rows, :keys], ds)
            if part == 0:
                ds, d_key, d_value = one(
                    mem_k, mem_v, q_head[cols], d_head[cols], lm_ref[0, head : head + 1, :], None
                )
                dq = dq + dot(mk_t[rows], ds)
                d_mem_k = d_key if d_mem_k is None else d_mem_k + d_key
                d_mem_v = d_value if d_mem_v is None else d_mem_v + d_value
            turned[rows, cols] = dq
            if head == 0 and part == 0:
                dk_acc[:HALF] = dk
                dv_acc[:HALF] = dv
            elif head == 0:
                dk_acc[:HALF] += dk[:HALF]
                dv_acc[:HALF] += dv[:HALF]
                dk_acc[HALF:] = dk[HALF:]
                dv_acc[HALF:] = dv[HALF:]
            else:
                dk_acc[:keys] += dk
                dv_acc[:keys] += dv
    scale = HD**-0.5
    d_q = (turned[...].T * scale).astype(bf16)
    d_v = dv_acc[...].astype(bf16)
    dqkv_ref[0] = d_q
    dqkv_ref[1] = (dk_acc[...] * scale).astype(bf16)
    dqkv_ref[2] = d_v
    d_mem_k = (d_mem_k * scale).astype(bf16)
    d_mem_v = d_mem_v.astype(bf16)
    dtail_ref[0] = dot(bt_ref[...], d_mem_k).astype(bf16)
    dtail_ref[1] = dot(bt_ref[...], d_mem_v).astype(bf16)
    sums_ref[0:1] = jnp.sum(d_q.astype(f32), axis=0, keepdims=True)
    sums_ref[1:2] = jnp.sum(d_v.astype(f32), axis=0, keepdims=True) + jnp.sum(
        d_mem_v.astype(f32), axis=0, keepdims=True
    )


HIDDEN = pl.CostEstimate(flops=1000, bytes_accessed=1000, transcendentals=0)


def attention_backward(
    first, pairs, lens, qkv, mem_k, mem_v, d_branch, attn_out, lse_local, lse_mem, basis_t
):
    column = lambda k: pl.BlockSpec((L, LANES), lambda i: (0, k * PAIRS + first + i))
    whole = lambda shape: pl.BlockSpec(shape, lambda i: (0,) * len(shape))
    width = pairs * LANES
    return pl.pallas_call(
        backward_kernel,
        grid=(pairs,),
        in_specs=[
            pl.BlockSpec(memory_space=pltpu.SMEM),
            column(0),
            column(1),
            column(2),
            column(0),
            column(0),
            whole((L, D)),
            pl.BlockSpec((LANES, D), lambda i: (first + i, 0)),
            pl.BlockSpec((1, 8, L), lambda i: (first + i, 0, 0)),
            pl.BlockSpec((1, 8, HALF), lambda i: (first + i, 0, 0)),
            whole((HALF, NB)),
        ],
        out_specs=[
            pl.BlockSpec((3, L, LANES), lambda i: (0, 0, i)),
            pl.BlockSpec((2, HALF, LANES), lambda i: (0, 0, i)),
            pl.BlockSpec((8, LANES), lambda i: (0, i)),
        ],
        out_shape=[
            jax.ShapeDtypeStruct((3, L, width), bf16),
            jax.ShapeDtypeStruct((2, HALF, width), bf16),
            jax.ShapeDtypeStruct((8, width), f32),
        ],
        scratch_shapes=[
            pltpu.VMEM((L, L), f32),
            pltpu.VMEM((LANES, L), f32),
            pltpu.VMEM((L, LANES), f32),
            pltpu.VMEM((L, LANES), f32),
        ],
        cost_estimate=pl.CostEstimate(
            flops=2 * pairs * 56 * HALF * HALF * 256,
            bytes_accessed=20 * L * width,
            transcendentals=2 * pairs * L * L,
        ),
        name="attention_backward",
    )(lens, qkv, qkv, qkv, mem_k, mem_v, d_branch, attn_out, lse_local, lse_mem, basis_t)


def normalized(matrix):
    centered = matrix - jnp.mean(matrix, axis=-1, keepdims=True)
    scale = lax.rsqrt(jnp.mean(centered * centered, axis=-1, keepdims=True) + 1e-05)
    return centered * scale, scale


def norm_slope(unit, scale, grown):
    inner = jnp.mean(grown * unit, axis=-1, keepdims=True)
    return (grown - jnp.mean(grown, axis=-1, keepdims=True) - unit * inner) * scale


def column_sum(matrix):
    return jnp.sum(matrix, axis=0, keepdims=True)


def middle_backward(d_own, returned, cotangent, middle, rows):
    count = len(returned[0])

    def kernel(d_ref, ct_ref, middle_ref, rows_ref, *refs):
        shares = refs[: 2 * count]
        d_middle_ref, d_branch_ref, sums_ref = refs[2 * count :]
        part = pl.program_id(0)
        total = d_ref[...].astype(f32)
        for i in range(count):
            total = total + jnp.where(part == 0, shares[i][...], shares[count + i][...]).astype(f32)
        upstream = ct_ref[...].astype(f32)
        unit, scale = normalized(middle_ref[...])
        d_middle = upstream + norm_slope(unit, scale, total * rows_ref[1:2])
        d_branch = d_middle.astype(bf16)
        d_middle_ref[...] = d_middle
        d_branch_ref[...] = d_branch
        sums = jnp.concatenate(
            [
                column_sum(d_branch.astype(f32)),
                column_sum(total * unit),
                column_sum(total),
                column_sum(upstream),
                jnp.zeros((4, D), f32),
            ],
            axis=0,
        )

        @pl.when(part == 0)
        def _():
            sums_ref[...] = sums

        @pl.when(part > 0)
        def _():
            sums_ref[...] += sums

    half = pl.BlockSpec((HALF, D), lambda i: (i, 0))
    fixed = pl.BlockSpec((HALF, D), lambda i: (0, 0))
    eight = pl.BlockSpec((8, D), lambda i: (0, 0))
    return pl.pallas_call(
        kernel,
        grid=(2,),
        in_specs=[half, half, half, eight] + [fixed] * (2 * count),
        out_specs=[half, half, eight],
        out_shape=[
            jax.ShapeDtypeStruct((L, D), f32),
            jax.ShapeDtypeStruct((L, D), bf16),
            jax.ShapeDtypeStruct((8, D), f32),
        ],
        cost_estimate=pl.CostEstimate(
            flops=20 * L * D, bytes_accessed=14 * L * D, transcendentals=0
        ),
        name="middle_backward",
    )(d_own, cotangent, middle, rows, *returned[0], *returned[1])


def qkv_backward(d_one, d_two, d_tail_one, d_tail_two, attn_in, inputs, tail_rows):
    cut = d_one.shape[2]

    def kernel(
        one_ref, two_ref, t_one_ref, t_two_ref, w_ref, x_ref, xt_ref, dn_ref, dt_ref, sums_ref, tail
    ):
        step = pl.program_id(0)
        left, right = w_ref[:, :cut], w_ref[:, cut:]
        part = dot_nt(one_ref[0], left) + dot_nt(two_ref[0], right)

        @pl.when(step == 0)
        def _():
            dn_ref[...] = part
            tail[...] = jnp.zeros_like(tail)

        @pl.when(step > 0)
        def _():
            dn_ref[...] += part
            tail[...] += dot_nt(t_one_ref[0], left) + dot_nt(t_two_ref[0], right)

        @pl.when(step == 2)
        def _():
            dt_ref[...] = tail[...].astype(bf16)
            unit, unused = normalized(x_ref[...].astype(f32))
            tail_unit, unused = normalized(xt_ref[...].astype(f32))
            sums_ref[0:1] = column_sum(dn_ref[...] * unit) + column_sum(tail[...] * tail_unit)
            sums_ref[1:2] = column_sum(dn_ref[...]) + column_sum(tail[...])

    fixed = lambda count: pl.BlockSpec((count, D), lambda i: (0, 0))
    return pl.pallas_call(
        kernel,
        grid=(3,),
        in_specs=[
            pl.BlockSpec((1, L, cut), lambda i: (i, 0, 0)),
            pl.BlockSpec((1, L, D - cut), lambda i: (i, 0, 0)),
            pl.BlockSpec((1, HALF, cut), lambda i: (jnp.maximum(i - 1, 0), 0, 0)),
            pl.BlockSpec((1, HALF, D - cut), lambda i: (jnp.maximum(i - 1, 0), 0, 0)),
            pl.BlockSpec((D, D), lambda i: (0, i)),
            fixed(L),
            fixed(HALF),
        ],
        out_specs=[fixed(L), fixed(HALF), fixed(8)],
        out_shape=[
            jax.ShapeDtypeStruct((L, D), f32),
            jax.ShapeDtypeStruct((HALF, D), bf16),
            jax.ShapeDtypeStruct((8, D), f32),
        ],
        scratch_shapes=[pltpu.VMEM((HALF, D), f32)],
        cost_estimate=pl.CostEstimate(
            flops=8 * L * D * D, bytes_accessed=20 * L * D, transcendentals=0
        ),
        name="qkv_backward",
    )(d_one, d_two, d_tail_one, d_tail_two, attn_in, inputs, tail_rows)


def input_backward(d_normed, from_next, inputs, d_middle, rows):
    def kernel(dn_ref, next_ref, x_ref, dm_ref, rows_ref, out_ref):
        unit, scale = normalized(x_ref[...].astype(f32))
        shared = jnp.where(pl.program_id(0) == 0, 0.0, next_ref[...].astype(f32))
        grown = (dn_ref[...] + shared) * rows_ref[3:4]
        out_ref[...] = (dm_ref[...] + norm_slope(unit, scale, grown)).astype(bf16)

    half = pl.BlockSpec((HALF, D), lambda i: (i, 0))
    return pl.pallas_call(
        kernel,
        grid=(2,),
        in_specs=[
            half,
            pl.BlockSpec((HALF, D), lambda i: (0, 0)),
            half,
            half,
            pl.BlockSpec((8, D), lambda i: (0, 0)),
        ],
        out_specs=half,
        out_shape=jax.ShapeDtypeStruct((L, D), bf16),
        cost_estimate=pl.CostEstimate(
            flops=20 * L * D, bytes_accessed=12 * L * D, transcendentals=0
        ),
        name="input_backward",
    )(d_normed, from_next, inputs, d_middle, rows)


def widened(first, second):
    steps = 6

    def kernel(a_ref, b_ref, a_out, b_out):
        a_out[...] = a_ref[...].astype(f32)
        b_out[...] = b_ref[...].astype(f32)

    specs = [
        pl.BlockSpec((matrix.shape[0] // steps, matrix.shape[1]), lambda i: (i, 0))
        for matrix in (first, second)
    ]
    return pl.pallas_call(
        kernel,
        grid=(steps,),
        in_specs=specs,
        out_specs=specs,
        out_shape=[jax.ShapeDtypeStruct(matrix.shape, f32) for matrix in (first, second)],
        cost_estimate=pl.CostEstimate(
            flops=0, bytes_accessed=6 * (first.size + second.size), transcendentals=0
        ),
        name="widened",
    )(first, second)


def rotated(value, axis, by):
    count = lax.axis_size(axis)
    return lax.ppermute(value, axis, [(i, (i + by) % count) for i in range(count)])


fence = lax.optimization_barrier
GRID = ("batch", "mlp")


def flipped(value, mask):
    count = lax.axis_size("batch") * lax.axis_size("mlp")
    return lax.ppermute(value, GRID, [(i, i ^ mask) for i in range(count)])


def place_in(bits):
    number = lax.axis_index(GRID)
    return sum(((number >> bit) & 1) << i for i, bit in enumerate(bits))


def peers(bits):
    return [sum(((q >> i) & 1) << bit for i, bit in enumerate(bits)) for q in range(1, 1 << len(bits))]


def grouped(bits):
    odd = len(bits) % 2
    return ([bits[:1]] if odd else []) + [bits[i : i + 2] for i in range(odd, len(bits), 2)]


class Chain:
    def __init__(self, kept, given, groups):
        self.stages = [(True, bits) for bits in groups] + [(False, bits) for bits in groups[::-1]]
        self.turn()
        self.kept, self.given = kept, [given]

    def left(self):
        return len(self.stages) + 1

    def turn(self):
        self.scatters, self.bits = self.stages.pop(0)
        self.place = place_in(self.bits)

    def prepare(self):
        self.turn()
        count = 1 << len(self.bits)
        if self.scatters:
            size = self.value.shape[0] // count
            piece = lambda i: lax.dynamic_slice_in_dim(self.value, i * size, size, 0)
            self.kept = piece(self.place)
            self.given = [piece(self.place ^ q) for q in range(1, count)]
        else:
            self.kept = self.value
            self.given = [self.value]

    def fly(self):
        masks = peers(self.bits)
        given = self.given if self.scatters else self.given * len(masks)
        self.got = [flipped(piece, mask) for piece, mask in zip(given, masks)]

    @classmethod
    def gathering(cls, value, groups):
        chain = cls.__new__(cls)
        chain.stages = [(False, bits) for bits in groups]
        chain.turn()
        chain.kept, chain.given = value, [value]
        return chain

    def land(self):
        if self.scatters and self.stages[0][0] and len(self.stages[0][1]) > 1:
            kept, got = self.kept, self.got[0]
            self.turn()
            self.kept, *self.given = split_sum(kept, got, self.place, 1 << len(self.bits))
            return True
        if self.scatters:
            total = self.kept.astype(f32)
            for piece in self.got:
                total = total + piece.astype(f32)
            self.value = total.astype(self.kept.dtype)
        else:
            pieces = [self.kept] + self.got
            order = [
                lax.select_n(self.place ^ i, *pieces)
                if len(pieces) > 2
                else jnp.where(self.place == i, *pieces)
                for i in range(len(pieces))
            ]
            self.value = jnp.concatenate(order, axis=0)
        if self.stages:
            self.prepare()
            return True
        return False


class Total:
    def __init__(self, value, bits):
        self.value, self.bits = value, list(bits)

    def fly(self):
        self.got = flipped(self.value, 1 << self.bits.pop(0))

    def land(self):
        self.value = self.value + self.got
        self.given = [self.value]

    def left(self):
        return len(self.bits)


def weight_grads(turned, d, d_tail, pair, side):
    width = d.shape[2]
    tile = width if pair is None else 256
    each = width // tile
    extra = 0 if pair is None else pair[1].shape[1] // tile
    paired = 2 if extra else 0
    half = D // 2
    fresh = turned[0].shape[0] == L

    def kernel(side_ref, n_ref, nt_ref, d_ref, dt_ref, *refs):
        step = pl.program_id(0)
        kept_ref, given_ref = refs[paired : paired + 2]
        if extra:

            @pl.when(step == 0)
            def _():
                refs[-1][...] = refs[0][...].T

        if fresh:
            turn_refs = refs[paired + 2 : paired + 4]

            @pl.when(step == 0)
            def _():
                turn_refs[0][...] = n_ref[...].T
                turn_refs[1][...] = nt_ref[...].T

        else:
            turn_refs = (n_ref, nt_ref)

        def rows(which, ref):
            return ref[pl.ds(pl.multiple_of(which * half, half), half), :]

        for which, out_ref in ((side_ref[0], kept_ref), (1 - side_ref[0], given_ref)):

            @pl.when(step < each)
            def _():
                out_ref[...] = dot(rows(which, turn_refs[0]), d_ref[0]).astype(bf16)

            @pl.when((step >= each) & (step < 3 * each))
            def _():
                out_ref[...] = (
                    dot(rows(which, turn_refs[0]), d_ref[0])
                    + dot(rows(which, turn_refs[1]), dt_ref[0])
                ).astype(bf16)

            if extra:

                @pl.when(step >= 3 * each)
                def _():
                    out_ref[...] = dot(rows(which, refs[-1]), refs[1][...]).astype(bf16)

    column = lambda i: jnp.where(i < 3 * each, i % each, each - 1)
    fixed = lambda matrix: pl.BlockSpec(matrix.shape, lambda i: (0, 0))
    in_specs = [
        pl.BlockSpec(memory_space=pltpu.SMEM),
        fixed(turned[0]),
        fixed(turned[1]),
        pl.BlockSpec((1, L, tile), lambda i: (jnp.minimum(i // each, 2), 0, column(i))),
        pl.BlockSpec((1, HALF, tile), lambda i: (jnp.clip(i // each - 1, 0, 1), 0, column(i))),
    ]
    operands = [side, *turned, d, d_tail]
    if extra:
        in_specs.append(fixed(pair[0]))
        in_specs.append(pl.BlockSpec((L, tile), lambda i: (0, jnp.maximum(i - 3 * each, 0))))
        operands += pair
    steps = 3 * each + extra
    shapes = [jax.ShapeDtypeStruct((half, steps * tile), bf16)] * 2
    specs = [pl.BlockSpec((half, tile), lambda i: (0, i))] * 2
    if fresh:
        turns = [jax.ShapeDtypeStruct((D, L), bf16), jax.ShapeDtypeStruct((D, HALF), bf16)]
        shapes, specs = shapes + turns, specs + [fixed(turn) for turn in turns]
    kept, given, *turns = pl.pallas_call(
        kernel,
        grid=(steps,),
        in_specs=in_specs,
        out_specs=specs,
        out_shape=shapes,
        scratch_shapes=[pltpu.VMEM((D, L), bf16)] if extra else [],
        cost_estimate=pl.CostEstimate(
            flops=8 * L * D * width, bytes_accessed=8 * D * width, transcendentals=0
        ),
        name="weight_grads",
    )(*operands)
    return kept, given, turns or turned


def split_sum(kept, got, number, count):
    size = kept.shape[0] // count

    def kernel(number_ref, kept_ref, got_ref, *outs):
        for q, out_ref in enumerate(outs):
            rows = pl.ds(pl.multiple_of((number_ref[0] ^ q) * size, size), size)
            out_ref[...] = (kept_ref[rows, :].astype(f32) + got_ref[rows, :].astype(f32)).astype(
                out_ref.dtype
            )

    whole = lambda matrix: pl.BlockSpec(matrix.shape, lambda: (0, 0))
    out = jax.ShapeDtypeStruct((size, kept.shape[1]), kept.dtype)
    return pl.pallas_call(
        kernel,
        in_specs=[pl.BlockSpec(memory_space=pltpu.SMEM), whole(kept), whole(got)],
        out_specs=[whole(out)] * count,
        out_shape=[out] * count,
        cost_estimate=HIDDEN,
        name="split_sum",
    )(number.reshape(1), kept, got)


def shards(
    inputs,
    doc_lengths,
    ln1_gain,
    ln1_bias,
    attn_in,
    qv_bias,
    attn_out,
    attn_out_bias,
    ln2_gain,
    second_norm_bias,
    mlp_in,
    mlp_in_bias,
    mlp_out,
    mlp_out_bias,
    cotangent,
):
    n_mlp = lax.axis_size("mlp")
    place = lax.axis_index("mlp")
    gain_one = ln1_gain.astype(f32)
    bias_one = ln1_bias.astype(f32)
    gain_two = ln2_gain.astype(f32)
    bias_two = second_norm_bias.astype(f32)

    tail = rotated(inputs[HALF:], "mlp", 1)
    tail_lengths = rotated(doc_lengths, "mlp", 1)
    cotangents = [cotangent] + [rotated(cotangent, "mlp", by) for by in range(1, n_mlp)]

    activations = inputs.astype(f32)
    normed = layer_norm(activations, gain_one, bias_one).astype(bf16)
    zeros = jnp.zeros((D,), f32)
    qkv_bias = jnp.concatenate([qv_bias[0].astype(f32), zeros, qv_bias[1].astype(f32)])
    qkv = (dot(normed, attn_in) + qkv_bias).astype(bf16)
    rows = jnp.concatenate(
        [
            jnp.stack(
                [
                    attn_out_bias.astype(f32),
                    gain_two,
                    bias_two,
                    gain_one,
                    bias_one,
                    qv_bias[1].astype(f32),
                ]
            ),
            jnp.zeros((2, D), f32),
        ]
    )
    local, lse_local, mixture, middle, normed_two, sent = local_attention(
        doc_lengths, qkv, attn_out, inputs, rows
    )
    steps = range(1, n_mlp)
    arrived_hi = [rotated(sent, "mlp", by) for by in steps]

    normed_tail, tail_kv = tail_projection(tail, rows, attn_in)
    reads = jnp.where(place == 0, 0, doc_lengths[:, :1])
    tail_kv, *cotangents[1:] = fence((tail_kv, *cotangents[1:]))
    mixture, mem_k, mem_v, lse_mem, middle, normed_two, basis_t, sent = memory_attention(
        reads,
        tail_lengths,
        qkv,
        tail_kv,
        rows,
        local,
        attn_out,
        inputs,
        rows,
        mixture,
        middle,
        normed_two,
    )
    arrived_lo = [rotated(sent, "mlp", by) for by in steps]
    mem_k, arrived_hi = fence((mem_k, arrived_hi))

    bias_rows = jnp.broadcast_to(mlp_in_bias.astype(f32), (8, mlp_in.shape[1]))
    kept = ()
    d_mlp_in_bias = 0.0
    returned_y, returned_dx = [], []
    calls = [(by, part) for by in steps for part in (1, 0)]
    for by, part in calls:
        block = (arrived_lo, arrived_hi)[part][by - 1]
        hidden, d_pre, d_bias, y, dx = mlp_block(
            block, cotangents[by], part, mlp_in, bias_rows, mlp_out, n_mlp * L, 2 * by + part, kept
        )
        kept = (hidden, d_pre)
        d_mlp_in_bias = d_mlp_in_bias + d_bias[0]
        returned_dx.append(rotated(dx, "mlp", -by))
        returned_y.append(y)
    hidden, d_pre, d_bias, y_own, dx_own = mlp_block(
        normed_two, cotangent, 0, mlp_in, bias_rows, mlp_out, n_mlp * L, 0, kept
    )
    d_mlp_in_bias = d_mlp_in_bias + d_bias[0]
    hidden, d_pre, returned_dx = fence((hidden, d_pre, returned_dx))
    over_rows = lambda a, b: lax.dot_general(
        a, b, (((0,), (0,)), ((), ())), preferred_element_type=f32
    )
    all_rows = jnp.concatenate(
        [normed_two] + [piece for pair in zip(arrived_lo, arrived_hi) for piece in pair], axis=0
    )
    d_mlp_in = over_rows(all_rows, d_pre).astype(bf16)
    d_mlp_out = over_rows(hidden, jnp.concatenate(cotangents, axis=0)).astype(bf16)

    hidden_count = mlp_in.shape[1]
    mlp_count = n_mlp.bit_length() - 1
    batch_count = lax.axis_size("batch").bit_length() - 1
    mlp_bits = list(range(mlp_count))
    core = [[mlp_count]]
    rest = list(range(mlp_count + 1, mlp_count + batch_count))
    groups = core + [mlp_bits[:1] + rest[:1]] + [[bit] for bit in mlp_bits[1:] + rest[1:]]

    d_mlp_in, d_mlp_out = lax.psum((d_mlp_in, d_mlp_out), "batch")

    def finish():
        shares = [[dx for (by, part), dx in zip(calls, returned_dx) if part == half] for half in (0, 1)]
        d_middle, d_branch, middle_sums = middle_backward(dx_own, shares, cotangent, middle, rows)
        backward = lambda first, pairs, d: attention_backward(
            first, pairs, doc_lengths, qkv, mem_k, mem_v, d, attn_out, lse_local, lse_mem, basis_t
        )
        early = PAIRS // 3
        side = place_in(core[0]).reshape(1)
        d_one, d_tail_one, sums_one = backward(0, early, d_branch)
        kept, given, turned = weight_grads(
            (normed, normed_tail), d_one, d_tail_one, (mixture, d_branch), side
        )
        chain_one = Chain(kept, given, groups)
        chain_one.fly()
        chain_one.land()
        d_branch, chain_one.given = fence((d_branch, chain_one.given))
        chain_one.fly()
        d_two, d_tail_two, sums_two = backward(early, PAIRS - early, d_branch)
        d_two, d_tail_two, chain_one.got = fence((d_two, d_tail_two, chain_one.got))
        chain_one.land()
        d_two, d_tail_two, chain_one.given = fence((d_two, d_tail_two, chain_one.given))
        chain_one.fly()
        kept, given, turned = weight_grads(turned, d_two, d_tail_two, None, side)
        chain_two = Chain(kept, given, groups)
        chain_two.fly()
        chain_two.land()
        d_one, d_two, d_tails, sums, later, chain_two.given = fence(
            (
                d_one,
                d_two,
                (d_tail_one, d_tail_two),
                (sums_one, sums_two),
                (d_mlp_in_bias, returned_y, y_own),
                chain_two.given,
            )
        )
        bias_grad, y_given, y_mine = later
        chain_two.fly()
        chain_one.got, unused = fence((chain_one.got, chain_two.given))
        chain_one.land()
        d_one, chain_one.given = fence((d_one, chain_one.given))
        chain_one.fly()
        d_normed, d_tail_rows, input_sums = qkv_backward(
            d_one, d_two, *d_tails, attn_in, inputs, tail
        )
        chain_one.got, chain_two.got, d_normed, d_tail_rows, input_sums = fence(
            (chain_one.got, chain_two.got, d_normed, d_tail_rows, input_sums)
        )
        chain_one.land()
        chain_one.fly()
        chain_two.land()
        chain_two.fly()
        y_given, unused = fence((y_given, chain_two.given))
        shares = [
            jnp.concatenate([y for (by, part), y in zip(calls, y_given) if by == step][::-1], axis=0)
            for step in steps
        ]
        returned = [rotated(y, "mlp", -step) for step, y in zip(steps, shares)]
        from_next = rotated(d_tail_rows, "mlp", -1)
        placed_bias = lax.dynamic_update_slice(
            jnp.zeros((n_mlp * hidden_count,), f32), bias_grad, (place * hidden_count,)
        )
        vectors = Total(
            jnp.concatenate(
                [
                    input_sums[:2],
                    middle_sums[:4],
                    jnp.concatenate(sums, axis=1)[:2],
                    placed_bias.reshape(-1, D),
                ],
                axis=0,
            ),
            core[0] + rest + mlp_bits,
        )
        vectors.fly()

        chains = {"one": chain_one, "two": chain_two, "all": vectors}
        held = {"one": 1, "two": 2, "all": 1}
        order = ["two", "one", "all"] * 2 + ["two", "all"] * 2 + ["one"]
        token = chain_two.given
        input_grad = layer_output = None
        turns = 0
        while any(chains[name].left() > held[name] or name in order for name in chains):
            for name in order:
                chain = chains[name]
                chain.got, token = fence((chain.got, token))
                turns += 1
                if turns == 9:
                    chain.got, returned = fence((chain.got, returned))
                if turns == 10:
                    input_grad = input_backward(d_normed, from_next, inputs, d_middle, rows)
                    chain.got, input_grad = fence((chain.got, input_grad))
                if turns == 11:
                    result = y_mine.astype(f32)
                    for y in returned:
                        result = result + y.astype(f32)
                    layer_output = (middle + (result + mlp_out_bias)).astype(bf16)
                    chain.got, layer_output = fence((chain.got, layer_output))
                chain.land()
                token = chain.given
                if chain.left() > held[name]:
                    chain.fly()
            order = [name for name in chains if chains[name].left() > held[name]]

        return chain_one.value, chain_two.value, vectors.value, input_grad, layer_output

    shapes = jax.eval_shape(finish)
    done = lax.cond(
        doc_lengths[0, 0] > 0,
        finish,
        lambda: jax.tree.map(lambda leaf: jnp.zeros(leaf.shape, leaf.dtype), shapes),
    )
    one, two, summed, input_grad, layer_output = done
    chain_two = Chain.gathering(two, [groups[1], core[0]])
    chain_two.fly()
    chain_one = Chain.gathering(one, core)
    chain_one.fly()
    vectors = Total(summed, mlp_bits[-1:])
    vectors.fly()
    d_mlp_in, d_mlp_out = widened(d_mlp_in, d_mlp_out)
    vectors.got, d_mlp_in, d_mlp_out = fence((vectors.got, d_mlp_in, d_mlp_out))
    vectors.land()
    bias_grad = lax.dynamic_slice(
        vectors.value[8:].reshape(-1), (place * hidden_count,), (hidden_count,)
    )
    summed = [vectors.value[i] for i in range(6)] + [vectors.value[6:8], bias_grad]
    chain_two.got, summed, d_mlp_in, d_mlp_out = fence(
        (chain_two.got, summed, d_mlp_in, d_mlp_out)
    )
    chain_two.land()
    chain_two.fly()
    chain_one.land()
    chain_two.land()

    width = PAIRS // 3 * LANES
    late = D - width
    d_attn_in = jnp.concatenate(
        [
            piece
            for i in range(3)
            for piece in (
                chain_one.value[:, i * width : (i + 1) * width],
                chain_two.value[:, i * late : (i + 1) * late],
            )
        ],
        axis=1,
    )
    return (
        layer_output,
        input_grad,
        summed[0],
        summed[1],
        d_attn_in.astype(f32),
        summed[6],
        chain_one.value[:, 3 * width :].astype(f32),
        summed[2],
        summed[3],
        summed[4],
        d_mlp_in,
        summed[7],
        d_mlp_out,
        summed[5],
    )


def solution(mesh):
    rows, whole = P(("batch", "mlp"), None), P()
    columns, hidden, depth = P(None, "mlp"), P("mlp"), P("mlp", None)
    return jax.shard_map(
        shards,
        mesh=mesh,
        in_specs=(rows, rows) + (whole,) * 8 + (columns, hidden, depth, whole, rows),
        out_specs=(rows, rows) + (whole,) * 8 + (columns, hidden, depth, whole),
        check_vma=False,
    )
```
